32 devices in a mesh: dp: 8 (over y, x, core), ctx: 4 (over z).
Axes of the slice: x: 2, y: 2, z: 4, core: 2. Of those that a mesh axis runs over, the one named last changes fastest.
Arguments:
- layer_input: bfloat16 [24, 2048, 1024], P('dp', 'ctx'), may hold values from -6 to 6
- segments: int32 [24, 2048], P('dp'), may hold values from 0 to 34, as said below
- positions: int32 [24, 2048], P('dp', 'ctx'), may hold values from 0 to 2047, as said below
- gain_one: bfloat16 [1024], P(('dp', 'ctx')), may hold values from 0.5 to 1.5
- w_in: bfloat16 [1024, 3352], P(('dp', 'ctx')), may hold values from -0.1875 to 0.1875
- conv_w: bfloat16 [4, 1792], P(None, ('dp', 'ctx')), may hold values from -3 to 3
- conv_b: bfloat16 [1792], P(('dp', 'ctx')), may hold values from -3 to 3
- head_params: float32 [3, 24], replicated, as said below
- gain_m: bfloat16 [1536], P(('dp', 'ctx')), may hold values from 0.5 to 1.5
- w_out: bfloat16 [1536, 1024], P(('dp', 'ctx')), may hold values from -0.15625 to 0.15625
- w_q: bfloat16 [1024, 512], P(('dp', 'ctx')), may hold values from -0.1875 to 0.1875
- w_k: bfloat16 [1024, 128], P(('dp', 'ctx')), may hold values from -0.1875 to 0.1875
- w_v: bfloat16 [1024, 128], P(('dp', 'ctx')), may hold values from -0.1875 to 0.1875
- w_o: bfloat16 [512, 1024], P(None, ('dp', 'ctx')), may hold values from -1 to 1
- gain_two: bfloat16 [1024], P(('dp', 'ctx')), may hold values from 0.5 to 1.5
- w_gate: bfloat16 [1024, 2048], P(('dp', 'ctx')), may hold values from -0.1875 to 0.1875
- w_up: bfloat16 [1024, 2048], P(('dp', 'ctx')), may hold values from -0.1875 to 0.1875
- w_down: bfloat16 [2048, 1024], P(('dp', 'ctx')), may hold values from -0.125 to 0.125
- cotangent: bfloat16 [24, 2048, 1024], P('dp', 'ctx'), may hold values from -6 to 6
Outputs:
- block_out: bfloat16 [24, 2048, 1024], P('dp', 'ctx')
- grad_input: bfloat16 [24, 2048, 1024], P('dp', 'ctx')
- grad_gain_one: float32 [1024], P(('dp', 'ctx'))
- grad_w_in: float32 [1024, 3352], P(('dp', 'ctx'))
- grad_conv_w: float32 [4, 1792], P(None, ('dp', 'ctx'))
- grad_conv_b: float32 [1792], P(('dp', 'ctx'))
- grad_head_params: float32 [3, 24], replicated
- grad_gain_m: float32 [1536], P(('dp', 'ctx'))
- grad_w_out: float32 [1536, 1024], P(('dp', 'ctx'))
- grad_w_q: float32 [1024, 512], P(('dp', 'ctx'))
- grad_w_k: float32 [1024, 128], P(('dp', 'ctx'))
- grad_w_v: float32 [1024, 128], P(('dp', 'ctx'))
- grad_w_o: float32 [512, 1024], P(None, ('dp', 'ctx'))
- grad_gain_two: float32 [1024], P(('dp', 'ctx'))
- grad_w_gate: float32 [1024, 2048], P(('dp', 'ctx'))
- grad_w_up: float32 [1024, 2048], P(('dp', 'ctx'))
- grad_w_down: float32 [2048, 1024], P(('dp', 'ctx'))
The draws below stay inside these ranges and needn't reach their ends.
Inputs may be any that keep to these rules, and one draw needn't show every extreme that they name: `segments`: segment numbers never fall along a sequence and start at 0; documents hold 60 to 800 tokens except a sequence's last one; one sequence among the 3 of each index of dp is a single document; one sequence holds only documents of 60 tokens. Within a document positions rise by one from token to token. `head_params`: row 0 holds logarithms of decay magnitudes, row 1 biases of the step sizes, row 2 skip weights.
All inputs are finite; a program needn't handle non-finite values.
Results may differ from the reference program's by a relative error of at most 0.019.
Values may be sent and summed in bfloat16 or wider, within the bound.
No kernel may reach another device: no remote copies, remote signals or barrier semaphores. Data moves between devices by JAX's collectives and lax.ppermute only.
A program may use at most 512 MiB of HBM per device.

```python
import jax
import jax.numpy as jnp
from jax import lax

D = 1024
MH = 24
MP = 64
NS = 128
KC = 4
QH = 8
KVH = 2
HD = 64
FF = 2048
SEQ_DEV = 3
DOC_MIN = 60
DOC_MAX = 800
DI = 1536
CC = 1792
INC = 3352
SPAN = 512
LEN = 2048
SEQS = 24
NDOCS = 35


def document_table(key):
    lengths = jax.random.randint(jax.random.fold_in(key, 11), (SEQS, NDOCS), DOC_MIN, DOC_MAX + 1)
    whole_pick = jax.random.randint(jax.random.fold_in(key, 12), (SEQS // SEQ_DEV,), 0, SEQ_DEV)
    seq_index = jnp.arange(SEQS)
    short_seq = (whole_pick[0] + 1) % SEQ_DEV
    lengths = jnp.where((seq_index == short_seq)[:, None], DOC_MIN, lengths)
    ends = jnp.cumsum(lengths, axis=1)
    places = jnp.arange(LEN, dtype=jnp.int32)
    seg_ids = jnp.sum((ends[:, None, :] <= places[None, :, None]).astype(jnp.int32), axis=2)
    chosen = seq_index % SEQ_DEV == jnp.repeat(whole_pick, SEQ_DEV)
    seg_ids = jnp.where(chosen[:, None], 0, seg_ids)
    starts = ends - lengths
    offsets = jax.random.randint(jax.random.fold_in(key, 13), (SEQS, NDOCS), 0, LEN - lengths + 1)
    offsets = jnp.where(chosen[:, None], 0, offsets)
    starts = jnp.where(chosen[:, None], 0, starts)
    one_hot = (seg_ids[:, :, None] == jnp.arange(NDOCS)[None, None, :]).astype(jnp.int32)
    doc_start = jnp.sum(one_hot * starts[:, None, :], axis=2)
    doc_offset = jnp.sum(one_hot * offsets[:, None, :], axis=2)
    positions = places[None, :] - doc_start + doc_offset
    return (seg_ids.astype(jnp.int32), positions.astype(jnp.int32))


def draw_segments(key, part):
    return document_table(key)[0]


def draw_positions(key, part):
    return document_table(key)[1]


def draw_head_params(key, part):
    head_pick = jax.random.randint(jax.random.fold_in(key, 21), (MH,), 0, 8)
    slow_heads = head_pick < 4
    spread = jax.random.uniform(jax.random.fold_in(key, 22), (MH,), jnp.float32, 0.5, 2.0)
    decay_log = jnp.where(slow_heads, jnp.log(spread / LEN), jnp.log(spread * 0.1))
    step_bias = jax.random.uniform(jax.random.fold_in(key, 23), (MH,), jnp.float32, -2.0, -0.5)
    skip_gain = jax.random.uniform(jax.random.fold_in(key, 24), (MH,), jnp.float32, 0.5, 1.5)
    return jnp.stack([decay_log, step_bias, skip_gain]).astype(jnp.float32)


def block_scale(own_key, shape, shards, smallest, high):
    loudness = 1.0
    for position, blocks in shards:
        heights = jax.random.uniform(jax.random.fold_in(jax.random.fold_in(own_key, 6), position), (blocks,), jnp.float32, smallest / len(shards), high / len(shards))
        loudness = loudness * jnp.repeat(jnp.exp(heights), shape[position] // blocks).reshape((-1,) + (1,) * (len(shape) - 1 - position))
    return loudness


def gaussian(stream_key, shape, scale, limit, split=(), kind=jnp.bfloat16):
    factor_of = block_scale(stream_key, shape, split, -0.22, 0.18) if split else 1.0
    result = jax.random.normal(stream_key, shape, jnp.float32) * scale * factor_of
    return jnp.minimum(jnp.maximum(result, -limit), limit).astype(kind)


def setup_inputs(seed: int = 0) -> dict:
    streams_of = jax.random.split(jax.random.key(seed), 20)
    layer_input = gaussian(streams_of[0], (SEQS, LEN, D), 1.0, 6.0, ((0, 8), (1, 4)))
    segments = draw_segments(jax.random.fold_in(streams_of[19], 71), 0)
    positions = draw_positions(jax.random.fold_in(streams_of[19], 71), 0)
    gain_one = jnp.clip(1.0 + 0.1 * jax.random.normal(streams_of[3], (D,), jnp.float32), 0.5, 1.5).astype(jnp.bfloat16)
    w_in = gaussian(streams_of[4], (D, INC), D ** -0.5, 0.1875, ((0, 32),))
    conv_w = gaussian(streams_of[5], (KC, CC), KC ** -0.5, 3.0, ((1, 32),))
    conv_b = gaussian(streams_of[6], (CC,), 0.5, 3.0, ((0, 32),))
    head_params = draw_head_params(jax.random.fold_in(streams_of[19], 71), 0)
    gain_m = jnp.clip(1.0 + 0.1 * jax.random.normal(streams_of[8], (DI,), jnp.float32), 0.5, 1.5).astype(jnp.bfloat16)
    w_out = gaussian(streams_of[9], (DI, D), DI ** -0.5, 0.15625, ((0, 32),))
    w_q = gaussian(streams_of[10], (D, QH * HD), D ** -0.5, 0.1875, ((0, 32),))
    w_k = gaussian(streams_of[11], (D, KVH * HD), D ** -0.5, 0.1875, ((0, 32),))
    w_v = gaussian(streams_of[12], (D, KVH * HD), D ** -0.5, 0.1875, ((0, 32),))
    w_o = gaussian(streams_of[13], (QH * HD, D), (QH * HD // 16) ** -0.5, 1.0, ((1, 32),))
    gain_two = jnp.clip(1.0 + 0.1 * jax.random.normal(streams_of[14], (D,), jnp.float32), 0.5, 1.5).astype(jnp.bfloat16)
    w_gate = gaussian(streams_of[15], (D, FF), D ** -0.5, 0.1875, ((0, 32),))
    w_up = gaussian(streams_of[16], (D, FF), D ** -0.5, 0.1875, ((0, 32),))
    w_down = gaussian(streams_of[17], (FF, D), FF ** -0.5, 0.125, ((0, 32),))
    cotangent = gaussian(streams_of[18], (SEQS, LEN, D), 1.0, 6.0, ((0, 8), (1, 4)))
    return {"layer_input": layer_input, "segments": segments, "positions": positions, "gain_one": gain_one, "w_in": w_in, "conv_w": conv_w, "conv_b": conv_b, "head_params": head_params, "gain_m": gain_m, "w_out": w_out, "w_q": w_q, "w_k": w_k, "w_v": w_v, "w_o": w_o, "gain_two": gain_two, "w_gate": w_gate, "w_up": w_up, "w_down": w_down, "cotangent": cotangent}


EPSILON = 1e-05
ROPE_BASE = 10000.0
MASKED = -1e+30
HIGHEST_PREC = lax.Precision.HIGHEST

@jax.custom_vjp
def low(v):
    return lax.optimization_barrier(v.astype(jnp.bfloat16)).astype(jnp.float32)

@jax.custom_vjp
def low_back(v):
    return v

def low_keep(v):
    return (low(v), None)

def low_pass(kept, grad):
    return (grad,)

def back_keep(v):
    return (v, None)

def back_low(kept, grad):
    return (low(grad),)
low.defvjp(low_keep, low_pass)
low_back.defvjp(back_keep, back_low)

def product_hi(left, right):
    return jnp.dot(left, right, precision=HIGHEST_PREC, preferred_element_type=jnp.float32)

def rms_scale(values, gain_vec):
    return values * lax.rsqrt(lax.optimization_barrier(jnp.mean(values * values, axis=-1, keepdims=True)) + EPSILON) * gain_vec

def rotary(values, places):
    half_width = values.shape[-1] // 2
    frequency = ROPE_BASE ** (-jnp.arange(half_width, dtype=jnp.float32) / half_width)
    angles = places.astype(jnp.float32)[..., None] * frequency
    cosine = jnp.cos(angles)[..., None, :]
    sine_part = jnp.sin(angles)[..., None, :]
    first_half = values[..., :half_width]
    second_half = values[..., half_width:]
    return jnp.concatenate([first_half * cosine - second_half * sine_part, second_half * cosine + first_half * sine_part], axis=-1)

def conv_silu(pre_conv, seg_ids, taps, shift):
    padded = jnp.concatenate([jnp.zeros((KC - 1, pre_conv.shape[1]), jnp.float32), pre_conv], axis=0)
    seg_pad = jnp.concatenate([jnp.full((KC - 1,), -1, jnp.int32), seg_ids.astype(jnp.int32)])
    total = shift
    for tap_idx in range(KC):
        tap_match = (seg_pad[tap_idx:tap_idx + LEN] == seg_ids).astype(jnp.float32)
        total = total + padded[tap_idx:tap_idx + LEN] * taps[tap_idx] * tap_match[:, None]
    return jax.nn.silu(total)

def ssm_block(skip_gain, carry_in, block_in):
    state, seg_prev = carry_in
    xs_block, b_block, c_block, step_size, log_decay, seg_ids = block_in
    count_len = seg_ids.shape[0]
    offsets = jnp.arange(count_len).astype(jnp.int32)
    pair_mask = (seg_ids[:, None] == seg_ids[None, :]) & (offsets[:, None] >= offsets[None, :])
    cumul = jnp.cumsum(log_decay, axis=0)
    differ = cumul[:, None, :] - cumul[None, :, :]
    inside = pair_mask[:, :, None]
    mixing = jnp.where(inside, jnp.exp(jnp.where(inside, differ, 0.0)), 0.0) * step_size[None, :, :]
    cross = low_back(product_hi(c_block, b_block.T))
    mix_low = low(cross[:, :, None] * mixing)
    y_inner = jnp.einsum('ijh,jhp->ihp', mix_low, xs_block, precision=HIGHEST_PREC)
    last_same = (seg_ids == seg_ids[-1]).astype(jnp.float32)
    weight_end = jnp.exp(cumul[-1][None, :] - cumul) * step_size * last_same[:, None]
    b_scaled = low(b_block[:, None, :] * weight_end[:, :, None])
    block_state = low_back(jnp.einsum('jhp,jhn->hpn', xs_block, b_scaled, precision=HIGHEST_PREC))
    prev_same = (seg_ids == seg_prev).astype(jnp.float32)
    entry = jnp.exp(cumul) * prev_same[:, None]
    carried = low_back(jnp.einsum('in,hpn->ihp', c_block, low(state), precision=HIGHEST_PREC))
    mixer_y = y_inner + entry[:, :, None] * carried + skip_gain[None, :, None] * xs_block
    carry_gain = jnp.exp(cumul[-1]) * (seg_ids[-1] == seg_prev).astype(jnp.float32)
    return ((carry_gain[:, None, None] * state + block_state, seg_ids[-1]), mixer_y)

def attend(queries, key_rows, value_rows, seg_ids):
    group_size = QH // KVH
    key_all = jnp.repeat(key_rows, group_size, axis=1)
    value_all = jnp.repeat(value_rows, group_size, axis=1)
    qk_scale = HD ** (-0.5)
    block_len = min(512, LEN)
    key_index = jnp.arange(LEN).astype(jnp.int32)

    def one_block(begin):
        query_block = lax.dynamic_slice_in_dim(queries, begin, block_len, 0)
        seg_block = lax.dynamic_slice_in_dim(seg_ids, begin, block_len, 0)
        query_index = begin + jnp.arange(block_len).astype(jnp.int32)
        raw_scores = low_back(jnp.einsum('qhd,khd->hqk', query_block, key_all, precision=HIGHEST_PREC))
        allowed = ((seg_block[:, None] == seg_ids[None, :]) & (key_index[None, :] <= query_index[:, None]))[None]
        scores = jnp.where(allowed, raw_scores * qk_scale, MASKED)
        row_max = lax.optimization_barrier(jnp.max(scores, axis=-1, keepdims=True))
        weights = jnp.where(allowed, jnp.exp(scores - row_max), 0.0)
        probs = low(weights / lax.optimization_barrier(jnp.sum(weights, axis=-1, keepdims=True)))
        return jnp.einsum('hqk,khd->qhd', probs, value_all, precision=HIGHEST_PREC)
    starts = (jnp.arange(LEN // block_len) * block_len).astype(jnp.int32)
    blocks_out = lax.map(jax.checkpoint(one_block), starts)
    return blocks_out.reshape(LEN, QH, HD)

def sequence(params, tokens, seg_ids, places):
    gain_one, w_in, conv_w, conv_b, head_params, gain_m, w_out, w_q, w_k, w_v, w_o, gain_two, w_gate, w_up, w_down = params
    inner_width = MH * MP
    channels = inner_width + 2 * NS
    hidden = low(rms_scale(tokens, gain_one))
    projected = low(low_back(product_hi(hidden, w_in)))
    gate_vals = projected[:, :inner_width]
    pre_conv = projected[:, inner_width:inner_width + channels]
    rate_raw = projected[:, inner_width + channels:]
    conv_act = low(conv_silu(pre_conv, seg_ids, conv_w, conv_b))
    xs_all = conv_act[:, :inner_width].reshape(LEN, MH, MP)
    b_all = conv_act[:, inner_width:inner_width + NS]
    c_all = conv_act[:, inner_width + NS:]
    step_size = jax.nn.softplus(rate_raw + head_params[1])
    log_decay = -step_size * jnp.exp(head_params[0])
    n_blocks = LEN // SPAN
    blocks = (xs_all.reshape(n_blocks, SPAN, MH, MP), b_all.reshape(n_blocks, SPAN, NS), c_all.reshape(n_blocks, SPAN, NS), step_size.reshape(n_blocks, SPAN, MH), log_decay.reshape(n_blocks, SPAN, MH), seg_ids.reshape(n_blocks, SPAN))
    start_state = (jnp.zeros((MH, MP, NS), jnp.float32), jnp.int32(-1))

    def block_step(carry_in, block_in):
        return ssm_block(head_params[2], carry_in, block_in)
    final_carry, mixer_y = lax.scan(jax.checkpoint(block_step), start_state, blocks)
    mixer_y = low_back(mixer_y.reshape(LEN, inner_width))
    mixer_in = low(rms_scale(mixer_y * jax.nn.silu(gate_vals), gain_m))
    mixer_out = low_back(product_hi(mixer_in, w_out))
    queries = low(rotary(low_back(product_hi(hidden, w_q)).reshape(LEN, QH, HD), places))
    key_rows = low(rotary(low_back(product_hi(hidden, w_k)).reshape(LEN, KVH, HD), places))
    value_rows = low(low_back(product_hi(hidden, w_v))).reshape(LEN, KVH, HD)
    att_out = low(low_back(attend(queries, key_rows, value_rows, seg_ids))).reshape(LEN, QH * HD)
    attn_branch = low_back(product_hi(att_out, w_o))
    middle = tokens + mixer_out + attn_branch
    normed_two = low(rms_scale(middle, gain_two))
    gate_lin = low_back(product_hi(normed_two, w_gate))
    up_lin = low_back(product_hi(normed_two, w_up))
    act_rows = low(jax.nn.silu(gate_lin) * up_lin)
    return middle + low_back(product_hi(act_rows, w_down))

def reference(layer_input, segments, positions, gain_one, w_in, conv_w, conv_b, head_params, gain_m, w_out, w_q, w_k, w_v, w_o, gain_two, w_gate, w_up, w_down, cotangent):
    params = tuple((weight.astype(jnp.float32) for weight in (gain_one, w_in, conv_w, conv_b, head_params, gain_m, w_out, w_q, w_k, w_v, w_o, gain_two, w_gate, w_up, w_down)))
    tokens_all = layer_input.astype(jnp.float32)

    def forward(params_in, tokens_in):

        def per_sequence(item_in):
            return sequence(params_in, item_in[0], item_in[1], item_in[2])
        return lax.map(jax.checkpoint(per_sequence), (tokens_in, segments, positions))
    layer_result, pull_back = jax.vjp(forward, params, tokens_all)
    param_grads, token_grad = pull_back(cotangent.astype(jnp.float32))
    return (layer_result.astype(jnp.bfloat16), token_grad.astype(jnp.bfloat16), param_grads[0], param_grads[1], param_grads[2], param_grads[3], param_grads[4], param_grads[5], param_grads[6], param_grads[7], param_grads[8], param_grads[9], param_grads[10], param_grads[11], param_grads[12], param_grads[13], param_grads[14])
```

```python
import jax
import jax.numpy as jnp
from jax import lax
from jax.sharding import PartitionSpec as P

MH = 24
MP = 64
NS = 128
KC = 4
QH = 8
KVH = 2
HD = 64


EPSILON = 1e-05
ROPE_BASE = 10000.0
MASKED = -1e30


def from_behind(block, axis, distance):
    devices = range(lax.axis_size(axis))
    route = [(i - distance, i) for i in devices if i - distance in devices]
    return lax.ppermute(block, axis, route)


def entering(shard, axis, combine, identity, reverse):
    count, place = (lax.axis_size(axis), lax.axis_index(axis))
    everything = jax.tree.map(
        lambda part, kind: lax.all_gather(part.astype(kind), axis),
        shard,
        (jnp.bfloat16, jnp.bfloat16),
    )
    start = jax.tree.map(
        lambda part, zero: jnp.broadcast_to(jnp.asarray(zero, part.dtype), part.shape),
        shard,
        identity,
    )

    def hop(k, before):
        at = count - 1 - k if reverse else k
        reached = at > place if reverse else at < place
        new = combine(
            before, jax.tree.map(lambda part, own: part[at].astype(own.dtype), everything, shard)
        )
        return jax.tree.map(lambda a, b: jnp.where(reached, a, b), new, before)

    return lax.fori_loop(0, count, hop, start)


def rms_scale(values, gain_vec):
    return (
        values * lax.rsqrt(jnp.mean(values * values, axis=-1, keepdims=True) + EPSILON) * gain_vec
    )


def rotary(values, places):
    half_width = values.shape[-1] // 2
    frequency = ROPE_BASE ** (-jnp.arange(half_width, dtype=jnp.float32) / half_width)
    angles = places.astype(jnp.float32)[..., None] * frequency
    cosine = jnp.cos(angles)[..., None, :]
    sine_part = jnp.sin(angles)[..., None, :]
    first_half = values[..., :half_width]
    second_half = values[..., half_width:]
    return jnp.concatenate(
        [
            first_half * cosine - second_half * sine_part,
            second_half * cosine + first_half * sine_part,
        ],
        axis=-1,
    )


def silu_product(gate_lin, up_lin):
    return jax.nn.silu(gate_lin) * up_lin


def gated_norm(mixer_y, gate_vals, gain_vec):
    return rms_scale(mixer_y * jax.nn.silu(gate_vals), gain_vec)


def conv_silu(extended, taps, shift, tap_match):
    out_len = tap_match.shape[2]
    total = shift
    for tap_idx in range(taps.shape[0]):
        total = (
            total
            + extended[:, tap_idx : tap_idx + out_len]
            * taps[tap_idx]
            * tap_match[:, tap_idx, :, None]
        )
    return jax.nn.silu(total)


def decay_terms(rate_raw, decay_log, step_bias, pair_mask, last_same, prev_same, flag_gain):
    step_size = jax.nn.softplus(rate_raw + step_bias)
    log_decay = -step_size * jnp.exp(decay_log)
    span_len = log_decay.shape[1]
    lower = jnp.tril(jnp.ones((span_len, span_len), jnp.float32))
    cumul = jnp.einsum("ij,sjh->sih", lower, log_decay, precision=lax.Precision.HIGHEST)
    by_head = jnp.swapaxes(cumul, 1, 2)
    differ = by_head[:, :, :, None] - by_head[:, :, None, :]
    inside = pair_mask[:, None]
    mixing = (
        jnp.where(inside, jnp.exp(jnp.where(inside, differ, 0.0)), 0.0)
        * jnp.swapaxes(step_size, 1, 2)[:, :, None, :]
    )
    weight_end = jnp.exp(cumul[:, -1:, :] - cumul) * step_size * last_same[..., None]
    entry = jnp.exp(cumul) * prev_same[..., None]
    carry_gain = jnp.exp(cumul[:, -1, :]) * flag_gain[:, None]
    return (mixing, weight_end, entry, carry_gain)


def combine_states(early_part, later_part):
    return (
        early_part[0] * later_part[0],
        later_part[0][..., None, None] * early_part[1] + later_part[1],
    )


def key_allowed(segments, seg_own, query_index, piece_len):
    key_index = jnp.arange(piece_len, dtype=jnp.int32)
    allowed = (seg_own[:, :, None] == segments[:, None, :]) & (
        key_index[None, None, :] <= query_index[None, :, None]
    )
    return allowed[:, None, None]


def body(
    layer_input,
    segments,
    positions,
    gain_one,
    w_in,
    conv_w,
    conv_b,
    head_params,
    gain_m,
    w_out,
    w_q,
    w_k,
    w_v,
    w_o,
    gain_two,
    w_gate,
    w_up,
    w_down,
    cotangent,
):
    seq_count, span_len, model_width = layer_input.shape
    tok_rows = seq_count * span_len
    inner_width = MH * MP
    channels = inner_width + 2 * NS
    group_size = QH // KVH
    qk_scale = HD ** (-0.5)
    axes = ("dp", "ctx")
    own_rows = w_q.shape[0]
    own_small = jnp.concatenate(
        [gain_one, gain_two, gain_m, conv_b, conv_w.reshape(-1)], axis=0
    )
    small_sizes = (gain_one.shape[0], gain_two.shape[0], gain_m.shape[0], conv_b.shape[0])
    slots = own_rows * 128
    small_block = jnp.pad(own_small, (0, slots - own_small.shape[0])).reshape(own_rows, 128)
    first_all = lax.all_gather(
        jnp.concatenate([w_q, w_k, w_v, small_block], axis=1), axes, axis=0, tiled=True
    )
    w_in_all = lax.all_gather(w_in, axes, axis=0, tiled=True)
    w_out_all = lax.all_gather(w_out, axes, axis=0, tiled=True)
    w_o_all = lax.all_gather(w_o.T, axes, axis=0, tiled=True).T
    w_gate_all = lax.all_gather(w_gate, axes, axis=0, tiled=True)
    w_up_all = lax.all_gather(w_up, axes, axis=0, tiled=True)
    w_down_all = lax.all_gather(w_down, axes, axis=0, tiled=True)
    q_width, k_width = w_q.shape[1], w_k.shape[1]
    w_q_all = first_all[:, :q_width]
    w_k_all = first_all[:, q_width : q_width + k_width]
    w_v_all = first_all[:, q_width + k_width : q_width + 2 * k_width]
    small_all = first_all[:, q_width + 2 * k_width :].reshape(-1, slots)
    parts, at = [], 0
    for size in small_sizes:
        parts.append(small_all[:, at : at + size].reshape(-1))
        at += size
    gain1_all, gain2_all, gain_m_all, conv_b_all = parts
    conv_w_all = jnp.swapaxes(
        small_all[:, at : at + KC * small_sizes[3]].reshape(-1, KC, small_sizes[3]), 0, 1
    ).reshape(KC, -1)
    span_start = lax.axis_index("ctx") * span_len
    has_prev = lax.axis_index("ctx") > 0
    offsets = jnp.arange(span_len, dtype=jnp.int32)
    query_index = span_start + offsets
    seg_own = lax.dynamic_slice_in_dim(segments, span_start, span_len, 1)
    seg_rim = jnp.where(
        has_prev,
        lax.dynamic_slice_in_dim(segments, jnp.maximum(span_start - (KC - 1), 0), KC - 1, 1),
        -1,
    )
    seg_prev = seg_rim[:, -1]
    tokens_f = layer_input.astype(jnp.float32).reshape(tok_rows, model_width)
    normed_one, norm1_pull = jax.vjp(rms_scale, tokens_f, gain1_all.astype(jnp.float32))
    hidden = normed_one.astype(jnp.bfloat16)
    projected = jnp.dot(hidden, w_in_all, preferred_element_type=jnp.float32).astype(jnp.bfloat16)
    gate_vals = projected[:, :inner_width].astype(jnp.float32)
    pre_conv = projected[:, inner_width : inner_width + channels].reshape(
        seq_count, span_len, channels
    )
    rate_raw = (
        projected[:, inner_width + channels :].astype(jnp.float32).reshape(seq_count, span_len, MH)
    )
    rim_rows = from_behind(pre_conv[:, span_len - (KC - 1) :], "ctx", 1)
    extended = jnp.concatenate([rim_rows, pre_conv], axis=1).astype(jnp.float32)
    seg_ext = jnp.concatenate([seg_rim, seg_own], axis=1)
    tap_match = jnp.stack(
        [seg_ext[:, tap_idx : tap_idx + span_len] == seg_own for tap_idx in range(KC)], axis=1
    ).astype(jnp.float32)
    conv_out, conv_pull = jax.vjp(
        lambda ext_in, taps_in, shift_in: conv_silu(ext_in, taps_in, shift_in, tap_match),
        extended,
        conv_w_all.astype(jnp.float32),
        conv_b_all.astype(jnp.float32),
    )
    conv_act = conv_out.astype(jnp.bfloat16)
    xs_rows = conv_act[..., :inner_width].reshape(seq_count, span_len, MH, MP)
    b_rows = conv_act[..., inner_width : inner_width + NS]
    c_rows = conv_act[..., inner_width + NS :]
    pair_mask = (seg_own[:, :, None] == seg_own[:, None, :]) & (
        offsets[None, :, None] >= offsets[None, None, :]
    )
    last_same = (seg_own == seg_own[:, -1:]).astype(jnp.float32)
    prev_same = (seg_own == seg_prev[:, None]).astype(jnp.float32)
    flag_gain = (seg_own[:, -1] == seg_prev).astype(jnp.float32)
    decays, decay_pull = jax.vjp(
        lambda rate_in, log_in, bias_in: decay_terms(
            rate_in, log_in, bias_in, pair_mask, last_same, prev_same, flag_gain
        ),
        rate_raw,
        head_params[0],
        head_params[1],
    )
    mixing, weight_end, entry, carry_gain = decays
    cross = jnp.einsum("sin,sjn->sij", c_rows, b_rows, preferred_element_type=jnp.float32)
    mix_low = (cross[:, None] * mixing).astype(jnp.bfloat16)
    y_inner = jnp.einsum("shij,sjhp->sihp", mix_low, xs_rows, preferred_element_type=jnp.float32)
    b_scaled = (b_rows[:, :, None, :].astype(jnp.float32) * weight_end[..., None]).astype(
        jnp.bfloat16
    )
    block_state = jnp.einsum(
        "sjhp,sjhn->shpn", xs_rows, b_scaled, preferred_element_type=jnp.float32
    )
    state_identity = (jnp.ones_like(carry_gain), jnp.zeros_like(block_state))
    gain_before, state_in = entering(
        (carry_gain, block_state), "ctx", combine_states, state_identity, False
    )
    state_low = state_in.astype(jnp.bfloat16)
    carried = jnp.einsum("sin,shpn->sihp", c_rows, state_low, preferred_element_type=jnp.float32)
    skip_gain = head_params[2]
    xs_float = xs_rows.astype(jnp.float32)
    mixer_y = y_inner + entry[..., None] * carried + skip_gain[:, None] * xs_float
    normed_mix, gate_pull = jax.vjp(
        gated_norm,
        mixer_y.reshape(tok_rows, inner_width),
        gate_vals,
        gain_m_all.astype(jnp.float32),
    )
    mixer_in = normed_mix.astype(jnp.bfloat16)
    mixer_out = jnp.dot(mixer_in, w_out_all, preferred_element_type=jnp.float32)
    query_lin = jnp.dot(hidden, w_q_all, preferred_element_type=jnp.float32).reshape(
        seq_count, span_len, QH, HD
    )
    key_lin = jnp.dot(hidden, w_k_all, preferred_element_type=jnp.float32).reshape(
        seq_count, span_len, KVH, HD
    )
    query_rot, query_pull = jax.vjp(lambda vals_in: rotary(vals_in, positions), query_lin)
    key_rot, key_pull = jax.vjp(lambda vals_in: rotary(vals_in, positions), key_lin)
    queries = query_rot.astype(jnp.bfloat16).reshape(seq_count, span_len, KVH, group_size, HD)
    key_rows = key_rot.astype(jnp.bfloat16).reshape(seq_count, span_len, KVH * HD)
    value_rows = (
        jnp.dot(hidden, w_v_all, preferred_element_type=jnp.float32)
        .astype(jnp.bfloat16)
        .reshape(seq_count, span_len, KVH * HD)
    )
    kv_width = KVH * HD
    kv_all = lax.all_gather(
        jnp.concatenate([key_rows, value_rows], axis=2), "ctx", axis=1, tiled=True
    )
    block_in = (kv_all[..., :kv_width], kv_all[..., kv_width:])
    run_max = jnp.full((seq_count, KVH, group_size, span_len), MASKED, jnp.float32)
    run_acc = jnp.zeros((seq_count, span_len, KVH, group_size, HD), jnp.float32)
    piece_len = block_in[0].shape[1]
    key_piece = block_in[0].reshape(seq_count, piece_len, KVH, HD)
    value_piece = block_in[1].reshape(seq_count, piece_len, KVH, HD)
    allowed = key_allowed(segments, seg_own, query_index, piece_len)
    scores = (
        jnp.einsum("sigrd,sjgd->sgrij", queries, key_piece, preferred_element_type=jnp.float32)
        * qk_scale
    )
    scores = jnp.where(allowed, scores, MASKED)
    new_max = jnp.maximum(run_max, jnp.max(scores, axis=-1))
    rescale = jnp.exp(run_max - new_max)
    weights = jnp.where(allowed, jnp.exp(scores - new_max[..., None]), 0.0)
    run_sum = jnp.sum(weights, axis=-1)
    run_acc = run_acc * jnp.moveaxis(rescale, 3, 1)[..., None] + jnp.einsum(
        "sgrij,sjgd->sigrd",
        weights.astype(jnp.bfloat16),
        value_piece,
        preferred_element_type=jnp.float32,
    )
    run_max, run_sum, run_acc = (new_max, run_sum, run_acc)
    att_full = run_acc / jnp.moveaxis(run_sum, 3, 1)[..., None]
    log_total = run_max + jnp.log(run_sum)
    att_low = att_full.astype(jnp.bfloat16).reshape(tok_rows, QH * HD)
    attn_branch = jnp.dot(att_low, w_o_all, preferred_element_type=jnp.float32)
    middle = tokens_f + mixer_out + attn_branch
    normed_mid, norm2_pull = jax.vjp(rms_scale, middle, gain2_all.astype(jnp.float32))
    normed_two = normed_mid.astype(jnp.bfloat16)
    gate_lin = jnp.dot(normed_two, w_gate_all, preferred_element_type=jnp.float32)
    up_lin = jnp.dot(normed_two, w_up_all, preferred_element_type=jnp.float32)
    act_float, act_pull = jax.vjp(silu_product, gate_lin, up_lin)
    act_rows = act_float.astype(jnp.bfloat16)
    layer_result = (
        (middle + jnp.dot(act_rows, w_down_all, preferred_element_type=jnp.float32))
        .astype(jnp.bfloat16)
        .reshape(seq_count, span_len, model_width)
    )
    cot_rows = cotangent.reshape(tok_rows, model_width)
    grad_down = jnp.einsum("rf,rd->fd", act_rows, cot_rows, preferred_element_type=jnp.float32)
    grad_act = jnp.einsum("rd,fd->rf", cot_rows, w_down_all, preferred_element_type=jnp.float32)
    grad_gate_f, grad_up_f = act_pull(grad_act)
    grad_gate_low = grad_gate_f.astype(jnp.bfloat16)
    grad_up_low = grad_up_f.astype(jnp.bfloat16)
    grad_wgate = jnp.einsum(
        "rd,rf->df", normed_two, grad_gate_low, preferred_element_type=jnp.float32
    )
    grad_wup = jnp.einsum("rd,rf->df", normed_two, grad_up_low, preferred_element_type=jnp.float32)
    grad_normed = jnp.einsum(
        "rf,df->rd", grad_gate_low, w_gate_all, preferred_element_type=jnp.float32
    ) + jnp.einsum("rf,df->rd", grad_up_low, w_up_all, preferred_element_type=jnp.float32)
    grad_mid_norm, grad_gain_second = norm2_pull(grad_normed)
    grad_middle = cot_rows.astype(jnp.float32) + grad_mid_norm
    grad_mid_low = grad_middle.astype(jnp.bfloat16)
    grad_wout = jnp.einsum("ri,rd->id", mixer_in, grad_mid_low, preferred_element_type=jnp.float32)
    grad_wo = jnp.einsum("ra,rd->ad", att_low, grad_mid_low, preferred_element_type=jnp.float32)
    grad_mixer_in = jnp.einsum(
        "rd,id->ri", grad_mid_low, w_out_all, preferred_element_type=jnp.float32
    )
    grad_att = (
        jnp.einsum("rd,ad->ra", grad_mid_low, w_o_all, preferred_element_type=jnp.float32)
        .astype(jnp.bfloat16)
        .reshape(seq_count, span_len, KVH, group_size, HD)
    )
    grad_mixer_y, grad_gate_vals, grad_gain_mix = gate_pull(grad_mixer_in)
    grad_y_low = grad_mixer_y.reshape(seq_count, span_len, MH, MP).astype(jnp.bfloat16)
    grad_y_float = grad_y_low.astype(jnp.float32)
    grad_mix = jnp.einsum(
        "sihp,sjhp->shij", grad_y_low, xs_rows, preferred_element_type=jnp.float32
    )
    grad_xs = (
        jnp.einsum("shij,sihp->sjhp", mix_low, grad_y_low, preferred_element_type=jnp.float32)
        + skip_gain[:, None] * grad_y_float
    )
    grad_carried = (entry[..., None] * grad_y_float).astype(jnp.bfloat16)
    grad_entry = jnp.sum(grad_y_float * carried, axis=-1)
    grad_c = jnp.einsum(
        "sihp,shpn->sin", grad_carried, state_low, preferred_element_type=jnp.float32
    )
    grad_state_local = jnp.einsum(
        "sihp,sin->shpn", grad_carried, c_rows, preferred_element_type=jnp.float32
    )
    grad_skip = jnp.sum(grad_y_float * xs_float, axis=(0, 1, 3))
    gain_after, grad_state_out = entering(
        (carry_gain, grad_state_local), "ctx", combine_states, state_identity, True
    )
    grad_carry_gain = jnp.sum(grad_state_out * state_in, axis=(2, 3))
    grad_state_low = grad_state_out.astype(jnp.bfloat16)
    grad_xs = grad_xs + jnp.einsum(
        "sjhn,shpn->sjhp", b_scaled, grad_state_low, preferred_element_type=jnp.float32
    )
    grad_bscaled = jnp.einsum(
        "sjhp,shpn->sjhn", xs_rows, grad_state_low, preferred_element_type=jnp.float32
    )
    grad_b = jnp.sum(grad_bscaled * weight_end[..., None], axis=2)
    grad_weight_end = jnp.sum(grad_bscaled * b_rows.astype(jnp.float32)[:, :, None, :], axis=-1)
    grad_cross = jnp.sum(grad_mix * mixing, axis=1).astype(jnp.bfloat16)
    grad_mixing = grad_mix * cross[:, None]
    grad_c = grad_c + jnp.einsum(
        "sij,sjn->sin", grad_cross, b_rows, preferred_element_type=jnp.float32
    )
    grad_b = grad_b + jnp.einsum(
        "sij,sin->sjn", grad_cross, c_rows, preferred_element_type=jnp.float32
    )
    grad_rates, grad_decay_log, grad_step_bias = decay_pull(
        (grad_mixing, grad_weight_end, grad_entry, grad_carry_gain)
    )
    grad_conv_out = jnp.concatenate(
        [grad_xs.reshape(seq_count, span_len, inner_width), grad_b, grad_c], axis=-1
    )
    grad_ext, grad_conv_taps, grad_conv_shift = conv_pull(grad_conv_out)
    back_rim = from_behind(grad_ext[:, : KC - 1].astype(jnp.bfloat16), "ctx", -1).astype(
        jnp.float32
    )
    grad_pre = grad_ext[:, KC - 1 :] + jnp.concatenate(
        [jnp.zeros((seq_count, span_len - (KC - 1), channels), jnp.float32), back_rim], axis=1
    )
    grad_proj = jnp.concatenate(
        [grad_gate_vals, grad_pre.reshape(tok_rows, channels), grad_rates.reshape(tok_rows, MH)],
        axis=1,
    ).astype(jnp.bfloat16)
    grad_win = jnp.einsum("rd,rc->dc", hidden, grad_proj, preferred_element_type=jnp.float32)
    grad_hidden = jnp.einsum("rc,dc->rd", grad_proj, w_in_all, preferred_element_type=jnp.float32)
    row_delta = jnp.einsum("sigrd,sigrd->sgri", grad_att.astype(jnp.float32), att_full)
    piece_len = block_in[0].shape[1]
    key_piece = block_in[0].reshape(seq_count, piece_len, KVH, HD)
    value_piece = block_in[1].reshape(seq_count, piece_len, KVH, HD)
    allowed = key_allowed(segments, seg_own, query_index, piece_len)
    scores = (
        jnp.einsum("sigrd,sjgd->sgrij", queries, key_piece, preferred_element_type=jnp.float32)
        * qk_scale
    )
    scores = jnp.where(allowed, scores, MASKED)
    probs = jnp.where(allowed, jnp.exp(scores - log_total[..., None]), 0.0)
    probs_low = probs.astype(jnp.bfloat16)
    grad_probs = jnp.einsum(
        "sigrd,sjgd->sgrij", grad_att, value_piece, preferred_element_type=jnp.float32
    )
    grad_scores = (probs * (grad_probs - row_delta[..., None]) * qk_scale).astype(jnp.bfloat16)
    grad_query = jnp.einsum(
        "sgrij,sjgd->sigrd", grad_scores, key_piece, preferred_element_type=jnp.float32
    )
    part_key = jnp.einsum(
        "sgrij,sigrd->sjgd", grad_scores, queries, preferred_element_type=jnp.float32
    ).reshape(seq_count, piece_len, KVH * HD)
    part_value = jnp.einsum(
        "sgrij,sigrd->sjgd", probs_low, grad_att, preferred_element_type=jnp.float32
    ).reshape(seq_count, piece_len, KVH * HD)
    grad_key_all = part_key
    grad_value_all = part_value
    grad_query, grad_key_all, grad_value_all = (grad_query, grad_key_all, grad_value_all)
    grad_kv = lax.psum_scatter(
        jnp.concatenate([grad_key_all, grad_value_all], axis=2).astype(jnp.bfloat16),
        "ctx",
        scatter_dimension=1,
        tiled=True,
    ).astype(jnp.float32)
    grad_key_rot, grad_value = (grad_kv[..., :kv_width], grad_kv[..., kv_width:])
    grad_query_lin = (
        query_pull(grad_query.reshape(seq_count, span_len, QH, HD))[0]
        .astype(jnp.bfloat16)
        .reshape(tok_rows, QH * HD)
    )
    grad_key_lin = (
        key_pull(grad_key_rot.reshape(seq_count, span_len, KVH, HD))[0]
        .astype(jnp.bfloat16)
        .reshape(tok_rows, KVH * HD)
    )
    grad_value_low = grad_value.astype(jnp.bfloat16).reshape(tok_rows, KVH * HD)
    grad_wq = jnp.einsum("rd,ra->da", hidden, grad_query_lin, preferred_element_type=jnp.float32)
    grad_wk = jnp.einsum("rd,ra->da", hidden, grad_key_lin, preferred_element_type=jnp.float32)
    grad_wv = jnp.einsum("rd,ra->da", hidden, grad_value_low, preferred_element_type=jnp.float32)
    grad_hidden = grad_hidden + jnp.einsum(
        "ra,da->rd", grad_query_lin, w_q_all, preferred_element_type=jnp.float32
    )
    grad_hidden = grad_hidden + jnp.einsum(
        "ra,da->rd", grad_key_lin, w_k_all, preferred_element_type=jnp.float32
    )
    grad_hidden = grad_hidden + jnp.einsum(
        "ra,da->rd", grad_value_low, w_v_all, preferred_element_type=jnp.float32
    )
    grad_tokens_norm, grad_gain_first = norm1_pull(grad_hidden)
    grad_tokens = (
        (grad_middle + grad_tokens_norm)
        .astype(jnp.bfloat16)
        .reshape(seq_count, span_len, model_width)
    )
    def scatter(grad):
        return lax.psum_scatter(
            grad.astype(jnp.bfloat16), axes, scatter_dimension=0, tiled=True
        ).astype(jnp.float32)

    devices = w_q_all.shape[0] // own_rows
    small_grads = jnp.concatenate(
        [
            grad_gain_first.reshape(devices, -1),
            grad_gain_second.reshape(devices, -1),
            grad_gain_mix.reshape(devices, -1),
            grad_conv_shift.reshape(devices, -1),
            jnp.swapaxes(grad_conv_taps.reshape(KC, devices, -1), 0, 1).reshape(devices, -1),
        ],
        axis=1,
    )
    small_grads = jnp.pad(small_grads, ((0, 0), (0, slots - small_grads.shape[1])))
    out_down = scatter(grad_down)
    out_gate = scatter(grad_wgate)
    out_up = scatter(grad_wup)
    out_wout = scatter(grad_wout)
    out_wo = scatter(grad_wo.T).T
    out_win = scatter(grad_win)
    out_first = scatter(
        jnp.concatenate([grad_wq, grad_wk, grad_wv, small_grads.reshape(-1, 128)], axis=1)
    )
    out_small = out_first[:, q_width + 2 * k_width :].reshape(-1)
    pieces, at = [], 0
    for size in small_sizes:
        pieces.append(out_small[at : at + size])
        at += size
    out_taps = out_small[at : at + KC * small_sizes[3]].reshape(KC, small_sizes[3])
    head_grad = lax.psum(jnp.stack([grad_decay_log, grad_step_bias, grad_skip]), axes)
    return (
        layer_result,
        grad_tokens,
        pieces[0],
        out_win,
        out_taps,
        pieces[3],
        head_grad,
        pieces[2],
        out_wout,
        out_first[:, :q_width],
        out_first[:, q_width : q_width + k_width],
        out_first[:, q_width + k_width : q_width + 2 * k_width],
        out_wo,
        pieces[1],
        out_gate,
        out_up,
        out_down,
    )


def solution(mesh):
    in_specs = (
        P("dp", "ctx", None),
        P("dp", None),
        P("dp", "ctx"),
        P(("dp", "ctx")),
        P(("dp", "ctx"), None),
        P(None, ("dp", "ctx")),
        P(("dp", "ctx")),
        P(),
        P(("dp", "ctx")),
        P(("dp", "ctx"), None),
        P(("dp", "ctx"), None),
        P(("dp", "ctx"), None),
        P(("dp", "ctx"), None),
        P(None, ("dp", "ctx")),
        P(("dp", "ctx")),
        P(("dp", "ctx"), None),
        P(("dp", "ctx"), None),
        P(("dp", "ctx"), None),
        P("dp", "ctx", None),
    )
    out_specs = (
        P("dp", "ctx", None),
        P("dp", "ctx", None),
        P(("dp", "ctx")),
        P(("dp", "ctx"), None),
        P(None, ("dp", "ctx")),
        P(("dp", "ctx")),
        P(),
        P(("dp", "ctx")),
        P(("dp", "ctx"), None),
        P(("dp", "ctx"), None),
        P(("dp", "ctx"), None),
        P(("dp", "ctx"), None),
        P(None, ("dp", "ctx")),
        P(("dp", "ctx")),
        P(("dp", "ctx"), None),
        P(("dp", "ctx"), None),
        P(("dp", "ctx"), None),
    )
    return jax.shard_map(body, mesh=mesh, in_specs=in_specs, out_specs=out_specs, check_vma=False)
```

```python
import jax
import jax.numpy as jnp
from jax import lax
from jax.experimental import pallas as pl
from jax.experimental.pallas import tpu as pltpu
from jax.sharding import PartitionSpec as P

MH = 24
MP = 64
NS = 128
KC = 4
QH = 8
KVH = 2
HD = 64
EPSILON = 1e-05
ROPE_BASE = 10000.0
MASKED = -1e30
LOG2E = 1.4426950408889634
KEY_TILE = 256
VMEM_BYTES = 56 * 1024 * 1024

F32 = jnp.float32
BF16 = jnp.bfloat16


def contract(left, right, left_dim, right_dim):
    return lax.dot_general(
        left, right, (((left_dim,), (right_dim,)), ((), ())), preferred_element_type=F32
    )


def lanes(shape):
    return lax.broadcasted_iota(jnp.int32, shape, len(shape) - 1)


def swap_halves(values):
    lane = lanes(values.shape)
    return jnp.where(lane < 32, pltpu.roll(values, 96, 1), pltpu.roll(values, 32, 1))


def project_kernel(x_ref, gain_ref, w_ref, cos_ref, sin_ref, hidden_ref, q_ref, kv_ref):
    x = x_ref[...].astype(F32)
    scale = lax.rsqrt(jnp.mean(x * x, axis=-1, keepdims=True) + EPSILON)
    hidden = (x * scale * gain_ref[...]).astype(BF16)
    hidden_ref[...] = hidden
    lin = contract(hidden, w_ref[...], 1, 0)
    cosine, sine = cos_ref[...], sin_ref[...]
    lane = lanes(cosine.shape)
    for pair in range(QH // 2):
        both = lin[:, pair * 128 : (pair + 1) * 128]
        other = pltpu.roll(both, 64, 1)
        even = both * cosine + swap_halves(both) * sine
        odd = other * cosine + swap_halves(other) * sine
        q_ref[:, pair * 128 : (pair + 1) * 128] = jnp.where(
            lane < 64, even, pltpu.roll(odd, 64, 1)
        ).astype(BF16)
    for group in range(KVH):
        at = QH * HD + group * 128
        part = lin[:, at : at + 128]
        kv_ref[:, group * 128 : (group + 1) * 128] = (
            part * cosine + swap_halves(part) * sine
        ).astype(BF16)


def project(x, gain, w_first, cosine, sine):
    rows, width = x.shape
    tile = 256
    block = lambda cols: pl.BlockSpec((tile, cols), lambda i: (i, 0))
    fixed = lambda shape: pl.BlockSpec(shape, lambda i: (0, 0))
    kv_width = 2 * KVH * HD
    return pl.pallas_call(
        project_kernel,
        grid=(rows // tile,),
        in_specs=[
            block(width),
            fixed((1, width)),
            fixed((width, QH * HD + kv_width)),
            block(128),
            block(128),
        ],
        out_specs=[block(width), block(QH * HD), block(kv_width)],
        out_shape=[
            jax.ShapeDtypeStruct((rows, width), BF16),
            jax.ShapeDtypeStruct((rows, QH * HD), BF16),
            jax.ShapeDtypeStruct((rows, kv_width), BF16),
        ],
        compiler_params=pltpu.CompilerParams(vmem_limit_bytes=VMEM_BYTES),
        name="project",
    )(x, gain, w_first, cosine, sine)


def visible(segk_ref, segq, query_row, at):
    segk = segk_ref[0, pl.ds(at, KEY_TILE), :]
    key_col = at + lax.broadcasted_iota(jnp.int32, (KEY_TILE, 1), 0)
    return jnp.where((segk == segq) & (key_col <= query_row), 0.0, MASKED)


def attend_kernel(
    low_ref, high_ref, base_ref, q_ref, kv_ref, segk_ref, segq_ref, out_ref, lse_ref,
    q_s, m_s, l_s, acc_s,
):
    seq, tile = pl.program_id(0), pl.program_id(1)
    rows = q_ref.shape[1]
    place = seq * pl.num_programs(1) + tile
    lane = lanes((rows, 128))
    for pair in range(QH // 2):
        both = q_ref[0, :, pair * 128 : (pair + 1) * 128].astype(F32)
        q_s[2 * pair] = jnp.where(lane < 64, both, 0.0).astype(BF16)
        q_s[2 * pair + 1] = jnp.where(lane < 64, pltpu.roll(both, 64, 1), 0.0).astype(BF16)
    m_s[...] = jnp.full(m_s.shape, MASKED, F32)
    l_s[...] = jnp.zeros(l_s.shape, F32)
    acc_s[...] = jnp.zeros(acc_s.shape, F32)
    query_row = base_ref[0] + tile * rows + lanes((1, rows))
    segq = segq_ref[0]
    factor = HD ** (-0.5) * LOG2E

    def step(key_tile, carry):
        at = pl.multiple_of(key_tile * KEY_TILE, KEY_TILE)
        bias = visible(segk_ref, segq, query_row, at)
        for group in range(KVH):
            kv = kv_ref[0, pl.ds(at, KEY_TILE), group * 128 : (group + 1) * 128]
            kv_t = kv.astype(F32).T.astype(BF16)
            for member in range(QH // KVH):
                head = group * (QH // KVH) + member
                scores = contract(kv, q_s[head], 1, 1) * factor + bias
                before = m_s[head : head + 1, :]
                top = jnp.maximum(before, jnp.max(scores, axis=0, keepdims=True))
                weights = jnp.exp2(scores - top)
                fade = jnp.exp2(before - top)
                l_s[head : head + 1, :] = l_s[head : head + 1, :] * fade + jnp.sum(
                    weights, axis=0, keepdims=True
                )
                acc_s[head] = acc_s[head] * fade + contract(kv_t, weights.astype(BF16), 1, 0)
                m_s[head : head + 1, :] = top
        return carry

    lax.fori_loop(low_ref[place], high_ref[place], step, 0)
    lse_ref[0] = m_s[...] + jnp.log2(l_s[...])
    for pair in range(QH // 2):
        even = (acc_s[2 * pair] / l_s[2 * pair : 2 * pair + 1, :]).T
        odd = (acc_s[2 * pair + 1] / l_s[2 * pair + 1 : 2 * pair + 2, :]).T
        out_ref[0, :, pair * 128 : (pair + 1) * 128] = jnp.where(
            lane < 64, pltpu.roll(even, 64, 1), odd
        ).astype(BF16)


def attend_back_kernel(
    low_ref, high_ref, base_ref, q_ref, kv_ref, segk_ref, segq_ref, att_ref, gatt_ref, lse_ref,
    cos_ref, sin_ref, dq_ref, dkv_ref,
    q_s, g_s, delta_s, dq_s, dkv_s,
):
    seq, tile = pl.program_id(0), pl.program_id(1)
    rows = q_ref.shape[1]
    place = seq * pl.num_programs(1) + tile
    lane = lanes((rows, 128))

    @pl.when(tile == 0)
    def _():
        dkv_s[...] = jnp.zeros(dkv_s.shape, F32)

    for pair in range(QH // 2):
        cols = slice(pair * 128, (pair + 1) * 128)
        both = q_ref[0, :, cols].astype(F32)
        q_s[2 * pair] = jnp.where(lane < 64, both, 0.0).astype(BF16)
        q_s[2 * pair + 1] = jnp.where(lane < 64, pltpu.roll(both, 64, 1), 0.0).astype(BF16)
        grad = gatt_ref[0, :, cols].astype(F32)
        g_s[2 * pair] = jnp.where(lane >= 64, pltpu.roll(grad, 64, 1), 0.0).astype(BF16)
        g_s[2 * pair + 1] = jnp.where(lane >= 64, grad, 0.0).astype(BF16)
        product = (grad * att_ref[0, :, cols].astype(F32)).T
        delta_s[2 * pair : 2 * pair + 1, :] = jnp.sum(product[:64], axis=0, keepdims=True)
        delta_s[2 * pair + 1 : 2 * pair + 2, :] = jnp.sum(product[64:], axis=0, keepdims=True)
    dq_s[...] = jnp.zeros(dq_s.shape, F32)
    query_row = base_ref[0] + tile * rows + lanes((1, rows))
    segq = segq_ref[0]
    qk_scale = HD ** (-0.5)
    factor = qk_scale * LOG2E

    def step(key_tile, carry):
        at = pl.multiple_of(key_tile * KEY_TILE, KEY_TILE)
        bias = visible(segk_ref, segq, query_row, at)
        for group in range(KVH):
            kv = kv_ref[0, pl.ds(at, KEY_TILE), group * 128 : (group + 1) * 128]
            kv_t = kv.astype(F32).T.astype(BF16)
            total = jnp.zeros((KEY_TILE, 128), F32)
            for member in range(QH // KVH):
                head = group * (QH // KVH) + member
                q, g = q_s[head], g_s[head]
                scores = contract(kv, q, 1, 1) * factor + bias
                probs = jnp.exp2(scores - lse_ref[0, head : head + 1, :])
                d_probs = contract(kv, g, 1, 1)
                d_scores = (probs * (d_probs - delta_s[head : head + 1, :]) * qk_scale).astype(BF16)
                total = total + contract(d_scores, q, 1, 0) + contract(probs.astype(BF16), g, 1, 0)
                dq_s[head] += contract(kv_t, d_scores, 1, 0)
            cols = slice(group * 128, (group + 1) * 128)
            dkv_s[pl.ds(at, KEY_TILE), cols] += total
        return carry

    lax.fori_loop(low_ref[place], high_ref[place], step, 0)
    cosine, sine = cos_ref[0], sin_ref[0]
    for pair in range(QH // 2):
        even, odd = dq_s[2 * pair].T, dq_s[2 * pair + 1].T
        even = even * cosine + swap_halves(even * sine)
        odd = odd * cosine + swap_halves(odd * sine)
        dq_ref[0, :, pair * 128 : (pair + 1) * 128] = jnp.where(
            lane < 64, even, pltpu.roll(odd, 64, 1)
        ).astype(BF16)

    @pl.when(tile == pl.num_programs(1) - 1)
    def _():
        dkv_ref[0] = dkv_s[...].astype(BF16)


def attention_specs(seqs, span, length, rows):
    tile = lambda cols: pl.BlockSpec((1, rows, cols), lambda s, t, *_: (s, t, 0))
    whole = lambda cols: pl.BlockSpec((1, length, cols), lambda s, t, *_: (s, 0, 0))
    row = lambda n: pl.BlockSpec((1, n, rows), lambda s, t, *_: (s, 0, t))
    return tile, whole, row


def attend(bounds, q, kv_all, segk, segq):
    seqs, span, q_width = q.shape
    length, kv_width = kv_all.shape[1:]
    rows = min(256, span)
    tile, whole, row = attention_specs(seqs, span, length, rows)
    return pl.pallas_call(
        attend_kernel,
        grid_spec=pltpu.PrefetchScalarGridSpec(
            num_scalar_prefetch=3,
            grid=(seqs, span // rows),
            in_specs=[tile(q_width), whole(kv_width), whole(1), row(1)],
            out_specs=[tile(q_width), row(QH)],
            scratch_shapes=[
                pltpu.VMEM((QH, rows, 128), BF16),
                pltpu.VMEM((QH, rows), F32),
                pltpu.VMEM((QH, rows), F32),
                pltpu.VMEM((QH, 128, rows), F32),
            ],
        ),
        out_shape=[
            jax.ShapeDtypeStruct(q.shape, BF16),
            jax.ShapeDtypeStruct((seqs, QH, span), F32),
        ],
        compiler_params=pltpu.CompilerParams(vmem_limit_bytes=VMEM_BYTES),
        name="attend",
    )(*bounds, q, kv_all, segk, segq)


def attend_back(bounds, q, kv_all, segk, segq, att, grad_att, lse, cosine, sine):
    seqs, span, q_width = q.shape
    length, kv_width = kv_all.shape[1:]
    rows = min(256, span)
    tile, whole, row = attention_specs(seqs, span, length, rows)
    return pl.pallas_call(
        attend_back_kernel,
        grid_spec=pltpu.PrefetchScalarGridSpec(
            num_scalar_prefetch=3,
            grid=(seqs, span // rows),
            in_specs=[
                tile(q_width), whole(kv_width), whole(1), row(1), tile(q_width), tile(q_width),
                row(QH), tile(128), tile(128),
            ],
            out_specs=[tile(q_width), whole(kv_width)],
            scratch_shapes=[
                pltpu.VMEM((QH, rows, 128), BF16),
                pltpu.VMEM((QH, rows, 128), BF16),
                pltpu.VMEM((QH, rows), F32),
                pltpu.VMEM((QH, 128, rows), F32),
                pltpu.VMEM((length, kv_width), F32),
            ],
        ),
        out_shape=[
            jax.ShapeDtypeStruct(q.shape, BF16),
            jax.ShapeDtypeStruct(kv_all.shape, BF16),
        ],
        compiler_params=pltpu.CompilerParams(vmem_limit_bytes=VMEM_BYTES),
        name="attend_back",
    )(*bounds, q, kv_all, segk, segq, att, grad_att, lse, cosine, sine)


def rope_tables(positions):
    half = HD // 2
    frequency = ROPE_BASE ** (-jnp.arange(half, dtype=F32) / half)
    angles = positions.astype(F32)[..., None] * frequency
    cosine, sine = jnp.cos(angles), jnp.sin(angles)
    one, zero = jnp.ones(cosine.shape[:-1] + (HD,), F32), jnp.zeros(cosine.shape[:-1] + (HD,), F32)
    return (
        jnp.concatenate([cosine, cosine, one], axis=-1),
        jnp.concatenate([-sine, sine, zero], axis=-1),
    )


def attention_bounds(segments, seg_own, span_start):
    seqs, span = seg_own.shape
    rows = min(256, span)
    first = seg_own[:, ::rows]
    begin = jnp.sum((segments[:, None, :] < first[:, :, None]).astype(jnp.int32), axis=2)
    tiles = jnp.arange(span // rows, dtype=jnp.int32)
    high = (span_start + (tiles + 1) * rows + KEY_TILE - 1) // KEY_TILE
    high = jnp.broadcast_to(high[None], first.shape)
    return (
        (begin // KEY_TILE).reshape(-1),
        high.reshape(-1).astype(jnp.int32),
        jnp.full((1,), span_start, jnp.int32),
    )


CHUNK = 128
DI = MH * MP
CC = DI + 2 * NS
TAP_LANES, PREV_LANE, LAST_LANE, SEG_LANE = 0, 4, 5, 6


def split_three(values):
    high = values.astype(BF16)
    rest = values - high.astype(F32)
    middle = rest.astype(BF16)
    return high, middle, (rest - middle.astype(F32)).astype(BF16)


def product_exact(matrix, values):
    return sum(contract(matrix, part, 1, 0) for part in split_three(values))


def widen(values, spread):
    kept = jnp.where(lanes(values.shape) < 32, values, 0.0)
    high, middle, rest = (part.astype(F32) for part in split_three(kept))
    packed = high + pltpu.roll(middle, 32, 1) + pltpu.roll(rest, 64, 1)
    return contract(packed.astype(BF16), spread, 1, 0)


def gather_heads(values, spread_first):
    high = values.astype(BF16)
    rest = (values - high.astype(F32)).astype(BF16)
    return contract(high, spread_first, 1, 1) + contract(rest, spread_first, 1, 1)


def spread_matrix():
    row = lax.broadcasted_iota(jnp.int32, (128, DI), 0)
    col = lax.broadcasted_iota(jnp.int32, (128, DI), 1)
    return ((row % 32 == col // MP) & (row < 96)).astype(BF16)


def spread_first_matrix():
    row = lax.broadcasted_iota(jnp.int32, (32, DI), 0)
    col = lax.broadcasted_iota(jnp.int32, (32, DI), 1)
    return (row == col // MP).astype(BF16)


def lower_mask():
    row = lax.broadcasted_iota(jnp.int32, (CHUNK, CHUNK), 0)
    return row >= lanes((CHUNK, CHUNK))


def decay_rows(rate, head_ref, token):
    raw = rate.astype(F32) + head_ref[1:2, :]
    step = jnp.maximum(raw, 0.0) + jnp.log1p(jnp.exp(-jnp.abs(raw)))
    log_decay = -step * jnp.exp(head_ref[0:1, :])
    running = product_exact(lower_mask().astype(BF16), log_decay)
    last = running[CHUNK - 1 :, :]
    weight_end = jnp.exp(last - running) * step * token[:, LAST_LANE : LAST_LANE + 1]
    entry = jnp.exp(running) * token[:, PREV_LANE : PREV_LANE + 1]
    gain = jnp.exp(last) * token[CHUNK - 1 :, PREV_LANE : PREV_LANE + 1]
    return raw, step, log_decay, running, weight_end, entry, gain


def conv_total(ext_s, token, taps_ref, shift_ref):
    total = shift_ref[...] + ext_s[8 : 8 + CHUNK, :] * taps_ref[KC - 1 : KC, :]
    for tap in range(KC - 1):
        total = total + ext_s[5 + tap : 5 + tap + CHUNK, :] * (
            taps_ref[tap : tap + 1, :] * token[:, TAP_LANES + tap : TAP_LANES + tap + 1]
        )
    return total


def mixer_scan_kernel(
    proj_ref, rim_ref, token_ref, head_ref, taps_ref, shift_ref, spread_ref,
    act_ref, states_ref, gains_ref, final_ref, final_gain_ref,
    ext_s, state_s, gain_s,
):
    chunk = pl.program_id(1)

    @pl.when(chunk == 0)
    def _():
        ext_s[0:8, :] = rim_ref[0].astype(F32)
        state_s[...] = jnp.zeros(state_s.shape, F32)
        gain_s[...] = jnp.ones(gain_s.shape, F32)

    @pl.when(chunk > 0)
    def _():
        ext_s[0:8, :] = ext_s[CHUNK : CHUNK + 8, :]

    token = token_ref[0]
    ext_s[8 : 8 + CHUNK, :] = proj_ref[0, :, DI : DI + CC].astype(F32)
    total = conv_total(ext_s, token, taps_ref, shift_ref)
    act = (total * jax.nn.sigmoid(total)).astype(BF16)
    act_ref[0] = act
    weight_end, _, gain = decay_rows(proj_ref[0, :, DI + CC :], head_ref, token)[-3:]
    states_ref[0, 0] = state_s[...].astype(BF16)
    before = gain_s[...]
    gains_ref[0, 0] = before
    spread = spread_ref[...]
    scaled = (act[:, :DI].astype(F32) * widen(weight_end, spread)).astype(BF16)
    gain_rows = jnp.broadcast_to(gain, (8, 128))
    state = state_s[...] * widen(gain_rows, spread)[0:1, :] + contract(
        act[:, DI : DI + NS], scaled, 0, 0
    )
    state_s[...] = state
    gain_s[...] = before * gain_rows

    @pl.when(chunk == pl.num_programs(1) - 1)
    def _():
        final_ref[0] = state
        final_gain_ref[0] = before * gain_rows


def entering_state(local_ref, gains_ref, state_ref, spread):
    factor = widen(gains_ref[0, 0], spread)[0:1, :]
    return (local_ref[0, 0].astype(F32) + factor * state_ref[0].astype(F32)).astype(BF16)


def pair_decay(running, rest_t, bias, head):
    parts = []
    for at in (head, head + 1):
        column = jnp.broadcast_to(running[:, at : at + 1], (CHUNK, CHUNK))
        parts.append(jnp.exp2(column + (rest_t[at : at + 1, :] + bias)))
    return parts


def stack_pair(values):
    lane = lanes(values.shape)
    wide = values.astype(F32)
    return jnp.concatenate(
        [jnp.where(lane < 64, wide, 0.0), jnp.where(lane >= 64, wide, 0.0)], axis=0
    ).astype(BF16)


def inside_terms(running, step, token):
    seg = jnp.broadcast_to(token[:, SEG_LANE : SEG_LANE + 1], (CHUNK, CHUNK))
    bias = jnp.where((seg == seg.T) & lower_mask(), 0.0, MASKED)
    running_two = running * LOG2E
    rest_t = (jnp.log2(step) - running_two).T
    return running_two, rest_t, bias


def mixer_out_kernel(
    proj_ref, act_ref, token_ref, states_ref, gains_ref, state_ref, head_ref, skip_ref, gain_ref,
    spread_ref, y_ref, out_ref,
):
    token, spread = token_ref[0], spread_ref[...]
    _, step, _, running, _, entry, _ = decay_rows(proj_ref[0, :, DI + CC :], head_ref, token)
    b_rows, c_rows = act_ref[0, :, DI : DI + NS], act_ref[0, :, DI + NS :]
    state = entering_state(states_ref, gains_ref, state_ref, spread)
    carried = contract(c_rows, state, 1, 0) * widen(entry, spread)
    cross = contract(c_rows, b_rows, 1, 1)
    running_two, rest_t, bias = inside_terms(running, step, token)
    square = jnp.zeros((CHUNK, 128), F32)
    for pair in range(MH // 2):
        cols = slice(pair * 128, (pair + 1) * 128)
        xs = act_ref[0, :, cols]
        mix = jnp.concatenate(
            [
                (cross * part).astype(BF16)
                for part in pair_decay(running_two, rest_t, bias, 2 * pair)
            ],
            axis=1,
        )
        y = (
            contract(mix, stack_pair(xs), 1, 0)
            + carried[:, cols]
            + skip_ref[:, cols] * xs.astype(F32)
        )
        y_ref[0, :, cols] = y
        gate = proj_ref[0, :, cols].astype(F32)
        gated = y * (gate * jax.nn.sigmoid(gate))
        square = square + gated * gated
    scale = lax.rsqrt(jnp.sum(square, axis=1, keepdims=True) * (1.0 / DI) + EPSILON)
    for pair in range(MH // 2):
        cols = slice(pair * 128, (pair + 1) * 128)
        gate = proj_ref[0, :, cols].astype(F32)
        gated = y_ref[0, :, cols] * (gate * jax.nn.sigmoid(gate))
        out_ref[0, :, cols] = (gated * scale * gain_ref[:, cols]).astype(BF16)


def mixer_gate_back_kernel(
    gmix_ref, y_ref, proj_ref, act_ref, token_ref, head_ref, gain_ref, spread_ref,
    gy_ref, dgate_ref, gstates_ref, gains_ref, final_ref, dgain_ref, dskip_ref,
    state_s, gain_s, dgain_s, dskip_s,
):
    seq, chunk = pl.program_id(0), pl.program_id(1)

    @pl.when((seq == 0) & (chunk == 0))
    def _():
        dgain_s[...] = jnp.zeros(dgain_s.shape, F32)
        dskip_s[...] = jnp.zeros(dskip_s.shape, F32)

    @pl.when(chunk == 0)
    def _():
        state_s[...] = jnp.zeros(state_s.shape, F32)
        gain_s[...] = jnp.ones(gain_s.shape, F32)

    token, spread = token_ref[0], spread_ref[...]
    entry, gain = decay_rows(proj_ref[0, :, DI + CC :], head_ref, token)[-2:]
    y = y_ref[0]
    gate = proj_ref[0, :, :DI].astype(F32)
    sig = jax.nn.sigmoid(gate)
    swish = gate * sig
    gated = y * swish
    scale = lax.rsqrt(jnp.mean(gated * gated, axis=1, keepdims=True) + EPSILON)
    grad = gmix_ref[0].astype(F32)
    scaled = grad * gain_ref[...]
    shrink = jnp.mean(scaled * gated, axis=1, keepdims=True) * (scale * scale * scale)
    d_gated = scaled * scale - gated * shrink
    gy = (d_gated * swish).astype(BF16)
    gy_ref[0] = gy
    dgate_ref[0] = (d_gated * y * (sig * (1.0 + gate * (1.0 - sig)))).astype(BF16)
    dgain_s[0:1, :] += jnp.sum(grad * gated * scale, axis=0, keepdims=True)
    gy_float = gy.astype(F32)
    dskip_s[0:1, :] += jnp.sum(gy_float * act_ref[0, :, :DI].astype(F32), axis=0, keepdims=True)
    gstates_ref[0, 0] = state_s[...].astype(BF16)
    after = gain_s[...]
    gains_ref[0, 0] = after
    gain_rows = jnp.broadcast_to(gain, (8, 128))
    carried = (gy_float * widen(entry, spread)).astype(BF16)
    state = state_s[...] * widen(gain_rows, spread)[0:1, :] + contract(
        act_ref[0, :, DI + NS :], carried, 0, 0
    )
    state_s[...] = state
    gain_s[...] = after * gain_rows

    @pl.when(chunk == pl.num_programs(1) - 1)
    def _():
        final_ref[0] = state

    dgain_ref[...] = dgain_s[...]
    dskip_ref[...] = dskip_s[...]


def mixer_back_kernel(
    gy_ref, y_ref, dgate_ref, proj_ref, halo_ref, rim_ref, act_ref, token_ref,
    states_ref, gains_ref, state_ref, gstates_ref, ggains_ref, gstate_ref,
    head_ref, skip_ref, taps_ref, shift_ref, spread_ref, spread_first_ref,
    dproj_ref, drim_ref, dconv_ref, dhead_ref,
    ext_s, grad_s, carry_s, dconv_s, dhead_s,
):
    seq, step_index = pl.program_id(0), pl.program_id(1)
    last_step = pl.num_programs(1) - 1

    @pl.when((seq == 0) & (step_index == 0))
    def _():
        dconv_s[...] = jnp.zeros(dconv_s.shape, F32)
        dhead_s[...] = jnp.zeros(dhead_s.shape, F32)

    @pl.when(step_index == 0)
    def _():
        carry_s[...] = jnp.zeros(carry_s.shape, F32)

    @pl.when(step_index == last_step)
    def _():
        ext_s[0:8, :] = rim_ref[0].astype(F32)

    @pl.when(step_index < last_step)
    def _():
        ext_s[0:8, :] = halo_ref[0, :, DI : DI + CC].astype(F32)[8:16]

    ext_s[8 : 8 + CHUNK, :] = proj_ref[0, :, DI : DI + CC].astype(F32)
    token, spread, spread_first = token_ref[0], spread_ref[...], spread_first_ref[...]
    raw, step, log_decay, running, weight_end, entry, gain = decay_rows(
        proj_ref[0, :, DI + CC :], head_ref, token
    )
    b_rows, c_rows = act_ref[0, :, DI : DI + NS], act_ref[0, :, DI + NS :]
    state = entering_state(states_ref, gains_ref, state_ref, spread)
    gstate = entering_state(gstates_ref, ggains_ref, gstate_ref, spread)
    wide_end = widen(weight_end, spread)
    gy = gy_ref[0]
    gy_float = gy.astype(F32)
    gcarried = (gy_float * widen(entry, spread)).astype(BF16)
    xs_float = act_ref[0, :, :DI].astype(F32)
    grad_c = contract(gcarried, state, 1, 1)
    grad_b = contract((xs_float * wide_end).astype(BF16), gstate, 1, 1)
    from_end = contract(b_rows, gstate, 1, 0) * wide_end
    dgain_row = jnp.sum(gstate.astype(F32) * state.astype(F32), axis=0, keepdims=True)
    cross = contract(c_rows, b_rows, 1, 1)
    running_two, rest_t, bias = inside_terms(running, step, token)
    grad_cross = jnp.zeros((CHUNK, CHUNK), F32)
    lane = lanes((CHUNK, 128))
    for pair in range(MH // 2):
        cols = slice(pair * 128, (pair + 1) * 128)
        stacked = stack_pair(act_ref[0, :, cols])
        gy_pair = gy_ref[0, :, cols]
        first, second = pair_decay(running_two, rest_t, bias, 2 * pair)
        mix = jnp.concatenate([(cross * first).astype(BF16), (cross * second).astype(BF16)], axis=1)
        grad_mix = contract(gy_pair, stacked, 1, 1)
        grad_cross = grad_cross + grad_mix[:, :CHUNK] * first + grad_mix[:, CHUNK:] * second
        both = contract(mix, gy_pair, 0, 0)
        grad_s[8 : 8 + CHUNK, cols] = jnp.where(lane < 64, both[:CHUNK], both[CHUNK:])
    inner = grad_s[8 : 8 + CHUNK, :DI]
    skip = skip_ref[...]
    cross_low = grad_cross.astype(BF16)
    grad_c = grad_c + contract(cross_low, b_rows, 1, 0)
    grad_b = grad_b + contract(cross_low, c_rows, 0, 0)
    narrow = lambda values: jnp.concatenate(
        [gather_heads(values, spread_first), jnp.zeros((values.shape[0], 96), F32)], axis=1
    )
    query_part = narrow(gy_float * (y_ref[0] - skip * xs_float))
    key_inner = narrow(xs_float * inner)
    key_end = narrow(xs_float * from_end)
    extra = jnp.sum(key_end, axis=0, keepdims=True) + gain * narrow(
        jnp.broadcast_to(dgain_row, (8, DI))
    )[0:1, :]
    upper = (~lower_mask() | (lax.broadcasted_iota(jnp.int32, (CHUNK, CHUNK), 0) == lanes((CHUNK, CHUNK))))
    grad_log = product_exact(upper.astype(BF16), query_part - key_inner - key_end) + extra
    sig = jax.nn.sigmoid(raw)
    ratio = jnp.where(raw < -15.0, 1.0, sig / jnp.maximum(step, 1e-30))
    grad_rate = (key_inner + key_end) * ratio - grad_log * jnp.exp(head_ref[0:1, :]) * sig
    dhead_s[0:1, :] += jnp.sum(grad_log * log_decay, axis=0, keepdims=True)
    dhead_s[1:2, :] += jnp.sum(grad_rate, axis=0, keepdims=True)
    total = conv_total(ext_s, token, taps_ref, shift_ref)
    grad_act = jnp.concatenate([inner + from_end + skip * gy_float, grad_b, grad_c], axis=1)
    csig = jax.nn.sigmoid(total)
    grad_total = grad_act * (csig * (1.0 + total * (1.0 - csig)))
    dconv_s[KC : KC + 1, :] += jnp.sum(grad_total, axis=0, keepdims=True)
    grad_s[0:8, :] = jnp.zeros((8, CC), F32)
    grad_s[8 : 8 + CHUNK, :] = grad_total * taps_ref[KC - 1 : KC, :]
    dconv_s[KC - 1 : KC, :] += jnp.sum(grad_total * ext_s[8 : 8 + CHUNK, :], axis=0, keepdims=True)
    for tap in range(KC - 1):
        part = grad_total * token[:, TAP_LANES + tap : TAP_LANES + tap + 1]
        dconv_s[tap : tap + 1, :] += jnp.sum(
            part * ext_s[5 + tap : 5 + tap + CHUNK, :], axis=0, keepdims=True
        )
        grad_s[5 + tap : 5 + tap + CHUNK, :] += part * taps_ref[tap : tap + 1, :]
    grad_s[CHUNK : CHUNK + 8, :] += carry_s[...]
    carry_s[...] = grad_s[0:8, :]
    dproj_ref[0, :, :DI] = dgate_ref[0]
    dproj_ref[0, :, DI : DI + CC] = grad_s[8 : 8 + CHUNK, :].astype(BF16)
    dproj_ref[0, :, DI + CC :] = grad_rate.astype(BF16)

    @pl.when(step_index == last_step)
    def _():
        drim_ref[0] = carry_s[...]

    dconv_ref[...] = dconv_s[...]
    dhead_ref[...] = dhead_s[...]


def mixer_specs(chunks, reverse):
    place = (lambda c: chunks - 1 - c) if reverse else (lambda c: c)
    block = lambda cols: pl.BlockSpec((1, CHUNK, cols), lambda s, c: (s, place(c), 0))
    per_chunk = lambda rows, cols: pl.BlockSpec(
        (1, 1, rows, cols), lambda s, c: (s, place(c), 0, 0)
    )
    per_seq = lambda rows, cols: pl.BlockSpec((1, rows, cols), lambda s, c: (s, 0, 0))
    fixed = lambda rows, cols: pl.BlockSpec((rows, cols), lambda s, c: (0, 0))
    return block, per_chunk, per_seq, fixed


MIXER_PARAMS = pltpu.CompilerParams(vmem_limit_bytes=VMEM_BYTES)


def mixer_scan(proj, rim, token, heads, taps, shift, spread):
    seqs, span, width = proj.shape
    chunks = span // CHUNK
    block, per_chunk, per_seq, fixed = mixer_specs(chunks, False)
    return pl.pallas_call(
        mixer_scan_kernel,
        grid=(seqs, chunks),
        in_specs=[
            block(width), per_seq(8, CC), block(128), fixed(8, 128), fixed(8, CC), fixed(1, CC),
            fixed(128, DI),
        ],
        out_specs=[
            block(CC), per_chunk(NS, DI), per_chunk(8, 128), per_seq(NS, DI), per_seq(8, 128),
        ],
        out_shape=[
            jax.ShapeDtypeStruct((seqs, span, CC), BF16),
            jax.ShapeDtypeStruct((seqs, chunks, NS, DI), BF16),
            jax.ShapeDtypeStruct((seqs, chunks, 8, 128), F32),
            jax.ShapeDtypeStruct((seqs, NS, DI), F32),
            jax.ShapeDtypeStruct((seqs, 8, 128), F32),
        ],
        scratch_shapes=[
            pltpu.VMEM((CHUNK + 8, CC), F32), pltpu.VMEM((NS, DI), F32), pltpu.VMEM((8, 128), F32),
        ],
        compiler_params=MIXER_PARAMS,
        name="mixer_scan",
    )(proj, rim, token, heads, taps, shift, spread)


def mixer_out(proj, act, token, states, gains, state, heads, skip, gain, spread):
    seqs, span, width = proj.shape
    block, per_chunk, per_seq, fixed = mixer_specs(span // CHUNK, False)
    return pl.pallas_call(
        mixer_out_kernel,
        grid=(seqs, span // CHUNK),
        in_specs=[
            block(width), block(CC), block(128), per_chunk(NS, DI), per_chunk(8, 128),
            per_seq(NS, DI), fixed(8, 128), fixed(1, DI), fixed(1, DI), fixed(128, DI),
        ],
        out_specs=[block(DI), block(DI)],
        out_shape=[
            jax.ShapeDtypeStruct((seqs, span, DI), F32),
            jax.ShapeDtypeStruct((seqs, span, DI), BF16),
        ],
        compiler_params=MIXER_PARAMS,
        name="mixer_out",
    )(proj, act, token, states, gains, state, heads, skip, gain, spread)


def mixer_gate_back(gmix, y, proj, act, token, heads, gain, spread):
    seqs, span, width = proj.shape
    chunks = span // CHUNK
    block, per_chunk, per_seq, fixed = mixer_specs(chunks, True)
    return pl.pallas_call(
        mixer_gate_back_kernel,
        grid=(seqs, chunks),
        in_specs=[
            block(DI), block(DI), block(width), block(CC), block(128), fixed(8, 128),
            fixed(1, DI), fixed(128, DI),
        ],
        out_specs=[
            block(DI), block(DI), per_chunk(NS, DI), per_chunk(8, 128), per_seq(NS, DI),
            fixed(8, DI), fixed(8, DI),
        ],
        out_shape=[
            jax.ShapeDtypeStruct((seqs, span, DI), BF16),
            jax.ShapeDtypeStruct((seqs, span, DI), BF16),
            jax.ShapeDtypeStruct((seqs, chunks, NS, DI), BF16),
            jax.ShapeDtypeStruct((seqs, chunks, 8, 128), F32),
            jax.ShapeDtypeStruct((seqs, NS, DI), F32),
            jax.ShapeDtypeStruct((8, DI), F32),
            jax.ShapeDtypeStruct((8, DI), F32),
        ],
        scratch_shapes=[
            pltpu.VMEM((NS, DI), F32), pltpu.VMEM((8, 128), F32),
            pltpu.VMEM((8, DI), F32), pltpu.VMEM((8, DI), F32),
        ],
        compiler_params=MIXER_PARAMS,
        name="mixer_gate_back",
    )(gmix, y, proj, act, token, heads, gain, spread)


def mixer_back(
    gy, y, dgate, proj, rim, act, token, states, gains, state, gstates, ggains, gstate,
    heads, skip, taps, shift, spread, spread_first,
):
    seqs, span, width = proj.shape
    chunks = span // CHUNK
    block, per_chunk, per_seq, fixed = mixer_specs(chunks, True)
    steps = CHUNK // 16
    halo = pl.BlockSpec(
        (1, 16, width), lambda s, c: (s, jnp.maximum((chunks - 1 - c) * steps - 1, 0), 0)
    )
    return pl.pallas_call(
        mixer_back_kernel,
        grid=(seqs, chunks),
        in_specs=[
            block(DI), block(DI), block(DI), block(width), halo, per_seq(8, CC), block(CC),
            block(128), per_chunk(NS, DI), per_chunk(8, 128), per_seq(NS, DI),
            per_chunk(NS, DI), per_chunk(8, 128), per_seq(NS, DI),
            fixed(8, 128), fixed(1, DI), fixed(8, CC), fixed(1, CC), fixed(128, DI), fixed(32, DI),
        ],
        out_specs=[block(width), per_seq(8, CC), fixed(8, CC), fixed(8, 128)],
        out_shape=[
            jax.ShapeDtypeStruct((seqs, span, width), BF16),
            jax.ShapeDtypeStruct((seqs, 8, CC), F32),
            jax.ShapeDtypeStruct((8, CC), F32),
            jax.ShapeDtypeStruct((8, 128), F32),
        ],
        scratch_shapes=[
            pltpu.VMEM((CHUNK + 8, CC), F32), pltpu.VMEM((CHUNK + 8, CC), F32),
            pltpu.VMEM((8, CC), F32), pltpu.VMEM((8, CC), F32), pltpu.VMEM((8, 128), F32),
        ],
        compiler_params=MIXER_PARAMS,
        name="mixer_back",
    )(
        gy, y, dgate, proj, proj, rim, act, token, states, gains, state, gstates, ggains, gstate,
        heads, skip, taps, shift, spread, spread_first,
    )


def token_table(seg_own, seg_rim):
    seqs, span = seg_own.shape
    extended = jnp.concatenate([seg_rim, seg_own], axis=1)
    matches = [extended[:, tap : tap + span] == seg_own for tap in range(KC - 1)]
    by_chunk = seg_own.reshape(seqs, -1, CHUNK)
    last = by_chunk[:, :, -1:]
    before = jnp.concatenate([seg_rim[:, None, -1:], last[:, :-1]], axis=1)
    spare = jnp.zeros((seqs, span), F32)
    rows = [match.astype(F32) for match in matches] + [
        spare,
        (by_chunk == before).reshape(seqs, span).astype(F32),
        (by_chunk == last).reshape(seqs, span).astype(F32),
        seg_own.astype(F32),
        spare,
    ]
    return jnp.pad(jnp.stack(rows, axis=-1), ((0, 0), (0, 0), (0, 120)))


def from_behind(block, axis, distance):
    devices = range(lax.axis_size(axis))
    route = [(i - distance, i) for i in devices if i - distance in devices]
    return lax.ppermute(block, axis, route)


def chain_states(local, gain, reverse):
    count, place = lax.axis_size("ctx"), lax.axis_index("ctx")
    state = jnp.zeros(local.shape, BF16)
    for hop in range(count - 1):
        source = count - 1 - hop if reverse else hop
        target = source - 1 if reverse else source + 1
        sent = (gain * state.astype(F32) + local).astype(BF16)
        received = lax.ppermute(sent, "ctx", [(source, target)])
        state = jnp.where(place == target, received, state)
    return state


def sum_everywhere(values, axes):
    for axis in axes:
        count, distance = lax.axis_size(axis), 1
        while distance < count:
            route = [(i, i ^ distance) for i in range(count)]
            values = values + lax.ppermute(values, axis, route)
            distance *= 2
    return values


def rms_scale(values, gain_vec):
    return (
        values * lax.rsqrt(jnp.mean(values * values, axis=-1, keepdims=True) + EPSILON) * gain_vec
    )


def silu_product(gate_lin, up_lin):
    return jax.nn.silu(gate_lin) * up_lin


def body(
    layer_input, segments, positions, gain_one, w_in, conv_w, conv_b, head_params, gain_m, w_out,
    w_q, w_k, w_v, w_o, gain_two, w_gate, w_up, w_down, cotangent,
):
    seqs, span, width = layer_input.shape
    rows = seqs * span
    axes = ("dp", "ctx")
    own_rows = w_q.shape[0]
    q_width, kv_width = QH * HD, 2 * KVH * HD
    low_dot = lambda a, b: jnp.dot(a, b, preferred_element_type=F32)

    small_parts = [gain_one, gain_two, gain_m, conv_b, conv_w.reshape(-1)]
    small_sizes = [part.shape[0] for part in small_parts]
    slots = own_rows * 128
    small_block = jnp.concatenate(small_parts, axis=0)
    small_block = jnp.pad(small_block, (0, slots - sum(small_sizes))).reshape(own_rows, 128)
    w_kv = jnp.stack(
        [w_k.reshape(own_rows, KVH, HD), w_v.reshape(own_rows, KVH, HD)], axis=2
    ).reshape(own_rows, kv_width)
    gather = lambda shard: lax.all_gather(shard, axes, axis=0, tiled=True)
    first_all = gather(jnp.concatenate([w_q, w_kv, small_block], axis=1))
    in_width = DI + CC + 128
    w_in_all = gather(jnp.pad(w_in, ((0, 0), (0, in_width - w_in.shape[1]))))
    w_out_all = gather(w_out)
    w_o_all = gather(w_o.T)
    w_gate_all = gather(w_gate)
    w_up_all = gather(w_up)
    w_down_all = gather(w_down)
    small_all = first_all[:, q_width + kv_width :].reshape(-1, slots).astype(F32)
    parts, at = [], 0
    for size in small_sizes:
        parts.append(small_all[:, at : at + size])
        at += size
    gain1_all, gain2_all, gain_m_all, shift_all = [part.reshape(1, -1) for part in parts[:4]]
    taps_all = jnp.swapaxes(parts[4].reshape(-1, KC, small_sizes[3]), 0, 1).reshape(KC, CC)
    taps_all = jnp.pad(taps_all, ((0, 8 - KC), (0, 0)))

    place = lax.axis_index("ctx")
    span_start = place * span
    seg_own = lax.dynamic_slice_in_dim(segments, span_start, span, 1)
    seg_rim = jnp.where(
        place > 0,
        lax.dynamic_slice_in_dim(segments, jnp.maximum(span_start - (KC - 1), 0), KC - 1, 1),
        -1,
    )
    token = token_table(seg_own, seg_rim)
    bounds = attention_bounds(segments, seg_own, span_start)
    segk, segq = segments[:, :, None], seg_own[:, None, :]
    cosine, sine = rope_tables(positions)
    heads = jnp.pad(head_params, ((0, 5), (0, 128 - MH)))
    skip = jnp.repeat(head_params[2], MP)[None]
    spread, spread_first = spread_matrix(), spread_first_matrix()

    tokens = layer_input.reshape(rows, width)
    hidden, q, kv = project(
        tokens, gain1_all, first_all, cosine.reshape(rows, 128), sine.reshape(rows, 128)
    )
    q = q.reshape(seqs, span, q_width)
    kv_all = lax.all_gather(kv.reshape(seqs, span, kv_width), "ctx", axis=1, tiled=True)
    proj = low_dot(hidden, w_in_all).astype(BF16).reshape(seqs, span, in_width)
    rim = from_behind(proj[:, span - (KC - 1) :, DI : DI + CC], "ctx", 1)
    rim = jnp.pad(rim, ((0, 0), (8 - (KC - 1), 0), (0, 0)))
    act, states, gains, local_state, local_gain = mixer_scan(
        proj, rim, token, heads, taps_all, shift_all, spread
    )
    wide_gain = jnp.repeat(local_gain[:, :1, :MH], MP, axis=2)
    state_in = chain_states(local_state, wide_gain, False)
    att, lse = attend(bounds, q, kv_all, segk, segq)
    mixer_y, mixer_in = mixer_out(
        proj, act, token, states, gains, state_in, heads, skip, gain_m_all, spread
    )
    mixer_in = mixer_in.reshape(rows, DI)
    att_rows = att.reshape(rows, q_width)
    middle = (
        tokens.astype(F32)
        + low_dot(mixer_in, w_out_all)
        + jnp.einsum("ra,da->rd", att_rows, w_o_all, preferred_element_type=F32)
    )
    normed_mid, norm2_pull = jax.vjp(rms_scale, middle, gain2_all)
    normed_two = normed_mid.astype(BF16)
    gate_lin = low_dot(normed_two, w_gate_all)
    up_lin = low_dot(normed_two, w_up_all)
    act_float, act_pull = jax.vjp(silu_product, gate_lin, up_lin)
    act_rows = act_float.astype(BF16)
    layer_result = (middle + low_dot(act_rows, w_down_all)).astype(BF16)

    def scatter(grad):
        part = lax.psum_scatter(grad, "dp", scatter_dimension=0, tiled=True)
        return lax.psum_scatter(part, "ctx", scatter_dimension=0, tiled=True).astype(F32)

    def weight_grad(left, right):
        return jnp.einsum("ri,ro->io", left, right, preferred_element_type=F32).astype(BF16)

    def back_dot(grad, weight):
        return jnp.einsum("ro,io->ri", grad, weight, preferred_element_type=F32)

    cot_rows = cotangent.reshape(rows, width)
    grad_down = weight_grad(act_rows, cot_rows)
    grad_gate_f, grad_up_f = act_pull(back_dot(cot_rows, w_down_all))
    grad_gate_low, grad_up_low = grad_gate_f.astype(BF16), grad_up_f.astype(BF16)
    grad_wgate = weight_grad(normed_two, grad_gate_low)
    grad_wup = weight_grad(normed_two, grad_up_low)
    grad_normed = back_dot(grad_gate_low, w_gate_all) + back_dot(grad_up_low, w_up_all)
    grad_normed, grad_down, grad_wgate, grad_wup = lax.optimization_barrier(
        (grad_normed, grad_down, grad_wgate, grad_wup)
    )
    out_down, out_gate, out_up = scatter(grad_down), scatter(grad_wgate), scatter(grad_wup)
    grad_mid_norm, grad_gain_second = norm2_pull(grad_normed)
    grad_middle = cot_rows.astype(F32) + grad_mid_norm
    grad_mid_low = grad_middle.astype(BF16)
    grad_wout = weight_grad(mixer_in, grad_mid_low)
    grad_wo = weight_grad(grad_mid_low, att_rows)
    grad_mixer_in = back_dot(grad_mid_low, w_out_all).astype(BF16).reshape(seqs, span, DI)
    grad_att = low_dot(grad_mid_low, w_o_all).astype(BF16).reshape(seqs, span, q_width)
    grad_mixer_in, grad_att, grad_wout, grad_wo = lax.optimization_barrier(
        (grad_mixer_in, grad_att, grad_wout, grad_wo)
    )
    out_wout, out_wo = scatter(grad_wout), scatter(grad_wo)
    grad_y, grad_gate, gstates, ggains, local_gstate, grad_gain_mix, grad_skip = mixer_gate_back(
        grad_mixer_in, mixer_y, proj, act, token, heads, gain_m_all, spread
    )
    gstate_out = chain_states(local_gstate, wide_gain, True)
    dq, dkv_all = attend_back(
        bounds, q, kv_all, segk, segq, att, grad_att, lse, cosine, sine
    )
    dkv = lax.psum_scatter(dkv_all, "ctx", scatter_dimension=1, tiled=True)
    grad_proj, grad_rim, grad_conv, grad_heads = mixer_back(
        grad_y, mixer_y, grad_gate, proj, rim, act, token, states, gains, state_in,
        gstates, ggains, gstate_out, heads, skip, taps_all, shift_all, spread, spread_first,
    )
    back_rim = from_behind(grad_rim[:, 8 - (KC - 1) :].astype(BF16), "ctx", -1)
    edge = grad_proj[:, span - (KC - 1) :, DI : DI + CC].astype(F32) + back_rim.astype(F32)
    grad_proj = lax.dynamic_update_slice(
        grad_proj, edge.astype(BF16), (0, span - (KC - 1), DI)
    ).reshape(rows, in_width)
    grad_win = weight_grad(hidden, grad_proj)
    out_win = scatter(grad_win)[:, : w_in.shape[1]]
    grad_kv = dkv.astype(F32).reshape(seqs, span, KVH, 2 * HD)
    turned = grad_kv[..., :HD] * sine[:, :, None, :HD]
    turned = jnp.concatenate([turned[..., HD // 2 :], turned[..., : HD // 2]], axis=-1)
    grad_key = grad_kv[..., :HD] * cosine[:, :, None, :HD] + turned
    grad_kv = jnp.concatenate([grad_key, grad_kv[..., HD:]], axis=-1).astype(BF16)
    grad_first = jnp.concatenate(
        [dq.reshape(rows, q_width), grad_kv.reshape(rows, kv_width)], axis=1
    )
    grad_wfirst = weight_grad(hidden, grad_first)
    grad_hidden = back_dot(grad_proj, w_in_all) + back_dot(
        grad_first, first_all[:, : q_width + kv_width]
    )
    tokens_f = tokens.astype(F32)
    _, norm1_pull = jax.vjp(rms_scale, tokens_f, gain1_all)
    grad_tokens_norm, grad_gain_first = norm1_pull(grad_hidden)
    grad_tokens = (grad_middle + grad_tokens_norm).astype(BF16)

    devices = first_all.shape[0] // own_rows
    small_grads = jnp.concatenate(
        [
            grad_gain_first.reshape(devices, -1),
            grad_gain_second.reshape(devices, -1),
            grad_gain_mix[0].reshape(devices, -1),
            grad_conv[KC].reshape(devices, -1),
            jnp.swapaxes(grad_conv[:KC].reshape(KC, devices, -1), 0, 1).reshape(devices, -1),
        ],
        axis=1,
    )
    small_grads = jnp.pad(small_grads, ((0, 0), (0, slots - small_grads.shape[1])))
    out_first = scatter(
        jnp.concatenate([grad_wfirst, small_grads.reshape(-1, 128).astype(BF16)], axis=1)
    )
    out_small = out_first[:, q_width + kv_width :].reshape(-1)
    pieces, at = [], 0
    for size in small_sizes:
        pieces.append(out_small[at : at + size])
        at += size
    out_kv = out_first[:, q_width : q_width + kv_width].reshape(own_rows, KVH, 2, HD)
    head_grad = sum_everywhere(
        jnp.concatenate(
            [grad_heads[:2, :MH], grad_skip[0].reshape(MH, MP).sum(axis=1)[None]], axis=0
        ),
        axes,
    )
    return (
        layer_result.reshape(layer_input.shape),
        grad_tokens.reshape(layer_input.shape),
        pieces[0],
        out_win,
        pieces[4].reshape(KC, -1),
        pieces[3],
        head_grad,
        pieces[2],
        out_wout,
        out_first[:, :q_width],
        out_kv[:, :, 0].reshape(own_rows, -1),
        out_kv[:, :, 1].reshape(own_rows, -1),
        out_wo.T,
        pieces[1],
        out_gate,
        out_up,
        out_down,
    )


def solution(mesh):
    in_specs = (
        P("dp", "ctx", None),
        P("dp", None),
        P("dp", "ctx"),
        P(("dp", "ctx")),
        P(("dp", "ctx"), None),
        P(None, ("dp", "ctx")),
        P(("dp", "ctx")),
        P(),
        P(("dp", "ctx")),
        P(("dp", "ctx"), None),
        P(("dp", "ctx"), None),
        P(("dp", "ctx"), None),
        P(("dp", "ctx"), None),
        P(None, ("dp", "ctx")),
        P(("dp", "ctx")),
        P(("dp", "ctx"), None),
        P(("dp", "ctx"), None),
        P(("dp", "ctx"), None),
        P("dp", "ctx", None),
    )
    out_specs = (
        P("dp", "ctx", None),
        P("dp", "ctx", None),
        P(("dp", "ctx")),
        P(("dp", "ctx"), None),
        P(None, ("dp", "ctx")),
        P(("dp", "ctx")),
        P(),
        P(("dp", "ctx")),
        P(("dp", "ctx"), None),
        P(("dp", "ctx"), None),
        P(("dp", "ctx"), None),
        P(("dp", "ctx"), None),
        P(None, ("dp", "ctx")),
        P(("dp", "ctx")),
        P(("dp", "ctx"), None),
        P(("dp", "ctx"), None),
        P(("dp", "ctx"), None),
    )
    return jax.shard_map(body, mesh=mesh, in_specs=in_specs, out_specs=out_specs, check_vma=False)
```

```python
import functools
import jax
import jax.numpy as jnp
from jax import lax
from jax.experimental import pallas as pl
from jax.experimental.pallas import tpu as pltpu
from jax.sharding import PartitionSpec as P

MH = 24
MP = 64
NS = 128
KC = 4
QH = 8
KVH = 2
HD = 64
EPSILON = 1e-05
ROPE_BASE = 10000.0
MASKED = -1e30
LOG2E = 1.4426950408889634
KEY_TILE = 256
VMEM_BYTES = 56 * 1024 * 1024

F32 = jnp.float32
BF16 = jnp.bfloat16


def contract(left, right, left_dim, right_dim):
    return lax.dot_general(
        left, right, (((left_dim,), (right_dim,)), ((), ())), preferred_element_type=F32
    )


def lanes(shape):
    return lax.broadcasted_iota(jnp.int32, shape, len(shape) - 1)


def swap_halves(values):
    lane = lanes(values.shape)
    return jnp.where(lane < 32, pltpu.roll(values, 96, 1), pltpu.roll(values, 32, 1))


def project_kernel(x_ref, gain_ref, w_ref, cos_ref, sin_ref, hidden_ref, q_ref, kv_ref):
    x = x_ref[...].astype(F32)
    scale = lax.rsqrt(jnp.mean(x * x, axis=-1, keepdims=True) + EPSILON)
    hidden = (x * scale * gain_ref[...]).astype(BF16)
    hidden_ref[...] = hidden
    lin = contract(hidden, w_ref[...], 1, 0)
    cosine, sine = cos_ref[...], sin_ref[...]
    lane = lanes(cosine.shape)
    for pair in range(QH // 2):
        both = lin[:, pair * 128 : (pair + 1) * 128]
        other = pltpu.roll(both, 64, 1)
        even = both * cosine + swap_halves(both) * sine
        odd = other * cosine + swap_halves(other) * sine
        q_ref[:, pair * 128 : (pair + 1) * 128] = jnp.where(
            lane < 64, even, pltpu.roll(odd, 64, 1)
        ).astype(BF16)
    for group in range(KVH):
        at = QH * HD + group * 128
        part = lin[:, at : at + 128]
        kv_ref[:, group * 128 : (group + 1) * 128] = (
            part * cosine + swap_halves(part) * sine
        ).astype(BF16)


def project(x, gain, w_first, cosine, sine):
    rows, width = x.shape
    tile = 256
    block = lambda cols: pl.BlockSpec((tile, cols), lambda i: (i, 0))
    fixed = lambda shape: pl.BlockSpec(shape, lambda i: (0, 0))
    kv_width = 2 * KVH * HD
    return pl.pallas_call(
        project_kernel,
        grid=(rows // tile,),
        in_specs=[
            block(width),
            fixed((1, width)),
            fixed((width, QH * HD + kv_width)),
            block(128),
            block(128),
        ],
        out_specs=[block(width), block(QH * HD), block(kv_width)],
        out_shape=[
            jax.ShapeDtypeStruct((rows, width), BF16),
            jax.ShapeDtypeStruct((rows, QH * HD), BF16),
            jax.ShapeDtypeStruct((rows, kv_width), BF16),
        ],
        compiler_params=pltpu.CompilerParams(vmem_limit_bytes=VMEM_BYTES),
        name="project",
    )(x, gain, w_first, cosine, sine)


def visible(segk_ref, segq, query_row, at, key_rows):
    segk = segk_ref[0, pl.ds(at, key_rows), :]
    key_col = at + lax.broadcasted_iota(jnp.int32, (key_rows, 1), 0)
    return jnp.where((segk == segq) & (key_col <= query_row), 0.0, MASKED)


def attend_kernel(
    place_at, low_ref, high_ref, base_ref, q_ref, kv_ref, segk_ref, segq_ref, out_ref, lse_ref,
    q_s, m_s, l_s, acc_s,
):
    tile = pl.program_id(0)
    rows = q_ref.shape[1]
    place = place_at + tile
    lane = lanes((rows, 128))
    for pair in range(QH // 2):
        both = q_ref[0, :, pair * 128 : (pair + 1) * 128].astype(F32)
        q_s[2 * pair] = jnp.where(lane < 64, both, 0.0).astype(BF16)
        q_s[2 * pair + 1] = jnp.where(lane < 64, pltpu.roll(both, 64, 1), 0.0).astype(BF16)
    key_rows = min(KEY_TILE, kv_ref.shape[2])
    tiles_each = kv_ref.shape[2] // key_rows
    m_s[...] = jnp.full(m_s.shape, MASKED, F32)
    l_s[...] = jnp.zeros(l_s.shape, F32)
    acc_s[...] = jnp.zeros(acc_s.shape, F32)
    query_row = base_ref[0] + tile * rows + lanes((1, rows))
    segq = segq_ref[0]
    factor = HD ** (-0.5) * LOG2E

    def step(key_tile, carry):
        at = pl.multiple_of(key_tile * key_rows, key_rows)
        source = key_tile // tiles_each
        offset = pl.multiple_of((key_tile % tiles_each) * key_rows, key_rows)
        bias = visible(segk_ref, segq, query_row, at, key_rows)
        for group in range(KVH):
            kv = kv_ref[source, 0, pl.ds(offset, key_rows), group * 128 : (group + 1) * 128]
            kv_t = kv.astype(F32).T.astype(BF16)
            members = range(group * (QH // KVH), (group + 1) * (QH // KVH))
            scores = [contract(kv, q_s[head], 1, 1) * factor + bias for head in members]
            before = [m_s[head : head + 1, :] for head in members]
            tops = [
                jnp.maximum(old, jnp.max(part, axis=0, keepdims=True))
                for old, part in zip(before, scores)
            ]
            weights = [jnp.exp2(part - top) for part, top in zip(scores, tops)]
            sums = [jnp.sum(part, axis=0, keepdims=True) for part in weights]
            outs = [contract(kv_t, part.astype(BF16), 1, 0) for part in weights]
            for at_head, head in enumerate(members):
                fade = jnp.exp2(before[at_head] - tops[at_head])
                l_s[head : head + 1, :] = l_s[head : head + 1, :] * fade + sums[at_head]
                acc_s[head] = acc_s[head] * fade + outs[at_head]
                m_s[head : head + 1, :] = tops[at_head]
        return carry

    lax.fori_loop(low_ref[place], high_ref[place], step, 0)
    lse_ref[0] = m_s[...] + jnp.log2(l_s[...])
    for pair in range(QH // 2):
        even = (acc_s[2 * pair] / l_s[2 * pair : 2 * pair + 1, :]).T
        odd = (acc_s[2 * pair + 1] / l_s[2 * pair + 1 : 2 * pair + 2, :]).T
        out_ref[0, :, pair * 128 : (pair + 1) * 128] = jnp.where(
            lane < 64, pltpu.roll(even, 64, 1), odd
        ).astype(BF16)


def attend_back_kernel(
    place_at, low_ref, high_ref, base_ref, q_ref, kv_ref, segk_ref, segq_ref, att_ref, gatt_ref, lse_ref,
    cos_ref, sin_ref, dq_ref, dkv_ref,
    q_s, g_s, delta_s, dq_s, dkv_s,
):
    tile = pl.program_id(0)
    rows = q_ref.shape[1]
    place = place_at + tile
    lane = lanes((rows, 128))

    @pl.when(tile == 0)
    def _():
        dkv_s[...] = jnp.zeros(dkv_s.shape, F32)

    for pair in range(QH // 2):
        cols = slice(pair * 128, (pair + 1) * 128)
        both = q_ref[0, :, cols].astype(F32)
        q_s[2 * pair] = jnp.where(lane < 64, both, 0.0).astype(BF16)
        q_s[2 * pair + 1] = jnp.where(lane < 64, pltpu.roll(both, 64, 1), 0.0).astype(BF16)
        grad = gatt_ref[0, :, cols].astype(F32)
        g_s[2 * pair] = jnp.where(lane >= 64, pltpu.roll(grad, 64, 1), 0.0).astype(BF16)
        g_s[2 * pair + 1] = jnp.where(lane >= 64, grad, 0.0).astype(BF16)
        product = (grad * att_ref[0, :, cols].astype(F32)).T
        delta_s[2 * pair : 2 * pair + 1, :] = jnp.sum(product[:64], axis=0, keepdims=True)
        delta_s[2 * pair + 1 : 2 * pair + 2, :] = jnp.sum(product[64:], axis=0, keepdims=True)
    key_rows = min(KEY_TILE, kv_ref.shape[2])
    tiles_each = kv_ref.shape[2] // key_rows
    dq_s[...] = jnp.zeros(dq_s.shape, F32)
    query_row = base_ref[0] + tile * rows + lanes((1, rows))
    segq = segq_ref[0]
    qk_scale = HD ** (-0.5)
    factor = qk_scale * LOG2E

    def step(key_tile, carry):
        at = pl.multiple_of(key_tile * key_rows, key_rows)
        source = key_tile // tiles_each
        offset = pl.multiple_of((key_tile % tiles_each) * key_rows, key_rows)
        bias = visible(segk_ref, segq, query_row, at, key_rows)
        for group in range(KVH):
            kv = kv_ref[source, 0, pl.ds(offset, key_rows), group * 128 : (group + 1) * 128]
            kv_t = kv.astype(F32).T.astype(BF16)
            total = jnp.zeros((key_rows, 128), F32)
            for member in range(QH // KVH):
                head = group * (QH // KVH) + member
                q, g = q_s[head], g_s[head]
                scores = contract(kv, q, 1, 1) * factor + bias
                probs = jnp.exp2(scores - lse_ref[0, head : head + 1, :])
                d_probs = contract(kv, g, 1, 1)
                d_scores = (probs * (d_probs - delta_s[head : head + 1, :]) * qk_scale).astype(BF16)
                total = total + contract(d_scores, q, 1, 0) + contract(probs.astype(BF16), g, 1, 0)
                dq_s[head] += contract(kv_t, d_scores, 1, 0)
            cols = slice(group * 128, (group + 1) * 128)
            dkv_s[source, 0, pl.ds(offset, key_rows), cols] += total
        return carry

    lax.fori_loop(low_ref[place], high_ref[place], step, 0)
    cosine, sine = cos_ref[0], sin_ref[0]
    for pair in range(QH // 2):
        even, odd = dq_s[2 * pair].T, dq_s[2 * pair + 1].T
        even = even * cosine + swap_halves(even * sine)
        odd = odd * cosine + swap_halves(odd * sine)
        dq_ref[0, :, pair * 128 : (pair + 1) * 128] = jnp.where(
            lane < 64, even, pltpu.roll(odd, 64, 1)
        ).astype(BF16)

    @pl.when(tile == pl.num_programs(0) - 1)
    def _():
        dkv_ref[...] = dkv_s[...].astype(BF16)


def attention_specs(seq, length, rows):
    tile = lambda cols, at=seq: pl.BlockSpec((1, rows, cols), lambda t, *_: (at, t, 0))
    whole = lambda cols, at=seq: pl.BlockSpec((1, length, cols), lambda t, *_: (at, 0, 0))
    keys = lambda array, at=seq: pl.BlockSpec(
        (array.shape[0], 1) + array.shape[2:], lambda t, *_: (0, at, 0, 0)
    )
    row = lambda n, at=seq: pl.BlockSpec((1, n, rows), lambda t, *_: (at, 0, t))
    return tile, whole, keys, row


def attend(seq, bounds, q, kv_all, segk, segq):
    _, span, q_width = q.shape
    rows = min(256, span)
    tile, whole, keys, row = attention_specs(seq, segk.shape[1], rows)
    own_keys = kv_all.shape[:1] + (1,) + kv_all.shape[2:]
    return pl.pallas_call(
        functools.partial(attend_kernel, seq * (span // rows)),
        grid_spec=pltpu.PrefetchScalarGridSpec(
            num_scalar_prefetch=3,
            grid=(span // rows,),
            in_specs=[tile(q_width), keys(kv_all), whole(1), row(1)],
            out_specs=[tile(q_width, 0), row(QH, 0)],
            scratch_shapes=[
                pltpu.VMEM((QH, rows, 128), BF16),
                pltpu.VMEM((QH, rows), F32),
                pltpu.VMEM((QH, rows), F32),
                pltpu.VMEM((QH, 128, rows), F32),
            ],
        ),
        out_shape=[
            jax.ShapeDtypeStruct((1, span, q_width), BF16),
            jax.ShapeDtypeStruct((1, QH, span), F32),
        ],
        compiler_params=pltpu.CompilerParams(vmem_limit_bytes=VMEM_BYTES),
        name="attend",
    )(*bounds, q, kv_all, segk, segq)


def attend_back(seq, bounds, q, kv_all, segk, segq, att, grad_att, lse, cosine, sine):
    _, span, q_width = q.shape
    rows = min(256, span)
    tile, whole, keys, row = attention_specs(seq, segk.shape[1], rows)
    own_keys = kv_all.shape[:1] + (1,) + kv_all.shape[2:]
    return pl.pallas_call(
        functools.partial(attend_back_kernel, seq * (span // rows)),
        grid_spec=pltpu.PrefetchScalarGridSpec(
            num_scalar_prefetch=3,
            grid=(span // rows,),
            in_specs=[
                tile(q_width), keys(kv_all), whole(1), row(1), tile(q_width, 0), tile(q_width),
                row(QH, 0), tile(128), tile(128),
            ],
            out_specs=[tile(q_width, 0), keys(kv_all, 0)],
            scratch_shapes=[
                pltpu.VMEM((QH, rows, 128), BF16),
                pltpu.VMEM((QH, rows, 128), BF16),
                pltpu.VMEM((QH, rows), F32),
                pltpu.VMEM((QH, 128, rows), F32),
                pltpu.VMEM(own_keys, F32),
            ],
        ),
        out_shape=[
            jax.ShapeDtypeStruct((1, span, q_width), BF16),
            jax.ShapeDtypeStruct(own_keys, BF16),
        ],
        compiler_params=pltpu.CompilerParams(vmem_limit_bytes=VMEM_BYTES),
        name="attend_back",
    )(*bounds, q, kv_all, segk, segq, att, grad_att, lse, cosine, sine)


def rope_tables(positions):
    half = HD // 2
    frequency = ROPE_BASE ** (-jnp.arange(half, dtype=F32) / half)
    angles = positions.astype(F32)[..., None] * frequency
    cosine, sine = jnp.cos(angles), jnp.sin(angles)
    one, zero = jnp.ones(cosine.shape[:-1] + (HD,), F32), jnp.zeros(cosine.shape[:-1] + (HD,), F32)
    return (
        jnp.concatenate([cosine, cosine, one], axis=-1),
        jnp.concatenate([-sine, sine, zero], axis=-1),
    )


def attention_bounds(segments, seg_own, span_start):
    seqs, span = seg_own.shape
    rows, key_rows = min(256, span), min(KEY_TILE, span)
    first = seg_own[:, ::rows]
    begin = jnp.sum((segments[:, None, :] < first[:, :, None]).astype(jnp.int32), axis=2)
    tiles = jnp.arange(span // rows, dtype=jnp.int32)
    high = (span_start + (tiles + 1) * rows + key_rows - 1) // key_rows
    high = jnp.broadcast_to(high[None], first.shape)
    return (
        (begin // key_rows).reshape(-1),
        high.reshape(-1).astype(jnp.int32),
        jnp.full((1,), span_start, jnp.int32),
    )


CHUNK = 128
DI = MH * MP
CC = DI + 2 * NS
TAP_LANES, PREV_LANE, LAST_LANE, SEG_LANE = 0, 4, 5, 6


def split_three(values):
    high = values.astype(BF16)
    rest = values - high.astype(F32)
    middle = rest.astype(BF16)
    return high, middle, (rest - middle.astype(F32)).astype(BF16)


def product_exact(matrix, values):
    return sum(contract(matrix, part, 1, 0) for part in split_three(values))


def widen(values, spread):
    kept = jnp.where(lanes(values.shape) < 32, values, 0.0)
    high, middle, rest = (part.astype(F32) for part in split_three(kept))
    packed = high + pltpu.roll(middle, 32, 1) + pltpu.roll(rest, 64, 1)
    return contract(packed.astype(BF16), spread, 1, 0)


def gather_heads(values, spread_first):
    high = values.astype(BF16)
    rest = (values - high.astype(F32)).astype(BF16)
    return contract(high, spread_first, 1, 1) + contract(rest, spread_first, 1, 1)


def spread_matrix():
    row = lax.broadcasted_iota(jnp.int32, (128, DI), 0)
    col = lax.broadcasted_iota(jnp.int32, (128, DI), 1)
    return ((row % 32 == col // MP) & (row < 96)).astype(BF16)


def spread_first_matrix():
    row = lax.broadcasted_iota(jnp.int32, (32, DI), 0)
    col = lax.broadcasted_iota(jnp.int32, (32, DI), 1)
    return (row == col // MP).astype(BF16)


def lower_mask():
    row = lax.broadcasted_iota(jnp.int32, (CHUNK, CHUNK), 0)
    return row >= lanes((CHUNK, CHUNK))


def decay_rows(rate, head_ref, token):
    raw = rate.astype(F32) + head_ref[1:2, :]
    step = jnp.maximum(raw, 0.0) + jnp.log1p(jnp.exp(-jnp.abs(raw)))
    log_decay = -step * jnp.exp(head_ref[0:1, :])
    running = product_exact(lower_mask().astype(BF16), log_decay)
    last = running[CHUNK - 1 :, :]
    weight_end = jnp.exp(last - running) * step * token[:, LAST_LANE : LAST_LANE + 1]
    entry = jnp.exp(running) * token[:, PREV_LANE : PREV_LANE + 1]
    gain = jnp.exp(last) * token[CHUNK - 1 :, PREV_LANE : PREV_LANE + 1]
    return raw, step, log_decay, running, weight_end, entry, gain


def conv_total(ext_s, token, taps_ref, shift_ref):
    total = shift_ref[...] + ext_s[8 : 8 + CHUNK, :] * taps_ref[KC - 1 : KC, :]
    for tap in range(KC - 1):
        total = total + ext_s[5 + tap : 5 + tap + CHUNK, :] * (
            taps_ref[tap : tap + 1, :] * token[:, TAP_LANES + tap : TAP_LANES + tap + 1]
        )
    return total


def mixer_scan_kernel(
    proj_ref, rim_ref, token_ref, head_ref, taps_ref, shift_ref, spread_ref,
    act_ref, states_ref, gains_ref, final_ref, final_gain_ref,
    ext_s, state_s, gain_s,
):
    chunk = pl.program_id(0)

    @pl.when(chunk == 0)
    def _():
        ext_s[0:8, :] = rim_ref[0].astype(F32)
        state_s[...] = jnp.zeros(state_s.shape, F32)
        gain_s[...] = jnp.ones(gain_s.shape, F32)

    @pl.when(chunk > 0)
    def _():
        ext_s[0:8, :] = ext_s[CHUNK : CHUNK + 8, :]

    token = token_ref[0]
    ext_s[8 : 8 + CHUNK, :] = proj_ref[0, :, DI : DI + CC].astype(F32)
    total = conv_total(ext_s, token, taps_ref, shift_ref)
    act = (total * jax.nn.sigmoid(total)).astype(BF16)
    act_ref[0] = act
    weight_end, _, gain = decay_rows(proj_ref[0, :, DI + CC :], head_ref, token)[-3:]
    states_ref[0, 0] = state_s[...].astype(BF16)
    before = gain_s[...]
    gains_ref[0, 0] = before
    spread = spread_ref[...]
    scaled = (act[:, :DI].astype(F32) * widen(weight_end, spread)).astype(BF16)
    gain_rows = jnp.broadcast_to(gain, (8, 128))
    state = state_s[...] * widen(gain_rows, spread)[0:1, :] + contract(
        act[:, DI : DI + NS], scaled, 0, 0
    )
    state_s[...] = state
    gain_s[...] = before * gain_rows

    @pl.when(chunk == pl.num_programs(0) - 1)
    def _():
        final_ref[0] = state
        final_gain_ref[0] = before * gain_rows


def entering_state(local_ref, gains_ref, state_ref, spread):
    factor = widen(gains_ref[0, 0], spread)[0:1, :]
    return (local_ref[0, 0].astype(F32) + factor * state_ref[0].astype(F32)).astype(BF16)


def pair_decay(running, rest_t, bias, head):
    parts = []
    for at in (head, head + 1):
        column = jnp.broadcast_to(running[:, at : at + 1], (CHUNK, CHUNK))
        parts.append(jnp.exp2(column + (rest_t[at : at + 1, :] + bias)))
    return parts


def stack_pair(values):
    lane = lanes(values.shape)
    wide = values.astype(F32)
    return jnp.concatenate(
        [jnp.where(lane < 64, wide, 0.0), jnp.where(lane >= 64, wide, 0.0)], axis=0
    ).astype(BF16)


def inside_terms(running, step, token):
    seg = jnp.broadcast_to(token[:, SEG_LANE : SEG_LANE + 1], (CHUNK, CHUNK))
    bias = jnp.where((seg == seg.T) & lower_mask(), 0.0, MASKED)
    running_two = running * LOG2E
    rest_t = (jnp.log2(step) - running_two).T
    return running_two, rest_t, bias


def mixer_out_kernel(
    proj_ref, act_ref, token_ref, states_ref, gains_ref, state_ref, head_ref, skip_ref, gain_ref,
    spread_ref, y_ref, out_ref,
):
    token, spread = token_ref[0], spread_ref[...]
    _, step, _, running, _, entry, _ = decay_rows(proj_ref[0, :, DI + CC :], head_ref, token)
    b_rows, c_rows = act_ref[0, :, DI : DI + NS], act_ref[0, :, DI + NS :]
    state = entering_state(states_ref, gains_ref, state_ref, spread)
    carried = contract(c_rows, state, 1, 0) * widen(entry, spread)
    cross = contract(c_rows, b_rows, 1, 1)
    running_two, rest_t, bias = inside_terms(running, step, token)
    square = jnp.zeros((CHUNK, 128), F32)
    for pair in range(MH // 2):
        cols = slice(pair * 128, (pair + 1) * 128)
        xs = act_ref[0, :, cols]
        mix = jnp.concatenate(
            [
                (cross * part).astype(BF16)
                for part in pair_decay(running_two, rest_t, bias, 2 * pair)
            ],
            axis=1,
        )
        y = (
            contract(mix, stack_pair(xs), 1, 0)
            + carried[:, cols]
            + skip_ref[:, cols] * xs.astype(F32)
        )
        y_ref[0, :, cols] = y
        gate = proj_ref[0, :, cols].astype(F32)
        gated = y * (gate * jax.nn.sigmoid(gate))
        square = square + gated * gated
    scale = lax.rsqrt(jnp.sum(square, axis=1, keepdims=True) * (1.0 / DI) + EPSILON)
    for pair in range(MH // 2):
        cols = slice(pair * 128, (pair + 1) * 128)
        gate = proj_ref[0, :, cols].astype(F32)
        gated = y_ref[0, :, cols] * (gate * jax.nn.sigmoid(gate))
        out_ref[0, :, cols] = (gated * scale * gain_ref[:, cols]).astype(BF16)


def mixer_gate_back_kernel(
    gmix_ref, y_ref, proj_ref, act_ref, token_ref, head_ref, gain_ref, spread_ref,
    gy_ref, dgate_ref, gstates_ref, gains_ref, final_ref, dgain_ref, dskip_ref,
    state_s, gain_s, dgain_s, dskip_s,
):
    chunk = pl.program_id(0)

    @pl.when(chunk == 0)
    def _():
        dgain_s[...] = jnp.zeros(dgain_s.shape, F32)
        dskip_s[...] = jnp.zeros(dskip_s.shape, F32)

    @pl.when(chunk == 0)
    def _():
        state_s[...] = jnp.zeros(state_s.shape, F32)
        gain_s[...] = jnp.ones(gain_s.shape, F32)

    token, spread = token_ref[0], spread_ref[...]
    entry, gain = decay_rows(proj_ref[0, :, DI + CC :], head_ref, token)[-2:]
    y = y_ref[0]
    gate = proj_ref[0, :, :DI].astype(F32)
    sig = jax.nn.sigmoid(gate)
    swish = gate * sig
    gated = y * swish
    scale = lax.rsqrt(jnp.mean(gated * gated, axis=1, keepdims=True) + EPSILON)
    grad = gmix_ref[0].astype(F32)
    scaled = grad * gain_ref[...]
    shrink = jnp.mean(scaled * gated, axis=1, keepdims=True) * (scale * scale * scale)
    d_gated = scaled * scale - gated * shrink
    gy = (d_gated * swish).astype(BF16)
    gy_ref[0] = gy
    dgate_ref[0] = (d_gated * y * (sig * (1.0 + gate * (1.0 - sig)))).astype(BF16)
    dgain_s[0:1, :] += jnp.sum(grad * gated * scale, axis=0, keepdims=True)
    gy_float = gy.astype(F32)
    dskip_s[0:1, :] += jnp.sum(gy_float * act_ref[0, :, :DI].astype(F32), axis=0, keepdims=True)
    gstates_ref[0, 0] = state_s[...].astype(BF16)
    after = gain_s[...]
    gains_ref[0, 0] = after
    gain_rows = jnp.broadcast_to(gain, (8, 128))
    carried = (gy_float * widen(entry, spread)).astype(BF16)
    state = state_s[...] * widen(gain_rows, spread)[0:1, :] + contract(
        act_ref[0, :, DI + NS :], carried, 0, 0
    )
    state_s[...] = state
    gain_s[...] = after * gain_rows

    @pl.when(chunk == pl.num_programs(0) - 1)
    def _():
        final_ref[0] = state

    dgain_ref[...] = dgain_s[...]
    dskip_ref[...] = dskip_s[...]


def mixer_back_kernel(
    gy_ref, y_ref, dgate_ref, proj_ref, halo_ref, rim_ref, act_ref, token_ref,
    states_ref, gains_ref, state_ref, gstates_ref, ggains_ref, gstate_ref,
    head_ref, skip_ref, taps_ref, shift_ref, spread_ref, spread_first_ref,
    dproj_ref, drim_ref, dconv_ref, dhead_ref,
    ext_s, grad_s, carry_s, dconv_s, dhead_s,
):
    step_index = pl.program_id(0)
    last_step = pl.num_programs(0) - 1

    @pl.when(step_index == 0)
    def _():
        dconv_s[...] = jnp.zeros(dconv_s.shape, F32)
        dhead_s[...] = jnp.zeros(dhead_s.shape, F32)

    @pl.when(step_index == 0)
    def _():
        carry_s[...] = jnp.zeros(carry_s.shape, F32)

    @pl.when(step_index == last_step)
    def _():
        ext_s[0:8, :] = rim_ref[0].astype(F32)

    @pl.when(step_index < last_step)
    def _():
        ext_s[0:8, :] = halo_ref[0, :, DI : DI + CC].astype(F32)[8:16]

    ext_s[8 : 8 + CHUNK, :] = proj_ref[0, :, DI : DI + CC].astype(F32)
    token, spread, spread_first = token_ref[0], spread_ref[...], spread_first_ref[...]
    raw, step, log_decay, running, weight_end, entry, gain = decay_rows(
        proj_ref[0, :, DI + CC :], head_ref, token
    )
    b_rows, c_rows = act_ref[0, :, DI : DI + NS], act_ref[0, :, DI + NS :]
    state = entering_state(states_ref, gains_ref, state_ref, spread)
    gstate = entering_state(gstates_ref, ggains_ref, gstate_ref, spread)
    wide_end = widen(weight_end, spread)
    gy = gy_ref[0]
    gy_float = gy.astype(F32)
    gcarried = (gy_float * widen(entry, spread)).astype(BF16)
    xs_float = act_ref[0, :, :DI].astype(F32)
    grad_c = contract(gcarried, state, 1, 1)
    grad_b = contract((xs_float * wide_end).astype(BF16), gstate, 1, 1)
    from_end = contract(b_rows, gstate, 1, 0) * wide_end
    dgain_row = jnp.sum(gstate.astype(F32) * state.astype(F32), axis=0, keepdims=True)
    cross = contract(c_rows, b_rows, 1, 1)
    running_two, rest_t, bias = inside_terms(running, step, token)
    grad_cross = jnp.zeros((CHUNK, CHUNK), F32)
    lane = lanes((CHUNK, 128))
    for pair in range(MH // 2):
        cols = slice(pair * 128, (pair + 1) * 128)
        stacked = stack_pair(act_ref[0, :, cols])
        gy_pair = gy_ref[0, :, cols]
        first, second = pair_decay(running_two, rest_t, bias, 2 * pair)
        mix = jnp.concatenate([(cross * first).astype(BF16), (cross * second).astype(BF16)], axis=1)
        grad_mix = contract(gy_pair, stacked, 1, 1)
        grad_cross = grad_cross + grad_mix[:, :CHUNK] * first + grad_mix[:, CHUNK:] * second
        both = contract(mix, gy_pair, 0, 0)
        grad_s[8 : 8 + CHUNK, cols] = jnp.where(lane < 64, both[:CHUNK], both[CHUNK:])
    inner = grad_s[8 : 8 + CHUNK, :DI]
    skip = skip_ref[...]
    cross_low = grad_cross.astype(BF16)
    grad_c = grad_c + contract(cross_low, b_rows, 1, 0)
    grad_b = grad_b + contract(cross_low, c_rows, 0, 0)
    narrow = lambda values: jnp.concatenate(
        [gather_heads(values, spread_first), jnp.zeros((values.shape[0], 96), F32)], axis=1
    )
    query_part = narrow(gy_float * (y_ref[0] - skip * xs_float))
    key_inner = narrow(xs_float * inner)
    key_end = narrow(xs_float * from_end)
    extra = jnp.sum(key_end, axis=0, keepdims=True) + gain * narrow(
        jnp.broadcast_to(dgain_row, (8, DI))
    )[0:1, :]
    upper = (~lower_mask() | (lax.broadcasted_iota(jnp.int32, (CHUNK, CHUNK), 0) == lanes((CHUNK, CHUNK))))
    grad_log = product_exact(upper.astype(BF16), query_part - key_inner - key_end) + extra
    sig = jax.nn.sigmoid(raw)
    ratio = jnp.where(raw < -15.0, 1.0, sig / jnp.maximum(step, 1e-30))
    grad_rate = (key_inner + key_end) * ratio - grad_log * jnp.exp(head_ref[0:1, :]) * sig
    dhead_s[0:1, :] += jnp.sum(grad_log * log_decay, axis=0, keepdims=True)
    dhead_s[1:2, :] += jnp.sum(grad_rate, axis=0, keepdims=True)
    total = conv_total(ext_s, token, taps_ref, shift_ref)
    grad_act = jnp.concatenate([inner + from_end + skip * gy_float, grad_b, grad_c], axis=1)
    csig = jax.nn.sigmoid(total)
    grad_total = grad_act * (csig * (1.0 + total * (1.0 - csig)))
    dconv_s[KC : KC + 1, :] += jnp.sum(grad_total, axis=0, keepdims=True)
    grad_s[0:8, :] = jnp.zeros((8, CC), F32)
    grad_s[8 : 8 + CHUNK, :] = grad_total * taps_ref[KC - 1 : KC, :]
    dconv_s[KC - 1 : KC, :] += jnp.sum(grad_total * ext_s[8 : 8 + CHUNK, :], axis=0, keepdims=True)
    for tap in range(KC - 1):
        part = grad_total * token[:, TAP_LANES + tap : TAP_LANES + tap + 1]
        dconv_s[tap : tap + 1, :] += jnp.sum(
            part * ext_s[5 + tap : 5 + tap + CHUNK, :], axis=0, keepdims=True
        )
        grad_s[5 + tap : 5 + tap + CHUNK, :] += part * taps_ref[tap : tap + 1, :]
    grad_s[CHUNK : CHUNK + 8, :] += carry_s[...]
    carry_s[...] = grad_s[0:8, :]
    dproj_ref[0, :, :DI] = dgate_ref[0]
    dproj_ref[0, :, DI : DI + CC] = grad_s[8 : 8 + CHUNK, :].astype(BF16)
    dproj_ref[0, :, DI + CC :] = grad_rate.astype(BF16)

    @pl.when(step_index == last_step)
    def _():
        drim_ref[0] = carry_s[...]

    dconv_ref[...] = dconv_s[...]
    dhead_ref[...] = dhead_s[...]


def mixer_call(kernel, name, seq, chunks, reverse, inputs, outputs, scratch, earlier):
    place = (lambda c: chunks - 1 - c) if reverse else (lambda c: c)
    kinds = {
        "block": lambda array, at: pl.BlockSpec(
            (1, CHUNK, array.shape[2]), lambda c: (at, place(c), 0)
        ),
        "chunk": lambda array, at: pl.BlockSpec(
            (1, 1) + array.shape[2:], lambda c: (at, place(c), 0, 0)
        ),
        "seq": lambda array, at: pl.BlockSpec((1,) + array.shape[1:], lambda c: (at, 0, 0)),
        "own": lambda array, at: pl.BlockSpec((1,) + array.shape[1:], lambda c: (0, 0, 0)),
        "fixed": lambda array, at: pl.BlockSpec(array.shape, lambda c: (0, 0)),
        "halo": lambda array, at: pl.BlockSpec(
            (1, 16, array.shape[2]),
            lambda c: (at, jnp.maximum(place(c) * (CHUNK // 16) - 1, 0), 0),
        ),
    }
    arrays = [array for _, array in inputs]
    in_specs = [kinds[kind](array, seq) for kind, array in inputs]
    out_specs = [kinds[kind](shape, seq) for kind, shape in outputs]
    count = len(inputs)
    aliases, kept = {}, 0
    if earlier is not None:
        shared = [i for i, (kind, _) in enumerate(outputs) if kind in ("block", "chunk")]
        aliases = {count + i: out for i, out in enumerate(shared)}
        arrays += [earlier[out] for out in shared]
        in_specs += [pl.BlockSpec(memory_space=pl.ANY)] * len(shared)
        kept = len(shared)

    def run(*refs):
        kernel(*refs[:count], *refs[count + kept :])

    return pl.pallas_call(
        run,
        grid=(chunks,),
        in_specs=in_specs,
        out_specs=out_specs,
        out_shape=[shape for _, shape in outputs],
        scratch_shapes=[pltpu.VMEM(shape, F32) for shape in scratch],
        input_output_aliases=aliases,
        compiler_params=pltpu.CompilerParams(vmem_limit_bytes=VMEM_BYTES),
        name=name,
    )(*arrays)


def mixer_scan(seq, earlier, proj, rim, token, heads, taps, shift, spread):
    seqs, span, _ = proj.shape
    chunks = span // CHUNK
    return mixer_call(
        mixer_scan_kernel, "mixer_scan", seq, chunks, False,
        [
            ("block", proj), ("seq", rim), ("block", token), ("fixed", heads), ("fixed", taps),
            ("fixed", shift), ("fixed", spread),
        ],
        [
            ("block", jax.ShapeDtypeStruct((seqs, span, CC), BF16)),
            ("chunk", jax.ShapeDtypeStruct((seqs, chunks, NS, DI), BF16)),
            ("chunk", jax.ShapeDtypeStruct((seqs, chunks, 8, 128), F32)),
            ("own", jax.ShapeDtypeStruct((1, NS, DI), F32)),
            ("own", jax.ShapeDtypeStruct((1, 8, 128), F32)),
        ],
        [(CHUNK + 8, CC), (NS, DI), (8, 128)],
        earlier,
    )


def mixer_out(seq, earlier, proj, act, token, states, gains, state, heads, skip, gain, spread):
    seqs, span, _ = proj.shape
    return mixer_call(
        mixer_out_kernel, "mixer_out", seq, span // CHUNK, False,
        [
            ("block", proj), ("block", act), ("block", token), ("chunk", states),
            ("chunk", gains), ("own", state), ("fixed", heads), ("fixed", skip),
            ("fixed", gain), ("fixed", spread),
        ],
        [
            ("block", jax.ShapeDtypeStruct((seqs, span, DI), F32)),
            ("block", jax.ShapeDtypeStruct((seqs, span, DI), BF16)),
        ],
        [],
        earlier,
    )


def mixer_gate_back(seq, earlier, gmix, y, proj, act, token, heads, gain, spread):
    seqs, span, _ = proj.shape
    chunks = span // CHUNK
    return mixer_call(
        mixer_gate_back_kernel, "mixer_gate_back", seq, chunks, True,
        [
            ("block", gmix), ("block", y), ("block", proj), ("block", act), ("block", token),
            ("fixed", heads), ("fixed", gain), ("fixed", spread),
        ],
        [
            ("block", jax.ShapeDtypeStruct((seqs, span, DI), BF16)),
            ("block", jax.ShapeDtypeStruct((seqs, span, DI), BF16)),
            ("chunk", jax.ShapeDtypeStruct((seqs, chunks, NS, DI), BF16)),
            ("chunk", jax.ShapeDtypeStruct((seqs, chunks, 8, 128), F32)),
            ("own", jax.ShapeDtypeStruct((1, NS, DI), F32)),
            ("fixed", jax.ShapeDtypeStruct((8, DI), F32)),
            ("fixed", jax.ShapeDtypeStruct((8, DI), F32)),
        ],
        [(NS, DI), (8, 128), (8, DI), (8, DI)],
        earlier,
    )


def mixer_back(
    seq, earlier, gy, y, dgate, proj, rim, act, token, states, gains, state, gstates, ggains,
    gstate, heads, skip, taps, shift, spread, spread_first,
):
    seqs, span, width = proj.shape
    return mixer_call(
        mixer_back_kernel, "mixer_back", seq, span // CHUNK, True,
        [
            ("block", gy), ("block", y), ("block", dgate), ("block", proj), ("halo", proj),
            ("seq", rim), ("block", act), ("block", token), ("chunk", states), ("chunk", gains),
            ("own", state), ("chunk", gstates), ("chunk", ggains), ("own", gstate),
            ("fixed", heads), ("fixed", skip), ("fixed", taps), ("fixed", shift),
            ("fixed", spread), ("fixed", spread_first),
        ],
        [
            ("block", jax.ShapeDtypeStruct((seqs, span, width), BF16)),
            ("own", jax.ShapeDtypeStruct((1, 8, CC), F32)),
            ("fixed", jax.ShapeDtypeStruct((8, CC), F32)),
            ("fixed", jax.ShapeDtypeStruct((8, 128), F32)),
        ],
        [(CHUNK + 8, CC), (CHUNK + 8, CC), (8, CC), (8, CC), (8, 128)],
        earlier,
    )


def token_table(seg_own, seg_rim):
    seqs, span = seg_own.shape
    extended = jnp.concatenate([seg_rim, seg_own], axis=1)
    matches = [extended[:, tap : tap + span] == seg_own for tap in range(KC - 1)]
    by_chunk = seg_own.reshape(seqs, -1, CHUNK)
    last = by_chunk[:, :, -1:]
    before = jnp.concatenate([seg_rim[:, None, -1:], last[:, :-1]], axis=1)
    spare = jnp.zeros((seqs, span), F32)
    rows = [match.astype(F32) for match in matches] + [
        spare,
        (by_chunk == before).reshape(seqs, span).astype(F32),
        (by_chunk == last).reshape(seqs, span).astype(F32),
        seg_own.astype(F32),
        spare,
    ]
    return jnp.pad(jnp.stack(rows, axis=-1), ((0, 0), (0, 0), (0, 120)))


def from_behind(block, axis, distance):
    devices = range(lax.axis_size(axis))
    route = [(i - distance, i) for i in devices if i - distance in devices]
    return lax.ppermute(block, axis, route)


def after(value, *earlier):
    return lax.optimization_barrier((value, earlier))[0]


class Chain:
    def __init__(self, local, gain, reverse):
        self.local, self.gain, self.reverse = local, gain, reverse
        self.state, self.hop, self.flying = jnp.zeros(local.shape, BF16), 0, None
        self.count, self.place = lax.axis_size("ctx"), lax.axis_index("ctx")

    def send(self, *earlier):
        if self.hop == self.count - 1:
            return
        source = self.count - 1 - self.hop if self.reverse else self.hop
        target = source - 1 if self.reverse else source + 1
        sent = after((self.gain * self.state.astype(F32) + self.local).astype(BF16), *earlier)
        self.flying = (lax.ppermute(sent, "ctx", [(source, target)]), target)
        self.hop += 1

    def take(self):
        if self.flying is None:
            return
        received, target = self.flying
        self.state, self.flying = jnp.where(self.place == target, received, self.state), None

    def finish(self):
        self.take()
        while self.hop < self.count - 1:
            self.send()
            self.take()
        return self.state


def sum_everywhere(values, axes):
    for axis in axes:
        count, distance = lax.axis_size(axis), 1
        while distance < count:
            route = [(i, i ^ distance) for i in range(count)]
            values = values + lax.ppermute(values, axis, route)
            distance *= 2
    return values


def gather_all(shard):
    count, place = lax.axis_size("ctx"), lax.axis_index("ctx")
    devices, me = lax.axis_size("dp"), lax.axis_index("dp")
    relative = [shard] + [
        lax.ppermute(shard, "ctx", [(i, (i + d) % count) for i in range(count)])
        for d in range(1, count)
    ]
    ordered = jnp.stack([relative[-k % count] for k in range(count)])
    whole = lax.dynamic_slice_in_dim(
        jnp.concatenate([ordered, ordered]), (count - place) % count, count, 0
    )
    bits = devices.bit_length() - 1
    for bit in list(range(1, bits)) + [0]:
        other = lax.ppermute(whole, "dp", [(i, i ^ (1 << bit)) for i in range(devices)])
        low = ((me >> bit) & 1) == 0
        whole = jnp.stack(
            [jnp.where(low, whole, other), jnp.where(low, other, whole)],
            axis=0 if bit else bits - 1,
        )
    return whole.reshape((-1,) + shard.shape[1:])


def scatter_all(grad):
    count, place = lax.axis_size("ctx"), lax.axis_index("ctx")
    devices, me = lax.axis_size("dp"), lax.axis_index("dp")
    bits = devices.bit_length() - 1
    part = grad.reshape((2,) * bits + (count, -1, grad.shape[1]))
    for bit in [0] + list(range(bits - 1, 0, -1)):
        at = 0 if bit else bits - 1
        first, second = (lax.index_in_dim(part, side, at, False) for side in range(2))
        low = ((me >> bit) & 1) == 0
        sent = jnp.where(low, second, first).astype(BF16)
        received = lax.ppermute(sent, "dp", [(i, i ^ (1 << bit)) for i in range(devices)])
        part = jnp.where(low, first, second).astype(F32) + received.astype(F32)
    relative = lax.dynamic_slice_in_dim(jnp.concatenate([part, part]), place, count, 0)
    total, rounded = relative[0], relative.astype(BF16)
    for d in range(1, count):
        route = [(i, (i + d) % count) for i in range(count)]
        total = total + lax.ppermute(rounded[d], "ctx", route).astype(F32)
    return total


def rms_scale(values, gain_vec):
    return (
        values * lax.rsqrt(jnp.mean(values * values, axis=-1, keepdims=True) + EPSILON) * gain_vec
    )


def silu_product(gate_lin, up_lin):
    return jax.nn.silu(gate_lin) * up_lin


def body(
    layer_input, segments, positions, gain_one, w_in, conv_w, conv_b, head_params, gain_m, w_out,
    w_q, w_k, w_v, w_o, gain_two, w_gate, w_up, w_down, cotangent,
):
    seqs, span, width = layer_input.shape
    rows = seqs * span
    axes = ("dp", "ctx")
    own_rows = w_q.shape[0]
    q_width, kv_width = QH * HD, 2 * KVH * HD
    low_dot = lambda a, b: jnp.dot(a, b, preferred_element_type=F32)

    small_parts = [gain_one, gain_two, gain_m, conv_b, conv_w.reshape(-1)]
    small_sizes = [part.shape[0] for part in small_parts]
    slots = own_rows * 128
    small_block = jnp.concatenate(small_parts, axis=0)
    small_block = jnp.pad(small_block, (0, slots - sum(small_sizes))).reshape(own_rows, 128)
    w_kv = jnp.stack(
        [w_k.reshape(own_rows, KVH, HD), w_v.reshape(own_rows, KVH, HD)], axis=2
    ).reshape(own_rows, kv_width)
    gather = lambda shard: lax.all_gather(shard, axes, axis=0, tiled=True)
    first_all = gather_all(jnp.concatenate([w_q, w_kv, small_block], axis=1))
    in_width = DI + CC + 128
    w_in_all = gather(jnp.pad(w_in, ((0, 0), (0, in_width - w_in.shape[1]))))
    turned_o = w_o.T
    half_rows, ff = own_rows // 2, w_gate.shape[1]
    rest = [w_down, w_out, jnp.concatenate([turned_o[:half_rows], turned_o[half_rows:]], axis=1)]
    for matrix in (w_gate, w_up):
        rest += [matrix[:, at : at + width] for at in range(0, ff, width)]
    rest_sizes = [part.shape[0] for part in rest]
    rest_all = gather(jnp.concatenate(rest, axis=0)).reshape(-1, sum(rest_sizes), width)
    cuts, at = [], 0
    for size in rest_sizes:
        cuts.append(rest_all[:, at : at + size])
        at += size
    w_down_all, w_out_all = cuts[0].reshape(-1, width), cuts[1].reshape(-1, width)
    w_o_all = jnp.stack([cuts[2][..., :q_width], cuts[2][..., q_width:]], axis=1)
    w_o_all = w_o_all.reshape(width, q_width)
    w_gu_all = jnp.concatenate([cut.reshape(width, width) for cut in cuts[3:]], axis=1)
    small_all = first_all[:, q_width + kv_width :].reshape(-1, slots).astype(F32)
    parts, at = [], 0
    for size in small_sizes:
        parts.append(small_all[:, at : at + size])
        at += size
    gain1_all, gain2_all, gain_m_all, shift_all = [part.reshape(1, -1) for part in parts[:4]]
    taps_all = jnp.swapaxes(parts[4].reshape(-1, KC, small_sizes[3]), 0, 1).reshape(KC, CC)
    taps_all = jnp.pad(taps_all, ((0, 8 - KC), (0, 0)))

    place = lax.axis_index("ctx")
    span_start = place * span
    seg_own = lax.dynamic_slice_in_dim(segments, span_start, span, 1)
    seg_rim = jnp.where(
        place > 0,
        lax.dynamic_slice_in_dim(segments, jnp.maximum(span_start - (KC - 1), 0), KC - 1, 1),
        -1,
    )
    token = token_table(seg_own, seg_rim)
    count = lax.axis_size("ctx")
    bounds = attention_bounds(segments, seg_own, span_start)
    segk, segq = segments[:, :, None], seg_own[:, None, :]
    cosine, sine = rope_tables(positions)
    heads = jnp.pad(head_params, ((0, 5), (0, 128 - MH)))
    skip = jnp.repeat(head_params[2], MP)[None]
    spread, spread_first = spread_matrix(), spread_first_matrix()

    tokens = layer_input.reshape(rows, width)
    small = (token, bounds, segk, segq, cosine, sine, heads, skip, spread, spread_first)
    first_all, small = lax.optimization_barrier((first_all, small))
    token, bounds, segk, segq, cosine, sine, heads, skip, spread, spread_first = small
    hidden, q, kv = project(
        tokens, gain1_all, first_all, cosine.reshape(rows, 128), sine.reshape(rows, 128)
    )
    q = q.reshape(seqs, span, q_width)
    kv = kv.reshape(seqs, span, kv_width)
    exchange = lambda blocks: lax.all_to_all(blocks, "ctx", 0, 0, tiled=True)
    kv_all = exchange(jnp.broadcast_to(kv[None], (count,) + kv.shape))
    edge = from_behind(hidden.reshape(seqs, span, width)[:, span - (KC - 1) :], "ctx", 1)
    proj = low_dot(hidden, w_in_all).astype(BF16).reshape(seqs, span, in_width)
    rim = low_dot(edge.reshape(-1, width), w_in_all[:, DI : DI + CC]).astype(BF16)
    rim = jnp.pad(rim.reshape(seqs, KC - 1, CC), ((0, 0), (8 - (KC - 1), 0), (0, 0)))
    wide = lambda gain: jnp.repeat(gain[:, :1, :MH], MP, axis=2)
    scanned, chains, wide_gains = None, [], []
    for seq in range(seqs):
        scanned = mixer_scan(
            seq, scanned, proj, rim, token, heads, taps_all,
            shift_all, spread,
        )
        wide_gains.append(wide(scanned[4]))
        chains.append(Chain(scanned[3], wide_gains[seq], False))
        chains[seq].send()
    act, states, gains = scanned[:3]
    atts, lses, mixed = [], [], None
    for seq in range(seqs):
        for chain in chains[: seq + 1]:
            chain.take()
            chain.send()
        taken = [chain.state for chain in chains[: seq + 1]]
        att, lse = attend(seq, bounds, after(q, act, *taken), kv_all, segk, segq)
        atts.append(att)
        lses.append(lse)
    states_in = []
    for seq in range(seqs):
        states_in.append(chains[seq].finish())
        mixed = mixer_out(
            seq, mixed, proj, act, token, states, gains, states_in[seq], heads, skip, gain_m_all,
            spread,
        )
    mixer_y, mixer_in = mixed
    mixer_in = mixer_in.reshape(rows, DI)
    att_rows = jnp.concatenate(atts, axis=0).reshape(rows, q_width)
    middle = (
        tokens.astype(F32)
        + low_dot(mixer_in, w_out_all)
        + jnp.einsum("ra,da->rd", att_rows, w_o_all, preferred_element_type=F32)
    )
    normed_mid, norm2_pull = jax.vjp(rms_scale, middle, gain2_all)
    normed_two = normed_mid.astype(BF16)
    gate_up = low_dot(normed_two, w_gu_all).astype(BF16)
    act_float, act_pull = jax.vjp(
        silu_product, gate_up[:, :ff].astype(F32), gate_up[:, ff:].astype(F32)
    )
    act_rows = act_float.astype(BF16)
    layer_result = (middle + low_dot(act_rows, w_down_all)).astype(BF16)

    def scatter(grad):
        return lax.psum_scatter(grad, "dp", scatter_dimension=0, tiled=True)

    def weight_grad(left, right):
        return jnp.einsum("ri,ro->io", left, right, preferred_element_type=F32).astype(BF16)

    def back_dot(grad, weight):
        return jnp.einsum("ro,io->ri", grad, weight, preferred_element_type=F32)

    cot_rows = cotangent.reshape(rows, width)
    grad_down = weight_grad(act_rows, cot_rows)
    grad_gate_up = jnp.concatenate(act_pull(back_dot(cot_rows, w_down_all)), axis=1).astype(BF16)
    grad_wgu = weight_grad(normed_two, grad_gate_up)
    grad_normed = back_dot(grad_gate_up, w_gu_all)
    grad_normed, grad_down, grad_wgu = lax.optimization_barrier((grad_normed, grad_down, grad_wgu))
    part_down = scatter(grad_down)
    part_gu = scatter(grad_wgu)
    grad_mid_norm, grad_gain_second = norm2_pull(grad_normed)
    grad_middle = cot_rows.astype(F32) + grad_mid_norm
    grad_mid_low = grad_middle.astype(BF16)
    grad_wout = weight_grad(mixer_in, grad_mid_low)
    grad_wo = weight_grad(grad_mid_low, att_rows)
    grad_mixer_in = back_dot(grad_mid_low, w_out_all).astype(BF16).reshape(seqs, span, DI)
    grad_att = low_dot(grad_mid_low, w_o_all).astype(BF16).reshape(seqs, span, q_width)
    grad_mixer_in, grad_att, grad_wout, grad_wo = lax.optimization_barrier(
        (grad_mixer_in, grad_att, grad_wout, grad_wo)
    )
    grad_wo = grad_wo.reshape(-1, own_rows, q_width)
    gated, chains, grad_gain_mix, grad_skip = None, [], 0.0, 0.0
    for seq in range(seqs):
        gated = mixer_gate_back(
            seq, gated, grad_mixer_in, mixer_y, proj, act, token, heads, gain_m_all, spread
        )
        grad_gain_mix, grad_skip = grad_gain_mix + gated[5], grad_skip + gated[6]
        chains.append(Chain(gated[4], wide_gains[seq], True))
        chains[seq].send()
    grad_y, grad_gate, gstates, ggains = gated[:4]
    grad_wgates = weight_grad(hidden, grad_gate.reshape(rows, DI)).reshape(-1, own_rows, DI)
    blocks = grad_wo.shape[0]
    grad_out = jnp.concatenate(
        [
            grad_wout.reshape(blocks, -1, width),
            jnp.concatenate([grad_wo[:, :half_rows], grad_wo[:, half_rows:]], axis=2),
            grad_wgates[..., :width],
            jnp.concatenate(
                [grad_wgates[:, :half_rows, width:], grad_wgates[:, half_rows:, width:]], axis=2
            ),
        ],
        axis=1,
    )
    part_out = scatter(after(grad_out.reshape(-1, width), part_gu))
    dqs, dkvs = [], []
    for seq in range(seqs):
        for chain in chains[: seq + 1]:
            chain.take()
            chain.send(*dqs[-1:])
        taken = [chain.state for chain in chains[: seq + 1]]
        dq, dkv = attend_back(
            seq, bounds, after(q, part_down if seq < seqs - 1 else part_gu, *taken), kv_all, segk,
            segq, atts[seq], grad_att, lses[seq], cosine, sine,
        )
        dqs.append(dq)
        dkvs.append(dkv)
    dkv_all = exchange(jnp.concatenate(dkvs, axis=1))
    dq = jnp.concatenate(dqs, axis=0)
    last, rims, grad_conv, grad_heads = None, [], 0.0, 0.0
    waits = [(grad_out,)] + [()] * (seqs - 1)
    for seq in range(seqs):
        gstate = chains[seq].finish()
        last = mixer_back(
            seq, last, after(grad_y, dqs[-1], *waits[seq]), mixer_y, grad_gate, proj, rim, act, token, states,
            gains, states_in[seq], gstates, ggains, gstate, heads, skip, taps_all, shift_all,
            spread, spread_first,
        )
        rims.append(last[1])
        grad_conv, grad_heads = grad_conv + last[2], grad_heads + last[3]
    grad_proj, grad_rim = last[0], jnp.concatenate(rims, axis=0)
    back_rim = from_behind(grad_rim[:, 8 - (KC - 1) :].astype(BF16), "ctx", -1)
    edge = grad_proj[:, span - (KC - 1) :, DI : DI + CC].astype(F32) + back_rim.astype(F32)
    grad_proj = lax.dynamic_update_slice(
        grad_proj, after(edge.astype(BF16), part_out), (0, span - (KC - 1), DI)
    ).reshape(rows, in_width)
    grad_wconv = weight_grad(hidden, grad_proj[:, DI:])
    part_conv = scatter(grad_wconv)
    grad_kv = jnp.sum(after(dkv_all, grad_wconv).astype(F32), axis=0)
    out_conv = lax.psum_scatter(part_conv, "ctx", scatter_dimension=0, tiled=True).astype(F32)
    grad_kv = grad_kv.reshape(seqs, span, KVH, 2 * HD)
    turned = grad_kv[..., :HD] * sine[:, :, None, :HD]
    turned = jnp.concatenate([turned[..., HD // 2 :], turned[..., : HD // 2]], axis=-1)
    grad_key = grad_kv[..., :HD] * cosine[:, :, None, :HD] + turned
    grad_kv = jnp.concatenate([grad_key, grad_kv[..., HD:]], axis=-1).astype(BF16)
    grad_first = jnp.concatenate(
        [dq.reshape(rows, q_width), grad_kv.reshape(rows, kv_width)], axis=1
    )
    grad_wfirst = weight_grad(hidden, grad_first)
    grad_hidden = back_dot(after(grad_proj, grad_wconv), w_in_all) + back_dot(
        grad_first, first_all[:, : q_width + kv_width]
    )
    tokens_f = tokens.astype(F32)
    _, norm1_pull = jax.vjp(rms_scale, tokens_f, gain1_all)
    grad_tokens_norm, grad_gain_first = norm1_pull(grad_hidden)
    grad_tokens = (grad_middle + grad_tokens_norm).astype(BF16)

    devices = first_all.shape[0] // own_rows
    small_grads = jnp.concatenate(
        [
            grad_gain_first.reshape(devices, -1),
            grad_gain_second.reshape(devices, -1),
            grad_gain_mix[0].reshape(devices, -1),
            grad_conv[KC].reshape(devices, -1),
            jnp.swapaxes(grad_conv[:KC].reshape(KC, devices, -1), 0, 1).reshape(devices, -1),
        ],
        axis=1,
    )
    small_grads = jnp.pad(small_grads, ((0, 0), (0, slots - small_grads.shape[1])))
    out_first = scatter_all(
        jnp.concatenate([grad_wfirst, small_grads.reshape(-1, 128).astype(BF16)], axis=1)
    )
    parts = [part_down.reshape(count, -1, width), part_out.reshape(count, -1, width)]
    rest_sizes = rest_sizes[:3] + [own_rows, half_rows] + rest_sizes[3:]
    part_gu = part_gu.reshape(count, own_rows, 2 * ff)
    parts += [part_gu[..., at : at + width] for at in range(0, 2 * ff, width)]
    rest_out = lax.psum_scatter(
        after(jnp.concatenate(parts, axis=1).reshape(-1, width), part_conv),
        "ctx",
        scatter_dimension=0,
        tiled=True,
    ).astype(F32)
    outs, at = [], 0
    for size in rest_sizes:
        outs.append(rest_out[at : at + size])
        at += size
    out_down, out_wout = outs[0], outs[1]
    out_wo = jnp.concatenate([outs[2][:, :q_width], outs[2][:, q_width:]], axis=0)
    out_win = jnp.concatenate(
        [
            outs[3],
            jnp.concatenate([outs[4][:, : DI - width], outs[4][:, DI - width :]], axis=0),
            out_conv[:, : w_in.shape[1] - DI],
        ],
        axis=1,
    )
    halves = ff // width
    out_gate = jnp.concatenate(outs[5 : 5 + halves], axis=1)
    out_up = jnp.concatenate(outs[5 + halves :], axis=1)
    out_small = out_first[:, q_width + kv_width :].reshape(-1)
    pieces, at = [], 0
    for size in small_sizes:
        pieces.append(out_small[at : at + size])
        at += size
    out_kv = out_first[:, q_width : q_width + kv_width].reshape(own_rows, KVH, 2, HD)
    head_grad = sum_everywhere(
        jnp.concatenate(
            [grad_heads[:2, :MH], grad_skip[0].reshape(MH, MP).sum(axis=1)[None]], axis=0
        ),
        axes,
    )
    return (
        layer_result.reshape(layer_input.shape),
        grad_tokens.reshape(layer_input.shape),
        pieces[0],
        out_win,
        pieces[4].reshape(KC, -1),
        pieces[3],
        head_grad,
        pieces[2],
        out_wout,
        out_first[:, :q_width],
        out_kv[:, :, 0].reshape(own_rows, -1),
        out_kv[:, :, 1].reshape(own_rows, -1),
        out_wo.T,
        pieces[1],
        out_gate,
        out_up,
        out_down,
    )


def solution(mesh):
    in_specs = (
        P("dp", "ctx", None),
        P("dp", None),
        P("dp", "ctx"),
        P(("dp", "ctx")),
        P(("dp", "ctx"), None),
        P(None, ("dp", "ctx")),
        P(("dp", "ctx")),
        P(),
        P(("dp", "ctx")),
        P(("dp", "ctx"), None),
        P(("dp", "ctx"), None),
        P(("dp", "ctx"), None),
        P(("dp", "ctx"), None),
        P(None, ("dp", "ctx")),
        P(("dp", "ctx")),
        P(("dp", "ctx"), None),
        P(("dp", "ctx"), None),
        P(("dp", "ctx"), None),
        P("dp", "ctx", None),
    )
    out_specs = (
        P("dp", "ctx", None),
        P("dp", "ctx", None),
        P(("dp", "ctx")),
        P(("dp", "ctx"), None),
        P(None, ("dp", "ctx")),
        P(("dp", "ctx")),
        P(),
        P(("dp", "ctx")),
        P(("dp", "ctx"), None),
        P(("dp", "ctx"), None),
        P(("dp", "ctx"), None),
        P(("dp", "ctx"), None),
        P(None, ("dp", "ctx")),
        P(("dp", "ctx")),
        P(("dp", "ctx"), None),
        P(("dp", "ctx"), None),
        P(("dp", "ctx"), None),
    )
    return jax.shard_map(body, mesh=mesh, in_specs=in_specs, out_specs=out_specs, check_vma=False)
```

```python
import functools
import jax
import jax.numpy as jnp
from jax import lax
from jax.experimental import pallas as pl
from jax.experimental.pallas import tpu as pltpu
from jax.sharding import PartitionSpec as P

MH = 24
MP = 64
NS = 128
KC = 4
QH = 8
KVH = 2
HD = 64
EPSILON = 1e-05
ROPE_BASE = 10000.0
MASKED = -1e30
LOG2E = 1.4426950408889634
KEY_TILE = 256
VMEM_BYTES = 56 * 1024 * 1024

F32 = jnp.float32
BF16 = jnp.bfloat16


def contract(left, right, left_dim, right_dim):
    return lax.dot_general(
        left, right, (((left_dim,), (right_dim,)), ((), ())), preferred_element_type=F32
    )


def lanes(shape):
    return lax.broadcasted_iota(jnp.int32, shape, len(shape) - 1)


def swap_halves(values):
    lane = lanes(values.shape)
    return jnp.where(lane < 32, pltpu.roll(values, 96, 1), pltpu.roll(values, 32, 1))


CR = MH * MP + 2 * NS + 128
FIRST = CR + QH * HD + 2 * KVH * HD + 128


def project_kernel(x_ref, gain_ref, w_ref, cos_ref, sin_ref, hidden_ref, cr_ref, q_ref, kv_ref):
    x = x_ref[...].astype(F32)
    scale = lax.rsqrt(jnp.mean(x * x, axis=-1, keepdims=True) + EPSILON)
    hidden = (x * scale * gain_ref[...]).astype(BF16)
    hidden_ref[...] = hidden
    lin = contract(hidden, w_ref[:, CR : CR + QH * HD + 2 * KVH * HD], 1, 0)
    cosine, sine = cos_ref[...], sin_ref[...]
    lane = lanes(cosine.shape)
    for pair in range(QH // 2):
        both = lin[:, pair * 128 : (pair + 1) * 128]
        other = pltpu.roll(both, 64, 1)
        even = both * cosine + swap_halves(both) * sine
        odd = other * cosine + swap_halves(other) * sine
        q_ref[:, pair * 128 : (pair + 1) * 128] = jnp.where(
            lane < 64, even, pltpu.roll(odd, 64, 1)
        ).astype(BF16)
    for group in range(KVH):
        at = QH * HD + group * 128
        part = lin[:, at : at + 128]
        kv_ref[:, group * 128 : (group + 1) * 128] = (
            part * cosine + swap_halves(part) * sine
        ).astype(BF16)
    cr_ref[...] = contract(hidden, w_ref[:, :CR], 1, 0).astype(BF16)


def project(x, gain, w_first, cosine, sine):
    rows, width = x.shape
    tile = 256 if rows % 256 == 0 else 128
    block = lambda cols: pl.BlockSpec((tile, cols), lambda i: (i, 0))
    fixed = lambda array: pl.BlockSpec(array.shape, lambda i: (0, 0))
    cols = [width, CR, QH * HD, 2 * KVH * HD]
    return pl.pallas_call(
        project_kernel,
        grid=(rows // tile,),
        in_specs=[
            block(width), fixed(gain), pl.BlockSpec((width, FIRST), lambda i: (0, 0)), block(128),
            block(128),
        ],
        out_specs=[block(size) for size in cols],
        out_shape=[jax.ShapeDtypeStruct((rows, size), BF16) for size in cols],
        compiler_params=pltpu.CompilerParams(vmem_limit_bytes=VMEM_BYTES),
        name="project",
    )(x, gain, w_first, cosine, sine)


def finish_kernel(
    x_ref, gain_ref, dgate_ref, dcr_ref, dq_ref, dkv_ref, cos_ref, sin_ref, middle_ref, wg_ref,
    w_ref, dx_ref, dkv_out_ref, dgain_ref, dgain_s,
):
    @pl.when(pl.program_id(0) == 0)
    def _():
        dgain_s[...] = jnp.zeros(dgain_s.shape, F32)

    dkv = dkv_ref[0, 0].astype(F32)
    for source in range(1, dkv_ref.shape[0]):
        dkv = dkv + dkv_ref[source, 0].astype(F32)
    cosine, sine = cos_ref[...], sin_ref[...]
    turned = []
    for group in range(KVH):
        part = dkv[:, group * 128 : (group + 1) * 128]
        back = part * cosine + swap_halves(part * sine)
        turned.append(jnp.where(lanes(part.shape) < HD, back, part))
    dkv = jnp.concatenate(turned, axis=1).astype(BF16)
    dkv_out_ref[...] = dkv
    at = CR + QH * HD
    grad = (
        contract(dgate_ref[...], wg_ref[...], 1, 1)
        + contract(dcr_ref[...], w_ref[:, :CR], 1, 1)
        + contract(dq_ref[...], w_ref[:, CR:at], 1, 1)
        + contract(dkv, w_ref[:, at : at + 2 * KVH * HD], 1, 1)
    )
    x = x_ref[...].astype(F32)
    scale = lax.rsqrt(jnp.mean(x * x, axis=-1, keepdims=True) + EPSILON)
    scaled = grad * gain_ref[...]
    shrink = jnp.mean(scaled * x, axis=-1, keepdims=True) * (scale * scale * scale)
    dx_ref[...] = (middle_ref[...] + scaled * scale - x * shrink).astype(BF16)
    dgain_s[0:1, :] += jnp.sum(grad * x * scale, axis=0, keepdims=True)
    dgain_ref[...] = dgain_s[...]


def finish(x, gain, dgate, dcr, dq, dkv_all, cosine, sine, middle, w_gates, w_first):
    rows, width = x.shape
    span = dkv_all.shape[2]
    tile = min(256, span)
    per_seq = span // tile
    block = lambda array: pl.BlockSpec((tile, array.shape[1]), lambda i: (i, 0))
    fixed = lambda array: pl.BlockSpec(array.shape, lambda i: (0, 0))
    keys = pl.BlockSpec(
        (dkv_all.shape[0], 1, tile, dkv_all.shape[3]), lambda i: (0, i // per_seq, i % per_seq, 0)
    )
    kv_width = dkv_all.shape[3]
    return pl.pallas_call(
        finish_kernel,
        grid=(rows // tile,),
        in_specs=[
            block(x), fixed(gain), block(dgate), block(dcr), block(dq), keys, block(cosine),
            block(sine), block(middle), fixed(w_gates),
            pl.BlockSpec((width, FIRST), lambda i: (0, 0)),
        ],
        out_specs=[
            block(x),
            pl.BlockSpec((tile, kv_width), lambda i: (i, 0)),
            pl.BlockSpec((8, width), lambda i: (0, 0)),
        ],
        out_shape=[
            jax.ShapeDtypeStruct((rows, width), BF16),
            jax.ShapeDtypeStruct((rows, kv_width), BF16),
            jax.ShapeDtypeStruct((8, width), F32),
        ],
        scratch_shapes=[pltpu.VMEM((8, width), F32)],
        compiler_params=pltpu.CompilerParams(vmem_limit_bytes=VMEM_BYTES),
        name="finish",
    )(x, gain, dgate, dcr, dq, dkv_all, cosine, sine, middle, w_gates, w_first)


def visible(segk_ref, segq, query_row, at, key_rows):
    segk = segk_ref[0, pl.ds(at, key_rows), :]
    key_col = at + lax.broadcasted_iota(jnp.int32, (key_rows, 1), 0)
    return jnp.where((segk == segq) & (key_col <= query_row), 0.0, MASKED)


def attend_kernel(
    place_at, low_ref, high_ref, base_ref, q_ref, kv_ref, segk_ref, segq_ref, out_ref, lse_ref,
    q_s, m_s, l_s, acc_s,
):
    tile = pl.program_id(0)
    rows = q_ref.shape[1]
    place = place_at + tile
    lane = lanes((rows, 128))
    for pair in range(QH // 2):
        both = q_ref[0, :, pair * 128 : (pair + 1) * 128].astype(F32)
        q_s[2 * pair] = jnp.where(lane < 64, both, 0.0).astype(BF16)
        q_s[2 * pair + 1] = jnp.where(lane < 64, pltpu.roll(both, 64, 1), 0.0).astype(BF16)
    key_rows = min(KEY_TILE, kv_ref.shape[2])
    tiles_each = kv_ref.shape[2] // key_rows
    m_s[...] = jnp.full(m_s.shape, MASKED, F32)
    l_s[...] = jnp.zeros(l_s.shape, F32)
    acc_s[...] = jnp.zeros(acc_s.shape, F32)
    query_row = base_ref[0] + tile * rows + lanes((1, rows))
    segq = segq_ref[0]
    factor = HD ** (-0.5) * LOG2E

    def step(key_tile, carry):
        at = pl.multiple_of(key_tile * key_rows, key_rows)
        source = key_tile // tiles_each
        offset = pl.multiple_of((key_tile % tiles_each) * key_rows, key_rows)
        bias = visible(segk_ref, segq, query_row, at, key_rows)
        for group in range(KVH):
            kv = kv_ref[source, 0, pl.ds(offset, key_rows), group * 128 : (group + 1) * 128]
            kv_t = kv.astype(F32).T.astype(BF16)
            members = range(group * (QH // KVH), (group + 1) * (QH // KVH))
            scores = [contract(kv, q_s[head], 1, 1) * factor + bias for head in members]
            before = [m_s[head : head + 1, :] for head in members]
            tops = [
                jnp.maximum(old, jnp.max(part, axis=0, keepdims=True))
                for old, part in zip(before, scores)
            ]
            weights = [jnp.exp2(part - top) for part, top in zip(scores, tops)]
            sums = [jnp.sum(part, axis=0, keepdims=True) for part in weights]
            outs = [contract(kv_t, part.astype(BF16), 1, 0) for part in weights]
            for at_head, head in enumerate(members):
                fade = jnp.exp2(before[at_head] - tops[at_head])
                l_s[head : head + 1, :] = l_s[head : head + 1, :] * fade + sums[at_head]
                acc_s[head] = acc_s[head] * fade + outs[at_head]
                m_s[head : head + 1, :] = tops[at_head]
        return carry

    lax.fori_loop(low_ref[place], high_ref[place], step, 0)
    lse_ref[0] = m_s[...] + jnp.log2(l_s[...])
    for pair in range(QH // 2):
        even = (acc_s[2 * pair] / l_s[2 * pair : 2 * pair + 1, :]).T
        odd = (acc_s[2 * pair + 1] / l_s[2 * pair + 1 : 2 * pair + 2, :]).T
        out_ref[0, :, pair * 128 : (pair + 1) * 128] = jnp.where(
            lane < 64, pltpu.roll(even, 64, 1), odd
        ).astype(BF16)


def attend_back_kernel(
    place_at, low_ref, high_ref, base_ref, q_ref, kv_ref, segk_ref, segq_ref, att_ref, gatt_ref, lse_ref,
    cos_ref, sin_ref, dq_ref, dkv_ref,
    q_s, g_s, delta_s, dq_s, dkv_s,
):
    tile = pl.program_id(0)
    rows = q_ref.shape[1]
    place = place_at + tile
    lane = lanes((rows, 128))

    @pl.when(tile == 0)
    def _():
        dkv_s[...] = jnp.zeros(dkv_s.shape, F32)

    for pair in range(QH // 2):
        cols = slice(pair * 128, (pair + 1) * 128)
        both = q_ref[0, :, cols].astype(F32)
        q_s[2 * pair] = jnp.where(lane < 64, both, 0.0).astype(BF16)
        q_s[2 * pair + 1] = jnp.where(lane < 64, pltpu.roll(both, 64, 1), 0.0).astype(BF16)
        grad = gatt_ref[0, :, cols].astype(F32)
        g_s[2 * pair] = jnp.where(lane >= 64, pltpu.roll(grad, 64, 1), 0.0).astype(BF16)
        g_s[2 * pair + 1] = jnp.where(lane >= 64, grad, 0.0).astype(BF16)
        product = (grad * att_ref[0, :, cols].astype(F32)).T
        delta_s[2 * pair : 2 * pair + 1, :] = jnp.sum(product[:64], axis=0, keepdims=True)
        delta_s[2 * pair + 1 : 2 * pair + 2, :] = jnp.sum(product[64:], axis=0, keepdims=True)
    key_rows = min(KEY_TILE, kv_ref.shape[2])
    tiles_each = kv_ref.shape[2] // key_rows
    dq_s[...] = jnp.zeros(dq_s.shape, F32)
    query_row = base_ref[0] + tile * rows + lanes((1, rows))
    segq = segq_ref[0]
    qk_scale = HD ** (-0.5)
    factor = qk_scale * LOG2E

    def step(key_tile, carry):
        at = pl.multiple_of(key_tile * key_rows, key_rows)
        source = key_tile // tiles_each
        offset = pl.multiple_of((key_tile % tiles_each) * key_rows, key_rows)
        bias = visible(segk_ref, segq, query_row, at, key_rows)
        for group in range(KVH):
            kv = kv_ref[source, 0, pl.ds(offset, key_rows), group * 128 : (group + 1) * 128]
            kv_t = kv.astype(F32).T.astype(BF16)
            total = jnp.zeros((key_rows, 128), F32)
            for member in range(QH // KVH):
                head = group * (QH // KVH) + member
                q, g = q_s[head], g_s[head]
                scores = contract(kv, q, 1, 1) * factor + bias
                probs = jnp.exp2(scores - lse_ref[0, head : head + 1, :])
                d_probs = contract(kv, g, 1, 1)
                d_scores = (probs * (d_probs - delta_s[head : head + 1, :]) * qk_scale).astype(BF16)
                total = total + contract(d_scores, q, 1, 0) + contract(probs.astype(BF16), g, 1, 0)
                dq_s[head] += contract(kv_t, d_scores, 1, 0)
            cols = slice(group * 128, (group + 1) * 128)
            dkv_s[source, 0, pl.ds(offset, key_rows), cols] += total
        return carry

    lax.fori_loop(low_ref[place], high_ref[place], step, 0)
    cosine, sine = cos_ref[0], sin_ref[0]
    for pair in range(QH // 2):
        even, odd = dq_s[2 * pair].T, dq_s[2 * pair + 1].T
        even = even * cosine + swap_halves(even * sine)
        odd = odd * cosine + swap_halves(odd * sine)
        dq_ref[0, :, pair * 128 : (pair + 1) * 128] = jnp.where(
            lane < 64, even, pltpu.roll(odd, 64, 1)
        ).astype(BF16)

    @pl.when(tile == pl.num_programs(0) - 1)
    def _():
        dkv_ref[...] = dkv_s[...].astype(BF16)


def attention_specs(seq, length, rows):
    tile = lambda cols, at=seq: pl.BlockSpec((1, rows, cols), lambda t, *_: (at, t, 0))
    whole = lambda cols, at=seq: pl.BlockSpec((1, length, cols), lambda t, *_: (at, 0, 0))
    keys = lambda array, at=seq: pl.BlockSpec(
        (array.shape[0], 1) + array.shape[2:], lambda t, *_: (0, at, 0, 0)
    )
    row = lambda n, at=seq: pl.BlockSpec((1, n, rows), lambda t, *_: (at, 0, t))
    return tile, whole, keys, row


def attend(seq, bounds, q, kv_all, segk, segq):
    _, span, q_width = q.shape
    rows = min(256, span)
    tile, whole, keys, row = attention_specs(seq, segk.shape[1], rows)
    own_keys = kv_all.shape[:1] + (1,) + kv_all.shape[2:]
    return pl.pallas_call(
        functools.partial(attend_kernel, seq * (span // rows)),
        grid_spec=pltpu.PrefetchScalarGridSpec(
            num_scalar_prefetch=3,
            grid=(span // rows,),
            in_specs=[tile(q_width), keys(kv_all), whole(1), row(1)],
            out_specs=[tile(q_width, 0), row(QH, 0)],
            scratch_shapes=[
                pltpu.VMEM((QH, rows, 128), BF16),
                pltpu.VMEM((QH, rows), F32),
                pltpu.VMEM((QH, rows), F32),
                pltpu.VMEM((QH, 128, rows), F32),
            ],
        ),
        out_shape=[
            jax.ShapeDtypeStruct((1, span, q_width), BF16),
            jax.ShapeDtypeStruct((1, QH, span), F32),
        ],
        compiler_params=pltpu.CompilerParams(vmem_limit_bytes=VMEM_BYTES),
        name="attend",
    )(*bounds, q, kv_all, segk, segq)


def attend_back(seq, bounds, q, kv_all, segk, segq, att, grad_att, lse, cosine, sine):
    _, span, q_width = q.shape
    rows = min(256, span)
    tile, whole, keys, row = attention_specs(seq, segk.shape[1], rows)
    own_keys = kv_all.shape[:1] + (1,) + kv_all.shape[2:]
    return pl.pallas_call(
        functools.partial(attend_back_kernel, seq * (span // rows)),
        grid_spec=pltpu.PrefetchScalarGridSpec(
            num_scalar_prefetch=3,
            grid=(span // rows,),
            in_specs=[
                tile(q_width), keys(kv_all), whole(1), row(1), tile(q_width, 0), tile(q_width),
                row(QH, 0), tile(128), tile(128),
            ],
            out_specs=[tile(q_width, 0), keys(kv_all, 0)],
            scratch_shapes=[
                pltpu.VMEM((QH, rows, 128), BF16),
                pltpu.VMEM((QH, rows, 128), BF16),
                pltpu.VMEM((QH, rows), F32),
                pltpu.VMEM((QH, 128, rows), F32),
                pltpu.VMEM(own_keys, F32),
            ],
        ),
        out_shape=[
            jax.ShapeDtypeStruct((1, span, q_width), BF16),
            jax.ShapeDtypeStruct(own_keys, BF16),
        ],
        compiler_params=pltpu.CompilerParams(vmem_limit_bytes=VMEM_BYTES),
        name="attend_back",
    )(*bounds, q, kv_all, segk, segq, att, grad_att, lse, cosine, sine)


def rope_tables(positions):
    half = HD // 2
    frequency = ROPE_BASE ** (-jnp.arange(half, dtype=F32) / half)
    angles = positions.astype(F32)[..., None] * frequency
    cosine, sine = jnp.cos(angles), jnp.sin(angles)
    one, zero = jnp.ones(cosine.shape[:-1] + (HD,), F32), jnp.zeros(cosine.shape[:-1] + (HD,), F32)
    return (
        jnp.concatenate([cosine, cosine, one], axis=-1),
        jnp.concatenate([-sine, sine, zero], axis=-1),
    )


def attention_bounds(segments, seg_own, span_start):
    seqs, span = seg_own.shape
    rows, key_rows = min(256, span), min(KEY_TILE, span)
    first = seg_own[:, ::rows]
    begin = jnp.sum((segments[:, None, :] < first[:, :, None]).astype(jnp.int32), axis=2)
    tiles = jnp.arange(span // rows, dtype=jnp.int32)
    high = (span_start + (tiles + 1) * rows + key_rows - 1) // key_rows
    high = jnp.broadcast_to(high[None], first.shape)
    return (
        (begin // key_rows).reshape(-1),
        high.reshape(-1).astype(jnp.int32),
        jnp.full((1,), span_start, jnp.int32),
    )


CHUNK = 128
DI = MH * MP
CC = DI + 2 * NS
TAP_LANES, PREV_LANE, LAST_LANE, SEG_LANE = 0, 4, 5, 6


def split_three(values):
    high = values.astype(BF16)
    rest = values - high.astype(F32)
    middle = rest.astype(BF16)
    return high, middle, (rest - middle.astype(F32)).astype(BF16)


def product_exact(matrix, values):
    return sum(contract(matrix, part, 1, 0) for part in split_three(values))


def widen(values, spread):
    kept = jnp.where(lanes(values.shape) < 32, values, 0.0)
    high, middle, rest = (part.astype(F32) for part in split_three(kept))
    packed = high + pltpu.roll(middle, 32, 1) + pltpu.roll(rest, 64, 1)
    return contract(packed.astype(BF16), spread, 1, 0)


def gather_heads(values, spread_first):
    high = values.astype(BF16)
    rest = (values - high.astype(F32)).astype(BF16)
    return contract(high, spread_first, 1, 1) + contract(rest, spread_first, 1, 1)


def spread_matrix():
    row = lax.broadcasted_iota(jnp.int32, (128, DI), 0)
    col = lax.broadcasted_iota(jnp.int32, (128, DI), 1)
    return ((row % 32 == col // MP) & (row < 96)).astype(BF16)


def spread_first_matrix():
    row = lax.broadcasted_iota(jnp.int32, (32, DI), 0)
    col = lax.broadcasted_iota(jnp.int32, (32, DI), 1)
    return (row == col // MP).astype(BF16)


def lower_mask():
    row = lax.broadcasted_iota(jnp.int32, (CHUNK, CHUNK), 0)
    return row >= lanes((CHUNK, CHUNK))


def token_rows(token_ref):
    return jnp.concatenate([token_ref[0]] * 16, axis=0).T


def decay_rows(rate, head_ref, token):
    raw = rate.astype(F32) + head_ref[1:2, :]
    step = jnp.maximum(raw, 0.0) + jnp.log1p(jnp.exp(-jnp.abs(raw)))
    log_decay = -step * jnp.exp(head_ref[0:1, :])
    running = product_exact(lower_mask().astype(BF16), log_decay)
    last = running[CHUNK - 1 :, :]
    weight_end = jnp.exp(last - running) * step * token[:, LAST_LANE : LAST_LANE + 1]
    entry = jnp.exp(running) * token[:, PREV_LANE : PREV_LANE + 1]
    gain = jnp.exp(last) * token[CHUNK - 1 :, PREV_LANE : PREV_LANE + 1]
    return raw, step, log_decay, running, weight_end, entry, gain


def conv_total(ext_s, token, taps_ref, shift_ref):
    total = shift_ref[...] + ext_s[8 : 8 + CHUNK, :] * taps_ref[KC - 1 : KC, :]
    for tap in range(KC - 1):
        total = total + ext_s[5 + tap : 5 + tap + CHUNK, :] * (
            taps_ref[tap : tap + 1, :] * token[:, TAP_LANES + tap : TAP_LANES + tap + 1]
        )
    return total


def mixer_scan_kernel(
    cr_ref, rim_ref, token_ref, head_ref, taps_ref, shift_ref, spread_ref,
    act_ref, states_ref, gains_ref, final_ref, final_gain_ref,
    ext_s, state_s, gain_s,
):
    chunk = pl.program_id(0)

    @pl.when(chunk == 0)
    def _():
        ext_s[0:8, :] = rim_ref[0].astype(F32)
        state_s[...] = jnp.zeros(state_s.shape, F32)
        gain_s[...] = jnp.ones(gain_s.shape, F32)

    @pl.when(chunk > 0)
    def _():
        ext_s[0:8, :] = ext_s[CHUNK : CHUNK + 8, :]

    token = token_rows(token_ref)
    ext_s[8 : 8 + CHUNK, :] = cr_ref[0, :, :CC].astype(F32)
    total = conv_total(ext_s, token, taps_ref, shift_ref)
    act = (total * jax.nn.sigmoid(total)).astype(BF16)
    act_ref[0] = act
    weight_end, _, gain = decay_rows(cr_ref[0, :, CC:], head_ref, token)[-3:]
    states_ref[0, 0] = state_s[...].astype(BF16)
    before = gain_s[...]
    gains_ref[0, 0] = before
    spread = spread_ref[...]
    scaled = (act[:, :DI].astype(F32) * widen(weight_end, spread)).astype(BF16)
    gain_rows = jnp.broadcast_to(gain, (8, 128))
    state = state_s[...] * widen(gain_rows, spread)[0:1, :] + contract(
        act[:, DI : DI + NS], scaled, 0, 0
    )
    state_s[...] = state
    gain_s[...] = before * gain_rows

    @pl.when(chunk == pl.num_programs(0) - 1)
    def _():
        final_ref[0] = state.astype(BF16)
        final_gain_ref[0] = widen(before * gain_rows, spread)


def entering_state(local_ref, gains_ref, state_ref, spread):
    factor = widen(gains_ref[0, 0], spread)[0:1, :]
    return (local_ref[0, 0].astype(F32) + factor * state_ref[0].astype(F32)).astype(BF16)


def pair_decay(running, rest_t, bias, head):
    parts = []
    for at in (head, head + 1):
        column = jnp.broadcast_to(running[:, at : at + 1], (CHUNK, CHUNK))
        parts.append(jnp.exp2(column + (rest_t[at : at + 1, :] + bias)))
    return parts


def stack_pair(values):
    lane = lanes(values.shape)
    wide = values.astype(F32)
    return jnp.concatenate(
        [jnp.where(lane < 64, wide, 0.0), jnp.where(lane >= 64, wide, 0.0)], axis=0
    ).astype(BF16)


def inside_terms(running, step, token):
    seg = jnp.broadcast_to(token[:, SEG_LANE : SEG_LANE + 1], (CHUNK, CHUNK))
    bias = jnp.where((seg == seg.T) & lower_mask(), 0.0, MASKED)
    running_two = running * LOG2E
    rest_t = (jnp.log2(step) - running_two).T
    return running_two, rest_t, bias


def mixer_out_kernel(
    gate_ref, cr_ref, act_ref, token_ref, states_ref, gains_ref, state_ref, head_ref, skip_ref, gain_ref,
    spread_ref, y_ref, out_ref,
):
    token, spread = token_rows(token_ref), spread_ref[...]
    _, step, _, running, _, entry, _ = decay_rows(cr_ref[0, :, CC:], head_ref, token)
    b_rows, c_rows = act_ref[0, :, DI : DI + NS], act_ref[0, :, DI + NS :]
    state = entering_state(states_ref, gains_ref, state_ref, spread)
    carried = contract(c_rows, state, 1, 0) * widen(entry, spread)
    cross = contract(c_rows, b_rows, 1, 1)
    running_two, rest_t, bias = inside_terms(running, step, token)
    square = jnp.zeros((CHUNK, 128), F32)
    for pair in range(MH // 2):
        cols = slice(pair * 128, (pair + 1) * 128)
        xs = act_ref[0, :, cols]
        mix = jnp.concatenate(
            [
                (cross * part).astype(BF16)
                for part in pair_decay(running_two, rest_t, bias, 2 * pair)
            ],
            axis=1,
        )
        y = (
            contract(mix, stack_pair(xs), 1, 0)
            + carried[:, cols]
            + skip_ref[:, cols] * xs.astype(F32)
        )
        y_ref[0, :, cols] = y
        gate = gate_ref[0, :, cols].astype(F32)
        gated = y * (gate * jax.nn.sigmoid(gate))
        square = square + gated * gated
    scale = lax.rsqrt(jnp.sum(square, axis=1, keepdims=True) * (1.0 / DI) + EPSILON)
    for pair in range(MH // 2):
        cols = slice(pair * 128, (pair + 1) * 128)
        gate = gate_ref[0, :, cols].astype(F32)
        gated = y_ref[0, :, cols] * (gate * jax.nn.sigmoid(gate))
        out_ref[0, :, cols] = (gated * scale * gain_ref[:, cols]).astype(BF16)


def mixer_gate_back_kernel(
    gmix_ref, y_ref, gate_ref, cr_ref, act_ref, token_ref, head_ref, gain_ref, spread_ref,
    gy_ref, dgate_ref, gstates_ref, gains_ref, final_ref, dgain_ref, dskip_ref,
    state_s, gain_s, dgain_s, dskip_s,
):
    chunk = pl.program_id(0)

    @pl.when(chunk == 0)
    def _():
        dgain_s[...] = jnp.zeros(dgain_s.shape, F32)
        dskip_s[...] = jnp.zeros(dskip_s.shape, F32)

    @pl.when(chunk == 0)
    def _():
        state_s[...] = jnp.zeros(state_s.shape, F32)
        gain_s[...] = jnp.ones(gain_s.shape, F32)

    token, spread = token_rows(token_ref), spread_ref[...]
    entry, gain = decay_rows(cr_ref[0, :, CC:], head_ref, token)[-2:]
    y = y_ref[0]
    gate = gate_ref[0].astype(F32)
    sig = jax.nn.sigmoid(gate)
    swish = gate * sig
    gated = y * swish
    scale = lax.rsqrt(jnp.mean(gated * gated, axis=1, keepdims=True) + EPSILON)
    grad = gmix_ref[0].astype(F32)
    scaled = grad * gain_ref[...]
    shrink = jnp.mean(scaled * gated, axis=1, keepdims=True) * (scale * scale * scale)
    d_gated = scaled * scale - gated * shrink
    gy = (d_gated * swish).astype(BF16)
    gy_ref[0] = gy
    dgate_ref[0] = (d_gated * y * (sig * (1.0 + gate * (1.0 - sig)))).astype(BF16)
    dgain_s[0:1, :] += jnp.sum(grad * gated * scale, axis=0, keepdims=True)
    gy_float = gy.astype(F32)
    dskip_s[0:1, :] += jnp.sum(gy_float * act_ref[0, :, :DI].astype(F32), axis=0, keepdims=True)
    gstates_ref[0, 0] = state_s[...].astype(BF16)
    after = gain_s[...]
    gains_ref[0, 0] = after
    gain_rows = jnp.broadcast_to(gain, (8, 128))
    carried = (gy_float * widen(entry, spread)).astype(BF16)
    state = state_s[...] * widen(gain_rows, spread)[0:1, :] + contract(
        act_ref[0, :, DI + NS :], carried, 0, 0
    )
    state_s[...] = state
    gain_s[...] = after * gain_rows

    @pl.when(chunk == pl.num_programs(0) - 1)
    def _():
        final_ref[0] = state.astype(BF16)

    dgain_ref[...] = dgain_s[...]
    dskip_ref[...] = dskip_s[...]


def mixer_back_kernel(
    gy_ref, y_ref, cr_ref, halo_ref, rim_ref, act_ref, token_ref,
    states_ref, gains_ref, state_ref, gstates_ref, ggains_ref, gstate_ref,
    head_ref, skip_ref, taps_ref, shift_ref, spread_ref, spread_first_ref,
    dcr_ref, drim_ref, dconv_ref, dhead_ref,
    ext_s, grad_s, carry_s, dconv_s, dhead_s,
):
    step_index = pl.program_id(0)
    last_step = pl.num_programs(0) - 1

    @pl.when(step_index == 0)
    def _():
        dconv_s[...] = jnp.zeros(dconv_s.shape, F32)
        dhead_s[...] = jnp.zeros(dhead_s.shape, F32)

    @pl.when(step_index == 0)
    def _():
        carry_s[...] = jnp.zeros(carry_s.shape, F32)

    @pl.when(step_index == last_step)
    def _():
        ext_s[0:8, :] = rim_ref[0].astype(F32)

    @pl.when(step_index < last_step)
    def _():
        ext_s[0:8, :] = halo_ref[0, :, :CC].astype(F32)[8:16]

    ext_s[8 : 8 + CHUNK, :] = cr_ref[0, :, :CC].astype(F32)
    token, spread, spread_first = token_rows(token_ref), spread_ref[...], spread_first_ref[...]
    raw, step, log_decay, running, weight_end, entry, gain = decay_rows(
        cr_ref[0, :, CC:], head_ref, token
    )
    b_rows, c_rows = act_ref[0, :, DI : DI + NS], act_ref[0, :, DI + NS :]
    state = entering_state(states_ref, gains_ref, state_ref, spread)
    gstate = entering_state(gstates_ref, ggains_ref, gstate_ref, spread)
    wide_end = widen(weight_end, spread)
    gy = gy_ref[0]
    gy_float = gy.astype(F32)
    gcarried = (gy_float * widen(entry, spread)).astype(BF16)
    xs_float = act_ref[0, :, :DI].astype(F32)
    grad_c = contract(gcarried, state, 1, 1)
    grad_b = contract((xs_float * wide_end).astype(BF16), gstate, 1, 1)
    from_end = contract(b_rows, gstate, 1, 0) * wide_end
    dgain_row = jnp.sum(gstate.astype(F32) * state.astype(F32), axis=0, keepdims=True)
    cross = contract(c_rows, b_rows, 1, 1)
    running_two, rest_t, bias = inside_terms(running, step, token)
    grad_cross = jnp.zeros((CHUNK, CHUNK), F32)
    lane = lanes((CHUNK, 128))
    for pair in range(MH // 2):
        cols = slice(pair * 128, (pair + 1) * 128)
        stacked = stack_pair(act_ref[0, :, cols])
        gy_pair = gy_ref[0, :, cols]
        first, second = pair_decay(running_two, rest_t, bias, 2 * pair)
        mix = jnp.concatenate([(cross * first).astype(BF16), (cross * second).astype(BF16)], axis=1)
        grad_mix = contract(gy_pair, stacked, 1, 1)
        grad_cross = grad_cross + grad_mix[:, :CHUNK] * first + grad_mix[:, CHUNK:] * second
        both = contract(mix, gy_pair, 0, 0)
        grad_s[8 : 8 + CHUNK, cols] = jnp.where(lane < 64, both[:CHUNK], both[CHUNK:])
    inner = grad_s[8 : 8 + CHUNK, :DI]
    skip = skip_ref[...]
    cross_low = grad_cross.astype(BF16)
    grad_c = grad_c + contract(cross_low, b_rows, 1, 0)
    grad_b = grad_b + contract(cross_low, c_rows, 0, 0)
    narrow = lambda values: jnp.concatenate(
        [gather_heads(values, spread_first), jnp.zeros((values.shape[0], 96), F32)], axis=1
    )
    query_part = narrow(gy_float * (y_ref[0] - skip * xs_float))
    key_inner = narrow(xs_float * inner)
    key_end = narrow(xs_float * from_end)
    extra = jnp.sum(key_end, axis=0, keepdims=True) + gain * narrow(
        jnp.broadcast_to(dgain_row, (8, DI))
    )[0:1, :]
    upper = (~lower_mask() | (lax.broadcasted_iota(jnp.int32, (CHUNK, CHUNK), 0) == lanes((CHUNK, CHUNK))))
    grad_log = product_exact(upper.astype(BF16), query_part - key_inner - key_end) + extra
    sig = jax.nn.sigmoid(raw)
    ratio = jnp.where(raw < -15.0, 1.0, sig / jnp.maximum(step, 1e-30))
    grad_rate = (key_inner + key_end) * ratio - grad_log * jnp.exp(head_ref[0:1, :]) * sig
    dhead_s[0:1, :] += jnp.sum(grad_log * log_decay, axis=0, keepdims=True)
    dhead_s[1:2, :] += jnp.sum(grad_rate, axis=0, keepdims=True)
    total = conv_total(ext_s, token, taps_ref, shift_ref)
    grad_act = jnp.concatenate([inner + from_end + skip * gy_float, grad_b, grad_c], axis=1)
    csig = jax.nn.sigmoid(total)
    grad_total = grad_act * (csig * (1.0 + total * (1.0 - csig)))
    dconv_s[KC : KC + 1, :] += jnp.sum(grad_total, axis=0, keepdims=True)
    grad_s[0:8, :] = jnp.zeros((8, CC), F32)
    grad_s[8 : 8 + CHUNK, :] = grad_total * taps_ref[KC - 1 : KC, :]
    dconv_s[KC - 1 : KC, :] += jnp.sum(grad_total * ext_s[8 : 8 + CHUNK, :], axis=0, keepdims=True)
    for tap in range(KC - 1):
        part = grad_total * token[:, TAP_LANES + tap : TAP_LANES + tap + 1]
        dconv_s[tap : tap + 1, :] += jnp.sum(
            part * ext_s[5 + tap : 5 + tap + CHUNK, :], axis=0, keepdims=True
        )
        grad_s[5 + tap : 5 + tap + CHUNK, :] += part * taps_ref[tap : tap + 1, :]
    grad_s[CHUNK : CHUNK + 8, :] += carry_s[...]
    carry_s[...] = grad_s[0:8, :]
    dcr_ref[0, :, :CC] = grad_s[8 : 8 + CHUNK, :].astype(BF16)
    dcr_ref[0, :, CC:] = grad_rate.astype(BF16)

    @pl.when(step_index == last_step)
    def _():
        drim_ref[0] = carry_s[...]

    dconv_ref[...] = dconv_s[...]
    dhead_ref[...] = dhead_s[...]


def mixer_call(kernel, name, seq, chunks, reverse, inputs, outputs, scratch, earlier):
    place = (lambda c: chunks - 1 - c) if reverse else (lambda c: c)
    kinds = {
        "block": lambda array, at: pl.BlockSpec(
            (1, CHUNK, array.shape[2]), lambda c: (at, place(c), 0)
        ),
        "chunk": lambda array, at: pl.BlockSpec(
            (1, 1) + array.shape[2:], lambda c: (at, place(c), 0, 0)
        ),
        "token": lambda array, at: pl.BlockSpec((1, 8, CHUNK), lambda c: (at, 0, place(c))),
        "seq": lambda array, at: pl.BlockSpec((1,) + array.shape[1:], lambda c: (at, 0, 0)),
        "own": lambda array, at: pl.BlockSpec((1,) + array.shape[1:], lambda c: (0, 0, 0)),
        "fixed": lambda array, at: pl.BlockSpec(array.shape, lambda c: (0, 0)),
        "halo": lambda array, at: pl.BlockSpec(
            (1, 16, array.shape[2]),
            lambda c: (at, jnp.maximum(place(c) * (CHUNK // 16) - 1, 0), 0),
        ),
    }
    arrays = [array for _, array in inputs]
    in_specs = [kinds[kind](array, seq) for kind, array in inputs]
    out_specs = [kinds[kind](shape, seq) for kind, shape in outputs]
    count = len(inputs)
    aliases, kept = {}, 0
    if earlier is not None:
        shared = [i for i, (kind, _) in enumerate(outputs) if kind in ("block", "chunk")]
        aliases = {count + i: out for i, out in enumerate(shared)}
        arrays += [earlier[out] for out in shared]
        in_specs += [pl.BlockSpec(memory_space=pl.ANY)] * len(shared)
        kept = len(shared)

    def run(*refs):
        kernel(*refs[:count], *refs[count + kept :])

    return pl.pallas_call(
        run,
        grid=(chunks,),
        in_specs=in_specs,
        out_specs=out_specs,
        out_shape=[shape for _, shape in outputs],
        scratch_shapes=[pltpu.VMEM(shape, F32) for shape in scratch],
        input_output_aliases=aliases,
        compiler_params=pltpu.CompilerParams(vmem_limit_bytes=VMEM_BYTES),
        name=name,
    )(*arrays)


def mixer_scan(seq, earlier, cr, rim, token, heads, taps, shift, spread):
    seqs, span, _ = cr.shape
    chunks = span // CHUNK
    return mixer_call(
        mixer_scan_kernel, "mixer_scan", seq, chunks, False,
        [
            ("block", cr), ("seq", rim), ("token", token), ("fixed", heads), ("fixed", taps),
            ("fixed", shift), ("fixed", spread),
        ],
        [
            ("block", jax.ShapeDtypeStruct((seqs, span, CC), BF16)),
            ("chunk", jax.ShapeDtypeStruct((seqs, chunks, NS, DI), BF16)),
            ("chunk", jax.ShapeDtypeStruct((seqs, chunks, 8, 128), F32)),
            ("own", jax.ShapeDtypeStruct((1, NS, DI), BF16)),
            ("own", jax.ShapeDtypeStruct((1, 8, DI), F32)),
        ],
        [(CHUNK + 8, CC), (NS, DI), (8, 128)],
        earlier,
    )


def mixer_out(seq, earlier, gate, cr, act, token, states, gains, state, heads, skip, gain, spread):
    seqs, span, _ = cr.shape
    return mixer_call(
        mixer_out_kernel, "mixer_out", seq, span // CHUNK, False,
        [
            ("block", gate), ("block", cr), ("block", act), ("token", token), ("chunk", states),
            ("chunk", gains), ("own", state), ("fixed", heads), ("fixed", skip),
            ("fixed", gain), ("fixed", spread),
        ],
        [
            ("block", jax.ShapeDtypeStruct((seqs, span, DI), F32)),
            ("block", jax.ShapeDtypeStruct((seqs, span, DI), BF16)),
        ],
        [],
        earlier,
    )


def mixer_gate_back(
    seq, earlier, gmix, y, gate, cr, act, token, heads, gain, spread
):
    seqs, span, _ = cr.shape
    chunks = span // CHUNK
    return mixer_call(
        mixer_gate_back_kernel, "mixer_gate_back", seq, chunks, True,
        [
            ("block", gmix), ("block", y), ("block", gate), ("block", cr), ("block", act), ("token", token),
            ("fixed", heads), ("fixed", gain), ("fixed", spread),
        ],
        [
            ("block", jax.ShapeDtypeStruct((seqs, span, DI), BF16)),
            ("block", jax.ShapeDtypeStruct((seqs, span, DI), BF16)),
            ("chunk", jax.ShapeDtypeStruct((seqs, chunks, NS, DI), BF16)),
            ("chunk", jax.ShapeDtypeStruct((seqs, chunks, 8, 128), F32)),
            ("own", jax.ShapeDtypeStruct((1, NS, DI), BF16)),
            ("fixed", jax.ShapeDtypeStruct((8, DI), F32)),
            ("fixed", jax.ShapeDtypeStruct((8, DI), F32)),
        ],
        [(NS, DI), (8, 128), (8, DI), (8, DI)],
        earlier,
    )


def mixer_back(
    seq, earlier, gy, y, cr, rim, act, token, states, gains, state, gstates, ggains,
    gstate, heads, skip, taps, shift, spread, spread_first,
):
    seqs, span, width = cr.shape
    return mixer_call(
        mixer_back_kernel, "mixer_back", seq, span // CHUNK, True,
        [
            ("block", gy), ("block", y), ("block", cr), ("halo", cr),
            ("seq", rim), ("block", act), ("token", token), ("chunk", states), ("chunk", gains),
            ("own", state), ("chunk", gstates), ("chunk", ggains), ("own", gstate),
            ("fixed", heads), ("fixed", skip), ("fixed", taps), ("fixed", shift),
            ("fixed", spread), ("fixed", spread_first),
        ],
        [
            ("block", jax.ShapeDtypeStruct((seqs, span, width), BF16)),
            ("own", jax.ShapeDtypeStruct((1, 8, CC), F32)),
            ("fixed", jax.ShapeDtypeStruct((8, CC), F32)),
            ("fixed", jax.ShapeDtypeStruct((8, 128), F32)),
        ],
        [(CHUNK + 8, CC), (CHUNK + 8, CC), (8, CC), (8, CC), (8, 128)],
        earlier,
    )


def token_table(seg_own, seg_rim):
    seqs, span = seg_own.shape
    extended = jnp.concatenate([seg_rim, seg_own], axis=1)
    matches = [extended[:, tap : tap + span] == seg_own for tap in range(KC - 1)]
    by_chunk = seg_own.reshape(seqs, -1, CHUNK)
    last = by_chunk[:, :, -1:]
    before = jnp.concatenate([seg_rim[:, None, -1:], last[:, :-1]], axis=1)
    spare = jnp.zeros((seqs, span), F32)
    rows = [match.astype(F32) for match in matches] + [
        spare,
        (by_chunk == before).reshape(seqs, span).astype(F32),
        (by_chunk == last).reshape(seqs, span).astype(F32),
        seg_own.astype(F32),
        spare,
    ]
    return jnp.stack(rows, axis=1)


def from_behind(block, axis, distance):
    devices = range(lax.axis_size(axis))
    route = [(i - distance, i) for i in devices if i - distance in devices]
    return lax.ppermute(block, axis, route)


def after(value, *earlier):
    return lax.optimization_barrier((value, earlier))[0]


class Chain:
    def __init__(self, local, gain, reverse):
        self.local, self.gain, self.reverse = local, gain, reverse
        self.state, self.hop, self.flying = jnp.zeros(local.shape, BF16), 0, None
        self.count, self.place = lax.axis_size("ctx"), lax.axis_index("ctx")

    def send(self, *earlier):
        if self.hop == self.count - 1:
            return
        source = self.count - 1 - self.hop if self.reverse else self.hop
        target = source - 1 if self.reverse else source + 1
        sent = self.local
        if self.hop:
            sent = (self.gain * self.state.astype(F32) + sent.astype(F32)).astype(BF16)
        if earlier:
            sent = after(sent, *earlier)
        self.flying = (lax.ppermute(sent, "ctx", [(source, target)]), target)
        self.hop += 1

    def take(self):
        if self.flying is None:
            return
        received, target = self.flying
        self.state, self.flying = jnp.where(self.place == target, received, self.state), None

    def finish(self):
        self.take()
        while self.hop < self.count - 1:
            self.send()
            self.take()
        return self.state


def sum_everywhere(values, axes):
    for axis in axes:
        count, distance = lax.axis_size(axis), 1
        while distance < count:
            route = [(i, i ^ distance) for i in range(count)]
            values = values + lax.ppermute(values, axis, route)
            distance *= 2
    return values


def scatter_all(grad):
    count, place = lax.axis_size("ctx"), lax.axis_index("ctx")
    devices, me = lax.axis_size("dp"), lax.axis_index("dp")
    bits = devices.bit_length() - 1
    part = grad.reshape((2,) * bits + (count, -1, grad.shape[1]))
    for bit in [0] + list(range(bits - 1, 0, -1)):
        at = 0 if bit else bits - 1
        first, second = (lax.index_in_dim(part, side, at, False) for side in range(2))
        low = ((me >> bit) & 1) == 0
        sent = jnp.where(low, second, first).astype(BF16)
        received = lax.ppermute(sent, "dp", [(i, i ^ (1 << bit)) for i in range(devices)])
        part = jnp.where(low, first, second).astype(F32) + received.astype(F32)
    relative = lax.dynamic_slice_in_dim(jnp.concatenate([part, part]), place, count, 0)
    total, rounded = relative[0], relative.astype(BF16)
    for d in range(1, count):
        route = [(i, (i + d) % count) for i in range(count)]
        total = total + lax.ppermute(rounded[d], "ctx", route).astype(F32)
    return total


def rms_scale(values, gain_vec):
    return (
        values * lax.rsqrt(jnp.mean(values * values, axis=-1, keepdims=True) + EPSILON) * gain_vec
    )


def silu_product(gate_lin, up_lin):
    return jax.nn.silu(gate_lin) * up_lin


def body(
    layer_input, segments, positions, gain_one, w_in, conv_w, conv_b, head_params, gain_m, w_out,
    w_q, w_k, w_v, w_o, gain_two, w_gate, w_up, w_down, cotangent,
):
    seqs, span, width = layer_input.shape
    rows = seqs * span
    axes = ("dp", "ctx")
    own_rows = w_q.shape[0]
    q_width, kv_width = QH * HD, 2 * KVH * HD
    low_dot = lambda a, b: jnp.dot(a, b, preferred_element_type=F32)

    small_parts = [gain_one, gain_two, gain_m, conv_b, conv_w.reshape(-1)]
    small_sizes = [part.shape[0] for part in small_parts]
    slots = own_rows * 128
    small_block = jnp.concatenate(small_parts, axis=0)
    small_block = jnp.pad(small_block, (0, slots - sum(small_sizes))).reshape(own_rows, 128)
    w_kv = jnp.stack(
        [w_k.reshape(own_rows, KVH, HD), w_v.reshape(own_rows, KVH, HD)], axis=2
    ).reshape(own_rows, kv_width)
    gather = lambda shard: lax.all_gather(shard, axes, axis=0, tiled=True)
    w_cr = jnp.pad(w_in[:, DI:], ((0, 0), (0, CR - (w_in.shape[1] - DI))))
    first_all = gather(jnp.concatenate([w_cr, w_q, w_kv, small_block, w_in[:, :DI]], axis=1))
    turned_o = w_o.T
    half_rows, ff = own_rows // 2, w_gate.shape[1]

    def fold(block, cut):
        return jnp.concatenate([block[..., :half_rows, cut:], block[..., half_rows:, cut:]], axis=-1)

    def unfold(block):
        half = block.shape[-1] // 2
        return jnp.concatenate([block[..., :half], block[..., half:]], axis=-2)

    rest = [w_down, w_out, fold(turned_o, 0)]
    for matrix in (w_gate, w_up):
        rest += [matrix[:, at : at + width] for at in range(0, ff, width)]
    rest_sizes = [part.shape[0] for part in rest]
    rest_all = gather(jnp.concatenate(rest, axis=0)).reshape(-1, sum(rest_sizes), width)
    cuts, at = [], 0
    for size in rest_sizes:
        cuts.append(rest_all[:, at : at + size])
        at += size
    w_down_all, w_out_all = cuts[0].reshape(-1, width), cuts[1].reshape(-1, width)
    w_o_all = unfold(cuts[2]).reshape(width, q_width)
    w_gates = first_all[:, FIRST:]
    w_gu_all = jnp.concatenate([cut.reshape(width, width) for cut in cuts[3:]], axis=1)
    small_all = first_all[:, FIRST - 128 : FIRST].reshape(-1, slots).astype(F32)
    parts, at = [], 0
    for size in small_sizes:
        parts.append(small_all[:, at : at + size])
        at += size
    gain1_all, gain2_all, gain_m_all, shift_all = [part.reshape(1, -1) for part in parts[:4]]
    taps_all = jnp.swapaxes(parts[4].reshape(-1, KC, small_sizes[3]), 0, 1).reshape(KC, CC)
    taps_all = jnp.pad(taps_all, ((0, 8 - KC), (0, 0)))

    place = lax.axis_index("ctx")
    span_start = place * span
    seg_own = lax.dynamic_slice_in_dim(segments, span_start, span, 1)
    seg_rim = jnp.where(
        place > 0,
        lax.dynamic_slice_in_dim(segments, jnp.maximum(span_start - (KC - 1), 0), KC - 1, 1),
        -1,
    )
    token = token_table(seg_own, seg_rim)
    count = lax.axis_size("ctx")
    bounds = attention_bounds(segments, seg_own, span_start)
    segk, segq = segments[:, :, None], seg_own[:, None, :]
    cosine, sine = rope_tables(positions)
    heads = jnp.pad(head_params, ((0, 5), (0, 128 - MH)))
    skip = jnp.repeat(head_params[2], MP)[None]
    spread, spread_first = spread_matrix(), spread_first_matrix()

    tokens = layer_input.reshape(rows, width)
    small = (token, bounds, segk, segq, cosine, sine, heads, skip, spread, spread_first)
    first_all, small = lax.optimization_barrier((first_all, small))
    token, bounds, segk, segq, cosine, sine, heads, skip, spread, spread_first = small
    cosine, sine = cosine.reshape(rows, 128), sine.reshape(rows, 128)
    hidden, cr, q, kv = project(tokens, gain1_all, first_all, cosine, sine)
    q = q.reshape(seqs, span, q_width)
    kv = kv.reshape(seqs, span, kv_width)
    exchange = lambda blocks: lax.all_to_all(blocks, "ctx", 0, 0, tiled=True)
    kv_all = exchange(jnp.broadcast_to(kv[None], (count,) + kv.shape))
    cr = cr.reshape(seqs, span, CR)
    rim = from_behind(cr[:, span - (KC - 1) :, :CC], "ctx", 1)
    rim = jnp.pad(rim, ((0, 0), (8 - (KC - 1), 0), (0, 0)))
    scanned, chains, wide_gains = None, [], []
    for seq in range(seqs):
        scanned = mixer_scan(
            seq, scanned, cr, rim, token, heads, taps_all,
            shift_all, spread,
        )
        wide_gains.append(scanned[4][:, :1])
        chains.append(Chain(scanned[3], wide_gains[seq], False))
        chains[seq].send()
    act, states, gains = scanned[:3]
    atts, lses, mixed = [], [], None
    for seq in range(seqs):
        for chain in chains[: seq + 1]:
            chain.take()
            chain.send()
        taken = [chain.state for chain in chains[: seq + 1]]
        att, lse = attend(seq, bounds, after(q, act, *taken), kv_all, segk, segq)
        atts.append(att)
        lses.append(lse)
    gate = low_dot(hidden, w_gates).astype(BF16).reshape(seqs, span, DI)
    states_in = []
    for seq in range(seqs):
        states_in.append(chains[seq].finish())
        mixed = mixer_out(
            seq, mixed, gate, cr, act, token, states, gains, states_in[seq], heads, skip, gain_m_all,
            spread,
        )
    mixer_y, mixer_in = mixed
    mixer_in = mixer_in.reshape(rows, DI)
    att_rows = jnp.concatenate(atts, axis=0).reshape(rows, q_width)
    middle = (
        tokens.astype(F32)
        + low_dot(mixer_in, w_out_all)
        + jnp.einsum("ra,da->rd", att_rows, w_o_all, preferred_element_type=F32)
    )
    normed_mid, norm2_pull = jax.vjp(rms_scale, middle, gain2_all)
    normed_two = normed_mid.astype(BF16)
    gate_up = low_dot(normed_two, w_gu_all).astype(BF16)
    act_float, act_pull = jax.vjp(
        silu_product, gate_up[:, :ff].astype(F32), gate_up[:, ff:].astype(F32)
    )
    act_rows = act_float.astype(BF16)
    def scatter(grad):
        return lax.psum_scatter(grad, "dp", scatter_dimension=0, tiled=True)

    def weight_grad(left, right):
        return jnp.einsum("ri,ro->io", left, right, preferred_element_type=F32).astype(BF16)

    def back_dot(grad, weight):
        return jnp.einsum("ro,io->ri", grad, weight, preferred_element_type=F32)

    cot_rows = cotangent.reshape(rows, width)
    grad_down = weight_grad(act_rows, cot_rows)
    grad_gate_up = jnp.concatenate(act_pull(back_dot(cot_rows, w_down_all)), axis=1).astype(BF16)
    grad_wgu = weight_grad(normed_two, grad_gate_up)
    grad_normed = back_dot(grad_gate_up, w_gu_all)
    grad_normed, grad_down, grad_wgu = lax.optimization_barrier((grad_normed, grad_down, grad_wgu))
    part_gu = scatter(grad_wgu)
    grad_mid_norm, grad_gain_second = norm2_pull(grad_normed)
    grad_middle = cot_rows.astype(F32) + grad_mid_norm
    grad_mid_low = grad_middle.astype(BF16)
    grad_wout = weight_grad(mixer_in, grad_mid_low)
    grad_wo = weight_grad(grad_mid_low, att_rows)
    grad_mixer_in = back_dot(grad_mid_low, w_out_all).astype(BF16).reshape(seqs, span, DI)
    grad_att = low_dot(grad_mid_low, w_o_all).astype(BF16).reshape(seqs, span, q_width)
    grad_mixer_in, grad_att, grad_wout, grad_wo = lax.optimization_barrier(
        (grad_mixer_in, grad_att, grad_wout, grad_wo)
    )
    grad_wo = grad_wo.reshape(-1, own_rows, q_width)
    gated, chains, grad_gain_mix, grad_skip = None, [], 0.0, 0.0
    for seq in range(seqs):
        gated = mixer_gate_back(
            seq, gated, grad_mixer_in, mixer_y, gate, cr, act, token, heads, gain_m_all, spread
        )
        grad_gain_mix, grad_skip = grad_gain_mix + gated[5], grad_skip + gated[6]
        chains.append(Chain(gated[4], wide_gains[seq], True))
        chains[seq].send()
    grad_y, grad_gate, gstates, ggains = gated[:4]
    grad_wgates = weight_grad(hidden, grad_gate.reshape(rows, DI)).reshape(-1, own_rows, DI)
    blocks = grad_wo.shape[0]
    grad_rest = jnp.concatenate(
        [
            grad_down.reshape(blocks, -1, width), grad_wout.reshape(blocks, -1, width),
            fold(grad_wo, 0), grad_wgates[..., :width], fold(grad_wgates, width),
        ],
        axis=1,
    )
    part_rest = scatter(grad_rest.reshape(-1, width))
    cos3, sin3 = cosine.reshape(seqs, span, 128), sine.reshape(seqs, span, 128)
    dqs, dkvs = [], []
    for seq in range(seqs):
        for chain in chains[: seq + 1]:
            chain.take()
            chain.send(*dqs[-1:])
        taken = [chain.state for chain in chains[: seq + 1]]
        dq, dkv = attend_back(
            seq, bounds, after(q, *taken), kv_all, segk,
            segq, atts[seq], grad_att, lses[seq], cos3, sin3,
        )
        dqs.append(dq)
        dkvs.append(dkv)
    dkv_all = exchange(jnp.concatenate(dkvs, axis=1))
    dq = jnp.concatenate(dqs, axis=0)
    last, rims, grad_conv, grad_heads = None, [], 0.0, 0.0
    waits = [(grad_rest, part_gu)] + [()] * (seqs - 1)
    for seq in range(seqs):
        gstate = chains[seq].finish()
        if seq == seqs - 1:
            gu_blocks = part_gu.reshape(count, own_rows, 2 * ff)
            parts = [after(part_rest, *rims).reshape(count, -1, width)]
            parts += [gu_blocks[..., at : at + width] for at in range(0, 2 * ff, width)]
            rest_low = jnp.concatenate(parts, axis=1).reshape(-1, width)
            waits[seq] = (rest_low,)
        last = mixer_back(
            seq, last, after(grad_y, dqs[-1], *waits[seq]), mixer_y, cr, rim, act, token, states,
            gains, states_in[seq], gstates, ggains, gstate, heads, skip, taps_all, shift_all,
            spread, spread_first,
        )
        rims.append(last[1])
        grad_conv, grad_heads = grad_conv + last[2], grad_heads + last[3]
    grad_cr, grad_rim = last[0], jnp.concatenate(rims, axis=0)
    back_rim = from_behind(grad_rim[:, 8 - (KC - 1) :].astype(BF16), "ctx", -1)
    edge = grad_cr[:, span - (KC - 1) :, :CC].astype(F32) + back_rim.astype(F32)
    grad_cr = lax.dynamic_update_slice(
        grad_cr, edge.astype(BF16), (0, span - (KC - 1), 0)
    ).reshape(rows, CR)
    rest_out = lax.psum_scatter(rest_low, "ctx", scatter_dimension=0, tiled=True).astype(F32)
    grad_wcr = weight_grad(hidden, grad_cr)
    part_cr = scatter(grad_wcr)
    layer_result = (middle + low_dot(after(act_rows, part_cr), w_down_all)).astype(BF16)
    out_cr = lax.psum_scatter(part_cr, "ctx", scatter_dimension=0, tiled=True).astype(F32)
    grad_tokens, grad_kv, grad_gain_first = finish(
        tokens, gain1_all, grad_gate.reshape(rows, DI), after(grad_cr, grad_wcr, rest_out),
        dq.reshape(rows, q_width), dkv_all, cosine, sine, grad_middle, w_gates, first_all,
    )
    grad_first = jnp.concatenate([dq.reshape(rows, q_width), grad_kv], axis=1)
    grad_wfirst = weight_grad(hidden, grad_first)
    grad_gain_first = grad_gain_first[0]

    devices = first_all.shape[0] // own_rows
    small_grads = jnp.concatenate(
        [
            grad_gain_first.reshape(devices, -1),
            grad_gain_second.reshape(devices, -1),
            grad_gain_mix[0].reshape(devices, -1),
            grad_conv[KC].reshape(devices, -1),
            jnp.swapaxes(grad_conv[:KC].reshape(KC, devices, -1), 0, 1).reshape(devices, -1),
        ],
        axis=1,
    )
    small_grads = jnp.pad(small_grads, ((0, 0), (0, slots - small_grads.shape[1])))
    out_first = scatter_all(
        jnp.concatenate([grad_wfirst, small_grads.reshape(-1, 128).astype(BF16)], axis=1)
    )
    rest_sizes = rest_sizes[:3] + [own_rows, half_rows] + rest_sizes[3:]
    outs, at = [], 0
    for size in rest_sizes:
        outs.append(rest_out[at : at + size])
        at += size
    out_down, out_wout = outs[0], outs[1]
    out_wo = unfold(outs[2])
    out_win = jnp.concatenate(
        [outs[3], unfold(outs[4]), out_cr[:, : w_in.shape[1] - DI]], axis=1
    )
    halves = ff // width
    out_gate = jnp.concatenate(outs[5 : 5 + halves], axis=1)
    out_up = jnp.concatenate(outs[5 + halves :], axis=1)
    out_small = out_first[:, q_width + kv_width :].reshape(-1)
    pieces, at = [], 0
    for size in small_sizes:
        pieces.append(out_small[at : at + size])
        at += size
    out_kv = out_first[:, q_width : q_width + kv_width].reshape(own_rows, KVH, 2, HD)
    head_grad = sum_everywhere(
        jnp.concatenate(
            [grad_heads[:2, :MH], grad_skip[0].reshape(MH, MP).sum(axis=1)[None]], axis=0
        ),
        axes,
    )
    return (
        layer_result.reshape(layer_input.shape),
        grad_tokens.reshape(layer_input.shape),
        pieces[0],
        out_win,
        pieces[4].reshape(KC, -1),
        pieces[3],
        head_grad,
        pieces[2],
        out_wout,
        out_first[:, :q_width],
        out_kv[:, :, 0].reshape(own_rows, -1),
        out_kv[:, :, 1].reshape(own_rows, -1),
        out_wo.T,
        pieces[1],
        out_gate,
        out_up,
        out_down,
    )


def solution(mesh):
    in_specs = (
        P("dp", "ctx", None),
        P("dp", None),
        P("dp", "ctx"),
        P(("dp", "ctx")),
        P(("dp", "ctx"), None),
        P(None, ("dp", "ctx")),
        P(("dp", "ctx")),
        P(),
        P(("dp", "ctx")),
        P(("dp", "ctx"), None),
        P(("dp", "ctx"), None),
        P(("dp", "ctx"), None),
        P(("dp", "ctx"), None),
        P(None, ("dp", "ctx")),
        P(("dp", "ctx")),
        P(("dp", "ctx"), None),
        P(("dp", "ctx"), None),
        P(("dp", "ctx"), None),
        P("dp", "ctx", None),
    )
    out_specs = (
        P("dp", "ctx", None),
        P("dp", "ctx", None),
        P(("dp", "ctx")),
        P(("dp", "ctx"), None),
        P(None, ("dp", "ctx")),
        P(("dp", "ctx")),
        P(),
        P(("dp", "ctx")),
        P(("dp", "ctx"), None),
        P(("dp", "ctx"), None),
        P(("dp", "ctx"), None),
        P(("dp", "ctx"), None),
        P(None, ("dp", "ctx")),
        P(("dp", "ctx")),
        P(("dp", "ctx"), None),
        P(("dp", "ctx"), None),
        P(("dp", "ctx"), None),
    )
    return jax.shard_map(body, mesh=mesh, in_specs=in_specs, out_specs=out_specs, check_vma=False)
```

```python
import functools
import jax
import jax.numpy as jnp
from jax import lax
from jax.experimental import pallas as pl
from jax.experimental.pallas import tpu as pltpu
from jax.sharding import PartitionSpec as P

MH = 24
MP = 64
NS = 128
KC = 4
QH = 8
KVH = 2
HD = 64
EPSILON = 1e-05
ROPE_BASE = 10000.0
MASKED = -1e30
LOG2E = 1.4426950408889634
KEY_TILE = 256
VMEM_BYTES = 56 * 1024 * 1024

F32 = jnp.float32
BF16 = jnp.bfloat16


def contract(left, right, left_dim, right_dim):
    return lax.dot_general(
        left, right, (((left_dim,), (right_dim,)), ((), ())), preferred_element_type=F32
    )


def lanes(shape):
    return lax.broadcasted_iota(jnp.int32, shape, len(shape) - 1)


def swap_halves(values):
    lane = lanes(values.shape)
    return jnp.where(lane < 32, pltpu.roll(values, 96, 1), pltpu.roll(values, 32, 1))


CR = MH * MP + 2 * NS + 128
FIRST = CR + QH * HD + 2 * KVH * HD + 128


def project_kernel(x_ref, gain_ref, w_ref, cos_ref, sin_ref, hidden_ref, cr_ref, q_ref, kv_ref):
    x = x_ref[...].astype(F32)
    scale = lax.rsqrt(jnp.mean(x * x, axis=-1, keepdims=True) + EPSILON)
    hidden = (x * scale * gain_ref[...]).astype(BF16)
    hidden_ref[...] = hidden
    lin = contract(hidden, w_ref[:, CR : CR + QH * HD + 2 * KVH * HD], 1, 0)
    cosine, sine = cos_ref[...], sin_ref[...]
    lane = lanes(cosine.shape)
    for pair in range(QH // 2):
        both = lin[:, pair * 128 : (pair + 1) * 128]
        other = pltpu.roll(both, 64, 1)
        even = both * cosine + swap_halves(both) * sine
        odd = other * cosine + swap_halves(other) * sine
        q_ref[:, pair * 128 : (pair + 1) * 128] = jnp.where(
            lane < 64, even, pltpu.roll(odd, 64, 1)
        ).astype(BF16)
    for group in range(KVH):
        at = QH * HD + group * 128
        part = lin[:, at : at + 128]
        kv_ref[:, group * 128 : (group + 1) * 128] = (
            part * cosine + swap_halves(part) * sine
        ).astype(BF16)
    cr_ref[...] = contract(hidden, w_ref[:, :CR], 1, 0).astype(BF16)


def project(x, gain, w_first, cosine, sine):
    rows, width = x.shape
    tile = 256 if rows % 256 == 0 else 128
    block = lambda cols: pl.BlockSpec((tile, cols), lambda i: (i, 0))
    fixed = lambda array: pl.BlockSpec(array.shape, lambda i: (0, 0))
    cols = [width, CR, QH * HD, 2 * KVH * HD]
    return pl.pallas_call(
        project_kernel,
        grid=(rows // tile,),
        in_specs=[
            block(width), fixed(gain), pl.BlockSpec((width, FIRST), lambda i: (0, 0)), block(128),
            block(128),
        ],
        out_specs=[block(size) for size in cols],
        out_shape=[jax.ShapeDtypeStruct((rows, size), BF16) for size in cols],
        compiler_params=pltpu.CompilerParams(vmem_limit_bytes=VMEM_BYTES),
        name="project",
    )(x, gain, w_first, cosine, sine)


def finish_kernel(
    x_ref, gain_ref, dgate_ref, dcr_ref, dq_ref, dkv_ref, cos_ref, sin_ref, middle_ref, wg_ref,
    w_ref, dx_ref, dkv_out_ref, dgain_ref, dgain_s,
):
    @pl.when(pl.program_id(0) == 0)
    def _():
        dgain_s[...] = jnp.zeros(dgain_s.shape, F32)

    dkv = dkv_ref[0, 0].astype(F32)
    for source in range(1, dkv_ref.shape[0]):
        dkv = dkv + dkv_ref[source, 0].astype(F32)
    cosine, sine = cos_ref[...], sin_ref[...]
    turned = []
    for group in range(KVH):
        part = dkv[:, group * 128 : (group + 1) * 128]
        back = part * cosine + swap_halves(part * sine)
        turned.append(jnp.where(lanes(part.shape) < HD, back, part))
    dkv = jnp.concatenate(turned, axis=1).astype(BF16)
    dkv_out_ref[...] = dkv
    at = CR + QH * HD
    grad = (
        contract(dgate_ref[...], wg_ref[...], 1, 1)
        + contract(dcr_ref[...], w_ref[:, :CR], 1, 1)
        + contract(dq_ref[...], w_ref[:, CR:at], 1, 1)
        + contract(dkv, w_ref[:, at : at + 2 * KVH * HD], 1, 1)
    )
    x = x_ref[...].astype(F32)
    scale = lax.rsqrt(jnp.mean(x * x, axis=-1, keepdims=True) + EPSILON)
    scaled = grad * gain_ref[...]
    shrink = jnp.mean(scaled * x, axis=-1, keepdims=True) * (scale * scale * scale)
    dx_ref[...] = (middle_ref[...] + scaled * scale - x * shrink).astype(BF16)
    dgain_s[0:1, :] += jnp.sum(grad * x * scale, axis=0, keepdims=True)
    dgain_ref[...] = dgain_s[...]


def finish(x, gain, dgate, dcr, dq, dkv_all, cosine, sine, middle, w_gates, w_first):
    rows, width = x.shape
    span = dkv_all.shape[2]
    tile = min(256, span)
    per_seq = span // tile
    block = lambda array: pl.BlockSpec((tile, array.shape[1]), lambda i: (i, 0))
    fixed = lambda array: pl.BlockSpec(array.shape, lambda i: (0, 0))
    keys = pl.BlockSpec(
        (dkv_all.shape[0], 1, tile, dkv_all.shape[3]), lambda i: (0, i // per_seq, i % per_seq, 0)
    )
    kv_width = dkv_all.shape[3]
    return pl.pallas_call(
        finish_kernel,
        grid=(rows // tile,),
        in_specs=[
            block(x), fixed(gain), block(dgate), block(dcr), block(dq), keys, block(cosine),
            block(sine), block(middle), fixed(w_gates),
            pl.BlockSpec((width, FIRST), lambda i: (0, 0)),
        ],
        out_specs=[
            block(x),
            pl.BlockSpec((tile, kv_width), lambda i: (i, 0)),
            pl.BlockSpec((8, width), lambda i: (0, 0)),
        ],
        out_shape=[
            jax.ShapeDtypeStruct((rows, width), BF16),
            jax.ShapeDtypeStruct((rows, kv_width), BF16),
            jax.ShapeDtypeStruct((8, width), F32),
        ],
        scratch_shapes=[pltpu.VMEM((8, width), F32)],
        compiler_params=pltpu.CompilerParams(vmem_limit_bytes=VMEM_BYTES),
        name="finish",
    )(x, gain, dgate, dcr, dq, dkv_all, cosine, sine, middle, w_gates, w_first)


def visible(segk_ref, segq, query_row, at, key_rows):
    segk = segk_ref[0, pl.ds(at, key_rows), :]
    key_col = at + lax.broadcasted_iota(jnp.int32, (key_rows, 1), 0)
    return jnp.where((segk == segq) & (key_col <= query_row), 0.0, MASKED)


def attend_kernel(
    place_at, low_ref, high_ref, base_ref, q_ref, kv_ref, segk_ref, segq_ref, out_ref, lse_ref,
    q_s, m_s, l_s, acc_s,
):
    tile = pl.program_id(0)
    rows = q_ref.shape[1]
    place = place_at + tile
    lane = lanes((rows, 128))
    for pair in range(QH // 2):
        both = q_ref[0, :, pair * 128 : (pair + 1) * 128].astype(F32)
        q_s[2 * pair] = jnp.where(lane < 64, both, 0.0).astype(BF16)
        q_s[2 * pair + 1] = jnp.where(lane < 64, pltpu.roll(both, 64, 1), 0.0).astype(BF16)
    key_rows = min(KEY_TILE, kv_ref.shape[2])
    tiles_each = kv_ref.shape[2] // key_rows
    m_s[...] = jnp.full(m_s.shape, MASKED, F32)
    l_s[...] = jnp.zeros(l_s.shape, F32)
    acc_s[...] = jnp.zeros(acc_s.shape, F32)
    query_row = base_ref[0] + tile * rows + lanes((1, rows))
    segq = segq_ref[0]
    factor = HD ** (-0.5) * LOG2E

    def step(key_tile, carry):
        at = pl.multiple_of(key_tile * key_rows, key_rows)
        source = key_tile // tiles_each
        offset = pl.multiple_of((key_tile % tiles_each) * key_rows, key_rows)
        bias = visible(segk_ref, segq, query_row, at, key_rows)
        for group in range(KVH):
            kv = kv_ref[source, 0, pl.ds(offset, key_rows), group * 128 : (group + 1) * 128]
            kv_t = kv.astype(F32).T.astype(BF16)
            members = range(group * (QH // KVH), (group + 1) * (QH // KVH))
            scores = [contract(kv, q_s[head], 1, 1) * factor + bias for head in members]
            before = [m_s[head : head + 1, :] for head in members]
            tops = [
                jnp.maximum(old, jnp.max(part, axis=0, keepdims=True))
                for old, part in zip(before, scores)
            ]
            weights = [jnp.exp2(part - top) for part, top in zip(scores, tops)]
            sums = [jnp.sum(part, axis=0, keepdims=True) for part in weights]
            outs = [contract(kv_t, part.astype(BF16), 1, 0) for part in weights]
            for at_head, head in enumerate(members):
                fade = jnp.exp2(before[at_head] - tops[at_head])
                l_s[head : head + 1, :] = l_s[head : head + 1, :] * fade + sums[at_head]
                acc_s[head] = acc_s[head] * fade + outs[at_head]
                m_s[head : head + 1, :] = tops[at_head]
        return carry

    lax.fori_loop(low_ref[place], high_ref[place], step, 0)
    lse_ref[0] = m_s[...] + jnp.log2(l_s[...])
    for pair in range(QH // 2):
        even = (acc_s[2 * pair] / l_s[2 * pair : 2 * pair + 1, :]).T
        odd = (acc_s[2 * pair + 1] / l_s[2 * pair + 1 : 2 * pair + 2, :]).T
        out_ref[0, :, pair * 128 : (pair + 1) * 128] = jnp.where(
            lane < 64, pltpu.roll(even, 64, 1), odd
        ).astype(BF16)


def attend_back_kernel(
    place_at, low_ref, high_ref, base_ref, q_ref, kv_ref, segk_ref, segq_ref, att_ref, gatt_ref, lse_ref,
    cos_ref, sin_ref, dq_ref, dkv_ref,
    q_s, g_s, delta_s, dq_s, dkv_s,
):
    tile = pl.program_id(0)
    rows = q_ref.shape[1]
    place = place_at + tile
    lane = lanes((rows, 128))

    @pl.when(tile == 0)
    def _():
        dkv_s[...] = jnp.zeros(dkv_s.shape, F32)

    for pair in range(QH // 2):
        cols = slice(pair * 128, (pair + 1) * 128)
        both = q_ref[0, :, cols].astype(F32)
        q_s[2 * pair] = jnp.where(lane < 64, both, 0.0).astype(BF16)
        q_s[2 * pair + 1] = jnp.where(lane < 64, pltpu.roll(both, 64, 1), 0.0).astype(BF16)
        grad = gatt_ref[0, :, cols].astype(F32)
        g_s[2 * pair] = jnp.where(lane >= 64, pltpu.roll(grad, 64, 1), 0.0).astype(BF16)
        g_s[2 * pair + 1] = jnp.where(lane >= 64, grad, 0.0).astype(BF16)
        product = (grad * att_ref[0, :, cols].astype(F32)).T
        delta_s[2 * pair : 2 * pair + 1, :] = jnp.sum(product[:64], axis=0, keepdims=True)
        delta_s[2 * pair + 1 : 2 * pair + 2, :] = jnp.sum(product[64:], axis=0, keepdims=True)
    key_rows = min(KEY_TILE, kv_ref.shape[2])
    tiles_each = kv_ref.shape[2] // key_rows
    dq_s[...] = jnp.zeros(dq_s.shape, F32)
    query_row = base_ref[0] + tile * rows + lanes((1, rows))
    segq = segq_ref[0]
    qk_scale = HD ** (-0.5)
    factor = qk_scale * LOG2E

    def step(key_tile, carry):
        at = pl.multiple_of(key_tile * key_rows, key_rows)
        source = key_tile // tiles_each
        offset = pl.multiple_of((key_tile % tiles_each) * key_rows, key_rows)
        bias = visible(segk_ref, segq, query_row, at, key_rows)
        for group in range(KVH):
            kv = kv_ref[source, 0, pl.ds(offset, key_rows), group * 128 : (group + 1) * 128]
            kv_t = kv.astype(F32).T.astype(BF16)
            total = jnp.zeros((key_rows, 128), F32)
            for member in range(QH // KVH):
                head = group * (QH // KVH) + member
                q, g = q_s[head], g_s[head]
                scores = contract(kv, q, 1, 1) * factor + bias
                probs = jnp.exp2(scores - lse_ref[0, head : head + 1, :])
                d_probs = contract(kv, g, 1, 1)
                d_scores = (probs * (d_probs - delta_s[head : head + 1, :]) * qk_scale).astype(BF16)
                total = total + contract(d_scores, q, 1, 0) + contract(probs.astype(BF16), g, 1, 0)
                dq_s[head] += contract(kv_t, d_scores, 1, 0)
            cols = slice(group * 128, (group + 1) * 128)
            dkv_s[source, 0, pl.ds(offset, key_rows), cols] += total
        return carry

    lax.fori_loop(low_ref[place], high_ref[place], step, 0)
    cosine, sine = cos_ref[0], sin_ref[0]
    for pair in range(QH // 2):
        even, odd = dq_s[2 * pair].T, dq_s[2 * pair + 1].T
        even = even * cosine + swap_halves(even * sine)
        odd = odd * cosine + swap_halves(odd * sine)
        dq_ref[0, :, pair * 128 : (pair + 1) * 128] = jnp.where(
            lane < 64, even, pltpu.roll(odd, 64, 1)
        ).astype(BF16)

    @pl.when(tile == pl.num_programs(0) - 1)
    def _():
        dkv_ref[...] = dkv_s[...].astype(BF16)


def attention_specs(seq, length, rows):
    tile = lambda cols, at=seq: pl.BlockSpec((1, rows, cols), lambda t, *_: (at, t, 0))
    whole = lambda cols, at=seq: pl.BlockSpec((1, length, cols), lambda t, *_: (at, 0, 0))
    keys = lambda array, at=seq: pl.BlockSpec(
        (array.shape[0], 1) + array.shape[2:], lambda t, *_: (0, at, 0, 0)
    )
    row = lambda n, at=seq: pl.BlockSpec((1, n, rows), lambda t, *_: (at, 0, t))
    return tile, whole, keys, row


def attend(seq, bounds, q, kv_all, segk, segq):
    _, span, q_width = q.shape
    rows = min(256, span)
    tile, whole, keys, row = attention_specs(seq, segk.shape[1], rows)
    own_keys = kv_all.shape[:1] + (1,) + kv_all.shape[2:]
    return pl.pallas_call(
        functools.partial(attend_kernel, seq * (span // rows)),
        grid_spec=pltpu.PrefetchScalarGridSpec(
            num_scalar_prefetch=3,
            grid=(span // rows,),
            in_specs=[tile(q_width), keys(kv_all), whole(1), row(1)],
            out_specs=[tile(q_width, 0), row(QH, 0)],
            scratch_shapes=[
                pltpu.VMEM((QH, rows, 128), BF16),
                pltpu.VMEM((QH, rows), F32),
                pltpu.VMEM((QH, rows), F32),
                pltpu.VMEM((QH, 128, rows), F32),
            ],
        ),
        out_shape=[
            jax.ShapeDtypeStruct((1, span, q_width), BF16),
            jax.ShapeDtypeStruct((1, QH, span), F32),
        ],
        compiler_params=pltpu.CompilerParams(vmem_limit_bytes=VMEM_BYTES),
        name="attend",
    )(*bounds, q, kv_all, segk, segq)


def attend_back(seq, bounds, q, kv_all, segk, segq, att, grad_att, lse, cosine, sine):
    _, span, q_width = q.shape
    rows = min(256, span)
    tile, whole, keys, row = attention_specs(seq, segk.shape[1], rows)
    own_keys = kv_all.shape[:1] + (1,) + kv_all.shape[2:]
    return pl.pallas_call(
        functools.partial(attend_back_kernel, seq * (span // rows)),
        grid_spec=pltpu.PrefetchScalarGridSpec(
            num_scalar_prefetch=3,
            grid=(span // rows,),
            in_specs=[
                tile(q_width), keys(kv_all), whole(1), row(1), tile(q_width, 0), tile(q_width),
                row(QH, 0), tile(128), tile(128),
            ],
            out_specs=[tile(q_width, 0), keys(kv_all, 0)],
            scratch_shapes=[
                pltpu.VMEM((QH, rows, 128), BF16),
                pltpu.VMEM((QH, rows, 128), BF16),
                pltpu.VMEM((QH, rows), F32),
                pltpu.VMEM((QH, 128, rows), F32),
                pltpu.VMEM(own_keys, F32),
            ],
        ),
        out_shape=[
            jax.ShapeDtypeStruct((1, span, q_width), BF16),
            jax.ShapeDtypeStruct(own_keys, BF16),
        ],
        compiler_params=pltpu.CompilerParams(vmem_limit_bytes=VMEM_BYTES),
        name="attend_back",
    )(*bounds, q, kv_all, segk, segq, att, grad_att, lse, cosine, sine)


def rope_tables(positions):
    half = HD // 2
    frequency = ROPE_BASE ** (-jnp.arange(half, dtype=F32) / half)
    angles = positions.astype(F32)[..., None] * frequency
    cosine, sine = jnp.cos(angles), jnp.sin(angles)
    one, zero = jnp.ones(cosine.shape[:-1] + (HD,), F32), jnp.zeros(cosine.shape[:-1] + (HD,), F32)
    return (
        jnp.concatenate([cosine, cosine, one], axis=-1),
        jnp.concatenate([-sine, sine, zero], axis=-1),
    )


def attention_bounds(segments, seg_own, span_start):
    seqs, span = seg_own.shape
    rows, key_rows = min(256, span), min(KEY_TILE, span)
    first = seg_own[:, ::rows]
    begin = jnp.sum((segments[:, None, :] < first[:, :, None]).astype(jnp.int32), axis=2)
    tiles = jnp.arange(span // rows, dtype=jnp.int32)
    high = (span_start + (tiles + 1) * rows + key_rows - 1) // key_rows
    high = jnp.broadcast_to(high[None], first.shape)
    return (
        (begin // key_rows).reshape(-1),
        high.reshape(-1).astype(jnp.int32),
        jnp.full((1,), span_start, jnp.int32),
    )


CHUNK = 128
DI = MH * MP
CC = DI + 2 * NS
TAP_LANES, PREV_LANE, LAST_LANE, SEG_LANE = 0, 4, 5, 6


def split_three(values):
    high = values.astype(BF16)
    rest = values - high.astype(F32)
    middle = rest.astype(BF16)
    return high, middle, (rest - middle.astype(F32)).astype(BF16)


def product_exact(matrix, values):
    return sum(contract(matrix, part, 1, 0) for part in split_three(values))


def widen(values, spread):
    kept = jnp.where(lanes(values.shape) < 32, values, 0.0)
    high, middle, rest = (part.astype(F32) for part in split_three(kept))
    packed = high + pltpu.roll(middle, 32, 1) + pltpu.roll(rest, 64, 1)
    return contract(packed.astype(BF16), spread, 1, 0)


def gather_heads(values, spread_first):
    high = values.astype(BF16)
    rest = (values - high.astype(F32)).astype(BF16)
    return contract(high, spread_first, 1, 1) + contract(rest, spread_first, 1, 1)


def spread_matrix():
    row = lax.broadcasted_iota(jnp.int32, (128, DI), 0)
    col = lax.broadcasted_iota(jnp.int32, (128, DI), 1)
    return ((row % 32 == col // MP) & (row < 96)).astype(BF16)


def spread_first_matrix():
    row = lax.broadcasted_iota(jnp.int32, (32, DI), 0)
    col = lax.broadcasted_iota(jnp.int32, (32, DI), 1)
    return (row == col // MP).astype(BF16)


def lower_mask():
    row = lax.broadcasted_iota(jnp.int32, (CHUNK, CHUNK), 0)
    return row >= lanes((CHUNK, CHUNK))


def token_rows(token_ref):
    return jnp.concatenate([token_ref[0]] * 16, axis=0).T


def decay_rows(rate, head_ref, token):
    raw = rate.astype(F32) + head_ref[1:2, :]
    step = jnp.maximum(raw, 0.0) + jnp.log1p(jnp.exp(-jnp.abs(raw)))
    log_decay = -step * jnp.exp(head_ref[0:1, :])
    running = product_exact(lower_mask().astype(BF16), log_decay)
    last = running[CHUNK - 1 :, :]
    weight_end = jnp.exp(last - running) * step * token[:, LAST_LANE : LAST_LANE + 1]
    entry = jnp.exp(running) * token[:, PREV_LANE : PREV_LANE + 1]
    gain = jnp.exp(last) * token[CHUNK - 1 :, PREV_LANE : PREV_LANE + 1]
    return raw, step, log_decay, running, weight_end, entry, gain


def conv_total(ext_s, token, taps_ref, shift_ref):
    total = shift_ref[...] + ext_s[8 : 8 + CHUNK, :] * taps_ref[KC - 1 : KC, :]
    for tap in range(KC - 1):
        total = total + ext_s[5 + tap : 5 + tap + CHUNK, :] * (
            taps_ref[tap : tap + 1, :] * token[:, TAP_LANES + tap : TAP_LANES + tap + 1]
        )
    return total


def mixer_scan_kernel(
    cr_ref, rim_ref, token_ref, head_ref, taps_ref, shift_ref, spread_ref,
    act_ref, states_ref, gains_ref, final_ref, final_gain_ref,
    ext_s, state_s, gain_s,
):
    chunk = pl.program_id(0)

    @pl.when(chunk == 0)
    def _():
        ext_s[0:8, :] = rim_ref[0].astype(F32)
        state_s[...] = jnp.zeros(state_s.shape, F32)
        gain_s[...] = jnp.ones(gain_s.shape, F32)

    @pl.when(chunk > 0)
    def _():
        ext_s[0:8, :] = ext_s[CHUNK : CHUNK + 8, :]

    token = token_rows(token_ref)
    ext_s[8 : 8 + CHUNK, :] = cr_ref[0, :, :CC].astype(F32)
    total = conv_total(ext_s, token, taps_ref, shift_ref)
    act = (total * jax.nn.sigmoid(total)).astype(BF16)
    act_ref[0] = act
    weight_end, _, gain = decay_rows(cr_ref[0, :, CC:], head_ref, token)[-3:]
    states_ref[0, 0] = state_s[...].astype(BF16)
    before = gain_s[...]
    gains_ref[0, 0] = before
    spread = spread_ref[...]
    scaled = (act[:, :DI].astype(F32) * widen(weight_end, spread)).astype(BF16)
    gain_rows = jnp.broadcast_to(gain, (8, 128))
    state = state_s[...] * widen(gain_rows, spread)[0:1, :] + contract(
        act[:, DI : DI + NS], scaled, 0, 0
    )
    state_s[...] = state
    gain_s[...] = before * gain_rows

    @pl.when(chunk == pl.num_programs(0) - 1)
    def _():
        final_ref[0] = state.astype(BF16)
        final_gain_ref[0] = widen(before * gain_rows, spread)


def entering_state(local_ref, gains_ref, state_ref, spread):
    factor = widen(gains_ref[0, 0], spread)[0:1, :]
    return (local_ref[0, 0].astype(F32) + factor * state_ref[0].astype(F32)).astype(BF16)


def pair_decay(running, rest_t, bias, head):
    parts = []
    for at in (head, head + 1):
        column = jnp.broadcast_to(running[:, at : at + 1], (CHUNK, CHUNK))
        parts.append(jnp.exp2(column + (rest_t[at : at + 1, :] + bias)))
    return parts


def stack_pair(values):
    lane = lanes(values.shape)
    wide = values.astype(F32)
    return jnp.concatenate(
        [jnp.where(lane < 64, wide, 0.0), jnp.where(lane >= 64, wide, 0.0)], axis=0
    ).astype(BF16)


def inside_terms(running, step, token):
    seg = jnp.broadcast_to(token[:, SEG_LANE : SEG_LANE + 1], (CHUNK, CHUNK))
    bias = jnp.where((seg == seg.T) & lower_mask(), 0.0, MASKED)
    running_two = running * LOG2E
    rest_t = (jnp.log2(step) - running_two).T
    return running_two, rest_t, bias


def mixer_out_kernel(
    gate_ref, cr_ref, act_ref, token_ref, states_ref, gains_ref, state_ref, head_ref, skip_ref, gain_ref,
    spread_ref, y_ref, out_ref,
):
    token, spread = token_rows(token_ref), spread_ref[...]
    _, step, _, running, _, entry, _ = decay_rows(cr_ref[0, :, CC:], head_ref, token)
    b_rows, c_rows = act_ref[0, :, DI : DI + NS], act_ref[0, :, DI + NS :]
    state = entering_state(states_ref, gains_ref, state_ref, spread)
    carried = contract(c_rows, state, 1, 0) * widen(entry, spread)
    cross = contract(c_rows, b_rows, 1, 1)
    running_two, rest_t, bias = inside_terms(running, step, token)
    square = jnp.zeros((CHUNK, 128), F32)
    for pair in range(MH // 2):
        cols = slice(pair * 128, (pair + 1) * 128)
        xs = act_ref[0, :, cols]
        mix = jnp.concatenate(
            [
                (cross * part).astype(BF16)
                for part in pair_decay(running_two, rest_t, bias, 2 * pair)
            ],
            axis=1,
        )
        y = (
            contract(mix, stack_pair(xs), 1, 0)
            + carried[:, cols]
            + skip_ref[:, cols] * xs.astype(F32)
        )
        y_ref[0, :, cols] = y
        gate = gate_ref[0, :, cols].astype(F32)
        gated = y * (gate * jax.nn.sigmoid(gate))
        square = square + gated * gated
    scale = lax.rsqrt(jnp.sum(square, axis=1, keepdims=True) * (1.0 / DI) + EPSILON)
    for pair in range(MH // 2):
        cols = slice(pair * 128, (pair + 1) * 128)
        gate = gate_ref[0, :, cols].astype(F32)
        gated = y_ref[0, :, cols] * (gate * jax.nn.sigmoid(gate))
        out_ref[0, :, cols] = (gated * scale * gain_ref[:, cols]).astype(BF16)


def mixer_gate_back_kernel(
    gmix_ref, y_ref, gate_ref, cr_ref, act_ref, token_ref, head_ref, gain_ref, spread_ref,
    gy_ref, dgate_ref, gstates_ref, gains_ref, final_ref, dgain_ref, dskip_ref,
    state_s, gain_s, dgain_s, dskip_s,
):
    chunk = pl.program_id(0)

    @pl.when(chunk == 0)
    def _():
        dgain_s[...] = jnp.zeros(dgain_s.shape, F32)
        dskip_s[...] = jnp.zeros(dskip_s.shape, F32)

    @pl.when(chunk == 0)
    def _():
        state_s[...] = jnp.zeros(state_s.shape, F32)
        gain_s[...] = jnp.ones(gain_s.shape, F32)

    token, spread = token_rows(token_ref), spread_ref[...]
    entry, gain = decay_rows(cr_ref[0, :, CC:], head_ref, token)[-2:]
    y = y_ref[0]
    gate = gate_ref[0].astype(F32)
    sig = jax.nn.sigmoid(gate)
    swish = gate * sig
    gated = y * swish
    scale = lax.rsqrt(jnp.mean(gated * gated, axis=1, keepdims=True) + EPSILON)
    grad = gmix_ref[0].astype(F32)
    scaled = grad * gain_ref[...]
    shrink = jnp.mean(scaled * gated, axis=1, keepdims=True) * (scale * scale * scale)
    d_gated = scaled * scale - gated * shrink
    gy = (d_gated * swish).astype(BF16)
    gy_ref[0] = gy
    dgate_ref[0] = (d_gated * y * (sig * (1.0 + gate * (1.0 - sig)))).astype(BF16)
    dgain_s[0:1, :] += jnp.sum(grad * gated * scale, axis=0, keepdims=True)
    gy_float = gy.astype(F32)
    dskip_s[0:1, :] += jnp.sum(gy_float * act_ref[0, :, :DI].astype(F32), axis=0, keepdims=True)
    gstates_ref[0, 0] = state_s[...].astype(BF16)
    after = gain_s[...]
    gains_ref[0, 0] = after
    gain_rows = jnp.broadcast_to(gain, (8, 128))
    carried = (gy_float * widen(entry, spread)).astype(BF16)
    state = state_s[...] * widen(gain_rows, spread)[0:1, :] + contract(
        act_ref[0, :, DI + NS :], carried, 0, 0
    )
    state_s[...] = state
    gain_s[...] = after * gain_rows

    @pl.when(chunk == pl.num_programs(0) - 1)
    def _():
        final_ref[0] = state.astype(BF16)

    dgain_ref[...] = dgain_s[...]
    dskip_ref[...] = dskip_s[...]


def mixer_back_kernel(
    gy_ref, y_ref, cr_ref, halo_ref, rim_ref, act_ref, token_ref,
    states_ref, gains_ref, state_ref, gstates_ref, ggains_ref, gstate_ref,
    head_ref, skip_ref, taps_ref, shift_ref, spread_ref, spread_first_ref,
    dcr_ref, drim_ref, dconv_ref, dhead_ref,
    ext_s, grad_s, carry_s, dconv_s, dhead_s,
):
    step_index = pl.program_id(0)
    last_step = pl.num_programs(0) - 1

    @pl.when(step_index == 0)
    def _():
        dconv_s[...] = jnp.zeros(dconv_s.shape, F32)
        dhead_s[...] = jnp.zeros(dhead_s.shape, F32)

    @pl.when(step_index == 0)
    def _():
        carry_s[...] = jnp.zeros(carry_s.shape, F32)

    @pl.when(step_index == last_step)
    def _():
        ext_s[0:8, :] = rim_ref[0].astype(F32)

    @pl.when(step_index < last_step)
    def _():
        ext_s[0:8, :] = halo_ref[0, :, :CC].astype(F32)[8:16]

    ext_s[8 : 8 + CHUNK, :] = cr_ref[0, :, :CC].astype(F32)
    token, spread, spread_first = token_rows(token_ref), spread_ref[...], spread_first_ref[...]
    raw, step, log_decay, running, weight_end, entry, gain = decay_rows(
        cr_ref[0, :, CC:], head_ref, token
    )
    b_rows, c_rows = act_ref[0, :, DI : DI + NS], act_ref[0, :, DI + NS :]
    state = entering_state(states_ref, gains_ref, state_ref, spread)
    gstate = entering_state(gstates_ref, ggains_ref, gstate_ref, spread)
    wide_end = widen(weight_end, spread)
    gy = gy_ref[0]
    gy_float = gy.astype(F32)
    gcarried = (gy_float * widen(entry, spread)).astype(BF16)
    xs_float = act_ref[0, :, :DI].astype(F32)
    grad_c = contract(gcarried, state, 1, 1)
    grad_b = contract((xs_float * wide_end).astype(BF16), gstate, 1, 1)
    from_end = contract(b_rows, gstate, 1, 0) * wide_end
    dgain_row = jnp.sum(gstate.astype(F32) * state.astype(F32), axis=0, keepdims=True)
    cross = contract(c_rows, b_rows, 1, 1)
    running_two, rest_t, bias = inside_terms(running, step, token)
    grad_cross = jnp.zeros((CHUNK, CHUNK), F32)
    lane = lanes((CHUNK, 128))
    for pair in range(MH // 2):
        cols = slice(pair * 128, (pair + 1) * 128)
        stacked = stack_pair(act_ref[0, :, cols])
        gy_pair = gy_ref[0, :, cols]
        first, second = pair_decay(running_two, rest_t, bias, 2 * pair)
        mix = jnp.concatenate([(cross * first).astype(BF16), (cross * second).astype(BF16)], axis=1)
        grad_mix = contract(gy_pair, stacked, 1, 1)
        grad_cross = grad_cross + grad_mix[:, :CHUNK] * first + grad_mix[:, CHUNK:] * second
        both = contract(mix, gy_pair, 0, 0)
        grad_s[8 : 8 + CHUNK, cols] = jnp.where(lane < 64, both[:CHUNK], both[CHUNK:])
    inner = grad_s[8 : 8 + CHUNK, :DI]
    skip = skip_ref[...]
    cross_low = grad_cross.astype(BF16)
    grad_c = grad_c + contract(cross_low, b_rows, 1, 0)
    grad_b = grad_b + contract(cross_low, c_rows, 0, 0)
    narrow = lambda values: jnp.concatenate(
        [gather_heads(values, spread_first), jnp.zeros((values.shape[0], 96), F32)], axis=1
    )
    query_part = narrow(gy_float * (y_ref[0] - skip * xs_float))
    key_inner = narrow(xs_float * inner)
    key_end = narrow(xs_float * from_end)
    extra = jnp.sum(key_end, axis=0, keepdims=True) + gain * narrow(
        jnp.broadcast_to(dgain_row, (8, DI))
    )[0:1, :]
    upper = (~lower_mask() | (lax.broadcasted_iota(jnp.int32, (CHUNK, CHUNK), 0) == lanes((CHUNK, CHUNK))))
    grad_log = product_exact(upper.astype(BF16), query_part - key_inner - key_end) + extra
    sig = jax.nn.sigmoid(raw)
    ratio = jnp.where(raw < -15.0, 1.0, sig / jnp.maximum(step, 1e-30))
    grad_rate = (key_inner + key_end) * ratio - grad_log * jnp.exp(head_ref[0:1, :]) * sig
    dhead_s[0:1, :] += jnp.sum(grad_log * log_decay, axis=0, keepdims=True)
    dhead_s[1:2, :] += jnp.sum(grad_rate, axis=0, keepdims=True)
    total = conv_total(ext_s, token, taps_ref, shift_ref)
    grad_act = jnp.concatenate([inner + from_end + skip * gy_float, grad_b, grad_c], axis=1)
    csig = jax.nn.sigmoid(total)
    grad_total = grad_act * (csig * (1.0 + total * (1.0 - csig)))
    dconv_s[KC : KC + 1, :] += jnp.sum(grad_total, axis=0, keepdims=True)
    grad_s[0:8, :] = jnp.zeros((8, CC), F32)
    grad_s[8 : 8 + CHUNK, :] = grad_total * taps_ref[KC - 1 : KC, :]
    dconv_s[KC - 1 : KC, :] += jnp.sum(grad_total * ext_s[8 : 8 + CHUNK, :], axis=0, keepdims=True)
    for tap in range(KC - 1):
        part = grad_total * token[:, TAP_LANES + tap : TAP_LANES + tap + 1]
        dconv_s[tap : tap + 1, :] += jnp.sum(
            part * ext_s[5 + tap : 5 + tap + CHUNK, :], axis=0, keepdims=True
        )
        grad_s[5 + tap : 5 + tap + CHUNK, :] += part * taps_ref[tap : tap + 1, :]
    grad_s[CHUNK : CHUNK + 8, :] += carry_s[...]
    carry_s[...] = grad_s[0:8, :]
    dcr_ref[0, :, :CC] = grad_s[8 : 8 + CHUNK, :].astype(BF16)
    dcr_ref[0, :, CC:] = grad_rate.astype(BF16)

    @pl.when(step_index == last_step)
    def _():
        drim_ref[0] = carry_s[...]

    dconv_ref[...] = dconv_s[...]
    dhead_ref[...] = dhead_s[...]


def mixer_call(kernel, name, seq, chunks, reverse, inputs, outputs, scratch, earlier):
    place = (lambda c: chunks - 1 - c) if reverse else (lambda c: c)
    kinds = {
        "block": lambda array, at: pl.BlockSpec(
            (1, CHUNK, array.shape[2]), lambda c: (at, place(c), 0)
        ),
        "chunk": lambda array, at: pl.BlockSpec(
            (1, 1) + array.shape[2:], lambda c: (at, place(c), 0, 0)
        ),
        "token": lambda array, at: pl.BlockSpec((1, 8, CHUNK), lambda c: (at, 0, place(c))),
        "seq": lambda array, at: pl.BlockSpec((1,) + array.shape[1:], lambda c: (at, 0, 0)),
        "own": lambda array, at: pl.BlockSpec((1,) + array.shape[1:], lambda c: (0, 0, 0)),
        "fixed": lambda array, at: pl.BlockSpec(array.shape, lambda c: (0, 0)),
        "halo": lambda array, at: pl.BlockSpec(
            (1, 16, array.shape[2]),
            lambda c: (at, jnp.maximum(place(c) * (CHUNK // 16) - 1, 0), 0),
        ),
    }
    arrays = [array for _, array in inputs]
    in_specs = [kinds[kind](array, seq) for kind, array in inputs]
    out_specs = [kinds[kind](shape, seq) for kind, shape in outputs]
    count = len(inputs)
    aliases, kept = {}, 0
    if earlier is not None:
        shared = [i for i, (kind, _) in enumerate(outputs) if kind in ("block", "chunk")]
        aliases = {count + i: out for i, out in enumerate(shared)}
        arrays += [earlier[out] for out in shared]
        in_specs += [pl.BlockSpec(memory_space=pl.ANY)] * len(shared)
        kept = len(shared)

    def run(*refs):
        kernel(*refs[:count], *refs[count + kept :])

    return pl.pallas_call(
        run,
        grid=(chunks,),
        in_specs=in_specs,
        out_specs=out_specs,
        out_shape=[shape for _, shape in outputs],
        scratch_shapes=[pltpu.VMEM(shape, F32) for shape in scratch],
        input_output_aliases=aliases,
        compiler_params=pltpu.CompilerParams(vmem_limit_bytes=VMEM_BYTES),
        name=name,
    )(*arrays)


def mixer_scan(seq, earlier, cr, rim, token, heads, taps, shift, spread):
    seqs, span, _ = cr.shape
    chunks = span // CHUNK
    return mixer_call(
        mixer_scan_kernel, "mixer_scan", seq, chunks, False,
        [
            ("block", cr), ("seq", rim), ("token", token), ("fixed", heads), ("fixed", taps),
            ("fixed", shift), ("fixed", spread),
        ],
        [
            ("block", jax.ShapeDtypeStruct((seqs, span, CC), BF16)),
            ("chunk", jax.ShapeDtypeStruct((seqs, chunks, NS, DI), BF16)),
            ("chunk", jax.ShapeDtypeStruct((seqs, chunks, 8, 128), F32)),
            ("own", jax.ShapeDtypeStruct((1, NS, DI), BF16)),
            ("own", jax.ShapeDtypeStruct((1, 8, DI), F32)),
        ],
        [(CHUNK + 8, CC), (NS, DI), (8, 128)],
        earlier,
    )


def mixer_out(seq, earlier, gate, cr, act, token, states, gains, state, heads, skip, gain, spread):
    seqs, span, _ = cr.shape
    return mixer_call(
        mixer_out_kernel, "mixer_out", seq, span // CHUNK, False,
        [
            ("block", gate), ("block", cr), ("block", act), ("token", token), ("chunk", states),
            ("chunk", gains), ("own", state), ("fixed", heads), ("fixed", skip),
            ("fixed", gain), ("fixed", spread),
        ],
        [
            ("block", jax.ShapeDtypeStruct((seqs, span, DI), F32)),
            ("block", jax.ShapeDtypeStruct((seqs, span, DI), BF16)),
        ],
        [],
        earlier,
    )


def mixer_gate_back(
    seq, earlier, gmix, y, gate, cr, act, token, heads, gain, spread
):
    seqs, span, _ = cr.shape
    chunks = span // CHUNK
    return mixer_call(
        mixer_gate_back_kernel, "mixer_gate_back", seq, chunks, True,
        [
            ("block", gmix), ("block", y), ("block", gate), ("block", cr), ("block", act), ("token", token),
            ("fixed", heads), ("fixed", gain), ("fixed", spread),
        ],
        [
            ("block", jax.ShapeDtypeStruct((seqs, span, DI), BF16)),
            ("block", jax.ShapeDtypeStruct((seqs, span, DI), BF16)),
            ("chunk", jax.ShapeDtypeStruct((seqs, chunks, NS, DI), BF16)),
            ("chunk", jax.ShapeDtypeStruct((seqs, chunks, 8, 128), F32)),
            ("own", jax.ShapeDtypeStruct((1, NS, DI), BF16)),
            ("fixed", jax.ShapeDtypeStruct((8, DI), F32)),
            ("fixed", jax.ShapeDtypeStruct((8, DI), F32)),
        ],
        [(NS, DI), (8, 128), (8, DI), (8, DI)],
        earlier,
    )


def mixer_back(
    seq, earlier, gy, y, cr, rim, act, token, states, gains, state, gstates, ggains,
    gstate, heads, skip, taps, shift, spread, spread_first,
):
    seqs, span, width = cr.shape
    return mixer_call(
        mixer_back_kernel, "mixer_back", seq, span // CHUNK, True,
        [
            ("block", gy), ("block", y), ("block", cr), ("halo", cr),
            ("seq", rim), ("block", act), ("token", token), ("chunk", states), ("chunk", gains),
            ("own", state), ("chunk", gstates), ("chunk", ggains), ("own", gstate),
            ("fixed", heads), ("fixed", skip), ("fixed", taps), ("fixed", shift),
            ("fixed", spread), ("fixed", spread_first),
        ],
        [
            ("block", jax.ShapeDtypeStruct((seqs, span, width), BF16)),
            ("own", jax.ShapeDtypeStruct((1, 8, CC), F32)),
            ("fixed", jax.ShapeDtypeStruct((8, CC), F32)),
            ("fixed", jax.ShapeDtypeStruct((8, 128), F32)),
        ],
        [(CHUNK + 8, CC), (CHUNK + 8, CC), (8, CC), (8, CC), (8, 128)],
        earlier,
    )


def token_table(seg_own, seg_rim):
    seqs, span = seg_own.shape
    extended = jnp.concatenate([seg_rim, seg_own], axis=1)
    matches = [extended[:, tap : tap + span] == seg_own for tap in range(KC - 1)]
    by_chunk = seg_own.reshape(seqs, -1, CHUNK)
    last = by_chunk[:, :, -1:]
    before = jnp.concatenate([seg_rim[:, None, -1:], last[:, :-1]], axis=1)
    spare = jnp.zeros((seqs, span), F32)
    rows = [match.astype(F32) for match in matches] + [
        spare,
        (by_chunk == before).reshape(seqs, span).astype(F32),
        (by_chunk == last).reshape(seqs, span).astype(F32),
        seg_own.astype(F32),
        spare,
    ]
    return jnp.stack(rows, axis=1)


def from_behind(block, axis, distance):
    devices = range(lax.axis_size(axis))
    route = [(i - distance, i) for i in devices if i - distance in devices]
    return lax.ppermute(block, axis, route)


def after(value, *earlier):
    return lax.optimization_barrier((value, earlier))[0]


class Chain:
    def __init__(self, local, gain, reverse):
        self.local, self.gain, self.reverse = local, gain, reverse
        self.state, self.hop, self.flying = jnp.zeros(local.shape, BF16), 0, None
        self.count, self.place = lax.axis_size("ctx"), lax.axis_index("ctx")

    def send(self, *earlier):
        if self.hop == self.count - 1:
            return
        source = self.count - 1 - self.hop if self.reverse else self.hop
        target = source - 1 if self.reverse else source + 1
        sent = self.local
        if self.hop:
            sent = (self.gain * self.state.astype(F32) + sent.astype(F32)).astype(BF16)
        if earlier:
            sent = after(sent, *earlier)
        self.flying = (lax.ppermute(sent, "ctx", [(source, target)]), target)
        self.hop += 1

    def take(self):
        if self.flying is None:
            return
        received, target = self.flying
        self.state, self.flying = jnp.where(self.place == target, received, self.state), None

    def finish(self):
        self.take()
        while self.hop < self.count - 1:
            self.send()
            self.take()
        return self.state


def sum_everywhere(values, axes):
    for axis in axes:
        count = lax.axis_size(axis)
        copies = jnp.broadcast_to(values[None], (count,) + values.shape)
        values = jnp.sum(lax.all_to_all(copies, axis, 0, 0, tiled=True), axis=0)
    return values


def scatter_all(grad):
    count, place = lax.axis_size("ctx"), lax.axis_index("ctx")
    devices, me = lax.axis_size("dp"), lax.axis_index("dp")
    bits = devices.bit_length() - 1
    part = grad.reshape((2,) * bits + (count, -1, grad.shape[1]))
    for bit in [0] + list(range(bits - 1, 0, -1)):
        at = 0 if bit else bits - 1
        first, second = (lax.index_in_dim(part, side, at, False) for side in range(2))
        low = ((me >> bit) & 1) == 0
        sent = jnp.where(low, second, first).astype(BF16)
        received = lax.ppermute(sent, "dp", [(i, i ^ (1 << bit)) for i in range(devices)])
        part = jnp.where(low, first, second).astype(F32) + received.astype(F32)
    relative = lax.dynamic_slice_in_dim(jnp.concatenate([part, part]), place, count, 0)
    total, rounded = relative[0], relative.astype(BF16)
    for d in range(1, count):
        route = [(i, (i + d) % count) for i in range(count)]
        total = total + lax.ppermute(rounded[d], "ctx", route).astype(F32)
    return total


def rms_scale(values, gain_vec):
    return (
        values * lax.rsqrt(jnp.mean(values * values, axis=-1, keepdims=True) + EPSILON) * gain_vec
    )


def silu_product(gate_lin, up_lin):
    return jax.nn.silu(gate_lin) * up_lin


def body(
    layer_input, segments, positions, gain_one, w_in, conv_w, conv_b, head_params, gain_m, w_out,
    w_q, w_k, w_v, w_o, gain_two, w_gate, w_up, w_down, cotangent,
):
    seqs, span, width = layer_input.shape
    rows = seqs * span
    axes = ("dp", "ctx")
    own_rows = w_q.shape[0]
    q_width, kv_width = QH * HD, 2 * KVH * HD
    low_dot = lambda a, b: jnp.dot(a, b, preferred_element_type=F32)

    small_parts = [gain_one, gain_two, gain_m, conv_b, conv_w.reshape(-1)]
    small_sizes = [part.shape[0] for part in small_parts]
    slots = own_rows * 128
    small_block = jnp.concatenate(small_parts, axis=0)
    small_block = jnp.pad(small_block, (0, slots - sum(small_sizes))).reshape(own_rows, 128)
    w_kv = jnp.stack(
        [w_k.reshape(own_rows, KVH, HD), w_v.reshape(own_rows, KVH, HD)], axis=2
    ).reshape(own_rows, kv_width)
    count = lax.axis_size("ctx")
    exchange = lambda blocks: lax.all_to_all(blocks, "ctx", 0, 0, tiled=True)
    copies = lambda block: jnp.broadcast_to(block[None], (count,) + block.shape)
    gather = lambda part: lax.all_gather(part, "dp", axis=0, tiled=True)
    w_cr = jnp.pad(w_in[:, DI:], ((0, 0), (0, CR - (w_in.shape[1] - DI))))
    first = jnp.concatenate([w_cr, w_q, w_kv, small_block, w_in[:, :DI]], axis=1)
    first_part = lax.all_gather(first, "ctx", axis=0, tiled=True)
    first_all = gather(first_part)
    turned_o = w_o.T
    half_rows, ff = own_rows // 2, w_gate.shape[1]

    def fold(block, cut):
        return jnp.concatenate([block[..., :half_rows, cut:], block[..., half_rows:, cut:]], axis=-1)

    def unfold(block):
        half = block.shape[-1] // 2
        return jnp.concatenate([block[..., :half], block[..., half:]], axis=-2)

    rest = [w_down, w_out, fold(turned_o, 0)]
    for matrix in (w_gate, w_up):
        rest += [matrix[:, at : at + width] for at in range(0, ff, width)]
    rest_sizes = [part.shape[0] for part in rest]
    rest_part = exchange(after(copies(jnp.concatenate(rest, axis=0)), first_part))
    rest_all = gather(rest_part.reshape(-1, width)).reshape(-1, sum(rest_sizes), width)
    cuts, at = [], 0
    for size in rest_sizes:
        cuts.append(rest_all[:, at : at + size])
        at += size
    w_down_all, w_out_all = cuts[0].reshape(-1, width), cuts[1].reshape(-1, width)
    w_o_all = unfold(cuts[2]).reshape(width, q_width)
    w_gates = first_all[:, FIRST:]
    w_gu_all = jnp.concatenate([cut.reshape(width, width) for cut in cuts[3:]], axis=1)
    small_all = first_all[:, FIRST - 128 : FIRST].reshape(-1, slots).astype(F32)
    parts, at = [], 0
    for size in small_sizes:
        parts.append(small_all[:, at : at + size])
        at += size
    gain1_all, gain2_all, gain_m_all, shift_all = [part.reshape(1, -1) for part in parts[:4]]
    taps_all = jnp.swapaxes(parts[4].reshape(-1, KC, small_sizes[3]), 0, 1).reshape(KC, CC)
    taps_all = jnp.pad(taps_all, ((0, 8 - KC), (0, 0)))

    place = lax.axis_index("ctx")
    span_start = place * span
    seg_own = lax.dynamic_slice_in_dim(segments, span_start, span, 1)
    seg_rim = jnp.where(
        place > 0,
        lax.dynamic_slice_in_dim(segments, jnp.maximum(span_start - (KC - 1), 0), KC - 1, 1),
        -1,
    )
    token = token_table(seg_own, seg_rim)
    bounds = attention_bounds(segments, seg_own, span_start)
    segk, segq = segments[:, :, None], seg_own[:, None, :]
    cosine, sine = rope_tables(positions)
    heads = jnp.pad(head_params, ((0, 5), (0, 128 - MH)))
    skip = jnp.repeat(head_params[2], MP)[None]
    spread, spread_first = spread_matrix(), spread_first_matrix()

    tokens = layer_input.reshape(rows, width)
    small = (token, bounds, segk, segq, cosine, sine, heads, skip, spread, spread_first)
    first_all, small = lax.optimization_barrier((first_all, small))
    token, bounds, segk, segq, cosine, sine, heads, skip, spread, spread_first = small
    cosine, sine = cosine.reshape(rows, 128), sine.reshape(rows, 128)
    hidden, cr, q, kv = project(tokens, gain1_all, first_all, cosine, sine)
    q = q.reshape(seqs, span, q_width)
    kv = kv.reshape(seqs, span, kv_width)
    kv_all = exchange(copies(kv))
    cr = cr.reshape(seqs, span, CR)
    rim = from_behind(cr[:, span - (KC - 1) :, :CC], "ctx", 1)
    rim = jnp.pad(rim, ((0, 0), (8 - (KC - 1), 0), (0, 0)))
    scanned, chains, wide_gains = None, [], []
    for seq in range(seqs):
        scanned = mixer_scan(
            seq, scanned, cr, rim, token, heads, taps_all,
            shift_all, spread,
        )
        wide_gains.append(scanned[4][:, :1])
        chains.append(Chain(scanned[3], wide_gains[seq], False))
        chains[seq].send()
    act, states, gains = scanned[:3]
    for chain in chains:
        chain.take()
        chain.send()
    atts, lses, mixed, mark = [], [], None, act
    for seq in range(seqs):
        att, lse = attend(seq, bounds, after(q, mark), kv_all, segk, segq)
        atts.append(att)
        lses.append(lse)
        chains[seq].take()
        chains[seq].send(lse)
        mark = lse
    gate = low_dot(hidden, w_gates).astype(BF16).reshape(seqs, span, DI)
    states_in = []
    for seq in range(seqs):
        states_in.append(chains[seq].finish())
        mixed = mixer_out(
            seq, mixed, gate, cr, act, token, states, gains, states_in[seq], heads, skip, gain_m_all,
            spread,
        )
    mixer_y, mixer_in = mixed
    mixer_in = mixer_in.reshape(rows, DI)
    att_rows = jnp.concatenate(atts, axis=0).reshape(rows, q_width)
    middle = (
        tokens.astype(F32)
        + low_dot(mixer_in, w_out_all)
        + jnp.einsum("ra,da->rd", att_rows, w_o_all, preferred_element_type=F32)
    )
    normed_mid, norm2_pull = jax.vjp(rms_scale, middle, gain2_all)
    normed_two = normed_mid.astype(BF16)
    gate_up = low_dot(normed_two, w_gu_all).astype(BF16)
    act_float, act_pull = jax.vjp(
        silu_product, gate_up[:, :ff].astype(F32), gate_up[:, ff:].astype(F32)
    )
    act_rows = act_float.astype(BF16)
    def scatter(grad):
        return lax.psum_scatter(grad, "dp", scatter_dimension=0, tiled=True)

    def weight_grad(left, right):
        return jnp.einsum("ri,ro->io", left, right, preferred_element_type=F32).astype(BF16)

    def back_dot(grad, weight):
        return jnp.einsum("ro,io->ri", grad, weight, preferred_element_type=F32)

    cot_rows = cotangent.reshape(rows, width)
    grad_down = weight_grad(act_rows, cot_rows)
    grad_gate_up = jnp.concatenate(act_pull(back_dot(cot_rows, w_down_all)), axis=1).astype(BF16)
    grad_wgu = weight_grad(normed_two, grad_gate_up)
    grad_normed = back_dot(grad_gate_up, w_gu_all)
    grad_normed, grad_down, grad_wgu = lax.optimization_barrier((grad_normed, grad_down, grad_wgu))
    part_gu = scatter(grad_wgu)
    grad_mid_norm, grad_gain_second = norm2_pull(grad_normed)
    grad_middle = cot_rows.astype(F32) + grad_mid_norm
    grad_mid_low = grad_middle.astype(BF16)
    grad_wout = weight_grad(mixer_in, grad_mid_low)
    grad_wo = weight_grad(grad_mid_low, att_rows)
    grad_mixer_in = back_dot(grad_mid_low, w_out_all).astype(BF16).reshape(seqs, span, DI)
    grad_att = low_dot(grad_mid_low, w_o_all).astype(BF16).reshape(seqs, span, q_width)
    grad_mixer_in, grad_att, grad_wout, grad_wo = lax.optimization_barrier(
        (grad_mixer_in, grad_att, grad_wout, grad_wo)
    )
    grad_wo = grad_wo.reshape(-1, own_rows, q_width)
    gated, chains, grad_gain_mix, grad_skip = None, [], 0.0, 0.0
    for seq in range(seqs):
        gated = mixer_gate_back(
            seq, gated, grad_mixer_in, mixer_y, gate, cr, act, token, heads, gain_m_all, spread
        )
        grad_gain_mix, grad_skip = grad_gain_mix + gated[5], grad_skip + gated[6]
        chains.append(Chain(gated[4], wide_gains[seq], True))
        chains[seq].send()
    grad_y, grad_gate, gstates, ggains = gated[:4]
    grad_wgates = weight_grad(hidden, grad_gate.reshape(rows, DI)).reshape(-1, own_rows, DI)
    blocks = grad_wo.shape[0]
    grad_rest = jnp.concatenate(
        [
            grad_down.reshape(blocks, -1, width), grad_wout.reshape(blocks, -1, width),
            fold(grad_wo, 0), grad_wgates[..., :width], fold(grad_wgates, width),
        ],
        axis=1,
    )
    part_rest = scatter(grad_rest.reshape(-1, width))
    cos3, sin3 = cosine.reshape(seqs, span, 128), sine.reshape(seqs, span, 128)
    dqs, dkvs = [], []
    for seq in range(seqs):
        if seq:
            for chain in chains:
                chain.take()
                chain.send(dqs[-1])
        mark = dqs[-1:] + [chain.state for chain in chains] if seq else []
        dq, dkv = attend_back(
            seq, bounds, after(q, grad_y, *mark), kv_all, segk,
            segq, atts[seq], grad_att, lses[seq], cos3, sin3,
        )
        dqs.append(dq)
        dkvs.append(dkv)
    dkv_all = exchange(jnp.concatenate(dkvs, axis=1))
    dq = jnp.concatenate(dqs, axis=0)
    last, rims, grad_conv, grad_heads = None, [], 0.0, 0.0
    waits = [(grad_rest, part_gu)] + [()] * (seqs - 1)
    finals = [chain.finish() for chain in chains]
    waits[1 % seqs] += tuple(finals)
    for seq in range(seqs):
        gstate = finals[seq]
        if seq == seqs - 1:
            gu_blocks = part_gu.reshape(count, own_rows, 2 * ff)
            parts = [after(part_rest, *rims).reshape(count, -1, width)]
            parts += [gu_blocks[..., at : at + width] for at in range(0, 2 * ff, width)]
            rest_low = jnp.concatenate(parts, axis=1).reshape(-1, width)
            waits[seq] = (rest_low,)
        last = mixer_back(
            seq, last, after(grad_y, dqs[-1], *waits[seq]), mixer_y, cr, rim, act, token, states,
            gains, states_in[seq], gstates, ggains, gstate, heads, skip, taps_all, shift_all,
            spread, spread_first,
        )
        rims.append(last[1])
        grad_conv, grad_heads = grad_conv + last[2], grad_heads + last[3]
    grad_cr, grad_rim = last[0], jnp.concatenate(rims, axis=0)
    back_rim = from_behind(grad_rim[:, 8 - (KC - 1) :].astype(BF16), "ctx", -1)
    edge = grad_cr[:, span - (KC - 1) :, :CC].astype(F32) + back_rim.astype(F32)
    grad_cr = lax.dynamic_update_slice(
        grad_cr, after(edge.astype(BF16), dkv_all), (0, span - (KC - 1), 0)
    ).reshape(rows, CR)
    rest_out = lax.psum_scatter(rest_low, "ctx", scatter_dimension=0, tiled=True).astype(F32)
    grad_wcr = weight_grad(hidden, grad_cr)
    part_cr = scatter(grad_wcr)
    layer_result = (middle + low_dot(after(act_rows, part_cr), w_down_all)).astype(BF16)
    out_cr = lax.psum_scatter(part_cr, "ctx", scatter_dimension=0, tiled=True).astype(F32)
    grad_tokens, grad_kv, grad_gain_first = finish(
        tokens, gain1_all, grad_gate.reshape(rows, DI), after(grad_cr, grad_wcr, rest_out),
        dq.reshape(rows, q_width), dkv_all, cosine, sine, grad_middle, w_gates, first_all,
    )
    grad_first = jnp.concatenate([dq.reshape(rows, q_width), grad_kv], axis=1)
    grad_wfirst = weight_grad(hidden, grad_first)
    grad_gain_first = grad_gain_first[0]

    devices = first_all.shape[0] // own_rows
    small_grads = jnp.concatenate(
        [
            grad_gain_first.reshape(devices, -1),
            grad_gain_second.reshape(devices, -1),
            grad_gain_mix[0].reshape(devices, -1),
            grad_conv[KC].reshape(devices, -1),
            jnp.swapaxes(grad_conv[:KC].reshape(KC, devices, -1), 0, 1).reshape(devices, -1),
        ],
        axis=1,
    )
    small_grads = jnp.pad(small_grads, ((0, 0), (0, slots - small_grads.shape[1])))
    out_first = scatter_all(
        jnp.concatenate([grad_wfirst, small_grads.reshape(-1, 128).astype(BF16)], axis=1)
    )
    rest_sizes = rest_sizes[:3] + [own_rows, half_rows] + rest_sizes[3:]
    outs, at = [], 0
    for size in rest_sizes:
        outs.append(rest_out[at : at + size])
        at += size
    out_down, out_wout = outs[0], outs[1]
    out_wo = unfold(outs[2])
    out_win = jnp.concatenate(
        [outs[3], unfold(outs[4]), out_cr[:, : w_in.shape[1] - DI]], axis=1
    )
    halves = ff // width
    out_gate = jnp.concatenate(outs[5 : 5 + halves], axis=1)
    out_up = jnp.concatenate(outs[5 + halves :], axis=1)
    out_small = out_first[:, q_width + kv_width :].reshape(-1)
    pieces, at = [], 0
    for size in small_sizes:
        pieces.append(out_small[at : at + size])
        at += size
    out_kv = out_first[:, q_width : q_width + kv_width].reshape(own_rows, KVH, 2, HD)
    head_grad = sum_everywhere(
        jnp.concatenate(
            [grad_heads[:2, :MH], grad_skip[0].reshape(MH, MP).sum(axis=1)[None]], axis=0
        ),
        axes,
    )
    return (
        layer_result.reshape(layer_input.shape),
        grad_tokens.reshape(layer_input.shape),
        pieces[0],
        out_win,
        pieces[4].reshape(KC, -1),
        pieces[3],
        head_grad,
        pieces[2],
        out_wout,
        out_first[:, :q_width],
        out_kv[:, :, 0].reshape(own_rows, -1),
        out_kv[:, :, 1].reshape(own_rows, -1),
        out_wo.T,
        pieces[1],
        out_gate,
        out_up,
        out_down,
    )


def solution(mesh):
    in_specs = (
        P("dp", "ctx", None),
        P("dp", None),
        P("dp", "ctx"),
        P(("dp", "ctx")),
        P(("dp", "ctx"), None),
        P(None, ("dp", "ctx")),
        P(("dp", "ctx")),
        P(),
        P(("dp", "ctx")),
        P(("dp", "ctx"), None),
        P(("dp", "ctx"), None),
        P(("dp", "ctx"), None),
        P(("dp", "ctx"), None),
        P(None, ("dp", "ctx")),
        P(("dp", "ctx")),
        P(("dp", "ctx"), None),
        P(("dp", "ctx"), None),
        P(("dp", "ctx"), None),
        P("dp", "ctx", None),
    )
    out_specs = (
        P("dp", "ctx", None),
        P("dp", "ctx", None),
        P(("dp", "ctx")),
        P(("dp", "ctx"), None),
        P(None, ("dp", "ctx")),
        P(("dp", "ctx")),
        P(),
        P(("dp", "ctx")),
        P(("dp", "ctx"), None),
        P(("dp", "ctx"), None),
        P(("dp", "ctx"), None),
        P(("dp", "ctx"), None),
        P(None, ("dp", "ctx")),
        P(("dp", "ctx")),
        P(("dp", "ctx"), None),
        P(("dp", "ctx"), None),
        P(("dp", "ctx"), None),
    )
    return jax.shard_map(body, mesh=mesh, in_specs=in_specs, out_specs=out_specs, check_vma=False)
```

```python
import functools
import jax
import jax.numpy as jnp
from jax import lax
from jax.experimental import pallas as pl
from jax.experimental.pallas import tpu as pltpu
from jax.sharding import PartitionSpec as P

MH = 24
MP = 64
NS = 128
KC = 4
QH = 8
KVH = 2
HD = 64
EPSILON = 1e-05
ROPE_BASE = 10000.0
MASKED = -1e30
LOG2E = 1.4426950408889634
KEY_TILE = 256
VMEM_BYTES = 56 * 1024 * 1024

F32 = jnp.float32
BF16 = jnp.bfloat16


def contract(left, right, left_dim, right_dim):
    return lax.dot_general(
        left, right, (((left_dim,), (right_dim,)), ((), ())), preferred_element_type=F32
    )


def lanes(shape):
    return lax.broadcasted_iota(jnp.int32, shape, len(shape) - 1)


def swap_halves(values):
    lane = lanes(values.shape)
    return jnp.where(lane < 32, pltpu.roll(values, 96, 1), pltpu.roll(values, 32, 1))


CR = MH * MP + 2 * NS + 128
FIRST = CR + QH * HD + 2 * KVH * HD + 128


def project_kernel(x_ref, gain_ref, w_ref, cos_ref, sin_ref, hidden_ref, cr_ref, q_ref, kv_ref):
    x = x_ref[...].astype(F32)
    scale = lax.rsqrt(jnp.mean(x * x, axis=-1, keepdims=True) + EPSILON)
    hidden = (x * scale * gain_ref[...]).astype(BF16)
    hidden_ref[...] = hidden
    lin = contract(hidden, w_ref[:, CR : CR + QH * HD + 2 * KVH * HD], 1, 0)
    cosine, sine = cos_ref[...], sin_ref[...]
    lane = lanes(cosine.shape)
    for pair in range(QH // 2):
        both = lin[:, pair * 128 : (pair + 1) * 128]
        other = pltpu.roll(both, 64, 1)
        even = both * cosine + swap_halves(both) * sine
        odd = other * cosine + swap_halves(other) * sine
        q_ref[:, pair * 128 : (pair + 1) * 128] = jnp.where(
            lane < 64, even, pltpu.roll(odd, 64, 1)
        ).astype(BF16)
    for group in range(KVH):
        at = QH * HD + group * 128
        part = lin[:, at : at + 128]
        kv_ref[:, group * 128 : (group + 1) * 128] = (
            part * cosine + swap_halves(part) * sine
        ).astype(BF16)
    cr_ref[...] = contract(hidden, w_ref[:, :CR], 1, 0).astype(BF16)


def project(x, gain, w_first, cosine, sine):
    rows, width = x.shape
    tile = 256 if rows % 256 == 0 else 128
    block = lambda cols: pl.BlockSpec((tile, cols), lambda i: (i, 0))
    fixed = lambda array: pl.BlockSpec(array.shape, lambda i: (0, 0))
    cols = [width, CR, QH * HD, 2 * KVH * HD]
    return pl.pallas_call(
        project_kernel,
        grid=(rows // tile,),
        in_specs=[
            block(width), fixed(gain), fixed(w_first), block(128), block(128),
        ],
        out_specs=[block(size) for size in cols],
        out_shape=[jax.ShapeDtypeStruct((rows, size), BF16) for size in cols],
        compiler_params=pltpu.CompilerParams(vmem_limit_bytes=VMEM_BYTES),
        name="project",
    )(x, gain, w_first, cosine, sine)


def finish_kernel(
    x_ref, gain_ref, dgate_ref, dcr_ref, dq_ref, dkv_ref, cos_ref, sin_ref, middle_ref,
    w_ref, dx_ref, dkv_out_ref, dgain_ref, dgain_s,
):
    @pl.when(pl.program_id(0) == 0)
    def _():
        dgain_s[...] = jnp.zeros(dgain_s.shape, F32)

    dkv = dkv_ref[0, 0].astype(F32)
    for source in range(1, dkv_ref.shape[0]):
        dkv = dkv + dkv_ref[source, 0].astype(F32)
    cosine, sine = cos_ref[...], sin_ref[...]
    turned = []
    for group in range(KVH):
        part = dkv[:, group * 128 : (group + 1) * 128]
        back = part * cosine + swap_halves(part * sine)
        turned.append(jnp.where(lanes(part.shape) < HD, back, part))
    dkv = jnp.concatenate(turned, axis=1).astype(BF16)
    dkv_out_ref[...] = dkv
    at = CR + QH * HD
    grad = (
        contract(dgate_ref[...], w_ref[:, FIRST:], 1, 1)
        + contract(dcr_ref[...], w_ref[:, :CR], 1, 1)
        + contract(dq_ref[...], w_ref[:, CR:at], 1, 1)
        + contract(dkv, w_ref[:, at : at + 2 * KVH * HD], 1, 1)
    )
    x = x_ref[...].astype(F32)
    scale = lax.rsqrt(jnp.mean(x * x, axis=-1, keepdims=True) + EPSILON)
    scaled = grad * gain_ref[...]
    shrink = jnp.mean(scaled * x, axis=-1, keepdims=True) * (scale * scale * scale)
    dx_ref[...] = (middle_ref[...] + scaled * scale - x * shrink).astype(BF16)
    dgain_s[0:1, :] += jnp.sum(grad * x * scale, axis=0, keepdims=True)
    dgain_ref[...] = dgain_s[...]


def finish(x, gain, dgate, dcr, dq, dkv_all, cosine, sine, middle, w_first):
    rows, width = x.shape
    span = dkv_all.shape[2]
    tile = min(256, span)
    per_seq = span // tile
    block = lambda array: pl.BlockSpec((tile, array.shape[1]), lambda i: (i, 0))
    fixed = lambda array: pl.BlockSpec(array.shape, lambda i: (0, 0))
    keys = pl.BlockSpec(
        (dkv_all.shape[0], 1, tile, dkv_all.shape[3]), lambda i: (0, i // per_seq, i % per_seq, 0)
    )
    kv_width = dkv_all.shape[3]
    return pl.pallas_call(
        finish_kernel,
        grid=(rows // tile,),
        in_specs=[
            block(x), fixed(gain), block(dgate), block(dcr), block(dq), keys, block(cosine),
            block(sine), block(middle), fixed(w_first),
        ],
        out_specs=[
            block(x),
            pl.BlockSpec((tile, kv_width), lambda i: (i, 0)),
            pl.BlockSpec((8, width), lambda i: (0, 0)),
        ],
        out_shape=[
            jax.ShapeDtypeStruct((rows, width), BF16),
            jax.ShapeDtypeStruct((rows, kv_width), BF16),
            jax.ShapeDtypeStruct((8, width), F32),
        ],
        scratch_shapes=[pltpu.VMEM((8, width), F32)],
        compiler_params=pltpu.CompilerParams(vmem_limit_bytes=VMEM_BYTES),
        name="finish",
    )(x, gain, dgate, dcr, dq, dkv_all, cosine, sine, middle, w_first)


def visible(segk_ref, segq, query_row, at, key_rows):
    segk = segk_ref[0, pl.ds(at, key_rows), :]
    key_col = at + lax.broadcasted_iota(jnp.int32, (key_rows, 1), 0)
    return jnp.where((segk == segq) & (key_col <= query_row), 0.0, MASKED)


def attend_kernel(
    place_at, low_ref, high_ref, base_ref, q_ref, kv_ref, segk_ref, segq_ref, out_ref, lse_ref,
    q_s, m_s, l_s, acc_s,
):
    tile = pl.program_id(0)
    rows = q_ref.shape[1]
    place = place_at + tile
    lane = lanes((rows, 128))
    for pair in range(QH // 2):
        both = q_ref[0, :, pair * 128 : (pair + 1) * 128].astype(F32)
        q_s[2 * pair] = jnp.where(lane < 64, both, 0.0).astype(BF16)
        q_s[2 * pair + 1] = jnp.where(lane < 64, pltpu.roll(both, 64, 1), 0.0).astype(BF16)
    key_rows = min(KEY_TILE, kv_ref.shape[2])
    tiles_each = kv_ref.shape[2] // key_rows
    m_s[...] = jnp.full(m_s.shape, MASKED, F32)
    l_s[...] = jnp.zeros(l_s.shape, F32)
    acc_s[...] = jnp.zeros(acc_s.shape, F32)
    query_row = base_ref[0] + tile * rows + lanes((1, rows))
    segq = segq_ref[0]
    factor = HD ** (-0.5) * LOG2E

    def step(key_tile, carry):
        at = pl.multiple_of(key_tile * key_rows, key_rows)
        source = key_tile // tiles_each
        offset = pl.multiple_of((key_tile % tiles_each) * key_rows, key_rows)
        bias = visible(segk_ref, segq, query_row, at, key_rows)
        for group in range(KVH):
            kv = kv_ref[source, 0, pl.ds(offset, key_rows), group * 128 : (group + 1) * 128]
            kv_t = kv.astype(F32).T.astype(BF16)
            members = range(group * (QH // KVH), (group + 1) * (QH // KVH))
            scores = [contract(kv, q_s[head], 1, 1) * factor + bias for head in members]
            before = [m_s[head : head + 1, :] for head in members]
            tops = [
                jnp.maximum(old, jnp.max(part, axis=0, keepdims=True))
                for old, part in zip(before, scores)
            ]
            weights = [jnp.exp2(part - top) for part, top in zip(scores, tops)]
            sums = [jnp.sum(part, axis=0, keepdims=True) for part in weights]
            outs = [contract(kv_t, part.astype(BF16), 1, 0) for part in weights]
            for at_head, head in enumerate(members):
                fade = jnp.exp2(before[at_head] - tops[at_head])
                l_s[head : head + 1, :] = l_s[head : head + 1, :] * fade + sums[at_head]
                acc_s[head] = acc_s[head] * fade + outs[at_head]
                m_s[head : head + 1, :] = tops[at_head]
        return carry

    lax.fori_loop(low_ref[place], high_ref[place], step, 0)
    lse_ref[0] = m_s[...] + jnp.log2(l_s[...])
    for pair in range(QH // 2):
        even = (acc_s[2 * pair] / l_s[2 * pair : 2 * pair + 1, :]).T
        odd = (acc_s[2 * pair + 1] / l_s[2 * pair + 1 : 2 * pair + 2, :]).T
        out_ref[0, :, pair * 128 : (pair + 1) * 128] = jnp.where(
            lane < 64, pltpu.roll(even, 64, 1), odd
        ).astype(BF16)


def attend_back_kernel(
    place_at, low_ref, high_ref, base_ref, q_ref, kv_ref, segk_ref, segq_ref, att_ref, gatt_ref, lse_ref,
    cos_ref, sin_ref, dq_ref, dkv_ref,
    q_s, g_s, delta_s, dq_s, dkv_s,
):
    tile = pl.program_id(0)
    rows = q_ref.shape[1]
    place = place_at + tile
    lane = lanes((rows, 128))

    @pl.when(tile == 0)
    def _():
        dkv_s[...] = jnp.zeros(dkv_s.shape, F32)

    for pair in range(QH // 2):
        cols = slice(pair * 128, (pair + 1) * 128)
        both = q_ref[0, :, cols].astype(F32)
        q_s[2 * pair] = jnp.where(lane < 64, both, 0.0).astype(BF16)
        q_s[2 * pair + 1] = jnp.where(lane < 64, pltpu.roll(both, 64, 1), 0.0).astype(BF16)
        grad = gatt_ref[0, :, cols].astype(F32)
        g_s[2 * pair] = jnp.where(lane >= 64, pltpu.roll(grad, 64, 1), 0.0).astype(BF16)
        g_s[2 * pair + 1] = jnp.where(lane >= 64, grad, 0.0).astype(BF16)
        product = (grad * att_ref[0, :, cols].astype(F32)).T
        delta_s[2 * pair : 2 * pair + 1, :] = jnp.sum(product[:64], axis=0, keepdims=True)
        delta_s[2 * pair + 1 : 2 * pair + 2, :] = jnp.sum(product[64:], axis=0, keepdims=True)
    key_rows = min(KEY_TILE, kv_ref.shape[2])
    tiles_each = kv_ref.shape[2] // key_rows
    dq_s[...] = jnp.zeros(dq_s.shape, F32)
    query_row = base_ref[0] + tile * rows + lanes((1, rows))
    segq = segq_ref[0]
    qk_scale = HD ** (-0.5)
    factor = qk_scale * LOG2E

    def step(key_tile, carry):
        at = pl.multiple_of(key_tile * key_rows, key_rows)
        source = key_tile // tiles_each
        offset = pl.multiple_of((key_tile % tiles_each) * key_rows, key_rows)
        bias = visible(segk_ref, segq, query_row, at, key_rows)
        for group in range(KVH):
            kv = kv_ref[source, 0, pl.ds(offset, key_rows), group * 128 : (group + 1) * 128]
            kv_t = kv.astype(F32).T.astype(BF16)
            total = jnp.zeros((key_rows, 128), F32)
            for member in range(QH // KVH):
                head = group * (QH // KVH) + member
                q, g = q_s[head], g_s[head]
                scores = contract(kv, q, 1, 1) * factor + bias
                probs = jnp.exp2(scores - lse_ref[0, head : head + 1, :])
                d_probs = contract(kv, g, 1, 1)
                d_scores = (probs * (d_probs - delta_s[head : head + 1, :]) * qk_scale).astype(BF16)
                total = total + contract(d_scores, q, 1, 0) + contract(probs.astype(BF16), g, 1, 0)
                dq_s[head] += contract(kv_t, d_scores, 1, 0)
            cols = slice(group * 128, (group + 1) * 128)
            dkv_s[source, 0, pl.ds(offset, key_rows), cols] += total
        return carry

    lax.fori_loop(low_ref[place], high_ref[place], step, 0)
    cosine, sine = cos_ref[0], sin_ref[0]
    for pair in range(QH // 2):
        even, odd = dq_s[2 * pair].T, dq_s[2 * pair + 1].T
        even = even * cosine + swap_halves(even * sine)
        odd = odd * cosine + swap_halves(odd * sine)
        dq_ref[0, :, pair * 128 : (pair + 1) * 128] = jnp.where(
            lane < 64, even, pltpu.roll(odd, 64, 1)
        ).astype(BF16)

    @pl.when(tile == pl.num_programs(0) - 1)
    def _():
        dkv_ref[...] = dkv_s[...].astype(BF16)


def attention_specs(seq, length, rows):
    tile = lambda cols, at=seq: pl.BlockSpec((1, rows, cols), lambda t, *_: (at, t, 0))
    whole = lambda cols, at=seq: pl.BlockSpec((1, length, cols), lambda t, *_: (at, 0, 0))
    keys = lambda array, at=seq: pl.BlockSpec(
        (array.shape[0], 1) + array.shape[2:], lambda t, *_: (0, at, 0, 0)
    )
    row = lambda n, at=seq: pl.BlockSpec((1, n, rows), lambda t, *_: (at, 0, t))
    return tile, whole, keys, row


def attend(seq, bounds, q, kv_all, segk, segq):
    _, span, q_width = q.shape
    rows = min(256, span)
    tile, whole, keys, row = attention_specs(seq, segk.shape[1], rows)
    own_keys = kv_all.shape[:1] + (1,) + kv_all.shape[2:]
    return pl.pallas_call(
        functools.partial(attend_kernel, seq * (span // rows)),
        grid_spec=pltpu.PrefetchScalarGridSpec(
            num_scalar_prefetch=3,
            grid=(span // rows,),
            in_specs=[tile(q_width), keys(kv_all), whole(1), row(1)],
            out_specs=[tile(q_width, 0), row(QH, 0)],
            scratch_shapes=[
                pltpu.VMEM((QH, rows, 128), BF16),
                pltpu.VMEM((QH, rows), F32),
                pltpu.VMEM((QH, rows), F32),
                pltpu.VMEM((QH, 128, rows), F32),
            ],
        ),
        out_shape=[
            jax.ShapeDtypeStruct((1, span, q_width), BF16),
            jax.ShapeDtypeStruct((1, QH, span), F32),
        ],
        compiler_params=pltpu.CompilerParams(vmem_limit_bytes=VMEM_BYTES),
        name="attend",
    )(*bounds, q, kv_all, segk, segq)


def attend_back(seq, bounds, q, kv_all, segk, segq, att, grad_att, lse, cosine, sine):
    _, span, q_width = q.shape
    rows = min(256, span)
    tile, whole, keys, row = attention_specs(seq, segk.shape[1], rows)
    own_keys = kv_all.shape[:1] + (1,) + kv_all.shape[2:]
    return pl.pallas_call(
        functools.partial(attend_back_kernel, seq * (span // rows)),
        grid_spec=pltpu.PrefetchScalarGridSpec(
            num_scalar_prefetch=3,
            grid=(span // rows,),
            in_specs=[
                tile(q_width), keys(kv_all), whole(1), row(1), tile(q_width, 0), tile(q_width),
                row(QH, 0), tile(128), tile(128),
            ],
            out_specs=[tile(q_width, 0), keys(kv_all, 0)],
            scratch_shapes=[
                pltpu.VMEM((QH, rows, 128), BF16),
                pltpu.VMEM((QH, rows, 128), BF16),
                pltpu.VMEM((QH, rows), F32),
                pltpu.VMEM((QH, 128, rows), F32),
                pltpu.VMEM(own_keys, F32),
            ],
        ),
        out_shape=[
            jax.ShapeDtypeStruct((1, span, q_width), BF16),
            jax.ShapeDtypeStruct(own_keys, BF16),
        ],
        compiler_params=pltpu.CompilerParams(vmem_limit_bytes=VMEM_BYTES),
        name="attend_back",
    )(*bounds, q, kv_all, segk, segq, att, grad_att, lse, cosine, sine)


def rope_tables(positions):
    half = HD // 2
    frequency = ROPE_BASE ** (-jnp.arange(half, dtype=F32) / half)
    angles = positions.astype(F32)[..., None] * frequency
    cosine, sine = jnp.cos(angles), jnp.sin(angles)
    one, zero = jnp.ones(cosine.shape[:-1] + (HD,), F32), jnp.zeros(cosine.shape[:-1] + (HD,), F32)
    return (
        jnp.concatenate([cosine, cosine, one], axis=-1),
        jnp.concatenate([-sine, sine, zero], axis=-1),
    )


def attention_bounds(segments, seg_own, span_start):
    seqs, span = seg_own.shape
    rows, key_rows = min(256, span), min(KEY_TILE, span)
    first = seg_own[:, ::rows]
    begin = jnp.sum((segments[:, None, :] < first[:, :, None]).astype(jnp.int32), axis=2)
    tiles = jnp.arange(span // rows, dtype=jnp.int32)
    high = (span_start + (tiles + 1) * rows + key_rows - 1) // key_rows
    high = jnp.broadcast_to(high[None], first.shape)
    return (
        (begin // key_rows).reshape(-1),
        high.reshape(-1).astype(jnp.int32),
        jnp.full((1,), span_start, jnp.int32),
    )


CHUNK = 128
DI = MH * MP
CC = DI + 2 * NS
TAP_LANES, PREV_LANE, LAST_LANE, SEG_LANE = 0, 4, 5, 6


def split_three(values):
    high = values.astype(BF16)
    rest = values - high.astype(F32)
    middle = rest.astype(BF16)
    return high, middle, (rest - middle.astype(F32)).astype(BF16)


def product_exact(matrix, values):
    return sum(contract(matrix, part, 1, 0) for part in split_three(values))


def widen(values, spread):
    kept = jnp.where(lanes(values.shape) < 32, values, 0.0)
    high, middle, rest = (part.astype(F32) for part in split_three(kept))
    packed = high + pltpu.roll(middle, 32, 1) + pltpu.roll(rest, 64, 1)
    return contract(packed.astype(BF16), spread, 1, 0)


def gather_heads(values, spread_first):
    high = values.astype(BF16)
    rest = (values - high.astype(F32)).astype(BF16)
    return contract(high, spread_first, 1, 1) + contract(rest, spread_first, 1, 1)


def spread_matrix():
    row = lax.broadcasted_iota(jnp.int32, (128, DI), 0)
    col = lax.broadcasted_iota(jnp.int32, (128, DI), 1)
    return ((row % 32 == col // MP) & (row < 96)).astype(BF16)


def spread_first_matrix():
    row = lax.broadcasted_iota(jnp.int32, (32, DI), 0)
    col = lax.broadcasted_iota(jnp.int32, (32, DI), 1)
    return (row == col // MP).astype(BF16)


def lower_mask():
    row = lax.broadcasted_iota(jnp.int32, (CHUNK, CHUNK), 0)
    return row >= lanes((CHUNK, CHUNK))


def token_rows(token_ref):
    return jnp.concatenate([token_ref[0]] * 16, axis=0).T


def decay_rows(rate, head_ref, token):
    raw = rate.astype(F32) + head_ref[1:2, :]
    step = jnp.maximum(raw, 0.0) + jnp.log1p(jnp.exp(-jnp.abs(raw)))
    log_decay = -step * jnp.exp(head_ref[0:1, :])
    running = product_exact(lower_mask().astype(BF16), log_decay)
    last = running[CHUNK - 1 :, :]
    weight_end = jnp.exp(last - running) * step * token[:, LAST_LANE : LAST_LANE + 1]
    entry = jnp.exp(running) * token[:, PREV_LANE : PREV_LANE + 1]
    gain = jnp.exp(last) * token[CHUNK - 1 :, PREV_LANE : PREV_LANE + 1]
    return raw, step, log_decay, running, weight_end, entry, gain


def conv_total(ext_s, token, taps_ref, shift_ref):
    total = shift_ref[...] + ext_s[8 : 8 + CHUNK, :] * taps_ref[KC - 1 : KC, :]
    for tap in range(KC - 1):
        total = total + ext_s[5 + tap : 5 + tap + CHUNK, :] * (
            taps_ref[tap : tap + 1, :] * token[:, TAP_LANES + tap : TAP_LANES + tap + 1]
        )
    return total


def mixer_scan_kernel(
    cr_ref, rim_ref, token_ref, head_ref, taps_ref, shift_ref, spread_ref,
    act_ref, states_ref, gains_ref, final_ref, final_gain_ref,
    ext_s, state_s, gain_s,
):
    chunk = pl.program_id(0)

    @pl.when(chunk == 0)
    def _():
        ext_s[0:8, :] = rim_ref[0].astype(F32)
        state_s[...] = jnp.zeros(state_s.shape, F32)
        gain_s[...] = jnp.ones(gain_s.shape, F32)

    @pl.when(chunk > 0)
    def _():
        ext_s[0:8, :] = ext_s[CHUNK : CHUNK + 8, :]

    token = token_rows(token_ref)
    ext_s[8 : 8 + CHUNK, :] = cr_ref[0, :, :CC].astype(F32)
    total = conv_total(ext_s, token, taps_ref, shift_ref)
    act = (total * jax.nn.sigmoid(total)).astype(BF16)
    act_ref[0] = act
    weight_end, _, gain = decay_rows(cr_ref[0, :, CC:], head_ref, token)[-3:]
    states_ref[0, 0] = state_s[...].astype(BF16)
    before = gain_s[...]
    gains_ref[0, 0] = before
    spread = spread_ref[...]
    scaled = (act[:, :DI].astype(F32) * widen(weight_end, spread)).astype(BF16)
    gain_rows = jnp.broadcast_to(gain, (8, 128))
    state = state_s[...] * widen(gain_rows, spread)[0:1, :] + contract(
        act[:, DI : DI + NS], scaled, 0, 0
    )
    state_s[...] = state
    gain_s[...] = before * gain_rows

    @pl.when(chunk == pl.num_programs(0) - 1)
    def _():
        final_ref[0] = state.astype(BF16)
        final_gain_ref[0] = widen(before * gain_rows, spread)


def entering_state(local_ref, gains_ref, state_ref, spread):
    factor = widen(gains_ref[0, 0], spread)[0:1, :]
    return (local_ref[0, 0].astype(F32) + factor * state_ref[0].astype(F32)).astype(BF16)


def pair_decay(running, rest_t, bias, head):
    parts = []
    for at in (head, head + 1):
        column = jnp.broadcast_to(running[:, at : at + 1], (CHUNK, CHUNK))
        parts.append(jnp.exp2(column + (rest_t[at : at + 1, :] + bias)))
    return parts


def stack_pair(values):
    lane = lanes(values.shape)
    wide = values.astype(F32)
    return jnp.concatenate(
        [jnp.where(lane < 64, wide, 0.0), jnp.where(lane >= 64, wide, 0.0)], axis=0
    ).astype(BF16)


def inside_terms(running, step, token):
    seg = jnp.broadcast_to(token[:, SEG_LANE : SEG_LANE + 1], (CHUNK, CHUNK))
    bias = jnp.where((seg == seg.T) & lower_mask(), 0.0, MASKED)
    running_two = running * LOG2E
    rest_t = (jnp.log2(step) - running_two).T
    return running_two, rest_t, bias


def mixer_out_kernel(
    gate_ref, cr_ref, act_ref, token_ref, states_ref, gains_ref, state_ref, head_ref, skip_ref, gain_ref,
    spread_ref, y_ref, out_ref,
):
    token, spread = token_rows(token_ref), spread_ref[...]
    _, step, _, running, _, entry, _ = decay_rows(cr_ref[0, :, CC:], head_ref, token)
    b_rows, c_rows = act_ref[0, :, DI : DI + NS], act_ref[0, :, DI + NS :]
    state = entering_state(states_ref, gains_ref, state_ref, spread)
    carried = contract(c_rows, state, 1, 0) * widen(entry, spread)
    cross = contract(c_rows, b_rows, 1, 1)
    running_two, rest_t, bias = inside_terms(running, step, token)
    square = jnp.zeros((CHUNK, 128), F32)
    for pair in range(MH // 2):
        cols = slice(pair * 128, (pair + 1) * 128)
        xs = act_ref[0, :, cols]
        mix = jnp.concatenate(
            [
                (cross * part).astype(BF16)
                for part in pair_decay(running_two, rest_t, bias, 2 * pair)
            ],
            axis=1,
        )
        y = (
            contract(mix, stack_pair(xs), 1, 0)
            + carried[:, cols]
            + skip_ref[:, cols] * xs.astype(F32)
        )
        y_ref[0, :, cols] = y
        gate = gate_ref[0, :, cols].astype(F32)
        gated = y * (gate * jax.nn.sigmoid(gate))
        square = square + gated * gated
    scale = lax.rsqrt(jnp.sum(square, axis=1, keepdims=True) * (1.0 / DI) + EPSILON)
    for pair in range(MH // 2):
        cols = slice(pair * 128, (pair + 1) * 128)
        gate = gate_ref[0, :, cols].astype(F32)
        gated = y_ref[0, :, cols] * (gate * jax.nn.sigmoid(gate))
        out_ref[0, :, cols] = (gated * scale * gain_ref[:, cols]).astype(BF16)


def mixer_gate_back_kernel(
    gmix_ref, y_ref, gate_ref, cr_ref, act_ref, token_ref, head_ref, gain_ref, spread_ref,
    gy_ref, dgate_ref, gstates_ref, gains_ref, final_ref, dgain_ref, dskip_ref,
    state_s, gain_s, dgain_s, dskip_s,
):
    chunk = pl.program_id(0)

    @pl.when(chunk == 0)
    def _():
        dgain_s[...] = jnp.zeros(dgain_s.shape, F32)
        dskip_s[...] = jnp.zeros(dskip_s.shape, F32)

    @pl.when(chunk == 0)
    def _():
        state_s[...] = jnp.zeros(state_s.shape, F32)
        gain_s[...] = jnp.ones(gain_s.shape, F32)

    token, spread = token_rows(token_ref), spread_ref[...]
    entry, gain = decay_rows(cr_ref[0, :, CC:], head_ref, token)[-2:]
    y = y_ref[0]
    gate = gate_ref[0].astype(F32)
    sig = jax.nn.sigmoid(gate)
    swish = gate * sig
    gated = y * swish
    scale = lax.rsqrt(jnp.mean(gated * gated, axis=1, keepdims=True) + EPSILON)
    grad = gmix_ref[0].astype(F32)
    scaled = grad * gain_ref[...]
    shrink = jnp.mean(scaled * gated, axis=1, keepdims=True) * (scale * scale * scale)
    d_gated = scaled * scale - gated * shrink
    gy = (d_gated * swish).astype(BF16)
    gy_ref[0] = gy
    dgate_ref[0] = (d_gated * y * (sig * (1.0 + gate * (1.0 - sig)))).astype(BF16)
    dgain_s[0:1, :] += jnp.sum(grad * gated * scale, axis=0, keepdims=True)
    gy_float = gy.astype(F32)
    dskip_s[0:1, :] += jnp.sum(gy_float * act_ref[0, :, :DI].astype(F32), axis=0, keepdims=True)
    gstates_ref[0, 0] = state_s[...].astype(BF16)
    after = gain_s[...]
    gains_ref[0, 0] = after
    gain_rows = jnp.broadcast_to(gain, (8, 128))
    carried = (gy_float * widen(entry, spread)).astype(BF16)
    state = state_s[...] * widen(gain_rows, spread)[0:1, :] + contract(
        act_ref[0, :, DI + NS :], carried, 0, 0
    )
    state_s[...] = state
    gain_s[...] = after * gain_rows

    @pl.when(chunk == pl.num_programs(0) - 1)
    def _():
        final_ref[0] = state.astype(BF16)

    dgain_ref[...] = dgain_s[...]
    dskip_ref[...] = dskip_s[...]


def mixer_back_kernel(
    gy_ref, y_ref, cr_ref, halo_ref, rim_ref, act_ref, token_ref,
    states_ref, gains_ref, state_ref, gstates_ref, ggains_ref, gstate_ref,
    head_ref, skip_ref, taps_ref, shift_ref, spread_ref, spread_first_ref,
    dcr_ref, drim_ref, dconv_ref, dhead_ref,
    ext_s, grad_s, carry_s, dconv_s, dhead_s,
):
    step_index = pl.program_id(0)
    last_step = pl.num_programs(0) - 1

    @pl.when(step_index == 0)
    def _():
        dconv_s[...] = jnp.zeros(dconv_s.shape, F32)
        dhead_s[...] = jnp.zeros(dhead_s.shape, F32)

    @pl.when(step_index == 0)
    def _():
        carry_s[...] = jnp.zeros(carry_s.shape, F32)

    @pl.when(step_index == last_step)
    def _():
        ext_s[0:8, :] = rim_ref[0].astype(F32)

    @pl.when(step_index < last_step)
    def _():
        ext_s[0:8, :] = halo_ref[0, :, :CC].astype(F32)[8:16]

    ext_s[8 : 8 + CHUNK, :] = cr_ref[0, :, :CC].astype(F32)
    token, spread, spread_first = token_rows(token_ref), spread_ref[...], spread_first_ref[...]
    raw, step, log_decay, running, weight_end, entry, gain = decay_rows(
        cr_ref[0, :, CC:], head_ref, token
    )
    b_rows, c_rows = act_ref[0, :, DI : DI + NS], act_ref[0, :, DI + NS :]
    state = entering_state(states_ref, gains_ref, state_ref, spread)
    gstate = entering_state(gstates_ref, ggains_ref, gstate_ref, spread)
    wide_end = widen(weight_end, spread)
    gy = gy_ref[0]
    gy_float = gy.astype(F32)
    gcarried = (gy_float * widen(entry, spread)).astype(BF16)
    xs_float = act_ref[0, :, :DI].astype(F32)
    grad_c = contract(gcarried, state, 1, 1)
    grad_b = contract((xs_float * wide_end).astype(BF16), gstate, 1, 1)
    from_end = contract(b_rows, gstate, 1, 0) * wide_end
    dgain_row = jnp.sum(gstate.astype(F32) * state.astype(F32), axis=0, keepdims=True)
    cross = contract(c_rows, b_rows, 1, 1)
    running_two, rest_t, bias = inside_terms(running, step, token)
    grad_cross = jnp.zeros((CHUNK, CHUNK), F32)
    lane = lanes((CHUNK, 128))
    for pair in range(MH // 2):
        cols = slice(pair * 128, (pair + 1) * 128)
        stacked = stack_pair(act_ref[0, :, cols])
        gy_pair = gy_ref[0, :, cols]
        first, second = pair_decay(running_two, rest_t, bias, 2 * pair)
        mix = jnp.concatenate([(cross * first).astype(BF16), (cross * second).astype(BF16)], axis=1)
        grad_mix = contract(gy_pair, stacked, 1, 1)
        grad_cross = grad_cross + grad_mix[:, :CHUNK] * first + grad_mix[:, CHUNK:] * second
        both = contract(mix, gy_pair, 0, 0)
        grad_s[8 : 8 + CHUNK, cols] = jnp.where(lane < 64, both[:CHUNK], both[CHUNK:])
    inner = grad_s[8 : 8 + CHUNK, :DI]
    skip = skip_ref[...]
    cross_low = grad_cross.astype(BF16)
    grad_c = grad_c + contract(cross_low, b_rows, 1, 0)
    grad_b = grad_b + contract(cross_low, c_rows, 0, 0)
    narrow = lambda values: jnp.concatenate(
        [gather_heads(values, spread_first), jnp.zeros((values.shape[0], 96), F32)], axis=1
    )
    query_part = narrow(gy_float * (y_ref[0] - skip * xs_float))
    key_inner = narrow(xs_float * inner)
    key_end = narrow(xs_float * from_end)
    extra = jnp.sum(key_end, axis=0, keepdims=True) + gain * narrow(
        jnp.broadcast_to(dgain_row, (8, DI))
    )[0:1, :]
    upper = (~lower_mask() | (lax.broadcasted_iota(jnp.int32, (CHUNK, CHUNK), 0) == lanes((CHUNK, CHUNK))))
    grad_log = product_exact(upper.astype(BF16), query_part - key_inner - key_end) + extra
    sig = jax.nn.sigmoid(raw)
    ratio = jnp.where(raw < -15.0, 1.0, sig / jnp.maximum(step, 1e-30))
    grad_rate = (key_inner + key_end) * ratio - grad_log * jnp.exp(head_ref[0:1, :]) * sig
    dhead_s[0:1, :] += jnp.sum(grad_log * log_decay, axis=0, keepdims=True)
    dhead_s[1:2, :] += jnp.sum(grad_rate, axis=0, keepdims=True)
    total = conv_total(ext_s, token, taps_ref, shift_ref)
    grad_act = jnp.concatenate([inner + from_end + skip * gy_float, grad_b, grad_c], axis=1)
    csig = jax.nn.sigmoid(total)
    grad_total = grad_act * (csig * (1.0 + total * (1.0 - csig)))
    dconv_s[KC : KC + 1, :] += jnp.sum(grad_total, axis=0, keepdims=True)
    grad_s[0:8, :] = jnp.zeros((8, CC), F32)
    grad_s[8 : 8 + CHUNK, :] = grad_total * taps_ref[KC - 1 : KC, :]
    dconv_s[KC - 1 : KC, :] += jnp.sum(grad_total * ext_s[8 : 8 + CHUNK, :], axis=0, keepdims=True)
    for tap in range(KC - 1):
        part = grad_total * token[:, TAP_LANES + tap : TAP_LANES + tap + 1]
        dconv_s[tap : tap + 1, :] += jnp.sum(
            part * ext_s[5 + tap : 5 + tap + CHUNK, :], axis=0, keepdims=True
        )
        grad_s[5 + tap : 5 + tap + CHUNK, :] += part * taps_ref[tap : tap + 1, :]
    grad_s[CHUNK : CHUNK + 8, :] += carry_s[...]
    carry_s[...] = grad_s[0:8, :]
    dcr_ref[0, :, :CC] = grad_s[8 : 8 + CHUNK, :].astype(BF16)
    dcr_ref[0, :, CC:] = grad_rate.astype(BF16)

    @pl.when(step_index == last_step)
    def _():
        drim_ref[0] = carry_s[...]

    dconv_ref[...] = dconv_s[...]
    dhead_ref[...] = dhead_s[...]


def mixer_call(kernel, name, seq, chunks, reverse, inputs, outputs, scratch, earlier):
    place = (lambda c: chunks - 1 - c) if reverse else (lambda c: c)
    kinds = {
        "block": lambda array, at: pl.BlockSpec(
            (1, CHUNK, array.shape[2]), lambda c: (at, place(c), 0)
        ),
        "chunk": lambda array, at: pl.BlockSpec(
            (1, 1) + array.shape[2:], lambda c: (at, place(c), 0, 0)
        ),
        "token": lambda array, at: pl.BlockSpec((1, 8, CHUNK), lambda c: (at, 0, place(c))),
        "seq": lambda array, at: pl.BlockSpec((1,) + array.shape[1:], lambda c: (at, 0, 0)),
        "own": lambda array, at: pl.BlockSpec((1,) + array.shape[1:], lambda c: (0, 0, 0)),
        "fixed": lambda array, at: pl.BlockSpec(array.shape, lambda c: (0, 0)),
        "halo": lambda array, at: pl.BlockSpec(
            (1, 16, array.shape[2]),
            lambda c: (at, jnp.maximum(place(c) * (CHUNK // 16) - 1, 0), 0),
        ),
    }
    arrays = [array for _, array in inputs]
    in_specs = [kinds[kind](array, seq) for kind, array in inputs]
    out_specs = [kinds[kind](shape, seq) for kind, shape in outputs]
    count = len(inputs)
    aliases, kept = {}, 0
    if earlier is not None:
        shared = [i for i, (kind, _) in enumerate(outputs) if kind in ("block", "chunk")]
        aliases = {count + i: out for i, out in enumerate(shared)}
        arrays += [earlier[out] for out in shared]
        in_specs += [pl.BlockSpec(memory_space=pl.ANY)] * len(shared)
        kept = len(shared)

    def run(*refs):
        kernel(*refs[:count], *refs[count + kept :])

    return pl.pallas_call(
        run,
        grid=(chunks,),
        in_specs=in_specs,
        out_specs=out_specs,
        out_shape=[shape for _, shape in outputs],
        scratch_shapes=[pltpu.VMEM(shape, F32) for shape in scratch],
        input_output_aliases=aliases,
        compiler_params=pltpu.CompilerParams(vmem_limit_bytes=VMEM_BYTES),
        name=name,
    )(*arrays)


def mixer_scan(seq, earlier, cr, rim, token, heads, taps, shift, spread):
    seqs, span, _ = cr.shape
    chunks = span // CHUNK
    return mixer_call(
        mixer_scan_kernel, "mixer_scan", seq, chunks, False,
        [
            ("block", cr), ("seq", rim), ("token", token), ("fixed", heads), ("fixed", taps),
            ("fixed", shift), ("fixed", spread),
        ],
        [
            ("block", jax.ShapeDtypeStruct((seqs, span, CC), BF16)),
            ("chunk", jax.ShapeDtypeStruct((seqs, chunks, NS, DI), BF16)),
            ("chunk", jax.ShapeDtypeStruct((seqs, chunks, 8, 128), F32)),
            ("own", jax.ShapeDtypeStruct((1, NS, DI), BF16)),
            ("own", jax.ShapeDtypeStruct((1, 8, DI), F32)),
        ],
        [(CHUNK + 8, CC), (NS, DI), (8, 128)],
        earlier,
    )


def mixer_out(seq, earlier, gate, cr, act, token, states, gains, state, heads, skip, gain, spread):
    seqs, span, _ = cr.shape
    return mixer_call(
        mixer_out_kernel, "mixer_out", seq, span // CHUNK, False,
        [
            ("block", gate), ("block", cr), ("block", act), ("token", token), ("chunk", states),
            ("chunk", gains), ("own", state), ("fixed", heads), ("fixed", skip),
            ("fixed", gain), ("fixed", spread),
        ],
        [
            ("block", jax.ShapeDtypeStruct((seqs, span, DI), F32)),
            ("block", jax.ShapeDtypeStruct((seqs, span, DI), BF16)),
        ],
        [],
        earlier,
    )


def mixer_gate_back(
    seq, earlier, gmix, y, gate, cr, act, token, heads, gain, spread
):
    seqs, span, _ = cr.shape
    chunks = span // CHUNK
    return mixer_call(
        mixer_gate_back_kernel, "mixer_gate_back", seq, chunks, True,
        [
            ("block", gmix), ("block", y), ("block", gate), ("block", cr), ("block", act), ("token", token),
            ("fixed", heads), ("fixed", gain), ("fixed", spread),
        ],
        [
            ("block", jax.ShapeDtypeStruct((seqs, span, DI), BF16)),
            ("block", jax.ShapeDtypeStruct((seqs, span, DI), BF16)),
            ("chunk", jax.ShapeDtypeStruct((seqs, chunks, NS, DI), BF16)),
            ("chunk", jax.ShapeDtypeStruct((seqs, chunks, 8, 128), F32)),
            ("own", jax.ShapeDtypeStruct((1, NS, DI), BF16)),
            ("fixed", jax.ShapeDtypeStruct((8, DI), F32)),
            ("fixed", jax.ShapeDtypeStruct((8, DI), F32)),
        ],
        [(NS, DI), (8, 128), (8, DI), (8, DI)],
        earlier,
    )


def mixer_back(
    seq, earlier, gy, y, cr, rim, act, token, states, gains, state, gstates, ggains,
    gstate, heads, skip, taps, shift, spread, spread_first,
):
    seqs, span, width = cr.shape
    return mixer_call(
        mixer_back_kernel, "mixer_back", seq, span // CHUNK, True,
        [
            ("block", gy), ("block", y), ("block", cr), ("halo", cr),
            ("seq", rim), ("block", act), ("token", token), ("chunk", states), ("chunk", gains),
            ("own", state), ("chunk", gstates), ("chunk", ggains), ("own", gstate),
            ("fixed", heads), ("fixed", skip), ("fixed", taps), ("fixed", shift),
            ("fixed", spread), ("fixed", spread_first),
        ],
        [
            ("block", jax.ShapeDtypeStruct((seqs, span, width), BF16)),
            ("own", jax.ShapeDtypeStruct((1, 8, CC), F32)),
            ("fixed", jax.ShapeDtypeStruct((8, CC), F32)),
            ("fixed", jax.ShapeDtypeStruct((8, 128), F32)),
        ],
        [(CHUNK + 8, CC), (CHUNK + 8, CC), (8, CC), (8, CC), (8, 128)],
        earlier,
    )


def token_table(seg_own, seg_rim):
    seqs, span = seg_own.shape
    extended = jnp.concatenate([seg_rim, seg_own], axis=1)
    matches = [extended[:, tap : tap + span] == seg_own for tap in range(KC - 1)]
    by_chunk = seg_own.reshape(seqs, -1, CHUNK)
    last = by_chunk[:, :, -1:]
    before = jnp.concatenate([seg_rim[:, None, -1:], last[:, :-1]], axis=1)
    spare = jnp.zeros((seqs, span), F32)
    rows = [match.astype(F32) for match in matches] + [
        spare,
        (by_chunk == before).reshape(seqs, span).astype(F32),
        (by_chunk == last).reshape(seqs, span).astype(F32),
        seg_own.astype(F32),
        spare,
    ]
    return jnp.stack(rows, axis=1)


def from_behind(block, axis, distance):
    devices = range(lax.axis_size(axis))
    route = [(i - distance, i) for i in devices if i - distance in devices]
    return lax.ppermute(block, axis, route)


def after(value, *earlier):
    return lax.optimization_barrier((value, earlier))[0]


class Chain:
    def __init__(self, local, gain, reverse):
        self.local, self.gain, self.reverse = local, gain, reverse
        self.state, self.hop, self.flying = jnp.zeros(local.shape, BF16), 0, None
        self.count, self.place = lax.axis_size("ctx"), lax.axis_index("ctx")

    def send(self, *earlier):
        if self.hop == self.count - 1:
            return
        source = self.count - 1 - self.hop if self.reverse else self.hop
        target = source - 1 if self.reverse else source + 1
        sent = self.local
        if self.hop:
            sent = (self.gain * self.state.astype(F32) + sent.astype(F32)).astype(BF16)
        if earlier:
            sent = after(sent, *earlier)
        self.flying = (lax.ppermute(sent, "ctx", [(source, target)]), target)
        self.hop += 1

    def take(self):
        if self.flying is None:
            return
        received, target = self.flying
        self.state, self.flying = jnp.where(self.place == target, received, self.state), None

    def finish(self):
        self.take()
        while self.hop < self.count - 1:
            self.send()
            self.take()
        return self.state


def sum_everywhere(values, axes):
    for axis in axes:
        count = lax.axis_size(axis)
        copies = jnp.broadcast_to(values[None], (count,) + values.shape)
        values = jnp.sum(lax.all_to_all(copies, axis, 0, 0, tiled=True), axis=0)
    return values


def scatter_all(grad):
    count, place = lax.axis_size("ctx"), lax.axis_index("ctx")
    devices, me = lax.axis_size("dp"), lax.axis_index("dp")
    bits = devices.bit_length() - 1
    part = grad.reshape((2,) * bits + (count, -1, grad.shape[1]))
    for bit in [0] + list(range(bits - 1, 0, -1)):
        at = 0 if bit else bits - 1
        first, second = (lax.index_in_dim(part, side, at, False) for side in range(2))
        low = ((me >> bit) & 1) == 0
        sent = jnp.where(low, second, first).astype(BF16)
        received = lax.ppermute(sent, "dp", [(i, i ^ (1 << bit)) for i in range(devices)])
        part = jnp.where(low, first, second).astype(F32) + received.astype(F32)
    relative = lax.dynamic_slice_in_dim(jnp.concatenate([part, part]), place, count, 0)
    total, rounded = relative[0], relative.astype(BF16)
    for d in range(1, count):
        route = [(i, (i + d) % count) for i in range(count)]
        total = total + lax.ppermute(rounded[d], "ctx", route).astype(F32)
    return total


def rms_scale(values, gain_vec):
    return (
        values * lax.rsqrt(jnp.mean(values * values, axis=-1, keepdims=True) + EPSILON) * gain_vec
    )


def silu_product(gate_lin, up_lin):
    return jax.nn.silu(gate_lin) * up_lin


def body(
    layer_input, segments, positions, gain_one, w_in, conv_w, conv_b, head_params, gain_m, w_out,
    w_q, w_k, w_v, w_o, gain_two, w_gate, w_up, w_down, cotangent,
):
    seqs, span, width = layer_input.shape
    rows = seqs * span
    axes = ("dp", "ctx")
    own_rows = w_q.shape[0]
    q_width, kv_width = QH * HD, 2 * KVH * HD
    low_dot = lambda a, b: jnp.dot(a, b, preferred_element_type=F32)

    small_parts = [gain_one, gain_two, gain_m, conv_b, conv_w.reshape(-1)]
    small_sizes = [part.shape[0] for part in small_parts]
    slots = own_rows * 128
    small_block = jnp.concatenate(small_parts, axis=0)
    small_block = jnp.pad(small_block, (0, slots - sum(small_sizes))).reshape(own_rows, 128)
    w_kv = jnp.stack(
        [w_k.reshape(own_rows, KVH, HD), w_v.reshape(own_rows, KVH, HD)], axis=2
    ).reshape(own_rows, kv_width)
    count = lax.axis_size("ctx")
    exchange = lambda blocks: lax.all_to_all(blocks, "ctx", 0, 0, tiled=True)
    copies = lambda block: jnp.broadcast_to(block[None], (count,) + block.shape)
    gather = lambda part: lax.all_gather(part, "dp", axis=0, tiled=True)
    w_cr = jnp.pad(w_in[:, DI:], ((0, 0), (0, CR - (w_in.shape[1] - DI))))
    first = jnp.concatenate([w_cr, w_q, w_kv, small_block, w_in[:, :DI]], axis=1)
    first_part = lax.all_gather(first, "ctx", axis=0, tiled=True)
    first_all = gather(first_part)
    turned_o = w_o.T
    half_rows, ff = own_rows // 2, w_gate.shape[1]

    def fold(block, cut):
        return jnp.concatenate([block[..., :half_rows, cut:], block[..., half_rows:, cut:]], axis=-1)

    def unfold(block):
        half = block.shape[-1] // 2
        return jnp.concatenate([block[..., :half], block[..., half:]], axis=-2)

    rest = [w_down, w_out, fold(turned_o, 0)]
    for matrix in (w_gate, w_up):
        rest += [matrix[:, at : at + width] for at in range(0, ff, width)]
    rest_sizes = [part.shape[0] for part in rest]
    place = lax.axis_index("ctx")
    span_start = place * span
    seg_own = lax.dynamic_slice_in_dim(segments, span_start, span, 1)
    seg_rim = jnp.where(
        place > 0,
        lax.dynamic_slice_in_dim(segments, jnp.maximum(span_start - (KC - 1), 0), KC - 1, 1),
        -1,
    )
    token = token_table(seg_own, seg_rim)
    bounds = attention_bounds(segments, seg_own, span_start)
    segk, segq = segments[:, :, None], seg_own[:, None, :]
    cosine, sine = rope_tables(positions)
    heads = jnp.pad(head_params, ((0, 5), (0, 128 - MH)))
    skip = jnp.repeat(head_params[2], MP)[None]
    spread, spread_first = spread_matrix(), spread_first_matrix()

    tokens = layer_input.reshape(rows, width)
    small = (token, bounds, segk, segq, cosine, sine, heads, skip, spread, spread_first)
    cosine, sine = cosine.reshape(rows, 128), sine.reshape(rows, 128)
    rest_part = exchange(after(copies(jnp.concatenate(rest, axis=0)), first_part, small))
    rest_all = gather(rest_part.reshape(-1, width)).reshape(-1, sum(rest_sizes), width)
    cuts, at = [], 0
    for size in rest_sizes:
        cuts.append(rest_all[:, at : at + size])
        at += size
    w_down_all, w_out_all = cuts[0].reshape(-1, width), cuts[1].reshape(-1, width)
    w_o_all = unfold(cuts[2]).reshape(width, q_width)
    w_gates = first_all[:, FIRST:]
    w_gu_all = jnp.concatenate([cut.reshape(width, width) for cut in cuts[3:]], axis=1)
    small_all = first_all[:, FIRST - 128 : FIRST].reshape(-1, slots).astype(F32)
    parts, at = [], 0
    for size in small_sizes:
        parts.append(small_all[:, at : at + size])
        at += size
    gain1_all, gain2_all, gain_m_all, shift_all = [part.reshape(1, -1) for part in parts[:4]]
    taps_all = jnp.swapaxes(parts[4].reshape(-1, KC, small_sizes[3]), 0, 1).reshape(KC, CC)
    taps_all = jnp.pad(taps_all, ((0, 8 - KC), (0, 0)))


    hidden, cr, q, kv = project(tokens, gain1_all, first_all, cosine, sine)
    q = q.reshape(seqs, span, q_width)
    kv = kv.reshape(seqs, span, kv_width)
    cr = cr.reshape(seqs, span, CR)
    rim = from_behind(cr[:, span - (KC - 1) :, :CC], "ctx", 1)
    kv_all = exchange(after(copies(kv), rim))
    rim = jnp.pad(rim, ((0, 0), (8 - (KC - 1), 0), (0, 0)))
    scanned, chains, wide_gains = None, [], []
    for seq in range(seqs):
        scanned = mixer_scan(
            seq, scanned, cr, rim, token, heads, taps_all,
            shift_all, spread,
        )
        wide_gains.append(scanned[4][:, :1])
        chains.append(Chain(scanned[3], wide_gains[seq], False))
        chains[seq].send()
    act, states, gains = scanned[:3]
    for chain in chains:
        chain.take()
        chain.send()
    atts, lses, mixed = [], [], None
    mark = (act, w_down_all, w_out_all, w_o_all, w_gu_all)
    for seq in range(seqs):
        att, lse = attend(seq, bounds, after(q, mark), kv_all, segk, segq)
        atts.append(att)
        lses.append(lse)
        chains[seq].take()
        chains[seq].send(lse)
        mark = lse
    gate = low_dot(hidden, w_gates).astype(BF16).reshape(seqs, span, DI)
    states_in = []
    for seq in range(seqs):
        states_in.append(chains[seq].finish())
        mixed = mixer_out(
            seq, mixed, gate, cr, act, token, states, gains, states_in[seq], heads, skip, gain_m_all,
            spread,
        )
    mixer_y, mixer_in = mixed
    mixer_in = mixer_in.reshape(rows, DI)
    att_rows = jnp.concatenate(atts, axis=0).reshape(rows, q_width)
    middle = (
        tokens.astype(F32)
        + low_dot(mixer_in, w_out_all)
        + jnp.einsum("ra,da->rd", att_rows, w_o_all, preferred_element_type=F32)
    )
    normed_mid, norm2_pull = jax.vjp(rms_scale, middle, gain2_all)
    normed_two = normed_mid.astype(BF16)
    gate_up = low_dot(normed_two, w_gu_all).astype(BF16)
    act_float, act_pull = jax.vjp(
        silu_product, gate_up[:, :ff].astype(F32), gate_up[:, ff:].astype(F32)
    )
    act_rows = act_float.astype(BF16)
    def scatter(grad):
        return lax.psum_scatter(grad, "dp", scatter_dimension=0, tiled=True)

    def weight_grad(left, right):
        return jnp.einsum("ri,ro->io", left, right, preferred_element_type=F32).astype(BF16)

    def back_dot(grad, weight):
        return jnp.einsum("ro,io->ri", grad, weight, preferred_element_type=F32)

    cot_rows = cotangent.reshape(rows, width)
    grad_down = weight_grad(act_rows, cot_rows)
    grad_gate_up = jnp.concatenate(act_pull(back_dot(cot_rows, w_down_all)), axis=1).astype(BF16)
    grad_wgu = weight_grad(normed_two, grad_gate_up)
    grad_normed = back_dot(grad_gate_up, w_gu_all)
    grad_normed, grad_down, grad_wgu = lax.optimization_barrier((grad_normed, grad_down, grad_wgu))
    part_gu = scatter(grad_wgu)
    grad_mid_norm, grad_gain_second = norm2_pull(grad_normed)
    grad_middle = cot_rows.astype(F32) + grad_mid_norm
    grad_mid_low = grad_middle.astype(BF16)
    grad_wout = weight_grad(mixer_in, grad_mid_low)
    grad_wo = weight_grad(grad_mid_low, att_rows)
    grad_mixer_in = back_dot(grad_mid_low, w_out_all).astype(BF16).reshape(seqs, span, DI)
    grad_att = low_dot(grad_mid_low, w_o_all).astype(BF16).reshape(seqs, span, q_width)
    grad_mixer_in, grad_att, grad_wout, grad_wo = lax.optimization_barrier(
        (grad_mixer_in, grad_att, grad_wout, grad_wo)
    )
    grad_wo = grad_wo.reshape(-1, own_rows, q_width)
    gated, chains, grad_gain_mix, grad_skip = None, [], 0.0, 0.0
    for seq in range(seqs):
        gated = mixer_gate_back(
            seq, gated, grad_mixer_in, mixer_y, gate, cr, act, token, heads, gain_m_all, spread
        )
        grad_gain_mix, grad_skip = grad_gain_mix + gated[5], grad_skip + gated[6]
        chains.append(Chain(gated[4], wide_gains[seq], True))
        chains[seq].send()
    grad_y, grad_gate, gstates, ggains = gated[:4]
    chains[0].take()
    chains[1 % seqs].take()
    grad_wgates = weight_grad(after(hidden, chains[0].state), grad_gate.reshape(rows, DI)).reshape(-1, own_rows, DI)
    blocks = grad_wo.shape[0]
    grad_rest = jnp.concatenate(
        [
            after(grad_down, chains[0].state, chains[1 % seqs].state).reshape(blocks, -1, width), grad_wout.reshape(blocks, -1, width),
            fold(grad_wo, 0), grad_wgates[..., :width], fold(grad_wgates, width),
        ],
        axis=1,
    )
    part_rest = scatter(grad_rest.reshape(-1, width))
    cos3, sin3 = cosine.reshape(seqs, span, 128), sine.reshape(seqs, span, 128)
    dqs, dkvs = [], []
    for seq in range(seqs):
        if seq < 2:
            for chain in chains:
                chain.take()
                chain.send(*dqs[-1:])
        mark = dqs[-1:] + [chain.state for chain in chains] + ([] if seq else [grad_rest])
        dq, dkv = attend_back(
            seq, bounds, after(q, grad_y, *mark), kv_all, segk,
            segq, atts[seq], grad_att, lses[seq], cos3, sin3,
        )
        dqs.append(dq)
        dkvs.append(dkv)
    dq = jnp.concatenate(dqs, axis=0)
    last, rims, grad_conv, grad_heads = None, [], 0.0, 0.0
    waits = [(grad_rest, part_gu)] + [()] * (seqs - 1)
    finals = [chain.finish() for chain in chains]
    dkv_all = exchange(after(jnp.concatenate(dkvs, axis=1), *finals))
    waits[1 % seqs] += tuple(finals)
    for seq in range(seqs):
        gstate = finals[seq]
        if seq == seqs - 1:
            gu_blocks = part_gu.reshape(count, own_rows, 2 * ff)
            parts = [after(part_rest, *rims).reshape(count, -1, width)]
            parts += [gu_blocks[..., at : at + width] for at in range(0, 2 * ff, width)]
            rest_low = jnp.concatenate(parts, axis=1).reshape(-1, width)
            waits[seq] = (rest_low,)
        last = mixer_back(
            seq, last, after(grad_y, dqs[-1], *waits[seq]), mixer_y, cr, rim, act, token, states,
            gains, states_in[seq], gstates, ggains, gstate, heads, skip, taps_all, shift_all,
            spread, spread_first,
        )
        rims.append(last[1])
        grad_conv, grad_heads = grad_conv + last[2], grad_heads + last[3]
    grad_cr, grad_rim = last[0], jnp.concatenate(rims, axis=0)
    back_rim = from_behind(grad_rim[:, 8 - (KC - 1) :].astype(BF16), "ctx", -1)
    edge = grad_cr[:, span - (KC - 1) :, :CC].astype(F32) + back_rim.astype(F32)
    grad_cr = lax.dynamic_update_slice(
        grad_cr, after(edge.astype(BF16), dkv_all), (0, span - (KC - 1), 0)
    ).reshape(rows, CR)
    rest_out = lax.psum_scatter(rest_low, "ctx", scatter_dimension=0, tiled=True).astype(F32)
    grad_wcr = weight_grad(hidden, grad_cr)
    part_cr = scatter(grad_wcr)
    layer_result = (middle + low_dot(after(act_rows, part_cr), w_down_all)).astype(BF16)
    out_cr = lax.psum_scatter(part_cr, "ctx", scatter_dimension=0, tiled=True).astype(F32)
    grad_tokens, grad_kv, grad_gain_first = finish(
        tokens, gain1_all, grad_gate.reshape(rows, DI), after(grad_cr, grad_wcr, rest_out),
        dq.reshape(rows, q_width), dkv_all, cosine, sine, grad_middle, first_all,
    )
    grad_first = jnp.concatenate([dq.reshape(rows, q_width), grad_kv], axis=1)
    grad_wfirst = weight_grad(hidden, grad_first)
    grad_gain_first = grad_gain_first[0]

    devices = first_all.shape[0] // own_rows
    small_grads = jnp.concatenate(
        [
            grad_gain_first.reshape(devices, -1),
            grad_gain_second.reshape(devices, -1),
            grad_gain_mix[0].reshape(devices, -1),
            grad_conv[KC].reshape(devices, -1),
            jnp.swapaxes(grad_conv[:KC].reshape(KC, devices, -1), 0, 1).reshape(devices, -1),
        ],
        axis=1,
    )
    small_grads = jnp.pad(small_grads, ((0, 0), (0, slots - small_grads.shape[1])))
    out_first = scatter_all(
        jnp.concatenate([grad_wfirst, small_grads.reshape(-1, 128).astype(BF16)], axis=1)
    )
    rest_sizes = rest_sizes[:3] + [own_rows, half_rows] + rest_sizes[3:]
    outs, at = [], 0
    for size in rest_sizes:
        outs.append(rest_out[at : at + size])
        at += size
    out_down, out_wout = outs[0], outs[1]
    out_wo = unfold(outs[2])
    out_win = jnp.concatenate(
        [outs[3], unfold(outs[4]), out_cr[:, : w_in.shape[1] - DI]], axis=1
    )
    halves = ff // width
    out_gate = jnp.concatenate(outs[5 : 5 + halves], axis=1)
    out_up = jnp.concatenate(outs[5 + halves :], axis=1)
    out_small = out_first[:, q_width + kv_width :].reshape(-1)
    pieces, at = [], 0
    for size in small_sizes:
        pieces.append(out_small[at : at + size])
        at += size
    out_kv = out_first[:, q_width : q_width + kv_width].reshape(own_rows, KVH, 2, HD)
    head_grad = sum_everywhere(
        jnp.concatenate(
            [grad_heads[:2, :MH], grad_skip[0].reshape(MH, MP).sum(axis=1)[None]], axis=0
        ),
        axes,
    )
    return (
        layer_result.reshape(layer_input.shape),
        grad_tokens.reshape(layer_input.shape),
        pieces[0],
        out_win,
        pieces[4].reshape(KC, -1),
        pieces[3],
        head_grad,
        pieces[2],
        out_wout,
        out_first[:, :q_width],
        out_kv[:, :, 0].reshape(own_rows, -1),
        out_kv[:, :, 1].reshape(own_rows, -1),
        out_wo.T,
        pieces[1],
        out_gate,
        out_up,
        out_down,
    )


def solution(mesh):
    in_specs = (
        P("dp", "ctx", None),
        P("dp", None),
        P("dp", "ctx"),
        P(("dp", "ctx")),
        P(("dp", "ctx"), None),
        P(None, ("dp", "ctx")),
        P(("dp", "ctx")),
        P(),
        P(("dp", "ctx")),
        P(("dp", "ctx"), None),
        P(("dp", "ctx"), None),
        P(("dp", "ctx"), None),
        P(("dp", "ctx"), None),
        P(None, ("dp", "ctx")),
        P(("dp", "ctx")),
        P(("dp", "ctx"), None),
        P(("dp", "ctx"), None),
        P(("dp", "ctx"), None),
        P("dp", "ctx", None),
    )
    out_specs = (
        P("dp", "ctx", None),
        P("dp", "ctx", None),
        P(("dp", "ctx")),
        P(("dp", "ctx"), None),
        P(None, ("dp", "ctx")),
        P(("dp", "ctx")),
        P(),
        P(("dp", "ctx")),
        P(("dp", "ctx"), None),
        P(("dp", "ctx"), None),
        P(("dp", "ctx"), None),
        P(("dp", "ctx"), None),
        P(None, ("dp", "ctx")),
        P(("dp", "ctx")),
        P(("dp", "ctx"), None),
        P(("dp", "ctx"), None),
        P(("dp", "ctx"), None),
    )
    return jax.shard_map(body, mesh=mesh, in_specs=in_specs, out_specs=out_specs, check_vma=False)
```

```python
import functools
import jax
import jax.numpy as jnp
from jax import lax
from jax.experimental import pallas as pl
from jax.experimental.pallas import tpu as pltpu
from jax.sharding import PartitionSpec as P

MH = 24
MP = 64
NS = 128
KC = 4
QH = 8
KVH = 2
HD = 64
EPSILON = 1e-05
ROPE_BASE = 10000.0
MASKED = -1e30
LOG2E = 1.4426950408889634
KEY_TILE = 256
VMEM_BYTES = 56 * 1024 * 1024

F32 = jnp.float32
BF16 = jnp.bfloat16


def contract(left, right, left_dim, right_dim):
    return lax.dot_general(
        left, right, (((left_dim,), (right_dim,)), ((), ())), preferred_element_type=F32
    )


def lanes(shape):
    return lax.broadcasted_iota(jnp.int32, shape, len(shape) - 1)


def swap_halves(values):
    lane = lanes(values.shape)
    return jnp.where(lane < 32, pltpu.roll(values, 96, 1), pltpu.roll(values, 32, 1))


CR = MH * MP + 2 * NS + 128
FIRST = CR + QH * HD + 2 * KVH * HD + 128


def project_kernel(x_ref, gain_ref, w_ref, cos_ref, sin_ref, hidden_ref, cr_ref, q_ref, kv_ref):
    x = x_ref[...].astype(F32)
    scale = lax.rsqrt(jnp.mean(x * x, axis=-1, keepdims=True) + EPSILON)
    hidden = (x * scale * gain_ref[...]).astype(BF16)
    hidden_ref[...] = hidden
    lin = contract(hidden, w_ref[:, CR : CR + QH * HD + 2 * KVH * HD], 1, 0)
    cosine, sine = cos_ref[...], sin_ref[...]
    lane = lanes(cosine.shape)
    for pair in range(QH // 2):
        both = lin[:, pair * 128 : (pair + 1) * 128]
        other = pltpu.roll(both, 64, 1)
        even = both * cosine + swap_halves(both) * sine
        odd = other * cosine + swap_halves(other) * sine
        q_ref[:, pair * 128 : (pair + 1) * 128] = jnp.where(
            lane < 64, even, pltpu.roll(odd, 64, 1)
        ).astype(BF16)
    for group in range(KVH):
        at = QH * HD + group * 128
        part = lin[:, at : at + 128]
        kv_ref[:, group * 128 : (group + 1) * 128] = (
            part * cosine + swap_halves(part) * sine
        ).astype(BF16)
    cr_ref[...] = contract(hidden, w_ref[:, :CR], 1, 0).astype(BF16)


def project(x, gain, w_first, cosine, sine):
    rows, width = x.shape
    tile = 256 if rows % 256 == 0 else 128
    block = lambda cols: pl.BlockSpec((tile, cols), lambda i: (i, 0))
    fixed = lambda array: pl.BlockSpec(array.shape, lambda i: (0, 0))
    cols = [width, CR, QH * HD, 2 * KVH * HD]
    return pl.pallas_call(
        project_kernel,
        grid=(rows // tile,),
        in_specs=[
            block(width), fixed(gain), fixed(w_first), block(128), block(128),
        ],
        out_specs=[block(size) for size in cols],
        out_shape=[jax.ShapeDtypeStruct((rows, size), BF16) for size in cols],
        compiler_params=pltpu.CompilerParams(vmem_limit_bytes=VMEM_BYTES),
        name="project",
    )(x, gain, w_first, cosine, sine)


def finish_kernel(
    x_ref, gain_ref, dgate_ref, dcr_ref, dq_ref, dkv_ref, cos_ref, sin_ref, middle_ref,
    w_ref, dx_ref, dkv_out_ref, dgain_ref, dgain_s,
):
    @pl.when(pl.program_id(0) == 0)
    def _():
        dgain_s[...] = jnp.zeros(dgain_s.shape, F32)

    dkv = dkv_ref[0, 0].astype(F32)
    for source in range(1, dkv_ref.shape[0]):
        dkv = dkv + dkv_ref[source, 0].astype(F32)
    cosine, sine = cos_ref[...], sin_ref[...]
    turned = []
    for group in range(KVH):
        part = dkv[:, group * 128 : (group + 1) * 128]
        back = part * cosine + swap_halves(part * sine)
        turned.append(jnp.where(lanes(part.shape) < HD, back, part))
    dkv = jnp.concatenate(turned, axis=1).astype(BF16)
    dkv_out_ref[...] = dkv
    at = CR + QH * HD
    grad = (
        contract(dgate_ref[...], w_ref[:, FIRST:], 1, 1)
        + contract(dcr_ref[...], w_ref[:, :CR], 1, 1)
        + contract(dq_ref[...], w_ref[:, CR:at], 1, 1)
        + contract(dkv, w_ref[:, at : at + 2 * KVH * HD], 1, 1)
    )
    x = x_ref[...].astype(F32)
    scale = lax.rsqrt(jnp.mean(x * x, axis=-1, keepdims=True) + EPSILON)
    scaled = grad * gain_ref[...]
    shrink = jnp.mean(scaled * x, axis=-1, keepdims=True) * (scale * scale * scale)
    dx_ref[...] = (middle_ref[...] + scaled * scale - x * shrink).astype(BF16)
    dgain_s[0:1, :] += jnp.sum(grad * x * scale, axis=0, keepdims=True)
    dgain_ref[...] = dgain_s[...]


def finish(x, gain, dgate, dcr, dq, dkv_all, cosine, sine, middle, w_first):
    rows, width = x.shape
    span = dkv_all.shape[2]
    tile = min(256, span)
    per_seq = span // tile
    block = lambda array: pl.BlockSpec((tile, array.shape[1]), lambda i: (i, 0))
    fixed = lambda array: pl.BlockSpec(array.shape, lambda i: (0, 0))
    keys = pl.BlockSpec(
        (dkv_all.shape[0], 1, tile, dkv_all.shape[3]), lambda i: (0, i // per_seq, i % per_seq, 0)
    )
    kv_width = dkv_all.shape[3]
    return pl.pallas_call(
        finish_kernel,
        grid=(rows // tile,),
        in_specs=[
            block(x), fixed(gain), block(dgate), block(dcr), block(dq), keys, block(cosine),
            block(sine), block(middle), fixed(w_first),
        ],
        out_specs=[
            block(x),
            pl.BlockSpec((tile, kv_width), lambda i: (i, 0)),
            pl.BlockSpec((8, width), lambda i: (0, 0)),
        ],
        out_shape=[
            jax.ShapeDtypeStruct((rows, width), BF16),
            jax.ShapeDtypeStruct((rows, kv_width), BF16),
            jax.ShapeDtypeStruct((8, width), F32),
        ],
        scratch_shapes=[pltpu.VMEM((8, width), F32)],
        compiler_params=pltpu.CompilerParams(vmem_limit_bytes=VMEM_BYTES),
        name="finish",
    )(x, gain, dgate, dcr, dq, dkv_all, cosine, sine, middle, w_first)


def visible(segk_ref, segq, query_row, at, key_rows):
    segk = segk_ref[0, pl.ds(at, key_rows), :]
    key_col = at + lax.broadcasted_iota(jnp.int32, (key_rows, 1), 0)
    return jnp.where((segk == segq) & (key_col <= query_row), 0.0, MASKED)


def attend_kernel(
    place_at, low_ref, high_ref, base_ref, q_ref, kv_ref, segk_ref, segq_ref, out_ref, lse_ref,
    q_s, m_s, l_s, acc_s,
):
    tile = pl.program_id(0)
    rows = q_ref.shape[1]
    place = place_at + tile
    lane = lanes((rows, 128))
    for pair in range(QH // 2):
        both = q_ref[0, :, pair * 128 : (pair + 1) * 128].astype(F32)
        q_s[2 * pair] = jnp.where(lane < 64, both, 0.0).astype(BF16)
        q_s[2 * pair + 1] = jnp.where(lane < 64, pltpu.roll(both, 64, 1), 0.0).astype(BF16)
    key_rows = min(KEY_TILE, kv_ref.shape[2])
    tiles_each = kv_ref.shape[2] // key_rows
    m_s[...] = jnp.full(m_s.shape, MASKED, F32)
    l_s[...] = jnp.zeros(l_s.shape, F32)
    acc_s[...] = jnp.zeros(acc_s.shape, F32)
    query_row = base_ref[0] + tile * rows + lanes((1, rows))
    segq = segq_ref[0]
    factor = HD ** (-0.5) * LOG2E

    def step(key_tile, carry):
        at = pl.multiple_of(key_tile * key_rows, key_rows)
        source = key_tile // tiles_each
        offset = pl.multiple_of((key_tile % tiles_each) * key_rows, key_rows)
        bias = visible(segk_ref, segq, query_row, at, key_rows)
        for group in range(KVH):
            kv = kv_ref[source, 0, pl.ds(offset, key_rows), group * 128 : (group + 1) * 128]
            kv_t = kv.astype(F32).T.astype(BF16)
            members = range(group * (QH // KVH), (group + 1) * (QH // KVH))
            scores = [contract(kv, q_s[head], 1, 1) * factor + bias for head in members]
            before = [m_s[head : head + 1, :] for head in members]
            tops = [
                jnp.maximum(old, jnp.max(part, axis=0, keepdims=True))
                for old, part in zip(before, scores)
            ]
            weights = [jnp.exp2(part - top) for part, top in zip(scores, tops)]
            sums = [jnp.sum(part, axis=0, keepdims=True) for part in weights]
            outs = [contract(kv_t, part.astype(BF16), 1, 0) for part in weights]
            for at_head, head in enumerate(members):
                fade = jnp.exp2(before[at_head] - tops[at_head])
                l_s[head : head + 1, :] = l_s[head : head + 1, :] * fade + sums[at_head]
                acc_s[head] = acc_s[head] * fade + outs[at_head]
                m_s[head : head + 1, :] = tops[at_head]
        return carry

    lax.fori_loop(low_ref[place], high_ref[place], step, 0)
    lse_ref[0] = m_s[...] + jnp.log2(l_s[...])
    for pair in range(QH // 2):
        even = (acc_s[2 * pair] / l_s[2 * pair : 2 * pair + 1, :]).T
        odd = (acc_s[2 * pair + 1] / l_s[2 * pair + 1 : 2 * pair + 2, :]).T
        out_ref[0, :, pair * 128 : (pair + 1) * 128] = jnp.where(
            lane < 64, pltpu.roll(even, 64, 1), odd
        ).astype(BF16)


def attend_back_kernel(
    place_at, low_ref, high_ref, base_ref, q_ref, kv_ref, segk_ref, segq_ref, att_ref, gatt_ref, lse_ref,
    cos_ref, sin_ref, dq_ref, dkv_ref,
    q_s, g_s, delta_s, dq_s, dkv_s,
):
    tile = pl.program_id(0)
    rows = q_ref.shape[1]
    place = place_at + tile
    lane = lanes((rows, 128))

    @pl.when(tile == 0)
    def _():
        dkv_s[...] = jnp.zeros(dkv_s.shape, F32)

    for pair in range(QH // 2):
        cols = slice(pair * 128, (pair + 1) * 128)
        both = q_ref[0, :, cols].astype(F32)
        q_s[2 * pair] = jnp.where(lane < 64, both, 0.0).astype(BF16)
        q_s[2 * pair + 1] = jnp.where(lane < 64, pltpu.roll(both, 64, 1), 0.0).astype(BF16)
        grad = gatt_ref[0, :, cols].astype(F32)
        g_s[2 * pair] = jnp.where(lane >= 64, pltpu.roll(grad, 64, 1), 0.0).astype(BF16)
        g_s[2 * pair + 1] = jnp.where(lane >= 64, grad, 0.0).astype(BF16)
        product = (grad * att_ref[0, :, cols].astype(F32)).T
        delta_s[2 * pair : 2 * pair + 1, :] = jnp.sum(product[:64], axis=0, keepdims=True)
        delta_s[2 * pair + 1 : 2 * pair + 2, :] = jnp.sum(product[64:], axis=0, keepdims=True)
    key_rows = min(KEY_TILE, kv_ref.shape[2])
    tiles_each = kv_ref.shape[2] // key_rows
    dq_s[...] = jnp.zeros(dq_s.shape, F32)
    query_row = base_ref[0] + tile * rows + lanes((1, rows))
    segq = segq_ref[0]
    qk_scale = HD ** (-0.5)
    factor = qk_scale * LOG2E

    def step(key_tile, carry):
        at = pl.multiple_of(key_tile * key_rows, key_rows)
        source = key_tile // tiles_each
        offset = pl.multiple_of((key_tile % tiles_each) * key_rows, key_rows)
        bias = visible(segk_ref, segq, query_row, at, key_rows)
        for group in range(KVH):
            kv = kv_ref[source, 0, pl.ds(offset, key_rows), group * 128 : (group + 1) * 128]
            kv_t = kv.astype(F32).T.astype(BF16)
            total = jnp.zeros((key_rows, 128), F32)
            for member in range(QH // KVH):
                head = group * (QH // KVH) + member
                q, g = q_s[head], g_s[head]
                scores = contract(kv, q, 1, 1) * factor + bias
                probs = jnp.exp2(scores - lse_ref[0, head : head + 1, :])
                d_probs = contract(kv, g, 1, 1)
                d_scores = (probs * (d_probs - delta_s[head : head + 1, :]) * qk_scale).astype(BF16)
                total = total + contract(d_scores, q, 1, 0) + contract(probs.astype(BF16), g, 1, 0)
                dq_s[head] += contract(kv_t, d_scores, 1, 0)
            cols = slice(group * 128, (group + 1) * 128)
            dkv_s[source, 0, pl.ds(offset, key_rows), cols] += total
        return carry

    lax.fori_loop(low_ref[place], high_ref[place], step, 0)
    cosine, sine = cos_ref[0], sin_ref[0]
    for pair in range(QH // 2):
        even, odd = dq_s[2 * pair].T, dq_s[2 * pair + 1].T
        even = even * cosine + swap_halves(even * sine)
        odd = odd * cosine + swap_halves(odd * sine)
        dq_ref[0, :, pair * 128 : (pair + 1) * 128] = jnp.where(
            lane < 64, even, pltpu.roll(odd, 64, 1)
        ).astype(BF16)

    @pl.when(tile == pl.num_programs(0) - 1)
    def _():
        dkv_ref[...] = dkv_s[...].astype(BF16)


def attention_specs(seq, length, rows):
    tile = lambda cols, at=seq: pl.BlockSpec((1, rows, cols), lambda t, *_: (at, t, 0))
    whole = lambda cols, at=seq: pl.BlockSpec((1, length, cols), lambda t, *_: (at, 0, 0))
    keys = lambda array, at=seq: pl.BlockSpec(
        (array.shape[0], 1) + array.shape[2:], lambda t, *_: (0, at, 0, 0)
    )
    row = lambda n, at=seq: pl.BlockSpec((1, n, rows), lambda t, *_: (at, 0, t))
    return tile, whole, keys, row


def attend(seq, bounds, q, kv_all, segk, segq):
    _, span, q_width = q.shape
    rows = min(256, span)
    tile, whole, keys, row = attention_specs(seq, segk.shape[1], rows)
    own_keys = kv_all.shape[:1] + (1,) + kv_all.shape[2:]
    return pl.pallas_call(
        functools.partial(attend_kernel, seq * (span // rows)),
        grid_spec=pltpu.PrefetchScalarGridSpec(
            num_scalar_prefetch=3,
            grid=(span // rows,),
            in_specs=[tile(q_width), keys(kv_all), whole(1), row(1)],
            out_specs=[tile(q_width, 0), row(QH, 0)],
            scratch_shapes=[
                pltpu.VMEM((QH, rows, 128), BF16),
                pltpu.VMEM((QH, rows), F32),
                pltpu.VMEM((QH, rows), F32),
                pltpu.VMEM((QH, 128, rows), F32),
            ],
        ),
        out_shape=[
            jax.ShapeDtypeStruct((1, span, q_width), BF16),
            jax.ShapeDtypeStruct((1, QH, span), F32),
        ],
        compiler_params=pltpu.CompilerParams(vmem_limit_bytes=VMEM_BYTES),
        name="attend",
    )(*bounds, q, kv_all, segk, segq)


def attend_back(seq, bounds, q, kv_all, segk, segq, att, grad_att, lse, cosine, sine):
    _, span, q_width = q.shape
    rows = min(256, span)
    tile, whole, keys, row = attention_specs(seq, segk.shape[1], rows)
    own_keys = kv_all.shape[:1] + (1,) + kv_all.shape[2:]
    return pl.pallas_call(
        functools.partial(attend_back_kernel, seq * (span // rows)),
        grid_spec=pltpu.PrefetchScalarGridSpec(
            num_scalar_prefetch=3,
            grid=(span // rows,),
            in_specs=[
                tile(q_width), keys(kv_all), whole(1), row(1), tile(q_width, 0), tile(q_width),
                row(QH, 0), tile(128), tile(128),
            ],
            out_specs=[tile(q_width, 0), keys(kv_all, 0)],
            scratch_shapes=[
                pltpu.VMEM((QH, rows, 128), BF16),
                pltpu.VMEM((QH, rows, 128), BF16),
                pltpu.VMEM((QH, rows), F32),
                pltpu.VMEM((QH, 128, rows), F32),
                pltpu.VMEM(own_keys, F32),
            ],
        ),
        out_shape=[
            jax.ShapeDtypeStruct((1, span, q_width), BF16),
            jax.ShapeDtypeStruct(own_keys, BF16),
        ],
        compiler_params=pltpu.CompilerParams(vmem_limit_bytes=VMEM_BYTES),
        name="attend_back",
    )(*bounds, q, kv_all, segk, segq, att, grad_att, lse, cosine, sine)


def rope_tables(positions):
    half = HD // 2
    frequency = ROPE_BASE ** (-jnp.arange(half, dtype=F32) / half)
    angles = positions.astype(F32)[..., None] * frequency
    cosine, sine = jnp.cos(angles), jnp.sin(angles)
    one, zero = jnp.ones(cosine.shape[:-1] + (HD,), F32), jnp.zeros(cosine.shape[:-1] + (HD,), F32)
    return (
        jnp.concatenate([cosine, cosine, one], axis=-1),
        jnp.concatenate([-sine, sine, zero], axis=-1),
    )


def attention_bounds(segments, seg_own, span_start):
    seqs, span = seg_own.shape
    rows, key_rows = min(256, span), min(KEY_TILE, span)
    first = seg_own[:, ::rows]
    begin = jnp.sum((segments[:, None, :] < first[:, :, None]).astype(jnp.int32), axis=2)
    tiles = jnp.arange(span // rows, dtype=jnp.int32)
    high = (span_start + (tiles + 1) * rows + key_rows - 1) // key_rows
    high = jnp.broadcast_to(high[None], first.shape)
    return (
        (begin // key_rows).reshape(-1),
        high.reshape(-1).astype(jnp.int32),
        jnp.full((1,), span_start, jnp.int32),
    )


CHUNK = 128
DI = MH * MP
CC = DI + 2 * NS
TAP_LANES, PREV_LANE, LAST_LANE, SEG_LANE = 0, 4, 5, 6


def split_three(values):
    high = values.astype(BF16)
    rest = values - high.astype(F32)
    middle = rest.astype(BF16)
    return high, middle, (rest - middle.astype(F32)).astype(BF16)


def product_exact(matrix, values):
    return sum(contract(matrix, part, 1, 0) for part in split_three(values))


def widen(values, spread):
    kept = jnp.where(lanes(values.shape) < 32, values, 0.0)
    high, middle, rest = (part.astype(F32) for part in split_three(kept))
    packed = high + pltpu.roll(middle, 32, 1) + pltpu.roll(rest, 64, 1)
    return contract(packed.astype(BF16), spread, 1, 0)


def gather_heads(values, spread_first):
    high = values.astype(BF16)
    rest = (values - high.astype(F32)).astype(BF16)
    return contract(high, spread_first, 1, 1) + contract(rest, spread_first, 1, 1)


def spread_matrix():
    row = lax.broadcasted_iota(jnp.int32, (128, DI), 0)
    col = lax.broadcasted_iota(jnp.int32, (128, DI), 1)
    return ((row % 32 == col // MP) & (row < 96)).astype(BF16)


def spread_first_matrix():
    row = lax.broadcasted_iota(jnp.int32, (32, DI), 0)
    col = lax.broadcasted_iota(jnp.int32, (32, DI), 1)
    return (row == col // MP).astype(BF16)


def lower_mask():
    row = lax.broadcasted_iota(jnp.int32, (CHUNK, CHUNK), 0)
    return row >= lanes((CHUNK, CHUNK))


def saved_terms(terms_ref):
    return [terms_ref[0, :, at * 128 : (at + 1) * 128] for at in range(6)]


def token_rows(token_ref):
    return jnp.concatenate([token_ref[0]] * 16, axis=0).T


def decay_rows(rate, head_ref, token):
    raw = rate.astype(F32) + head_ref[1:2, :]
    step = jnp.maximum(raw, 0.0) + jnp.log1p(jnp.exp(-jnp.abs(raw)))
    log_decay = -step * jnp.exp(head_ref[0:1, :])
    running = product_exact(lower_mask().astype(BF16), log_decay)
    last = running[CHUNK - 1 :, :]
    weight_end = jnp.exp(last - running) * step * token[:, LAST_LANE : LAST_LANE + 1]
    entry = jnp.exp(running) * token[:, PREV_LANE : PREV_LANE + 1]
    gain = jnp.exp(last) * token[CHUNK - 1 :, PREV_LANE : PREV_LANE + 1]
    return raw, step, log_decay, running, weight_end, entry, gain


def conv_total(ext_s, token, taps_ref, shift_ref):
    total = shift_ref[...] + ext_s[8 : 8 + CHUNK, :] * taps_ref[KC - 1 : KC, :]
    for tap in range(KC - 1):
        total = total + ext_s[5 + tap : 5 + tap + CHUNK, :] * (
            taps_ref[tap : tap + 1, :] * token[:, TAP_LANES + tap : TAP_LANES + tap + 1]
        )
    return total


def mixer_scan_kernel(
    cr_ref, rim_ref, token_ref, head_ref, taps_ref, shift_ref, spread_ref,
    act_ref, states_ref, gains_ref, final_ref, final_gain_ref, terms_ref,
    ext_s, state_s, gain_s,
):
    chunk = pl.program_id(0)

    @pl.when(chunk == 0)
    def _():
        ext_s[0:8, :] = rim_ref[0].astype(F32)
        state_s[...] = jnp.zeros(state_s.shape, F32)
        gain_s[...] = jnp.ones(gain_s.shape, F32)

    @pl.when(chunk > 0)
    def _():
        ext_s[0:8, :] = ext_s[CHUNK : CHUNK + 8, :]

    token = token_rows(token_ref)
    ext_s[8 : 8 + CHUNK, :] = cr_ref[0, :, :CC].astype(F32)
    total = conv_total(ext_s, token, taps_ref, shift_ref)
    act = (total * jax.nn.sigmoid(total)).astype(BF16)
    act_ref[0] = act
    raw, step, log_decay, running, weight_end, entry, gain = decay_rows(
        cr_ref[0, :, CC:], head_ref, token
    )
    for at, term in enumerate((raw, step, log_decay, running, weight_end, entry)):
        terms_ref[0, :, at * 128 : (at + 1) * 128] = term
    states_ref[0, 0] = state_s[...].astype(BF16)
    before = gain_s[...]
    row = lax.broadcasted_iota(jnp.int32, before.shape, 0)
    gains_ref[0, 0] = jnp.where(row == 1, jnp.broadcast_to(gain, before.shape), before)
    spread = spread_ref[...]
    scaled = (act[:, :DI].astype(F32) * widen(weight_end, spread)).astype(BF16)
    gain_rows = jnp.broadcast_to(gain, (8, 128))
    state = state_s[...] * widen(gain_rows, spread)[0:1, :] + contract(
        act[:, DI : DI + NS], scaled, 0, 0
    )
    state_s[...] = state
    gain_s[...] = before * gain_rows

    @pl.when(chunk == pl.num_programs(0) - 1)
    def _():
        final_ref[0] = state.astype(BF16)
        final_gain_ref[0] = widen(before * gain_rows, spread)


def entering_state(local_ref, gains_ref, state_ref, spread):
    factor = widen(gains_ref[0, 0], spread)[0:1, :]
    return (local_ref[0, 0].astype(F32) + factor * state_ref[0].astype(F32)).astype(BF16)


def pair_decay(running, rest_t, bias, head):
    parts = []
    for at in (head, head + 1):
        column = jnp.broadcast_to(running[:, at : at + 1], (CHUNK, CHUNK))
        parts.append(jnp.exp2(column + (rest_t[at : at + 1, :] + bias)))
    return parts


def stack_pair(values):
    lane = lanes(values.shape)
    wide = values.astype(F32)
    return jnp.concatenate(
        [jnp.where(lane < 64, wide, 0.0), jnp.where(lane >= 64, wide, 0.0)], axis=0
    ).astype(BF16)


def inside_terms(running, step, token):
    seg = jnp.broadcast_to(token[:, SEG_LANE : SEG_LANE + 1], (CHUNK, CHUNK))
    bias = jnp.where((seg == seg.T) & lower_mask(), 0.0, MASKED)
    running_two = running * LOG2E
    rest_t = (jnp.log2(step) - running_two).T
    return running_two, rest_t, bias


def mixer_out_kernel(
    gate_ref, terms_ref, act_ref, token_ref, states_ref, gains_ref, state_ref, skip_ref, gain_ref,
    spread_ref, y_ref, out_ref,
):
    token, spread = token_rows(token_ref), spread_ref[...]
    _, step, _, running, _, entry = saved_terms(terms_ref)
    b_rows, c_rows = act_ref[0, :, DI : DI + NS], act_ref[0, :, DI + NS :]
    state = entering_state(states_ref, gains_ref, state_ref, spread)
    carried = contract(c_rows, state, 1, 0) * widen(entry, spread)
    cross = contract(c_rows, b_rows, 1, 1)
    running_two, rest_t, bias = inside_terms(running, step, token)
    square = jnp.zeros((CHUNK, 128), F32)
    for pair in range(MH // 2):
        cols = slice(pair * 128, (pair + 1) * 128)
        xs = act_ref[0, :, cols]
        mix = jnp.concatenate(
            [
                (cross * part).astype(BF16)
                for part in pair_decay(running_two, rest_t, bias, 2 * pair)
            ],
            axis=1,
        )
        y = (
            contract(mix, stack_pair(xs), 1, 0)
            + carried[:, cols]
            + skip_ref[:, cols] * xs.astype(F32)
        )
        y_ref[0, :, cols] = y
        gate = gate_ref[0, :, cols].astype(F32)
        gated = y * (gate * jax.nn.sigmoid(gate))
        square = square + gated * gated
    scale = lax.rsqrt(jnp.sum(square, axis=1, keepdims=True) * (1.0 / DI) + EPSILON)
    for pair in range(MH // 2):
        cols = slice(pair * 128, (pair + 1) * 128)
        gate = gate_ref[0, :, cols].astype(F32)
        gated = y_ref[0, :, cols] * (gate * jax.nn.sigmoid(gate))
        out_ref[0, :, cols] = (gated * scale * gain_ref[:, cols]).astype(BF16)


def mixer_gate_back_kernel(
    gmix_ref, y_ref, gate_ref, terms_ref, act_ref, fgains_ref, gain_ref, spread_ref,
    gy_ref, dgate_ref, gstates_ref, gains_ref, final_ref, dgain_ref, dskip_ref,
    state_s, gain_s, dgain_s, dskip_s,
):
    chunk = pl.program_id(0)

    @pl.when(chunk == 0)
    def _():
        dgain_s[...] = jnp.zeros(dgain_s.shape, F32)
        dskip_s[...] = jnp.zeros(dskip_s.shape, F32)

    @pl.when(chunk == 0)
    def _():
        state_s[...] = jnp.zeros(state_s.shape, F32)
        gain_s[...] = jnp.ones(gain_s.shape, F32)

    spread = spread_ref[...]
    entry, gain = saved_terms(terms_ref)[-1], fgains_ref[0, 0, 1:2, :]
    y = y_ref[0]
    gate = gate_ref[0].astype(F32)
    sig = jax.nn.sigmoid(gate)
    swish = gate * sig
    gated = y * swish
    scale = lax.rsqrt(jnp.mean(gated * gated, axis=1, keepdims=True) + EPSILON)
    grad = gmix_ref[0].astype(F32)
    scaled = grad * gain_ref[...]
    shrink = jnp.mean(scaled * gated, axis=1, keepdims=True) * (scale * scale * scale)
    d_gated = scaled * scale - gated * shrink
    gy = (d_gated * swish).astype(BF16)
    gy_ref[0] = gy
    dgate_ref[0] = (d_gated * y * (sig * (1.0 + gate * (1.0 - sig)))).astype(BF16)
    dgain_s[0:1, :] += jnp.sum(grad * gated * scale, axis=0, keepdims=True)
    gy_float = gy.astype(F32)
    dskip_s[0:1, :] += jnp.sum(gy_float * act_ref[0, :, :DI].astype(F32), axis=0, keepdims=True)
    gstates_ref[0, 0] = state_s[...].astype(BF16)
    after = gain_s[...]
    gains_ref[0, 0] = after
    gain_rows = jnp.broadcast_to(gain, (8, 128))
    carried = (gy_float * widen(entry, spread)).astype(BF16)
    state = state_s[...] * widen(gain_rows, spread)[0:1, :] + contract(
        act_ref[0, :, DI + NS :], carried, 0, 0
    )
    state_s[...] = state
    gain_s[...] = after * gain_rows

    @pl.when(chunk == pl.num_programs(0) - 1)
    def _():
        final_ref[0] = state.astype(BF16)

    dgain_ref[...] = dgain_s[...]
    dskip_ref[...] = dskip_s[...]


def mixer_back_kernel(
    gy_ref, y_ref, terms_ref, cr_ref, halo_ref, rim_ref, act_ref, token_ref,
    states_ref, gains_ref, state_ref, gstates_ref, ggains_ref, gstate_ref,
    head_ref, skip_ref, taps_ref, shift_ref, spread_ref, spread_first_ref,
    dcr_ref, drim_ref, dconv_ref, dhead_ref,
    ext_s, grad_s, carry_s, dconv_s, dhead_s,
):
    step_index = pl.program_id(0)
    last_step = pl.num_programs(0) - 1

    @pl.when(step_index == 0)
    def _():
        dconv_s[...] = jnp.zeros(dconv_s.shape, F32)
        dhead_s[...] = jnp.zeros(dhead_s.shape, F32)

    @pl.when(step_index == 0)
    def _():
        carry_s[...] = jnp.zeros(carry_s.shape, F32)

    @pl.when(step_index == last_step)
    def _():
        ext_s[0:8, :] = rim_ref[0].astype(F32)

    @pl.when(step_index < last_step)
    def _():
        ext_s[0:8, :] = halo_ref[0, :, :CC].astype(F32)[8:16]

    ext_s[8 : 8 + CHUNK, :] = cr_ref[0, :, :CC].astype(F32)
    token, spread, spread_first = token_rows(token_ref), spread_ref[...], spread_first_ref[...]
    raw, step, log_decay, running, weight_end, entry = saved_terms(terms_ref)
    gain = gains_ref[0, 0, 1:2, :]
    b_rows, c_rows = act_ref[0, :, DI : DI + NS], act_ref[0, :, DI + NS :]
    state = entering_state(states_ref, gains_ref, state_ref, spread)
    gstate = entering_state(gstates_ref, ggains_ref, gstate_ref, spread)
    wide_end = widen(weight_end, spread)
    gy = gy_ref[0]
    gy_float = gy.astype(F32)
    gcarried = (gy_float * widen(entry, spread)).astype(BF16)
    xs_float = act_ref[0, :, :DI].astype(F32)
    grad_c = contract(gcarried, state, 1, 1)
    grad_b = contract((xs_float * wide_end).astype(BF16), gstate, 1, 1)
    from_end = contract(b_rows, gstate, 1, 0) * wide_end
    dgain_row = jnp.sum(gstate.astype(F32) * state.astype(F32), axis=0, keepdims=True)
    cross = contract(c_rows, b_rows, 1, 1)
    running_two, rest_t, bias = inside_terms(running, step, token)
    grad_cross = jnp.zeros((CHUNK, CHUNK), F32)
    lane = lanes((CHUNK, 128))
    for pair in range(MH // 2):
        cols = slice(pair * 128, (pair + 1) * 128)
        stacked = stack_pair(act_ref[0, :, cols])
        gy_pair = gy_ref[0, :, cols]
        first, second = pair_decay(running_two, rest_t, bias, 2 * pair)
        mix = jnp.concatenate([(cross * first).astype(BF16), (cross * second).astype(BF16)], axis=1)
        grad_mix = contract(gy_pair, stacked, 1, 1)
        grad_cross = grad_cross + grad_mix[:, :CHUNK] * first + grad_mix[:, CHUNK:] * second
        both = contract(mix, gy_pair, 0, 0)
        grad_s[8 : 8 + CHUNK, cols] = jnp.where(lane < 64, both[:CHUNK], both[CHUNK:])
    inner = grad_s[8 : 8 + CHUNK, :DI]
    skip = skip_ref[...]
    cross_low = grad_cross.astype(BF16)
    grad_c = grad_c + contract(cross_low, b_rows, 1, 0)
    grad_b = grad_b + contract(cross_low, c_rows, 0, 0)
    narrow = lambda values: jnp.concatenate(
        [gather_heads(values, spread_first), jnp.zeros((values.shape[0], 96), F32)], axis=1
    )
    query_part = narrow(gy_float * (y_ref[0] - skip * xs_float))
    key_inner = narrow(xs_float * inner)
    key_end = narrow(xs_float * from_end)
    extra = jnp.sum(key_end, axis=0, keepdims=True) + gain * narrow(
        jnp.broadcast_to(dgain_row, (8, DI))
    )[0:1, :]
    upper = (~lower_mask() | (lax.broadcasted_iota(jnp.int32, (CHUNK, CHUNK), 0) == lanes((CHUNK, CHUNK))))
    grad_log = product_exact(upper.astype(BF16), query_part - key_inner - key_end) + extra
    sig = jax.nn.sigmoid(raw)
    ratio = jnp.where(raw < -15.0, 1.0, sig / jnp.maximum(step, 1e-30))
    grad_rate = (key_inner + key_end) * ratio - grad_log * jnp.exp(head_ref[0:1, :]) * sig
    dhead_s[0:1, :] += jnp.sum(grad_log * log_decay, axis=0, keepdims=True)
    dhead_s[1:2, :] += jnp.sum(grad_rate, axis=0, keepdims=True)
    total = conv_total(ext_s, token, taps_ref, shift_ref)
    grad_act = jnp.concatenate([inner + from_end + skip * gy_float, grad_b, grad_c], axis=1)
    csig = jax.nn.sigmoid(total)
    grad_total = grad_act * (csig * (1.0 + total * (1.0 - csig)))
    dconv_s[KC : KC + 1, :] += jnp.sum(grad_total, axis=0, keepdims=True)
    grad_s[0:8, :] = jnp.zeros((8, CC), F32)
    grad_s[8 : 8 + CHUNK, :] = grad_total * taps_ref[KC - 1 : KC, :]
    dconv_s[KC - 1 : KC, :] += jnp.sum(grad_total * ext_s[8 : 8 + CHUNK, :], axis=0, keepdims=True)
    for tap in range(KC - 1):
        part = grad_total * token[:, TAP_LANES + tap : TAP_LANES + tap + 1]
        dconv_s[tap : tap + 1, :] += jnp.sum(
            part * ext_s[5 + tap : 5 + tap + CHUNK, :], axis=0, keepdims=True
        )
        grad_s[5 + tap : 5 + tap + CHUNK, :] += part * taps_ref[tap : tap + 1, :]
    grad_s[CHUNK : CHUNK + 8, :] += carry_s[...]
    carry_s[...] = grad_s[0:8, :]
    dcr_ref[0, :, :CC] = grad_s[8 : 8 + CHUNK, :].astype(BF16)
    dcr_ref[0, :, CC:] = grad_rate.astype(BF16)

    @pl.when(step_index == last_step)
    def _():
        drim_ref[0] = carry_s[...]

    dconv_ref[...] = dconv_s[...]
    dhead_ref[...] = dhead_s[...]


def mixer_call(kernel, name, seq, chunks, reverse, inputs, outputs, scratch, earlier):
    place = (lambda c: chunks - 1 - c) if reverse else (lambda c: c)
    kinds = {
        "block": lambda array, at: pl.BlockSpec(
            (1, CHUNK, array.shape[2]), lambda c: (at, place(c), 0)
        ),
        "chunk": lambda array, at: pl.BlockSpec(
            (1, 1) + array.shape[2:], lambda c: (at, place(c), 0, 0)
        ),
        "token": lambda array, at: pl.BlockSpec((1, 8, CHUNK), lambda c: (at, 0, place(c))),
        "seq": lambda array, at: pl.BlockSpec((1,) + array.shape[1:], lambda c: (at, 0, 0)),
        "own": lambda array, at: pl.BlockSpec((1,) + array.shape[1:], lambda c: (0, 0, 0)),
        "fixed": lambda array, at: pl.BlockSpec(array.shape, lambda c: (0, 0)),
        "halo": lambda array, at: pl.BlockSpec(
            (1, 16, array.shape[2]),
            lambda c: (at, jnp.maximum(place(c) * (CHUNK // 16) - 1, 0), 0),
        ),
    }
    arrays = [array for _, array in inputs]
    in_specs = [kinds[kind](array, seq) for kind, array in inputs]
    out_specs = [kinds[kind](shape, seq) for kind, shape in outputs]
    count = len(inputs)
    aliases, kept = {}, 0
    if earlier is not None:
        shared = [i for i, (kind, _) in enumerate(outputs) if kind in ("block", "chunk")]
        aliases = {count + i: out for i, out in enumerate(shared)}
        arrays += [earlier[out] for out in shared]
        in_specs += [pl.BlockSpec(memory_space=pl.ANY)] * len(shared)
        kept = len(shared)

    def run(*refs):
        kernel(*refs[:count], *refs[count + kept :])

    return pl.pallas_call(
        run,
        grid=(chunks,),
        in_specs=in_specs,
        out_specs=out_specs,
        out_shape=[shape for _, shape in outputs],
        scratch_shapes=[pltpu.VMEM(shape, F32) for shape in scratch],
        input_output_aliases=aliases,
        compiler_params=pltpu.CompilerParams(vmem_limit_bytes=VMEM_BYTES),
        name=name,
    )(*arrays)


def mixer_scan(seq, earlier, cr, rim, token, heads, taps, shift, spread):
    seqs, span, _ = cr.shape
    chunks = span // CHUNK
    return mixer_call(
        mixer_scan_kernel, "mixer_scan", seq, chunks, False,
        [
            ("block", cr), ("seq", rim), ("token", token), ("fixed", heads), ("fixed", taps),
            ("fixed", shift), ("fixed", spread),
        ],
        [
            ("block", jax.ShapeDtypeStruct((seqs, span, CC), BF16)),
            ("chunk", jax.ShapeDtypeStruct((seqs, chunks, NS, DI), BF16)),
            ("chunk", jax.ShapeDtypeStruct((seqs, chunks, 8, 128), F32)),
            ("own", jax.ShapeDtypeStruct((1, NS, DI), BF16)),
            ("own", jax.ShapeDtypeStruct((1, 8, DI), F32)),
            ("block", jax.ShapeDtypeStruct((seqs, span, 6 * 128), F32)),
        ],
        [(CHUNK + 8, CC), (NS, DI), (8, 128)],
        earlier,
    )


def mixer_out(seq, earlier, gate, terms, act, token, states, gains, state, skip, gain, spread):
    seqs, span, _ = gate.shape
    return mixer_call(
        mixer_out_kernel, "mixer_out", seq, span // CHUNK, False,
        [
            ("block", gate), ("block", terms), ("block", act), ("token", token), ("chunk", states),
            ("chunk", gains), ("own", state), ("fixed", skip),
            ("fixed", gain), ("fixed", spread),
        ],
        [
            ("block", jax.ShapeDtypeStruct((seqs, span, DI), F32)),
            ("block", jax.ShapeDtypeStruct((seqs, span, DI), BF16)),
        ],
        [],
        earlier,
    )


def mixer_gate_back(
    seq, earlier, gmix, y, gate, terms, act, gains, gain, spread
):
    seqs, span, _ = gate.shape
    chunks = span // CHUNK
    return mixer_call(
        mixer_gate_back_kernel, "mixer_gate_back", seq, chunks, True,
        [
            ("block", gmix), ("block", y), ("block", gate), ("block", terms), ("block", act), ("chunk", gains),
            ("fixed", gain), ("fixed", spread),
        ],
        [
            ("block", jax.ShapeDtypeStruct((seqs, span, DI), BF16)),
            ("block", jax.ShapeDtypeStruct((seqs, span, DI), BF16)),
            ("chunk", jax.ShapeDtypeStruct((seqs, chunks, NS, DI), BF16)),
            ("chunk", jax.ShapeDtypeStruct((seqs, chunks, 8, 128), F32)),
            ("own", jax.ShapeDtypeStruct((1, NS, DI), BF16)),
            ("fixed", jax.ShapeDtypeStruct((8, DI), F32)),
            ("fixed", jax.ShapeDtypeStruct((8, DI), F32)),
        ],
        [(NS, DI), (8, 128), (8, DI), (8, DI)],
        earlier,
    )


def mixer_back(
    seq, earlier, gy, y, terms, cr, rim, act, token, states, gains, state, gstates, ggains,
    gstate, heads, skip, taps, shift, spread, spread_first,
):
    seqs, span, width = cr.shape
    return mixer_call(
        mixer_back_kernel, "mixer_back", seq, span // CHUNK, True,
        [
            ("block", gy), ("block", y), ("block", terms), ("block", cr), ("halo", cr),
            ("seq", rim), ("block", act), ("token", token), ("chunk", states), ("chunk", gains),
            ("own", state), ("chunk", gstates), ("chunk", ggains), ("own", gstate),
            ("fixed", heads), ("fixed", skip), ("fixed", taps), ("fixed", shift),
            ("fixed", spread), ("fixed", spread_first),
        ],
        [
            ("block", jax.ShapeDtypeStruct((seqs, span, width), BF16)),
            ("own", jax.ShapeDtypeStruct((1, 8, CC), F32)),
            ("fixed", jax.ShapeDtypeStruct((8, CC), F32)),
            ("fixed", jax.ShapeDtypeStruct((8, 128), F32)),
        ],
        [(CHUNK + 8, CC), (CHUNK + 8, CC), (8, CC), (8, CC), (8, 128)],
        earlier,
    )


def token_table(seg_own, seg_rim):
    seqs, span = seg_own.shape
    extended = jnp.concatenate([seg_rim, seg_own], axis=1)
    matches = [extended[:, tap : tap + span] == seg_own for tap in range(KC - 1)]
    by_chunk = seg_own.reshape(seqs, -1, CHUNK)
    last = by_chunk[:, :, -1:]
    before = jnp.concatenate([seg_rim[:, None, -1:], last[:, :-1]], axis=1)
    spare = jnp.zeros((seqs, span), F32)
    rows = [match.astype(F32) for match in matches] + [
        spare,
        (by_chunk == before).reshape(seqs, span).astype(F32),
        (by_chunk == last).reshape(seqs, span).astype(F32),
        seg_own.astype(F32),
        spare,
    ]
    return jnp.stack(rows, axis=1)


def from_behind(block, axis, distance):
    devices = range(lax.axis_size(axis))
    route = [(i - distance, i) for i in devices if i - distance in devices]
    return lax.ppermute(block, axis, route)


def after(value, *earlier):
    return lax.optimization_barrier((value, earlier))[0]


class Chain:
    def __init__(self, local, gain, reverse):
        self.local, self.gain, self.reverse = local, gain, reverse
        self.state, self.hop, self.flying = jnp.zeros(local.shape, BF16), 0, None
        self.count, self.place = lax.axis_size("ctx"), lax.axis_index("ctx")

    def send(self, *earlier):
        if self.hop == self.count - 1:
            return
        source = self.count - 1 - self.hop if self.reverse else self.hop
        target = source - 1 if self.reverse else source + 1
        sent = self.local
        if self.hop:
            sent = (self.gain * self.state.astype(F32) + sent.astype(F32)).astype(BF16)
        if earlier:
            sent = after(sent, *earlier)
        self.flying = (lax.ppermute(sent, "ctx", [(source, target)]), target)
        self.hop += 1

    def take(self):
        if self.flying is None:
            return
        received, target = self.flying
        self.state, self.flying = jnp.where(self.place == target, received, self.state), None

    def finish(self):
        self.take()
        while self.hop < self.count - 1:
            self.send()
            self.take()
        return self.state


def sum_everywhere(values, axes):
    for axis in axes:
        count = lax.axis_size(axis)
        copies = jnp.broadcast_to(values[None], (count,) + values.shape)
        values = jnp.sum(lax.all_to_all(copies, axis, 0, 0, tiled=True), axis=0)
    return values


def scatter_all(grad, *late):
    count, place = lax.axis_size("ctx"), lax.axis_index("ctx")
    devices, me = lax.axis_size("dp"), lax.axis_index("dp")
    bits = devices.bit_length() - 1
    part = grad.reshape((2,) * bits + (count, -1, grad.shape[1]))
    for bit in [0] + list(range(bits - 1, 0, -1)):
        at = 0 if bit else bits - 1
        first, second = (lax.index_in_dim(part, side, at, False) for side in range(2))
        low = ((me >> bit) & 1) == 0
        sent = jnp.where(low, second, first).astype(BF16)
        received = lax.ppermute(sent, "dp", [(i, i ^ (1 << bit)) for i in range(devices)])
        part = jnp.where(low, first, second).astype(F32) + received.astype(F32)
    relative = lax.dynamic_slice_in_dim(jnp.concatenate([part, part]), place, count, 0)
    total, rounded = relative[0], after(relative.astype(BF16), *late)
    for d in range(1, count):
        route = [(i, (i + d) % count) for i in range(count)]
        total = total + lax.ppermute(rounded[d], "ctx", route).astype(F32)
    return total


def rms_scale(values, gain_vec):
    return (
        values * lax.rsqrt(jnp.mean(values * values, axis=-1, keepdims=True) + EPSILON) * gain_vec
    )


def silu_product(gate_lin, up_lin):
    return jax.nn.silu(gate_lin) * up_lin


def body(
    layer_input, segments, positions, gain_one, w_in, conv_w, conv_b, head_params, gain_m, w_out,
    w_q, w_k, w_v, w_o, gain_two, w_gate, w_up, w_down, cotangent,
):
    seqs, span, width = layer_input.shape
    rows = seqs * span
    axes = ("dp", "ctx")
    own_rows = w_q.shape[0]
    q_width, kv_width = QH * HD, 2 * KVH * HD
    low_dot = lambda a, b: jnp.dot(a, b, preferred_element_type=F32)

    small_parts = [gain_one, gain_two, gain_m, conv_b, conv_w.reshape(-1)]
    small_sizes = [part.shape[0] for part in small_parts]
    slots = own_rows * 128
    small_block = jnp.concatenate(small_parts, axis=0)
    small_block = jnp.pad(small_block, (0, slots - sum(small_sizes))).reshape(own_rows, 128)
    w_kv = jnp.stack(
        [w_k.reshape(own_rows, KVH, HD), w_v.reshape(own_rows, KVH, HD)], axis=2
    ).reshape(own_rows, kv_width)
    count = lax.axis_size("ctx")
    exchange = lambda blocks: lax.all_to_all(blocks, "ctx", 0, 0, tiled=True)
    copies = lambda block: jnp.broadcast_to(block[None], (count,) + block.shape)
    gather = lambda part: lax.all_gather(part, "dp", axis=0, tiled=True)
    w_cr = jnp.pad(w_in[:, DI:], ((0, 0), (0, CR - (w_in.shape[1] - DI))))
    first = jnp.concatenate([w_cr, w_q, w_kv, small_block, w_in[:, :DI]], axis=1)
    first_part = lax.all_gather(first, "ctx", axis=0, tiled=True)
    turned_o = w_o.T
    half_rows, ff = own_rows // 2, w_gate.shape[1]

    def fold(block, cut):
        return jnp.concatenate([block[..., :half_rows, cut:], block[..., half_rows:, cut:]], axis=-1)

    def unfold(block):
        half = block.shape[-1] // 2
        return jnp.concatenate([block[..., :half], block[..., half:]], axis=-2)

    rest = [w_down, w_out, fold(turned_o, 0)]
    for matrix in (w_gate, w_up):
        rest += [matrix[:, at : at + width] for at in range(0, ff, width)]
    rest_sizes = [part.shape[0] for part in rest]
    place = lax.axis_index("ctx")
    span_start = place * span
    seg_own = lax.dynamic_slice_in_dim(segments, span_start, span, 1)
    seg_rim = jnp.where(
        place > 0,
        lax.dynamic_slice_in_dim(segments, jnp.maximum(span_start - (KC - 1), 0), KC - 1, 1),
        -1,
    )
    token = token_table(seg_own, seg_rim)
    bounds = attention_bounds(segments, seg_own, span_start)
    segk, segq = segments[:, :, None], seg_own[:, None, :]
    cosine, sine = rope_tables(positions)
    heads = jnp.pad(head_params, ((0, 5), (0, 128 - MH)))
    skip = jnp.repeat(head_params[2], MP)[None]
    spread, spread_first = spread_matrix(), spread_first_matrix()

    tokens = layer_input.reshape(rows, width)
    small = (token, bounds, segk, segq, cosine, sine, heads, skip, spread, spread_first)
    rest_copies = copies(jnp.concatenate(rest, axis=0))
    first_all = gather(after(first_part, small, rest_copies))
    cosine, sine = cosine.reshape(rows, 128), sine.reshape(rows, 128)
    rest_part = exchange(after(rest_copies, first_part))
    rest_all = gather(rest_part.reshape(-1, width)).reshape(-1, sum(rest_sizes), width)
    cuts, at = [], 0
    for size in rest_sizes:
        cuts.append(rest_all[:, at : at + size])
        at += size
    w_down_all, w_out_all = cuts[0].reshape(-1, width), cuts[1].reshape(-1, width)
    w_o_all = unfold(cuts[2]).reshape(width, q_width)
    w_gates = first_all[:, FIRST:]
    w_gu_all = jnp.concatenate([cut.reshape(width, width) for cut in cuts[3:]], axis=1)
    small_all = first_all[:, FIRST - 128 : FIRST].reshape(-1, slots).astype(F32)
    parts, at = [], 0
    for size in small_sizes:
        parts.append(small_all[:, at : at + size])
        at += size
    gain1_all, gain2_all, gain_m_all, shift_all = [part.reshape(1, -1) for part in parts[:4]]
    taps_all = jnp.swapaxes(parts[4].reshape(-1, KC, small_sizes[3]), 0, 1).reshape(KC, CC)
    taps_all = jnp.pad(taps_all, ((0, 8 - KC), (0, 0)))


    hidden, cr, q, kv = project(tokens, gain1_all, first_all, cosine, sine)
    q = q.reshape(seqs, span, q_width)
    kv = kv.reshape(seqs, span, kv_width)
    cr = cr.reshape(seqs, span, CR)
    rim = from_behind(cr[:, span - (KC - 1) :, :CC], "ctx", 1)
    kv_all = exchange(after(copies(kv), rim))
    rim = jnp.pad(rim, ((0, 0), (8 - (KC - 1), 0), (0, 0)))
    scanned, chains, wide_gains = None, [], []
    for seq in range(seqs):
        scanned = mixer_scan(
            seq, scanned, cr, rim, token, heads, taps_all,
            shift_all, spread,
        )
        wide_gains.append(scanned[4][:, :1])
        chains.append(Chain(scanned[3], wide_gains[seq], False))
        chains[seq].send()
    act, states, gains, terms = scanned[0], scanned[1], scanned[2], scanned[5]
    for chain in chains:
        chain.take()
        chain.send()
    atts, lses, mixed = [], [], None
    mark = (act, w_down_all, w_out_all, w_o_all, w_gu_all)
    for seq in range(seqs):
        att, lse = attend(seq, bounds, after(q, mark), kv_all, segk, segq)
        atts.append(att)
        lses.append(lse)
        chains[seq].take()
        chains[seq].send(lse)
        mark = lse
    gate = low_dot(hidden, w_gates).astype(BF16).reshape(seqs, span, DI)
    states_in = []
    for seq in range(seqs):
        states_in.append(chains[seq].finish())
        mixed = mixer_out(
            seq, mixed, gate, terms, act, token, states, gains, states_in[seq], skip, gain_m_all,
            spread,
        )
    mixer_y, mixer_in = mixed
    mixer_in = mixer_in.reshape(rows, DI)
    att_rows = jnp.concatenate(atts, axis=0).reshape(rows, q_width)
    middle = (
        tokens.astype(F32)
        + low_dot(mixer_in, w_out_all)
        + jnp.einsum("ra,da->rd", att_rows, w_o_all, preferred_element_type=F32)
    )
    normed_mid, norm2_pull = jax.vjp(rms_scale, middle, gain2_all)
    normed_two = normed_mid.astype(BF16)
    gate_up = low_dot(normed_two, w_gu_all).astype(BF16)
    act_float, act_pull = jax.vjp(
        silu_product, gate_up[:, :ff].astype(F32), gate_up[:, ff:].astype(F32)
    )
    act_rows = act_float.astype(BF16)
    def scatter(grad):
        return lax.psum_scatter(grad, "dp", scatter_dimension=0, tiled=True)

    def weight_grad(left, right):
        return jnp.einsum("ri,ro->io", left, right, preferred_element_type=F32).astype(BF16)

    def back_dot(grad, weight):
        return jnp.einsum("ro,io->ri", grad, weight, preferred_element_type=F32)

    cot_rows = cotangent.reshape(rows, width)
    grad_down = weight_grad(act_rows, cot_rows)
    grad_gate_up = jnp.concatenate(act_pull(back_dot(cot_rows, w_down_all)), axis=1).astype(BF16)
    grad_wgu = weight_grad(normed_two, grad_gate_up)
    grad_normed = back_dot(grad_gate_up, w_gu_all)
    grad_normed, grad_down, grad_wgu = lax.optimization_barrier((grad_normed, grad_down, grad_wgu))
    part_gu = scatter(grad_wgu)
    grad_mid_norm, grad_gain_second = norm2_pull(grad_normed)
    grad_middle = cot_rows.astype(F32) + grad_mid_norm
    grad_mid_low = grad_middle.astype(BF16)
    grad_wout = weight_grad(mixer_in, grad_mid_low)
    grad_wo = weight_grad(grad_mid_low, att_rows)
    grad_mixer_in = back_dot(grad_mid_low, w_out_all).astype(BF16).reshape(seqs, span, DI)
    grad_att = low_dot(grad_mid_low, w_o_all).astype(BF16).reshape(seqs, span, q_width)
    grad_mixer_in, grad_att, grad_wout, grad_wo = lax.optimization_barrier(
        (grad_mixer_in, grad_att, grad_wout, grad_wo)
    )
    grad_wo = grad_wo.reshape(-1, own_rows, q_width)
    gated, chains, grad_gain_mix, grad_skip = None, [], 0.0, 0.0
    for seq in range(seqs):
        gated = mixer_gate_back(
            seq, gated, grad_mixer_in, mixer_y, gate, terms, act, gains, gain_m_all, spread
        )
        grad_gain_mix, grad_skip = grad_gain_mix + gated[5], grad_skip + gated[6]
        chains.append(Chain(gated[4], wide_gains[seq], True))
        chains[seq].send()
    grad_y, grad_gate, gstates, ggains = gated[:4]
    chains[0].take()
    chains[1 % seqs].take()
    grad_wgates = weight_grad(after(hidden, chains[0].state), grad_gate.reshape(rows, DI)).reshape(-1, own_rows, DI)
    blocks = grad_wo.shape[0]
    grad_rest = jnp.concatenate(
        [
            after(grad_down, chains[0].state, chains[1 % seqs].state).reshape(blocks, -1, width), grad_wout.reshape(blocks, -1, width),
            fold(grad_wo, 0), grad_wgates[..., :width], fold(grad_wgates, width),
        ],
        axis=1,
    )
    part_rest = scatter(grad_rest.reshape(-1, width))
    cos3, sin3 = cosine.reshape(seqs, span, 128), sine.reshape(seqs, span, 128)
    dqs, dkvs = [], []
    for seq in range(seqs):
        if seq < 2:
            for chain in chains:
                chain.take()
                chain.send(*dqs[-1:])
        mark = dqs[-1:] + [chain.state for chain in chains] + ([] if seq else [grad_rest])
        dq, dkv = attend_back(
            seq, bounds, after(q, grad_y, *mark), kv_all, segk,
            segq, atts[seq], grad_att, lses[seq], cos3, sin3,
        )
        dqs.append(dq)
        dkvs.append(dkv)
    dq = jnp.concatenate(dqs, axis=0)
    last, rims, grad_conv, grad_heads = None, [], 0.0, 0.0
    waits = [(grad_rest, part_gu)] + [()] * (seqs - 1)
    finals = [chain.finish() for chain in chains]
    dkv_all = exchange(after(jnp.concatenate(dkvs, axis=1), *finals))
    waits[1 % seqs] += tuple(finals)
    for seq in range(seqs):
        gstate = finals[seq]
        if seq == min(1, seqs - 1):
            gu_blocks = part_gu.reshape(count, own_rows, 2 * ff)
            parts = [after(part_rest, *rims).reshape(count, -1, width)]
            parts += [gu_blocks[..., at : at + width] for at in range(0, 2 * ff, width)]
            rest_low = jnp.concatenate(parts, axis=1).reshape(-1, width)
            waits[seq] += (rest_low,)
        last = mixer_back(
            seq, last, after(grad_y, dqs[-1], *waits[seq]), mixer_y, terms, cr, rim, act, token, states,
            gains, states_in[seq], gstates, ggains, gstate, heads, skip, taps_all, shift_all,
            spread, spread_first,
        )
        rims.append(last[1])
        grad_conv, grad_heads = grad_conv + last[2], grad_heads + last[3]
    grad_cr, grad_rim = last[0], jnp.concatenate(rims, axis=0)
    back_rim = from_behind(grad_rim[:, 8 - (KC - 1) :].astype(BF16), "ctx", -1)
    edge = grad_cr[:, span - (KC - 1) :, :CC].astype(F32) + back_rim.astype(F32)
    grad_cr = lax.dynamic_update_slice(
        grad_cr, after(edge.astype(BF16), dkv_all), (0, span - (KC - 1), 0)
    ).reshape(rows, CR)
    rest_out = lax.psum_scatter(rest_low, "ctx", scatter_dimension=0, tiled=True).astype(F32)
    grad_wcr = weight_grad(hidden, grad_cr)
    grad_wq = weight_grad(hidden, dq.reshape(rows, q_width))
    part_cr = scatter(jnp.concatenate([grad_wcr, grad_wq], axis=1))
    layer_result = (middle + low_dot(after(act_rows, part_cr), w_down_all)).astype(BF16)
    out_cr = lax.psum_scatter(part_cr, "ctx", scatter_dimension=0, tiled=True).astype(F32)
    grad_tokens, grad_kv, grad_gain_first = finish(
        tokens, gain1_all, grad_gate.reshape(rows, DI), after(grad_cr, grad_wcr, rest_out),
        dq.reshape(rows, q_width), dkv_all, cosine, sine, grad_middle, first_all,
    )
    grad_wfirst = weight_grad(hidden, grad_kv)
    grad_gain_first = grad_gain_first[0]

    devices = first_all.shape[0] // own_rows
    small_grads = jnp.concatenate(
        [
            grad_gain_first.reshape(devices, -1),
            grad_gain_second.reshape(devices, -1),
            grad_gain_mix[0].reshape(devices, -1),
            grad_conv[KC].reshape(devices, -1),
            jnp.swapaxes(grad_conv[:KC].reshape(KC, devices, -1), 0, 1).reshape(devices, -1),
        ],
        axis=1,
    )
    small_grads = jnp.pad(small_grads, ((0, 0), (0, slots - small_grads.shape[1])))
    out_first = scatter_all(
        jnp.concatenate([grad_wfirst, small_grads.reshape(-1, 128).astype(BF16)], axis=1), part_cr
    )
    rest_sizes = rest_sizes[:3] + [own_rows, half_rows] + rest_sizes[3:]
    outs, at = [], 0
    for size in rest_sizes:
        outs.append(rest_out[at : at + size])
        at += size
    out_down, out_wout = outs[0], outs[1]
    out_wo = unfold(outs[2])
    out_win = jnp.concatenate(
        [outs[3], unfold(outs[4]), out_cr[:, : w_in.shape[1] - DI]], axis=1
    )
    halves = ff // width
    out_gate = jnp.concatenate(outs[5 : 5 + halves], axis=1)
    out_up = jnp.concatenate(outs[5 + halves :], axis=1)
    out_small = out_first[:, kv_width:].reshape(-1)
    pieces, at = [], 0
    for size in small_sizes:
        pieces.append(out_small[at : at + size])
        at += size
    out_kv = out_first[:, :kv_width].reshape(own_rows, KVH, 2, HD)
    head_grad = sum_everywhere(
        jnp.concatenate(
            [grad_heads[:2, :MH], grad_skip[0].reshape(MH, MP).sum(axis=1)[None]], axis=0
        ),
        axes,
    )
    return (
        layer_result.reshape(layer_input.shape),
        grad_tokens.reshape(layer_input.shape),
        pieces[0],
        out_win,
        pieces[4].reshape(KC, -1),
        pieces[3],
        head_grad,
        pieces[2],
        out_wout,
        out_cr[:, CR:],
        out_kv[:, :, 0].reshape(own_rows, -1),
        out_kv[:, :, 1].reshape(own_rows, -1),
        out_wo.T,
        pieces[1],
        out_gate,
        out_up,
        out_down,
    )


def solution(mesh):
    in_specs = (
        P("dp", "ctx", None),
        P("dp", None),
        P("dp", "ctx"),
        P(("dp", "ctx")),
        P(("dp", "ctx"), None),
        P(None, ("dp", "ctx")),
        P(("dp", "ctx")),
        P(),
        P(("dp", "ctx")),
        P(("dp", "ctx"), None),
        P(("dp", "ctx"), None),
        P(("dp", "ctx"), None),
        P(("dp", "ctx"), None),
        P(None, ("dp", "ctx")),
        P(("dp", "ctx")),
        P(("dp", "ctx"), None),
        P(("dp", "ctx"), None),
        P(("dp", "ctx"), None),
        P("dp", "ctx", None),
    )
    out_specs = (
        P("dp", "ctx", None),
        P("dp", "ctx", None),
        P(("dp", "ctx")),
        P(("dp", "ctx"), None),
        P(None, ("dp", "ctx")),
        P(("dp", "ctx")),
        P(),
        P(("dp", "ctx")),
        P(("dp", "ctx"), None),
        P(("dp", "ctx"), None),
        P(("dp", "ctx"), None),
        P(("dp", "ctx"), None),
        P(None, ("dp", "ctx")),
        P(("dp", "ctx")),
        P(("dp", "ctx"), None),
        P(("dp", "ctx"), None),
        P(("dp", "ctx"), None),
    )
    return jax.shard_map(body, mesh=mesh, in_specs=in_specs, out_specs=out_specs, check_vma=False)
```

```python
import functools
import jax
import jax.numpy as jnp
from jax import lax
from jax.experimental import pallas as pl
from jax.experimental.pallas import tpu as pltpu
from jax.sharding import PartitionSpec as P

MH = 24
MP = 64
NS = 128
KC = 4
QH = 8
KVH = 2
HD = 64
EPSILON = 1e-05
ROPE_BASE = 10000.0
MASKED = -1e30
LOG2E = 1.4426950408889634
KEY_TILE = 256
VMEM_BYTES = 56 * 1024 * 1024

F32 = jnp.float32
BF16 = jnp.bfloat16


def contract(left, right, left_dim, right_dim):
    return lax.dot_general(
        left, right, (((left_dim,), (right_dim,)), ((), ())), preferred_element_type=F32
    )


def lanes(shape):
    return lax.broadcasted_iota(jnp.int32, shape, len(shape) - 1)


def swap_halves(values):
    lane = lanes(values.shape)
    return jnp.where(lane < 32, pltpu.roll(values, 96, 1), pltpu.roll(values, 32, 1))


CR = MH * MP + 2 * NS + 128
FIRST = CR + QH * HD + 2 * KVH * HD + 128


def project_kernel(x_ref, gain_ref, w_ref, cos_ref, sin_ref, hidden_ref, cr_ref, q_ref, kv_ref):
    x = x_ref[...].astype(F32)
    scale = lax.rsqrt(jnp.mean(x * x, axis=-1, keepdims=True) + EPSILON)
    hidden = (x * scale * gain_ref[...]).astype(BF16)
    hidden_ref[...] = hidden
    lin = contract(hidden, w_ref[:, CR : CR + QH * HD + 2 * KVH * HD], 1, 0)
    cosine, sine = cos_ref[...], sin_ref[...]
    lane = lanes(cosine.shape)
    for pair in range(QH // 2):
        both = lin[:, pair * 128 : (pair + 1) * 128]
        other = pltpu.roll(both, 64, 1)
        even = both * cosine + swap_halves(both) * sine
        odd = other * cosine + swap_halves(other) * sine
        q_ref[:, pair * 128 : (pair + 1) * 128] = jnp.where(
            lane < 64, even, pltpu.roll(odd, 64, 1)
        ).astype(BF16)
    for group in range(KVH):
        at = QH * HD + group * 128
        part = lin[:, at : at + 128]
        turned = (part * cosine + swap_halves(part) * sine).astype(BF16)
        for copy in range(kv_ref.shape[0]):
            kv_ref[copy, :, group * 128 : (group + 1) * 128] = turned
    cr_ref[...] = contract(hidden, w_ref[:, :CR], 1, 0).astype(BF16)


def project(x, gain, w_first, cosine, sine, copies):
    rows, width = x.shape
    tile = 256 if rows % 256 == 0 else 128
    block = lambda cols: pl.BlockSpec((tile, cols), lambda i: (i, 0))
    fixed = lambda array: pl.BlockSpec(array.shape, lambda i: (0, 0))
    cols = [width, CR, QH * HD]
    kv_width = 2 * KVH * HD
    return pl.pallas_call(
        project_kernel,
        grid=(rows // tile,),
        in_specs=[
            block(width), fixed(gain), fixed(w_first), block(128), block(128),
        ],
        out_specs=[block(size) for size in cols]
        + [pl.BlockSpec((copies, tile, kv_width), lambda i: (0, i, 0))],
        out_shape=[jax.ShapeDtypeStruct((rows, size), BF16) for size in cols]
        + [jax.ShapeDtypeStruct((copies, rows, kv_width), BF16)],
        compiler_params=pltpu.CompilerParams(vmem_limit_bytes=VMEM_BYTES),
        name="project",
    )(x, gain, w_first, cosine, sine)


def finish_kernel(
    x_ref, gain_ref, dgate_ref, dcr_ref, dq_ref, dkv_ref, cos_ref, sin_ref, middle_ref,
    w_ref, dx_ref, dkv_out_ref, dgain_ref, dgain_s,
):
    @pl.when(pl.program_id(0) == 0)
    def _():
        dgain_s[...] = jnp.zeros(dgain_s.shape, F32)

    dkv = dkv_ref[0, 0].astype(F32)
    for source in range(1, dkv_ref.shape[0]):
        dkv = dkv + dkv_ref[source, 0].astype(F32)
    cosine, sine = cos_ref[...], sin_ref[...]
    turned = []
    for group in range(KVH):
        part = dkv[:, group * 128 : (group + 1) * 128]
        back = part * cosine + swap_halves(part * sine)
        turned.append(jnp.where(lanes(part.shape) < HD, back, part))
    dkv = jnp.concatenate(turned, axis=1).astype(BF16)
    dkv_out_ref[...] = dkv
    at = CR + QH * HD
    grad = (
        contract(dgate_ref[...], w_ref[:, FIRST:], 1, 1)
        + contract(dcr_ref[...], w_ref[:, :CR], 1, 1)
        + contract(dq_ref[...], w_ref[:, CR:at], 1, 1)
        + contract(dkv, w_ref[:, at : at + 2 * KVH * HD], 1, 1)
    )
    x = x_ref[...].astype(F32)
    scale = lax.rsqrt(jnp.mean(x * x, axis=-1, keepdims=True) + EPSILON)
    scaled = grad * gain_ref[...]
    shrink = jnp.mean(scaled * x, axis=-1, keepdims=True) * (scale * scale * scale)
    dx_ref[...] = (middle_ref[...] + scaled * scale - x * shrink).astype(BF16)
    dgain_s[0:1, :] += jnp.sum(grad * x * scale, axis=0, keepdims=True)
    dgain_ref[...] = dgain_s[...]


def finish(x, gain, dgate, dcr, dq, dkv_all, cosine, sine, middle, w_first):
    rows, width = x.shape
    span = dkv_all.shape[2]
    tile = min(256, span)
    per_seq = span // tile
    block = lambda array: pl.BlockSpec((tile, array.shape[1]), lambda i: (i, 0))
    fixed = lambda array: pl.BlockSpec(array.shape, lambda i: (0, 0))
    keys = pl.BlockSpec(
        (dkv_all.shape[0], 1, tile, dkv_all.shape[3]), lambda i: (0, i // per_seq, i % per_seq, 0)
    )
    kv_width = dkv_all.shape[3]
    return pl.pallas_call(
        finish_kernel,
        grid=(rows // tile,),
        in_specs=[
            block(x), fixed(gain), block(dgate), block(dcr), block(dq), keys, block(cosine),
            block(sine), block(middle), fixed(w_first),
        ],
        out_specs=[
            block(x),
            pl.BlockSpec((tile, kv_width), lambda i: (i, 0)),
            pl.BlockSpec((8, width), lambda i: (0, 0)),
        ],
        out_shape=[
            jax.ShapeDtypeStruct((rows, width), BF16),
            jax.ShapeDtypeStruct((rows, kv_width), BF16),
            jax.ShapeDtypeStruct((8, width), F32),
        ],
        scratch_shapes=[pltpu.VMEM((8, width), F32)],
        compiler_params=pltpu.CompilerParams(vmem_limit_bytes=VMEM_BYTES),
        name="finish",
    )(x, gain, dgate, dcr, dq, dkv_all, cosine, sine, middle, w_first)


def visible(segk_ref, segq, query_row, at, key_rows):
    segk = segk_ref[0, pl.ds(at, key_rows), :]
    key_col = at + lax.broadcasted_iota(jnp.int32, (key_rows, 1), 0)
    return jnp.where((segk == segq) & (key_col <= query_row), 0.0, MASKED)


def attend_kernel(
    place_at, low_ref, high_ref, base_ref, q_ref, kv_ref, segk_ref, segq_ref, out_ref, lse_ref,
    q_s, m_s, l_s, acc_s,
):
    tile = pl.program_id(0)
    rows = q_ref.shape[1]
    place = place_at + tile
    lane = lanes((rows, 128))
    for pair in range(QH // 2):
        both = q_ref[0, :, pair * 128 : (pair + 1) * 128].astype(F32)
        q_s[2 * pair] = jnp.where(lane < 64, both, 0.0).astype(BF16)
        q_s[2 * pair + 1] = jnp.where(lane < 64, pltpu.roll(both, 64, 1), 0.0).astype(BF16)
    key_rows = min(KEY_TILE, kv_ref.shape[2])
    tiles_each = kv_ref.shape[2] // key_rows
    m_s[...] = jnp.full(m_s.shape, MASKED, F32)
    l_s[...] = jnp.zeros(l_s.shape, F32)
    acc_s[...] = jnp.zeros(acc_s.shape, F32)
    query_row = base_ref[0] + tile * rows + lanes((1, rows))
    segq = segq_ref[0]
    factor = HD ** (-0.5) * LOG2E

    def step(key_tile, carry):
        at = pl.multiple_of(key_tile * key_rows, key_rows)
        source = key_tile // tiles_each
        offset = pl.multiple_of((key_tile % tiles_each) * key_rows, key_rows)
        bias = visible(segk_ref, segq, query_row, at, key_rows)
        for group in range(KVH):
            kv = kv_ref[source, 0, pl.ds(offset, key_rows), group * 128 : (group + 1) * 128]
            kv_t = kv.astype(F32).T.astype(BF16)
            members = range(group * (QH // KVH), (group + 1) * (QH // KVH))
            scores = [contract(kv, q_s[head], 1, 1) * factor + bias for head in members]
            before = [m_s[head : head + 1, :] for head in members]
            tops = [
                jnp.maximum(old, jnp.max(part, axis=0, keepdims=True))
                for old, part in zip(before, scores)
            ]
            weights = [jnp.exp2(part - top) for part, top in zip(scores, tops)]
            sums = [jnp.sum(part, axis=0, keepdims=True) for part in weights]
            outs = [contract(kv_t, part.astype(BF16), 1, 0) for part in weights]
            for at_head, head in enumerate(members):
                fade = jnp.exp2(before[at_head] - tops[at_head])
                l_s[head : head + 1, :] = l_s[head : head + 1, :] * fade + sums[at_head]
                acc_s[head] = acc_s[head] * fade + outs[at_head]
                m_s[head : head + 1, :] = tops[at_head]
        return carry

    lax.fori_loop(low_ref[place], high_ref[place], step, 0)
    lse_ref[0] = m_s[...] + jnp.log2(l_s[...])
    for pair in range(QH // 2):
        even = (acc_s[2 * pair] / l_s[2 * pair : 2 * pair + 1, :]).T
        odd = (acc_s[2 * pair + 1] / l_s[2 * pair + 1 : 2 * pair + 2, :]).T
        out_ref[0, :, pair * 128 : (pair + 1) * 128] = jnp.where(
            lane < 64, pltpu.roll(even, 64, 1), odd
        ).astype(BF16)


def attend_back_kernel(
    place_at, low_ref, high_ref, base_ref, q_ref, kv_ref, segk_ref, segq_ref, att_ref, gatt_ref, lse_ref,
    cos_ref, sin_ref, dq_ref, dkv_ref,
    q_s, g_s, delta_s, dq_s, dkv_s,
):
    tile = pl.program_id(0)
    rows = q_ref.shape[1]
    place = place_at + tile
    lane = lanes((rows, 128))

    @pl.when(tile == 0)
    def _():
        dkv_s[...] = jnp.zeros(dkv_s.shape, F32)

    for pair in range(QH // 2):
        cols = slice(pair * 128, (pair + 1) * 128)
        both = q_ref[0, :, cols].astype(F32)
        q_s[2 * pair] = jnp.where(lane < 64, both, 0.0).astype(BF16)
        q_s[2 * pair + 1] = jnp.where(lane < 64, pltpu.roll(both, 64, 1), 0.0).astype(BF16)
        grad = gatt_ref[0, :, cols].astype(F32)
        g_s[2 * pair] = jnp.where(lane >= 64, pltpu.roll(grad, 64, 1), 0.0).astype(BF16)
        g_s[2 * pair + 1] = jnp.where(lane >= 64, grad, 0.0).astype(BF16)
        product = (grad * att_ref[0, :, cols].astype(F32)).T
        delta_s[2 * pair : 2 * pair + 1, :] = jnp.sum(product[:64], axis=0, keepdims=True)
        delta_s[2 * pair + 1 : 2 * pair + 2, :] = jnp.sum(product[64:], axis=0, keepdims=True)
    key_rows = min(KEY_TILE, kv_ref.shape[2])
    tiles_each = kv_ref.shape[2] // key_rows
    dq_s[...] = jnp.zeros(dq_s.shape, F32)
    query_row = base_ref[0] + tile * rows + lanes((1, rows))
    segq = segq_ref[0]
    qk_scale = HD ** (-0.5)
    factor = qk_scale * LOG2E

    def step(key_tile, carry):
        at = pl.multiple_of(key_tile * key_rows, key_rows)
        source = key_tile // tiles_each
        offset = pl.multiple_of((key_tile % tiles_each) * key_rows, key_rows)
        bias = visible(segk_ref, segq, query_row, at, key_rows)
        for group in range(KVH):
            kv = kv_ref[source, 0, pl.ds(offset, key_rows), group * 128 : (group + 1) * 128]
            kv_t = kv.astype(F32).T.astype(BF16)
            total = jnp.zeros((key_rows, 128), F32)
            for member in range(QH // KVH):
                head = group * (QH // KVH) + member
                q, g = q_s[head], g_s[head]
                scores = contract(kv, q, 1, 1) * factor + bias
                probs = jnp.exp2(scores - lse_ref[0, head : head + 1, :])
                d_probs = contract(kv, g, 1, 1)
                d_scores = (probs * (d_probs - delta_s[head : head + 1, :]) * qk_scale).astype(BF16)
                total = total + contract(d_scores, q, 1, 0) + contract(probs.astype(BF16), g, 1, 0)
                dq_s[head] += contract(kv_t, d_scores, 1, 0)
            cols = slice(group * 128, (group + 1) * 128)
            dkv_s[source, 0, pl.ds(offset, key_rows), cols] += total
        return carry

    lax.fori_loop(low_ref[place], high_ref[place], step, 0)
    cosine, sine = cos_ref[0], sin_ref[0]
    for pair in range(QH // 2):
        even, odd = dq_s[2 * pair].T, dq_s[2 * pair + 1].T
        even = even * cosine + swap_halves(even * sine)
        odd = odd * cosine + swap_halves(odd * sine)
        dq_ref[0, :, pair * 128 : (pair + 1) * 128] = jnp.where(
            lane < 64, even, pltpu.roll(odd, 64, 1)
        ).astype(BF16)

    @pl.when(tile == pl.num_programs(0) - 1)
    def _():
        dkv_ref[...] = dkv_s[...].astype(BF16)


def attention_specs(seq, length, rows):
    tile = lambda cols, at=seq: pl.BlockSpec((1, rows, cols), lambda t, *_: (at, t, 0))
    whole = lambda cols, at=seq: pl.BlockSpec((1, length, cols), lambda t, *_: (at, 0, 0))
    keys = lambda array, at=seq: pl.BlockSpec(
        (array.shape[0], 1) + array.shape[2:], lambda t, *_: (0, at, 0, 0)
    )
    row = lambda n, at=seq: pl.BlockSpec((1, n, rows), lambda t, *_: (at, 0, t))
    return tile, whole, keys, row


def attend(seq, bounds, q, kv_all, segk, segq):
    _, span, q_width = q.shape
    rows = min(256, span)
    tile, whole, keys, row = attention_specs(seq, segk.shape[1], rows)
    own_keys = kv_all.shape[:1] + (1,) + kv_all.shape[2:]
    return pl.pallas_call(
        functools.partial(attend_kernel, seq * (span // rows)),
        grid_spec=pltpu.PrefetchScalarGridSpec(
            num_scalar_prefetch=3,
            grid=(span // rows,),
            in_specs=[tile(q_width), keys(kv_all), whole(1), row(1)],
            out_specs=[tile(q_width, 0), row(QH, 0)],
            scratch_shapes=[
                pltpu.VMEM((QH, rows, 128), BF16),
                pltpu.VMEM((QH, rows), F32),
                pltpu.VMEM((QH, rows), F32),
                pltpu.VMEM((QH, 128, rows), F32),
            ],
        ),
        out_shape=[
            jax.ShapeDtypeStruct((1, span, q_width), BF16),
            jax.ShapeDtypeStruct((1, QH, span), F32),
        ],
        compiler_params=pltpu.CompilerParams(vmem_limit_bytes=VMEM_BYTES),
        name="attend",
    )(*bounds, q, kv_all, segk, segq)


def attend_back(seq, bounds, q, kv_all, segk, segq, att, grad_att, lse, cosine, sine):
    _, span, q_width = q.shape
    rows = min(256, span)
    tile, whole, keys, row = attention_specs(seq, segk.shape[1], rows)
    own_keys = kv_all.shape[:1] + (1,) + kv_all.shape[2:]
    return pl.pallas_call(
        functools.partial(attend_back_kernel, seq * (span // rows)),
        grid_spec=pltpu.PrefetchScalarGridSpec(
            num_scalar_prefetch=3,
            grid=(span // rows,),
            in_specs=[
                tile(q_width), keys(kv_all), whole(1), row(1), tile(q_width, 0), tile(q_width),
                row(QH, 0), tile(128), tile(128),
            ],
            out_specs=[tile(q_width, 0), keys(kv_all, 0)],
            scratch_shapes=[
                pltpu.VMEM((QH, rows, 128), BF16),
                pltpu.VMEM((QH, rows, 128), BF16),
                pltpu.VMEM((QH, rows), F32),
                pltpu.VMEM((QH, 128, rows), F32),
                pltpu.VMEM(own_keys, F32),
            ],
        ),
        out_shape=[
            jax.ShapeDtypeStruct((1, span, q_width), BF16),
            jax.ShapeDtypeStruct(own_keys, BF16),
        ],
        compiler_params=pltpu.CompilerParams(vmem_limit_bytes=VMEM_BYTES),
        name="attend_back",
    )(*bounds, q, kv_all, segk, segq, att, grad_att, lse, cosine, sine)


def rope_tables(positions):
    half = HD // 2
    frequency = ROPE_BASE ** (-jnp.arange(half, dtype=F32) / half)
    angles = positions.astype(F32)[..., None] * frequency
    cosine, sine = jnp.cos(angles), jnp.sin(angles)
    one, zero = jnp.ones(cosine.shape[:-1] + (HD,), F32), jnp.zeros(cosine.shape[:-1] + (HD,), F32)
    return (
        jnp.concatenate([cosine, cosine, one], axis=-1),
        jnp.concatenate([-sine, sine, zero], axis=-1),
    )


def attention_bounds(segments, seg_own, span_start):
    seqs, span = seg_own.shape
    rows, key_rows = min(256, span), min(KEY_TILE, span)
    first = seg_own[:, ::rows]
    begin = jnp.sum((segments[:, None, :] < first[:, :, None]).astype(jnp.int32), axis=2)
    tiles = jnp.arange(span // rows, dtype=jnp.int32)
    high = (span_start + (tiles + 1) * rows + key_rows - 1) // key_rows
    high = jnp.broadcast_to(high[None], first.shape)
    return (
        (begin // key_rows).reshape(-1),
        high.reshape(-1).astype(jnp.int32),
        jnp.full((1,), span_start, jnp.int32),
    )


CHUNK = 128
DI = MH * MP
CC = DI + 2 * NS
TAP_LANES, PREV_LANE, LAST_LANE, SEG_LANE = 0, 4, 5, 6


def split_three(values):
    high = values.astype(BF16)
    rest = values - high.astype(F32)
    middle = rest.astype(BF16)
    return high, middle, (rest - middle.astype(F32)).astype(BF16)


def product_exact(matrix, values):
    return sum(contract(matrix, part, 1, 0) for part in split_three(values))


def widen(values, spread):
    kept = jnp.where(lanes(values.shape) < 32, values, 0.0)
    high, middle, rest = (part.astype(F32) for part in split_three(kept))
    packed = high + pltpu.roll(middle, 32, 1) + pltpu.roll(rest, 64, 1)
    return contract(packed.astype(BF16), spread, 1, 0)


def gather_heads(values, spread_first):
    high = values.astype(BF16)
    rest = (values - high.astype(F32)).astype(BF16)
    return contract(high, spread_first, 1, 1) + contract(rest, spread_first, 1, 1)


def spread_matrix():
    row = lax.broadcasted_iota(jnp.int32, (128, DI), 0)
    col = lax.broadcasted_iota(jnp.int32, (128, DI), 1)
    return ((row % 32 == col // MP) & (row < 96)).astype(BF16)


def spread_first_matrix():
    row = lax.broadcasted_iota(jnp.int32, (32, DI), 0)
    col = lax.broadcasted_iota(jnp.int32, (32, DI), 1)
    return (row == col // MP).astype(BF16)


def lower_mask():
    row = lax.broadcasted_iota(jnp.int32, (CHUNK, CHUNK), 0)
    return row >= lanes((CHUNK, CHUNK))


def saved_terms(terms_ref):
    return [terms_ref[0, :, at * 128 : (at + 1) * 128] for at in range(6)]


def token_rows(token_ref):
    return jnp.concatenate([token_ref[0]] * 16, axis=0).T


def decay_rows(rate, head_ref, token):
    raw = rate.astype(F32) + head_ref[1:2, :]
    step = jnp.maximum(raw, 0.0) + jnp.log1p(jnp.exp(-jnp.abs(raw)))
    log_decay = -step * jnp.exp(head_ref[0:1, :])
    running = product_exact(lower_mask().astype(BF16), log_decay)
    last = running[CHUNK - 1 :, :]
    weight_end = jnp.exp(last - running) * step * token[:, LAST_LANE : LAST_LANE + 1]
    entry = jnp.exp(running) * token[:, PREV_LANE : PREV_LANE + 1]
    gain = jnp.exp(last) * token[CHUNK - 1 :, PREV_LANE : PREV_LANE + 1]
    return raw, step, log_decay, running, weight_end, entry, gain


def conv_total(ext_s, token, taps_ref, shift_ref):
    total = shift_ref[...] + ext_s[8 : 8 + CHUNK, :] * taps_ref[KC - 1 : KC, :]
    for tap in range(KC - 1):
        total = total + ext_s[5 + tap : 5 + tap + CHUNK, :] * (
            taps_ref[tap : tap + 1, :] * token[:, TAP_LANES + tap : TAP_LANES + tap + 1]
        )
    return total


def mixer_scan_kernel(
    cr_ref, rim_ref, token_ref, head_ref, taps_ref, shift_ref, spread_ref,
    act_ref, states_ref, gains_ref, final_ref, final_gain_ref, terms_ref,
    ext_s, state_s, gain_s,
):
    chunk = pl.program_id(0)

    @pl.when(chunk == 0)
    def _():
        ext_s[0:8, :] = rim_ref[0].astype(F32)
        state_s[...] = jnp.zeros(state_s.shape, F32)
        gain_s[...] = jnp.ones(gain_s.shape, F32)

    @pl.when(chunk > 0)
    def _():
        ext_s[0:8, :] = ext_s[CHUNK : CHUNK + 8, :]

    token = token_rows(token_ref)
    ext_s[8 : 8 + CHUNK, :] = cr_ref[0, :, :CC].astype(F32)
    total = conv_total(ext_s, token, taps_ref, shift_ref)
    act = (total * jax.nn.sigmoid(total)).astype(BF16)
    act_ref[0] = act
    raw, step, log_decay, running, weight_end, entry, gain = decay_rows(
        cr_ref[0, :, CC:], head_ref, token
    )
    for at, term in enumerate((raw, step, log_decay, running, weight_end, entry)):
        terms_ref[0, :, at * 128 : (at + 1) * 128] = term
    states_ref[0, 0] = state_s[...].astype(BF16)
    before = gain_s[...]
    row = lax.broadcasted_iota(jnp.int32, before.shape, 0)
    gains_ref[0, 0] = jnp.where(row == 1, jnp.broadcast_to(gain, before.shape), before)
    spread = spread_ref[...]
    scaled = (act[:, :DI].astype(F32) * widen(weight_end, spread)).astype(BF16)
    gain_rows = jnp.broadcast_to(gain, (8, 128))
    state = state_s[...] * widen(gain_rows, spread)[0:1, :] + contract(
        act[:, DI : DI + NS], scaled, 0, 0
    )
    state_s[...] = state
    gain_s[...] = before * gain_rows

    @pl.when(chunk == pl.num_programs(0) - 1)
    def _():
        final_ref[0] = state.astype(BF16)
        final_gain_ref[0] = widen(before * gain_rows, spread)


def entering_state(local_ref, gains_ref, state_ref, spread):
    factor = widen(gains_ref[0, 0], spread)[0:1, :]
    return (local_ref[0, 0].astype(F32) + factor * state_ref[0].astype(F32)).astype(BF16)


def pair_decay(running, rest_t, bias, head):
    parts = []
    for at in (head, head + 1):
        column = jnp.broadcast_to(running[:, at : at + 1], (CHUNK, CHUNK))
        parts.append(jnp.exp2(column + (rest_t[at : at + 1, :] + bias)))
    return parts


def stack_pair(values):
    lane = lanes(values.shape)
    wide = values.astype(F32)
    return jnp.concatenate(
        [jnp.where(lane < 64, wide, 0.0), jnp.where(lane >= 64, wide, 0.0)], axis=0
    ).astype(BF16)


def inside_terms(running, step, token):
    seg = jnp.broadcast_to(token[:, SEG_LANE : SEG_LANE + 1], (CHUNK, CHUNK))
    bias = jnp.where((seg == seg.T) & lower_mask(), 0.0, MASKED)
    running_two = running * LOG2E
    rest_t = (jnp.log2(step) - running_two).T
    return running_two, rest_t, bias


def mixer_out_kernel(
    gate_ref, terms_ref, act_ref, token_ref, states_ref, gains_ref, state_ref, skip_ref, gain_ref,
    spread_ref, y_ref, out_ref,
):
    token, spread = token_rows(token_ref), spread_ref[...]
    _, step, _, running, _, entry = saved_terms(terms_ref)
    b_rows, c_rows = act_ref[0, :, DI : DI + NS], act_ref[0, :, DI + NS :]
    state = entering_state(states_ref, gains_ref, state_ref, spread)
    carried = contract(c_rows, state, 1, 0) * widen(entry, spread)
    cross = contract(c_rows, b_rows, 1, 1)
    running_two, rest_t, bias = inside_terms(running, step, token)
    square = jnp.zeros((CHUNK, 128), F32)
    for pair in range(MH // 2):
        cols = slice(pair * 128, (pair + 1) * 128)
        xs = act_ref[0, :, cols]
        mix = jnp.concatenate(
            [
                (cross * part).astype(BF16)
                for part in pair_decay(running_two, rest_t, bias, 2 * pair)
            ],
            axis=1,
        )
        y = (
            contract(mix, stack_pair(xs), 1, 0)
            + carried[:, cols]
            + skip_ref[:, cols] * xs.astype(F32)
        )
        y_ref[0, :, cols] = y
        gate = gate_ref[0, :, cols].astype(F32)
        gated = y * (gate * jax.nn.sigmoid(gate))
        square = square + gated * gated
    scale = lax.rsqrt(jnp.sum(square, axis=1, keepdims=True) * (1.0 / DI) + EPSILON)
    for pair in range(MH // 2):
        cols = slice(pair * 128, (pair + 1) * 128)
        gate = gate_ref[0, :, cols].astype(F32)
        gated = y_ref[0, :, cols] * (gate * jax.nn.sigmoid(gate))
        out_ref[0, :, cols] = (gated * scale * gain_ref[:, cols]).astype(BF16)


def mixer_gate_back_kernel(
    gmix_ref, y_ref, gate_ref, terms_ref, act_ref, fgains_ref, gain_ref, spread_ref,
    gy_ref, dgate_ref, gstates_ref, gains_ref, final_ref, dgain_ref, dskip_ref,
    state_s, gain_s, dgain_s, dskip_s,
):
    chunk = pl.program_id(0)

    @pl.when(chunk == 0)
    def _():
        dgain_s[...] = jnp.zeros(dgain_s.shape, F32)
        dskip_s[...] = jnp.zeros(dskip_s.shape, F32)

    @pl.when(chunk == 0)
    def _():
        state_s[...] = jnp.zeros(state_s.shape, F32)
        gain_s[...] = jnp.ones(gain_s.shape, F32)

    spread = spread_ref[...]
    entry, gain = saved_terms(terms_ref)[-1], fgains_ref[0, 0, 1:2, :]
    y = y_ref[0]
    gate = gate_ref[0].astype(F32)
    sig = jax.nn.sigmoid(gate)
    swish = gate * sig
    gated = y * swish
    scale = lax.rsqrt(jnp.mean(gated * gated, axis=1, keepdims=True) + EPSILON)
    grad = gmix_ref[0].astype(F32)
    scaled = grad * gain_ref[...]
    shrink = jnp.mean(scaled * gated, axis=1, keepdims=True) * (scale * scale * scale)
    d_gated = scaled * scale - gated * shrink
    gy = (d_gated * swish).astype(BF16)
    gy_ref[0] = gy
    dgate_ref[0] = (d_gated * y * (sig * (1.0 + gate * (1.0 - sig)))).astype(BF16)
    dgain_s[0:1, :] += jnp.sum(grad * gated * scale, axis=0, keepdims=True)
    gy_float = gy.astype(F32)
    dskip_s[0:1, :] += jnp.sum(gy_float * act_ref[0, :, :DI].astype(F32), axis=0, keepdims=True)
    gstates_ref[0, 0] = state_s[...].astype(BF16)
    after = gain_s[...]
    gains_ref[0, 0] = after
    gain_rows = jnp.broadcast_to(gain, (8, 128))
    carried = (gy_float * widen(entry, spread)).astype(BF16)
    state = state_s[...] * widen(gain_rows, spread)[0:1, :] + contract(
        act_ref[0, :, DI + NS :], carried, 0, 0
    )
    state_s[...] = state
    gain_s[...] = after * gain_rows

    @pl.when(chunk == pl.num_programs(0) - 1)
    def _():
        final_ref[0] = state.astype(BF16)

    dgain_ref[...] = dgain_s[...]
    dskip_ref[...] = dskip_s[...]


def mixer_back_kernel(
    gy_ref, y_ref, terms_ref, cr_ref, halo_ref, rim_ref, act_ref, token_ref,
    states_ref, gains_ref, state_ref, gstates_ref, ggains_ref, gstate_ref,
    head_ref, skip_ref, taps_ref, shift_ref, spread_ref, spread_first_ref,
    dcr_ref, drim_ref, dconv_ref, dhead_ref,
    ext_s, grad_s, carry_s, dconv_s, dhead_s,
):
    step_index = pl.program_id(0)
    last_step = pl.num_programs(0) - 1

    @pl.when(step_index == 0)
    def _():
        dconv_s[...] = jnp.zeros(dconv_s.shape, F32)
        dhead_s[...] = jnp.zeros(dhead_s.shape, F32)

    @pl.when(step_index == 0)
    def _():
        carry_s[...] = jnp.zeros(carry_s.shape, F32)

    @pl.when(step_index == last_step)
    def _():
        ext_s[0:8, :] = rim_ref[0].astype(F32)

    @pl.when(step_index < last_step)
    def _():
        ext_s[0:8, :] = halo_ref[0, :, :CC].astype(F32)[8:16]

    ext_s[8 : 8 + CHUNK, :] = cr_ref[0, :, :CC].astype(F32)
    token, spread, spread_first = token_rows(token_ref), spread_ref[...], spread_first_ref[...]
    raw, step, log_decay, running, weight_end, entry = saved_terms(terms_ref)
    gain = gains_ref[0, 0, 1:2, :]
    b_rows, c_rows = act_ref[0, :, DI : DI + NS], act_ref[0, :, DI + NS :]
    state = entering_state(states_ref, gains_ref, state_ref, spread)
    gstate = entering_state(gstates_ref, ggains_ref, gstate_ref, spread)
    wide_end = widen(weight_end, spread)
    gy = gy_ref[0]
    gy_float = gy.astype(F32)
    gcarried = (gy_float * widen(entry, spread)).astype(BF16)
    xs_float = act_ref[0, :, :DI].astype(F32)
    grad_c = contract(gcarried, state, 1, 1)
    grad_b = contract((xs_float * wide_end).astype(BF16), gstate, 1, 1)
    from_end = contract(b_rows, gstate, 1, 0) * wide_end
    dgain_row = jnp.sum(gstate.astype(F32) * state.astype(F32), axis=0, keepdims=True)
    cross = contract(c_rows, b_rows, 1, 1)
    running_two, rest_t, bias = inside_terms(running, step, token)
    grad_cross = jnp.zeros((CHUNK, CHUNK), F32)
    lane = lanes((CHUNK, 128))
    for pair in range(MH // 2):
        cols = slice(pair * 128, (pair + 1) * 128)
        stacked = stack_pair(act_ref[0, :, cols])
        gy_pair = gy_ref[0, :, cols]
        first, second = pair_decay(running_two, rest_t, bias, 2 * pair)
        mix = jnp.concatenate([(cross * first).astype(BF16), (cross * second).astype(BF16)], axis=1)
        grad_mix = contract(gy_pair, stacked, 1, 1)
        grad_cross = grad_cross + grad_mix[:, :CHUNK] * first + grad_mix[:, CHUNK:] * second
        both = contract(mix, gy_pair, 0, 0)
        grad_s[8 : 8 + CHUNK, cols] = jnp.where(lane < 64, both[:CHUNK], both[CHUNK:])
    inner = grad_s[8 : 8 + CHUNK, :DI]
    skip = skip_ref[...]
    cross_low = grad_cross.astype(BF16)
    grad_c = grad_c + contract(cross_low, b_rows, 1, 0)
    grad_b = grad_b + contract(cross_low, c_rows, 0, 0)
    narrow = lambda values: jnp.concatenate(
        [gather_heads(values, spread_first), jnp.zeros((values.shape[0], 96), F32)], axis=1
    )
    query_part = narrow(gy_float * (y_ref[0] - skip * xs_float))
    key_inner = narrow(xs_float * inner)
    key_end = narrow(xs_float * from_end)
    extra = jnp.sum(key_end, axis=0, keepdims=True) + gain * narrow(
        jnp.broadcast_to(dgain_row, (8, DI))
    )[0:1, :]
    upper = (~lower_mask() | (lax.broadcasted_iota(jnp.int32, (CHUNK, CHUNK), 0) == lanes((CHUNK, CHUNK))))
    grad_log = product_exact(upper.astype(BF16), query_part - key_inner - key_end) + extra
    sig = jax.nn.sigmoid(raw)
    ratio = jnp.where(raw < -15.0, 1.0, sig / jnp.maximum(step, 1e-30))
    grad_rate = (key_inner + key_end) * ratio - grad_log * jnp.exp(head_ref[0:1, :]) * sig
    dhead_s[0:1, :] += jnp.sum(grad_log * log_decay, axis=0, keepdims=True)
    dhead_s[1:2, :] += jnp.sum(grad_rate, axis=0, keepdims=True)
    total = conv_total(ext_s, token, taps_ref, shift_ref)
    grad_act = jnp.concatenate([inner + from_end + skip * gy_float, grad_b, grad_c], axis=1)
    csig = jax.nn.sigmoid(total)
    grad_total = grad_act * (csig * (1.0 + total * (1.0 - csig)))
    dconv_s[KC : KC + 1, :] += jnp.sum(grad_total, axis=0, keepdims=True)
    grad_s[0:8, :] = jnp.zeros((8, CC), F32)
    grad_s[8 : 8 + CHUNK, :] = grad_total * taps_ref[KC - 1 : KC, :]
    dconv_s[KC - 1 : KC, :] += jnp.sum(grad_total * ext_s[8 : 8 + CHUNK, :], axis=0, keepdims=True)
    for tap in range(KC - 1):
        part = grad_total * token[:, TAP_LANES + tap : TAP_LANES + tap + 1]
        dconv_s[tap : tap + 1, :] += jnp.sum(
            part * ext_s[5 + tap : 5 + tap + CHUNK, :], axis=0, keepdims=True
        )
        grad_s[5 + tap : 5 + tap + CHUNK, :] += part * taps_ref[tap : tap + 1, :]
    grad_s[CHUNK : CHUNK + 8, :] += carry_s[...]
    carry_s[...] = grad_s[0:8, :]
    dcr_ref[0, :, :CC] = grad_s[8 : 8 + CHUNK, :].astype(BF16)
    dcr_ref[0, :, CC:] = grad_rate.astype(BF16)

    @pl.when(step_index == last_step)
    def _():
        drim_ref[0] = carry_s[...]

    dconv_ref[...] = dconv_s[...]
    dhead_ref[...] = dhead_s[...]


def mixer_call(kernel, name, seq, chunks, reverse, inputs, outputs, scratch, earlier):
    place = (lambda c: chunks - 1 - c) if reverse else (lambda c: c)
    kinds = {
        "block": lambda array, at: pl.BlockSpec(
            (1, CHUNK, array.shape[2]), lambda c: (at, place(c), 0)
        ),
        "chunk": lambda array, at: pl.BlockSpec(
            (1, 1) + array.shape[2:], lambda c: (at, place(c), 0, 0)
        ),
        "token": lambda array, at: pl.BlockSpec((1, 8, CHUNK), lambda c: (at, 0, place(c))),
        "seq": lambda array, at: pl.BlockSpec((1,) + array.shape[1:], lambda c: (at, 0, 0)),
        "own": lambda array, at: pl.BlockSpec((1,) + array.shape[1:], lambda c: (0, 0, 0)),
        "fixed": lambda array, at: pl.BlockSpec(array.shape, lambda c: (0, 0)),
        "halo": lambda array, at: pl.BlockSpec(
            (1, 16, array.shape[2]),
            lambda c: (at, jnp.maximum(place(c) * (CHUNK // 16) - 1, 0), 0),
        ),
    }
    arrays = [array for _, array in inputs]
    in_specs = [kinds[kind](array, seq) for kind, array in inputs]
    out_specs = [kinds[kind](shape, seq) for kind, shape in outputs]
    count = len(inputs)
    aliases, kept = {}, 0
    if earlier is not None:
        shared = [i for i, (kind, _) in enumerate(outputs) if kind in ("block", "chunk")]
        aliases = {count + i: out for i, out in enumerate(shared)}
        arrays += [earlier[out] for out in shared]
        in_specs += [pl.BlockSpec(memory_space=pl.ANY)] * len(shared)
        kept = len(shared)

    def run(*refs):
        kernel(*refs[:count], *refs[count + kept :])

    return pl.pallas_call(
        run,
        grid=(chunks,),
        in_specs=in_specs,
        out_specs=out_specs,
        out_shape=[shape for _, shape in outputs],
        scratch_shapes=[pltpu.VMEM(shape, F32) for shape in scratch],
        input_output_aliases=aliases,
        compiler_params=pltpu.CompilerParams(vmem_limit_bytes=VMEM_BYTES),
        name=name,
    )(*arrays)


def mixer_scan(seq, earlier, cr, rim, token, heads, taps, shift, spread):
    seqs, span, _ = cr.shape
    chunks = span // CHUNK
    return mixer_call(
        mixer_scan_kernel, "mixer_scan", seq, chunks, False,
        [
            ("block", cr), ("seq", rim), ("token", token), ("fixed", heads), ("fixed", taps),
            ("fixed", shift), ("fixed", spread),
        ],
        [
            ("block", jax.ShapeDtypeStruct((seqs, span, CC), BF16)),
            ("chunk", jax.ShapeDtypeStruct((seqs, chunks, NS, DI), BF16)),
            ("chunk", jax.ShapeDtypeStruct((seqs, chunks, 8, 128), F32)),
            ("own", jax.ShapeDtypeStruct((1, NS, DI), BF16)),
            ("own", jax.ShapeDtypeStruct((1, 8, DI), F32)),
            ("block", jax.ShapeDtypeStruct((seqs, span, 6 * 128), F32)),
        ],
        [(CHUNK + 8, CC), (NS, DI), (8, 128)],
        earlier,
    )


def mixer_out(seq, earlier, gate, terms, act, token, states, gains, state, skip, gain, spread):
    seqs, span, _ = gate.shape
    return mixer_call(
        mixer_out_kernel, "mixer_out", seq, span // CHUNK, False,
        [
            ("block", gate), ("block", terms), ("block", act), ("token", token), ("chunk", states),
            ("chunk", gains), ("own", state), ("fixed", skip),
            ("fixed", gain), ("fixed", spread),
        ],
        [
            ("block", jax.ShapeDtypeStruct((seqs, span, DI), F32)),
            ("block", jax.ShapeDtypeStruct((seqs, span, DI), BF16)),
        ],
        [],
        earlier,
    )


def mixer_gate_back(
    seq, earlier, gmix, y, gate, terms, act, gains, gain, spread
):
    seqs, span, _ = gate.shape
    chunks = span // CHUNK
    return mixer_call(
        mixer_gate_back_kernel, "mixer_gate_back", seq, chunks, True,
        [
            ("block", gmix), ("block", y), ("block", gate), ("block", terms), ("block", act), ("chunk", gains),
            ("fixed", gain), ("fixed", spread),
        ],
        [
            ("block", jax.ShapeDtypeStruct((seqs, span, DI), BF16)),
            ("block", jax.ShapeDtypeStruct((seqs, span, DI), BF16)),
            ("chunk", jax.ShapeDtypeStruct((seqs, chunks, NS, DI), BF16)),
            ("chunk", jax.ShapeDtypeStruct((seqs, chunks, 8, 128), F32)),
            ("own", jax.ShapeDtypeStruct((1, NS, DI), BF16)),
            ("fixed", jax.ShapeDtypeStruct((8, DI), F32)),
            ("fixed", jax.ShapeDtypeStruct((8, DI), F32)),
        ],
        [(NS, DI), (8, 128), (8, DI), (8, DI)],
        earlier,
    )


def mixer_back(
    seq, earlier, gy, y, terms, cr, rim, act, token, states, gains, state, gstates, ggains,
    gstate, heads, skip, taps, shift, spread, spread_first,
):
    seqs, span, width = cr.shape
    return mixer_call(
        mixer_back_kernel, "mixer_back", seq, span // CHUNK, True,
        [
            ("block", gy), ("block", y), ("block", terms), ("block", cr), ("halo", cr),
            ("seq", rim), ("block", act), ("token", token), ("chunk", states), ("chunk", gains),
            ("own", state), ("chunk", gstates), ("chunk", ggains), ("own", gstate),
            ("fixed", heads), ("fixed", skip), ("fixed", taps), ("fixed", shift),
            ("fixed", spread), ("fixed", spread_first),
        ],
        [
            ("block", jax.ShapeDtypeStruct((seqs, span, width), BF16)),
            ("own", jax.ShapeDtypeStruct((1, 8, CC), F32)),
            ("fixed", jax.ShapeDtypeStruct((8, CC), F32)),
            ("fixed", jax.ShapeDtypeStruct((8, 128), F32)),
        ],
        [(CHUNK + 8, CC), (CHUNK + 8, CC), (8, CC), (8, CC), (8, 128)],
        earlier,
    )


def token_table(seg_own, seg_rim):
    seqs, span = seg_own.shape
    extended = jnp.concatenate([seg_rim, seg_own], axis=1)
    matches = [extended[:, tap : tap + span] == seg_own for tap in range(KC - 1)]
    by_chunk = seg_own.reshape(seqs, -1, CHUNK)
    last = by_chunk[:, :, -1:]
    before = jnp.concatenate([seg_rim[:, None, -1:], last[:, :-1]], axis=1)
    spare = jnp.zeros((seqs, span), F32)
    rows = [match.astype(F32) for match in matches] + [
        spare,
        (by_chunk == before).reshape(seqs, span).astype(F32),
        (by_chunk == last).reshape(seqs, span).astype(F32),
        seg_own.astype(F32),
        spare,
    ]
    return jnp.stack(rows, axis=1)


def from_behind(block, axis, distance):
    devices = range(lax.axis_size(axis))
    route = [(i - distance, i) for i in devices if i - distance in devices]
    return lax.ppermute(block, axis, route)


def after(value, *earlier):
    return lax.optimization_barrier((value, earlier))[0]


class Chain:
    def __init__(self, local, gain, reverse):
        self.local, self.gain, self.reverse = local, gain, reverse
        self.state, self.hop, self.flying = jnp.zeros(local.shape, BF16), 0, None
        self.count, self.place = lax.axis_size("ctx"), lax.axis_index("ctx")

    def send(self, *earlier):
        if self.hop == self.count - 1:
            return
        source = self.count - 1 - self.hop if self.reverse else self.hop
        target = source - 1 if self.reverse else source + 1
        sent = self.local
        if self.hop:
            sent = (self.gain * self.state.astype(F32) + sent.astype(F32)).astype(BF16)
        if earlier:
            sent = after(sent, *earlier)
        self.flying = (lax.ppermute(sent, "ctx", [(source, target)]), target)
        self.hop += 1

    def take(self):
        if self.flying is None:
            return
        received, target = self.flying
        self.state, self.flying = jnp.where(self.place == target, received, self.state), None

    def finish(self):
        self.take()
        while self.hop < self.count - 1:
            self.send()
            self.take()
        return self.state


def sum_everywhere(values, axes):
    for axis in axes:
        count = lax.axis_size(axis)
        copies = jnp.broadcast_to(values[None], (count,) + values.shape)
        values = jnp.sum(lax.all_to_all(copies, axis, 0, 0, tiled=True), axis=0)
    return values


def scatter_all(grad, *late):
    count, place = lax.axis_size("ctx"), lax.axis_index("ctx")
    devices, me = lax.axis_size("dp"), lax.axis_index("dp")
    bits = devices.bit_length() - 1
    part = grad.reshape((2,) * bits + (count, -1, grad.shape[1]))
    for bit in [0] + list(range(bits - 1, 0, -1)):
        at = 0 if bit else bits - 1
        first, second = (lax.index_in_dim(part, side, at, False) for side in range(2))
        low = ((me >> bit) & 1) == 0
        sent = jnp.where(low, second, first).astype(BF16)
        received = lax.ppermute(sent, "dp", [(i, i ^ (1 << bit)) for i in range(devices)])
        part = jnp.where(low, first, second).astype(F32) + received.astype(F32)
    relative = lax.dynamic_slice_in_dim(jnp.concatenate([part, part]), place, count, 0)
    total, rounded = relative[0], after(relative.astype(BF16), *late)
    for d in range(1, count):
        route = [(i, (i + d) % count) for i in range(count)]
        total = total + lax.ppermute(rounded[d], "ctx", route).astype(F32)
    return total


def rms_scale(values, gain_vec):
    return (
        values * lax.rsqrt(jnp.mean(values * values, axis=-1, keepdims=True) + EPSILON) * gain_vec
    )


def silu_product(gate_lin, up_lin):
    return jax.nn.silu(gate_lin) * up_lin


def body(
    layer_input, segments, positions, gain_one, w_in, conv_w, conv_b, head_params, gain_m, w_out,
    w_q, w_k, w_v, w_o, gain_two, w_gate, w_up, w_down, cotangent,
):
    seqs, span, width = layer_input.shape
    rows = seqs * span
    axes = ("dp", "ctx")
    own_rows = w_q.shape[0]
    q_width, kv_width = QH * HD, 2 * KVH * HD
    low_dot = lambda a, b: jnp.dot(a, b, preferred_element_type=F32)

    small_parts = [gain_one, gain_two, gain_m, conv_b, conv_w.reshape(-1)]
    small_sizes = [part.shape[0] for part in small_parts]
    slots = own_rows * 128
    small_block = jnp.concatenate(small_parts, axis=0)
    small_block = jnp.pad(small_block, (0, slots - sum(small_sizes))).reshape(own_rows, 128)
    w_kv = jnp.stack(
        [w_k.reshape(own_rows, KVH, HD), w_v.reshape(own_rows, KVH, HD)], axis=2
    ).reshape(own_rows, kv_width)
    count = lax.axis_size("ctx")
    exchange = lambda blocks: lax.all_to_all(blocks, "ctx", 0, 0, tiled=True)
    copies = lambda block: jnp.broadcast_to(block[None], (count,) + block.shape)
    gather = lambda part: lax.all_gather(part, "dp", axis=0, tiled=True)
    w_cr = jnp.pad(w_in[:, DI:], ((0, 0), (0, CR - (w_in.shape[1] - DI))))
    first = jnp.concatenate([w_cr, w_q, w_kv, small_block, w_in[:, :DI]], axis=1)
    first_part = lax.all_gather(first, "ctx", axis=0, tiled=True)
    turned_o = w_o.T
    half_rows, ff = own_rows // 2, w_gate.shape[1]

    def fold(block, cut):
        return jnp.concatenate([block[..., :half_rows, cut:], block[..., half_rows:, cut:]], axis=-1)

    def unfold(block):
        half = block.shape[-1] // 2
        return jnp.concatenate([block[..., :half], block[..., half:]], axis=-2)

    rest = [w_down, w_out, fold(turned_o, 0)]
    for matrix in (w_gate, w_up):
        rest += [matrix[:, at : at + width] for at in range(0, ff, width)]
    rest_sizes = [part.shape[0] for part in rest]
    place = lax.axis_index("ctx")
    span_start = place * span
    seg_own = lax.dynamic_slice_in_dim(segments, span_start, span, 1)
    seg_rim = jnp.where(
        place > 0,
        lax.dynamic_slice_in_dim(segments, jnp.maximum(span_start - (KC - 1), 0), KC - 1, 1),
        -1,
    )
    token = token_table(seg_own, seg_rim)
    bounds = attention_bounds(segments, seg_own, span_start)
    segk, segq = segments[:, :, None], seg_own[:, None, :]
    cosine, sine = rope_tables(positions)
    heads = jnp.pad(head_params, ((0, 5), (0, 128 - MH)))
    skip = jnp.repeat(head_params[2], MP)[None]
    spread, spread_first = spread_matrix(), spread_first_matrix()

    tokens = layer_input.reshape(rows, width)
    small = (token, bounds, segk, segq, cosine, sine, heads, skip, spread, spread_first)
    rest_copies = copies(jnp.concatenate(rest, axis=0))
    first_all = gather(after(first_part, small, rest_copies))
    cosine, sine = cosine.reshape(rows, 128), sine.reshape(rows, 128)
    rest_part = exchange(after(rest_copies, first_part))
    rest_all = gather(rest_part.reshape(-1, width)).reshape(-1, sum(rest_sizes), width)
    cuts, at = [], 0
    for size in rest_sizes:
        cuts.append(rest_all[:, at : at + size])
        at += size
    w_down_all, w_out_all = cuts[0].reshape(-1, width), cuts[1].reshape(-1, width)
    w_o_all = unfold(cuts[2]).reshape(width, q_width)
    w_gates = first_all[:, FIRST:]
    w_gu_all = jnp.concatenate([cut.reshape(width, width) for cut in cuts[3:]], axis=1)
    small_all = first_all[:, FIRST - 128 : FIRST].reshape(-1, slots).astype(F32)
    parts, at = [], 0
    for size in small_sizes:
        parts.append(small_all[:, at : at + size])
        at += size
    gain1_all, gain2_all, gain_m_all, shift_all = [part.reshape(1, -1) for part in parts[:4]]
    taps_all = jnp.swapaxes(parts[4].reshape(-1, KC, small_sizes[3]), 0, 1).reshape(KC, CC)
    taps_all = jnp.pad(taps_all, ((0, 8 - KC), (0, 0)))


    hidden, cr, q, kv = project(tokens, gain1_all, first_all, cosine, sine, count)
    q = q.reshape(seqs, span, q_width)
    kv = kv.reshape(count, seqs, span, kv_width)
    cr = cr.reshape(seqs, span, CR)
    rim = from_behind(cr[:, span - (KC - 1) :, :CC], "ctx", 1)
    kv_all = exchange(after(kv, rim))
    rim = jnp.pad(rim, ((0, 0), (8 - (KC - 1), 0), (0, 0)))
    scanned, chains, wide_gains = None, [], []
    for seq in range(seqs):
        scanned = mixer_scan(
            seq, scanned, cr, rim, token, heads, taps_all,
            shift_all, spread,
        )
        wide_gains.append(scanned[4][:, :1])
        chains.append(Chain(scanned[3], wide_gains[seq], False))
        chains[seq].send()
    act, states, gains, terms = scanned[0], scanned[1], scanned[2], scanned[5]
    for chain in chains:
        chain.take()
        chain.send()
    atts, lses, mixed = [], [], None
    mark = (act, w_down_all, w_out_all, w_o_all, w_gu_all)
    for seq in range(seqs):
        att, lse = attend(seq, bounds, after(q, mark), kv_all, segk, segq)
        atts.append(att)
        lses.append(lse)
        chains[seq].take()
        chains[seq].send(lse)
        mark = lse
    gate = low_dot(hidden, w_gates).astype(BF16).reshape(seqs, span, DI)
    states_in = []
    for seq in range(seqs):
        states_in.append(chains[seq].finish())
        mixed = mixer_out(
            seq, mixed, gate, terms, act, token, states, gains, states_in[seq], skip, gain_m_all,
            spread,
        )
    mixer_y, mixer_in = mixed
    mixer_in = mixer_in.reshape(rows, DI)
    att_rows = jnp.concatenate(atts, axis=0).reshape(rows, q_width)
    middle = (
        tokens.astype(F32)
        + low_dot(mixer_in, w_out_all)
        + jnp.einsum("ra,da->rd", att_rows, w_o_all, preferred_element_type=F32)
    )
    normed_mid, norm2_pull = jax.vjp(rms_scale, middle, gain2_all)
    normed_two = normed_mid.astype(BF16)
    gate_up = low_dot(normed_two, w_gu_all).astype(BF16)
    act_float, act_pull = jax.vjp(
        silu_product, gate_up[:, :ff].astype(F32), gate_up[:, ff:].astype(F32)
    )
    act_rows = act_float.astype(BF16)
    def scatter(grad):
        return lax.psum_scatter(grad, "dp", scatter_dimension=0, tiled=True)

    def weight_grad(left, right):
        return jnp.einsum("ri,ro->io", left, right, preferred_element_type=F32).astype(BF16)

    def back_dot(grad, weight):
        return jnp.einsum("ro,io->ri", grad, weight, preferred_element_type=F32)

    cot_rows = cotangent.reshape(rows, width)
    grad_down = weight_grad(act_rows, cot_rows)
    grad_gate_up = jnp.concatenate(act_pull(back_dot(cot_rows, w_down_all)), axis=1).astype(BF16)
    grad_wgu = weight_grad(normed_two, grad_gate_up)
    grad_normed = back_dot(grad_gate_up, w_gu_all)
    grad_normed, grad_down, grad_wgu = lax.optimization_barrier((grad_normed, grad_down, grad_wgu))
    part_gu = scatter(grad_wgu)
    grad_mid_norm, grad_gain_second = norm2_pull(grad_normed)
    grad_middle = cot_rows.astype(F32) + grad_mid_norm
    grad_mid_low = grad_middle.astype(BF16)
    grad_wout = weight_grad(mixer_in, grad_mid_low)
    grad_wo = weight_grad(grad_mid_low, att_rows)
    grad_mixer_in = back_dot(grad_mid_low, w_out_all).astype(BF16).reshape(seqs, span, DI)
    grad_att = low_dot(grad_mid_low, w_o_all).astype(BF16).reshape(seqs, span, q_width)
    grad_mixer_in, grad_att, grad_wout, grad_wo = lax.optimization_barrier(
        (grad_mixer_in, grad_att, grad_wout, grad_wo)
    )
    grad_wo = grad_wo.reshape(-1, own_rows, q_width)
    gated, chains, grad_gain_mix, grad_skip = None, [], 0.0, 0.0
    for seq in range(seqs):
        gated = mixer_gate_back(
            seq, gated, grad_mixer_in, mixer_y, gate, terms, act, gains, gain_m_all, spread
        )
        grad_gain_mix, grad_skip = grad_gain_mix + gated[5], grad_skip + gated[6]
        chains.append(Chain(gated[4], wide_gains[seq], True))
        chains[seq].send()
    grad_y, grad_gate, gstates, ggains = gated[:4]
    chains[0].take()
    chains[1 % seqs].take()
    grad_wgates = weight_grad(after(hidden, chains[0].state), grad_gate.reshape(rows, DI)).reshape(-1, own_rows, DI)
    blocks = grad_wo.shape[0]
    grad_rest = jnp.concatenate(
        [
            after(grad_down, chains[0].state, chains[1 % seqs].state).reshape(blocks, -1, width), grad_wout.reshape(blocks, -1, width),
            fold(grad_wo, 0), grad_wgates[..., :width], fold(grad_wgates, width),
        ],
        axis=1,
    )
    part_rest = scatter(grad_rest.reshape(-1, width))
    cos3, sin3 = cosine.reshape(seqs, span, 128), sine.reshape(seqs, span, 128)
    dqs, dkvs = [], []
    for seq in range(seqs):
        if seq < 2:
            for chain in chains:
                chain.take()
                chain.send(*dqs[-1:])
        mark = dqs[-1:] + [chain.state for chain in chains] + ([] if seq else [grad_rest])
        dq, dkv = attend_back(
            seq, bounds, after(q, grad_y, *mark), kv_all, segk,
            segq, atts[seq], grad_att, lses[seq], cos3, sin3,
        )
        dqs.append(dq)
        dkvs.append(dkv)
    dq = jnp.concatenate(dqs, axis=0)
    last, rims, grad_conv, grad_heads = None, [], 0.0, 0.0
    waits = [(grad_rest, part_gu)] + [()] * (seqs - 1)
    finals = [chain.finish() for chain in chains]
    dkv_all = exchange(after(jnp.concatenate(dkvs, axis=1), *finals))
    waits[1 % seqs] += tuple(finals)
    for seq in range(seqs):
        gstate = finals[seq]
        if seq == min(1, seqs - 1):
            gu_blocks = part_gu.reshape(count, own_rows, 2 * ff)
            parts = [after(part_rest, *rims).reshape(count, -1, width)]
            parts += [gu_blocks[..., at : at + width] for at in range(0, 2 * ff, width)]
            rest_low = jnp.concatenate(parts, axis=1).reshape(-1, width)
            waits[seq] += (rest_low,)
        last = mixer_back(
            seq, last, after(grad_y, dqs[-1], *waits[seq]), mixer_y, terms, cr, rim, act, token, states,
            gains, states_in[seq], gstates, ggains, gstate, heads, skip, taps_all, shift_all,
            spread, spread_first,
        )
        rims.append(last[1])
        grad_conv, grad_heads = grad_conv + last[2], grad_heads + last[3]
    grad_cr, grad_rim = last[0], jnp.concatenate(rims, axis=0)
    back_rim = from_behind(grad_rim[:, 8 - (KC - 1) :].astype(BF16), "ctx", -1)
    edge = grad_cr[:, span - (KC - 1) :, :CC].astype(F32) + back_rim.astype(F32)
    grad_cr = lax.dynamic_update_slice(
        grad_cr, after(edge.astype(BF16), dkv_all), (0, span - (KC - 1), 0)
    ).reshape(rows, CR)
    rest_out = lax.psum_scatter(rest_low, "ctx", scatter_dimension=0, tiled=True).astype(F32)
    grad_wcr = weight_grad(hidden, grad_cr)
    grad_wq = weight_grad(hidden, dq.reshape(rows, q_width))
    part_cr = scatter(jnp.concatenate([grad_wcr, grad_wq], axis=1))
    layer_result = (middle + low_dot(after(act_rows, part_cr), w_down_all)).astype(BF16)
    out_cr = lax.psum_scatter(part_cr, "ctx", scatter_dimension=0, tiled=True).astype(F32)
    grad_tokens, grad_kv, grad_gain_first = finish(
        tokens, gain1_all, grad_gate.reshape(rows, DI), after(grad_cr, grad_wcr, rest_out),
        dq.reshape(rows, q_width), dkv_all, cosine, sine, grad_middle, first_all,
    )
    grad_wfirst = weight_grad(hidden, grad_kv)
    grad_gain_first = grad_gain_first[0]

    devices = first_all.shape[0] // own_rows
    small_grads = jnp.concatenate(
        [
            grad_gain_first.reshape(devices, -1),
            grad_gain_second.reshape(devices, -1),
            grad_gain_mix[0].reshape(devices, -1),
            grad_conv[KC].reshape(devices, -1),
            jnp.swapaxes(grad_conv[:KC].reshape(KC, devices, -1), 0, 1).reshape(devices, -1),
        ],
        axis=1,
    )
    small_grads = jnp.pad(small_grads, ((0, 0), (0, slots - small_grads.shape[1])))
    out_first = scatter_all(
        jnp.concatenate([grad_wfirst, small_grads.reshape(-1, 128).astype(BF16)], axis=1), part_cr
    )
    rest_sizes = rest_sizes[:3] + [own_rows, half_rows] + rest_sizes[3:]
    outs, at = [], 0
    for size in rest_sizes:
        outs.append(rest_out[at : at + size])
        at += size
    out_down, out_wout = outs[0], outs[1]
    out_wo = unfold(outs[2])
    out_win = jnp.concatenate(
        [outs[3], unfold(outs[4]), out_cr[:, : w_in.shape[1] - DI]], axis=1
    )
    halves = ff // width
    out_gate = jnp.concatenate(outs[5 : 5 + halves], axis=1)
    out_up = jnp.concatenate(outs[5 + halves :], axis=1)
    out_small = out_first[:, kv_width:].reshape(-1)
    pieces, at = [], 0
    for size in small_sizes:
        pieces.append(out_small[at : at + size])
        at += size
    out_kv = out_first[:, :kv_width].reshape(own_rows, KVH, 2, HD)
    head_grad = sum_everywhere(
        jnp.concatenate(
            [
                after(grad_heads, grad_kv)[:2, :MH],
                grad_skip[0].reshape(MH, MP).sum(axis=1)[None],
            ],
            axis=0,
        ),
        axes,
    )
    return (
        layer_result.reshape(layer_input.shape),
        grad_tokens.reshape(layer_input.shape),
        pieces[0],
        out_win,
        pieces[4].reshape(KC, -1),
        pieces[3],
        head_grad,
        pieces[2],
        out_wout,
        out_cr[:, CR:],
        out_kv[:, :, 0].reshape(own_rows, -1),
        out_kv[:, :, 1].reshape(own_rows, -1),
        out_wo.T,
        pieces[1],
        out_gate,
        out_up,
        out_down,
    )


def solution(mesh):
    in_specs = (
        P("dp", "ctx", None),
        P("dp", None),
        P("dp", "ctx"),
        P(("dp", "ctx")),
        P(("dp", "ctx"), None),
        P(None, ("dp", "ctx")),
        P(("dp", "ctx")),
        P(),
        P(("dp", "ctx")),
        P(("dp", "ctx"), None),
        P(("dp", "ctx"), None),
        P(("dp", "ctx"), None),
        P(("dp", "ctx"), None),
        P(None, ("dp", "ctx")),
        P(("dp", "ctx")),
        P(("dp", "ctx"), None),
        P(("dp", "ctx"), None),
        P(("dp", "ctx"), None),
        P("dp", "ctx", None),
    )
    out_specs = (
        P("dp", "ctx", None),
        P("dp", "ctx", None),
        P(("dp", "ctx")),
        P(("dp", "ctx"), None),
        P(None, ("dp", "ctx")),
        P(("dp", "ctx")),
        P(),
        P(("dp", "ctx")),
        P(("dp", "ctx"), None),
        P(("dp", "ctx"), None),
        P(("dp", "ctx"), None),
        P(("dp", "ctx"), None),
        P(None, ("dp", "ctx")),
        P(("dp", "ctx")),
        P(("dp", "ctx"), None),
        P(("dp", "ctx"), None),
        P(("dp", "ctx"), None),
    )
    return jax.shard_map(body, mesh=mesh, in_specs=in_specs, out_specs=out_specs, check_vma=False)
```

```python
import functools
import jax
import jax.numpy as jnp
from jax import lax
from jax.experimental import pallas as pl
from jax.experimental.pallas import tpu as pltpu
from jax.sharding import PartitionSpec as P

MH = 24
MP = 64
NS = 128
KC = 4
QH = 8
KVH = 2
HD = 64
EPSILON = 1e-05
ROPE_BASE = 10000.0
MASKED = -1e30
LOG2E = 1.4426950408889634
KEY_TILE = 256
VMEM_BYTES = 56 * 1024 * 1024

F32 = jnp.float32
BF16 = jnp.bfloat16


def contract(left, right, left_dim, right_dim):
    return lax.dot_general(
        left, right, (((left_dim,), (right_dim,)), ((), ())), preferred_element_type=F32
    )


def lanes(shape):
    return lax.broadcasted_iota(jnp.int32, shape, len(shape) - 1)


def swap_halves(values):
    lane = lanes(values.shape)
    return jnp.where(lane < 32, pltpu.roll(values, 96, 1), pltpu.roll(values, 32, 1))


CR = MH * MP + 2 * NS + 128
FIRST = CR + QH * HD + 2 * KVH * HD + 128


def project_kernel(x_ref, gain_ref, w_ref, cos_ref, sin_ref, hidden_ref, cr_ref, q_ref, kv_ref):
    x = x_ref[...].astype(F32)
    scale = lax.rsqrt(jnp.mean(x * x, axis=-1, keepdims=True) + EPSILON)
    hidden = (x * scale * gain_ref[...]).astype(BF16)
    hidden_ref[...] = hidden
    lin = contract(hidden, w_ref[:, CR : CR + QH * HD + 2 * KVH * HD], 1, 0)
    cosine, sine = cos_ref[...], sin_ref[...]
    lane = lanes(cosine.shape)
    for pair in range(QH // 2):
        both = lin[:, pair * 128 : (pair + 1) * 128]
        other = pltpu.roll(both, 64, 1)
        even = both * cosine + swap_halves(both) * sine
        odd = other * cosine + swap_halves(other) * sine
        q_ref[:, pair * 128 : (pair + 1) * 128] = jnp.where(
            lane < 64, even, pltpu.roll(odd, 64, 1)
        ).astype(BF16)
    for group in range(KVH):
        at = QH * HD + group * 128
        part = lin[:, at : at + 128]
        turned = (part * cosine + swap_halves(part) * sine).astype(BF16)
        for copy in range(kv_ref.shape[0]):
            kv_ref[copy, :, group * 128 : (group + 1) * 128] = turned
    cr_ref[...] = contract(hidden, w_ref[:, :CR], 1, 0).astype(BF16)


def project(x, gain, w_first, cosine, sine, copies):
    rows, width = x.shape
    tile = 256 if rows % 256 == 0 else 128
    block = lambda cols: pl.BlockSpec((tile, cols), lambda i: (i, 0))
    fixed = lambda array: pl.BlockSpec(array.shape, lambda i: (0, 0))
    cols = [width, CR, QH * HD]
    kv_width = 2 * KVH * HD
    return pl.pallas_call(
        project_kernel,
        grid=(rows // tile,),
        in_specs=[
            block(width), fixed(gain), fixed(w_first), block(128), block(128),
        ],
        out_specs=[block(size) for size in cols]
        + [pl.BlockSpec((copies, tile, kv_width), lambda i: (0, i, 0))],
        out_shape=[jax.ShapeDtypeStruct((rows, size), BF16) for size in cols]
        + [jax.ShapeDtypeStruct((copies, rows, kv_width), BF16)],
        compiler_params=pltpu.CompilerParams(vmem_limit_bytes=VMEM_BYTES),
        name="project",
    )(x, gain, w_first, cosine, sine)


def finish_kernel(
    x_ref, gain_ref, dgate_ref, dcr_ref, dq_ref, dkv_ref, cos_ref, sin_ref, middle_ref,
    w_ref, dx_ref, dkv_out_ref, dgain_ref, dgain_s,
):
    @pl.when(pl.program_id(0) == 0)
    def _():
        dgain_s[...] = jnp.zeros(dgain_s.shape, F32)

    dkv = dkv_ref[0, 0].astype(F32)
    for source in range(1, dkv_ref.shape[0]):
        dkv = dkv + dkv_ref[source, 0].astype(F32)
    cosine, sine = cos_ref[...], sin_ref[...]
    turned = []
    for group in range(KVH):
        part = dkv[:, group * 128 : (group + 1) * 128]
        back = part * cosine + swap_halves(part * sine)
        turned.append(jnp.where(lanes(part.shape) < HD, back, part))
    dkv = jnp.concatenate(turned, axis=1).astype(BF16)
    dkv_out_ref[...] = dkv
    at = CR + QH * HD
    grad = (
        contract(dgate_ref[...], w_ref[:, FIRST:], 1, 1)
        + contract(dcr_ref[...], w_ref[:, :CR], 1, 1)
        + contract(dq_ref[...], w_ref[:, CR:at], 1, 1)
        + contract(dkv, w_ref[:, at : at + 2 * KVH * HD], 1, 1)
    )
    x = x_ref[...].astype(F32)
    scale = lax.rsqrt(jnp.mean(x * x, axis=-1, keepdims=True) + EPSILON)
    scaled = grad * gain_ref[...]
    shrink = jnp.mean(scaled * x, axis=-1, keepdims=True) * (scale * scale * scale)
    dx_ref[...] = (middle_ref[...] + scaled * scale - x * shrink).astype(BF16)
    dgain_s[0:1, :] += jnp.sum(grad * x * scale, axis=0, keepdims=True)
    dgain_ref[...] = dgain_s[...]


def finish(x, gain, dgate, dcr, dq, dkv_all, cosine, sine, middle, w_first):
    rows, width = x.shape
    span = dkv_all.shape[2]
    tile = min(256, span)
    per_seq = span // tile
    block = lambda array: pl.BlockSpec((tile, array.shape[1]), lambda i: (i, 0))
    fixed = lambda array: pl.BlockSpec(array.shape, lambda i: (0, 0))
    keys = pl.BlockSpec(
        (dkv_all.shape[0], 1, tile, dkv_all.shape[3]), lambda i: (0, i // per_seq, i % per_seq, 0)
    )
    kv_width = dkv_all.shape[3]
    return pl.pallas_call(
        finish_kernel,
        grid=(rows // tile,),
        in_specs=[
            block(x), fixed(gain), block(dgate), block(dcr), block(dq), keys, block(cosine),
            block(sine), block(middle), fixed(w_first),
        ],
        out_specs=[
            block(x),
            pl.BlockSpec((tile, kv_width), lambda i: (i, 0)),
            pl.BlockSpec((8, width), lambda i: (0, 0)),
        ],
        out_shape=[
            jax.ShapeDtypeStruct((rows, width), BF16),
            jax.ShapeDtypeStruct((rows, kv_width), BF16),
            jax.ShapeDtypeStruct((8, width), F32),
        ],
        scratch_shapes=[pltpu.VMEM((8, width), F32)],
        compiler_params=pltpu.CompilerParams(vmem_limit_bytes=VMEM_BYTES),
        name="finish",
    )(x, gain, dgate, dcr, dq, dkv_all, cosine, sine, middle, w_first)


def visible(segk_ref, segq, query_row, at, key_rows):
    segk = segk_ref[0, pl.ds(at, key_rows), :]
    key_col = at + lax.broadcasted_iota(jnp.int32, (key_rows, 1), 0)
    return jnp.where((segk == segq) & (key_col <= query_row), 0.0, MASKED)


def attend_kernel(
    place_at, low_ref, high_ref, base_ref, q_ref, kv_ref, segk_ref, segq_ref, out_ref, lse_ref,
    q_s, m_s, l_s, acc_s,
):
    tile = pl.program_id(0)
    rows = q_ref.shape[1]
    place = place_at + tile
    lane = lanes((rows, 128))
    for pair in range(QH // 2):
        both = q_ref[0, :, pair * 128 : (pair + 1) * 128].astype(F32)
        q_s[2 * pair] = jnp.where(lane < 64, both, 0.0).astype(BF16)
        q_s[2 * pair + 1] = jnp.where(lane < 64, pltpu.roll(both, 64, 1), 0.0).astype(BF16)
    key_rows = min(KEY_TILE, kv_ref.shape[2])
    tiles_each = kv_ref.shape[2] // key_rows
    m_s[...] = jnp.full(m_s.shape, MASKED, F32)
    l_s[...] = jnp.zeros(l_s.shape, F32)
    acc_s[...] = jnp.zeros(acc_s.shape, F32)
    query_row = base_ref[0] + tile * rows + lanes((1, rows))
    segq = segq_ref[0]
    factor = HD ** (-0.5) * LOG2E

    def step(key_tile, carry):
        at = pl.multiple_of(key_tile * key_rows, key_rows)
        source = key_tile // tiles_each
        offset = pl.multiple_of((key_tile % tiles_each) * key_rows, key_rows)
        bias = visible(segk_ref, segq, query_row, at, key_rows)
        for group in range(KVH):
            kv = kv_ref[source, 0, pl.ds(offset, key_rows), group * 128 : (group + 1) * 128]
            kv_t = kv.astype(F32).T.astype(BF16)
            members = range(group * (QH // KVH), (group + 1) * (QH // KVH))
            scores = [contract(kv, q_s[head], 1, 1) * factor + bias for head in members]
            before = [m_s[head : head + 1, :] for head in members]
            tops = [
                jnp.maximum(old, jnp.max(part, axis=0, keepdims=True))
                for old, part in zip(before, scores)
            ]
            weights = [jnp.exp2(part - top) for part, top in zip(scores, tops)]
            sums = [jnp.sum(part, axis=0, keepdims=True) for part in weights]
            outs = [contract(kv_t, part.astype(BF16), 1, 0) for part in weights]
            for at_head, head in enumerate(members):
                fade = jnp.exp2(before[at_head] - tops[at_head])
                l_s[head : head + 1, :] = l_s[head : head + 1, :] * fade + sums[at_head]
                acc_s[head] = acc_s[head] * fade + outs[at_head]
                m_s[head : head + 1, :] = tops[at_head]
        return carry

    lax.fori_loop(low_ref[place], high_ref[place], step, 0)
    lse_ref[0] = m_s[...] + jnp.log2(l_s[...])
    for pair in range(QH // 2):
        even = (acc_s[2 * pair] / l_s[2 * pair : 2 * pair + 1, :]).T
        odd = (acc_s[2 * pair + 1] / l_s[2 * pair + 1 : 2 * pair + 2, :]).T
        out_ref[0, :, pair * 128 : (pair + 1) * 128] = jnp.where(
            lane < 64, pltpu.roll(even, 64, 1), odd
        ).astype(BF16)


def attend_back_kernel(
    place_at, low_ref, high_ref, base_ref, q_ref, kv_ref, segk_ref, segq_ref, att_ref, gatt_ref, lse_ref,
    cos_ref, sin_ref, dq_ref, dkv_ref,
    q_s, g_s, delta_s, dq_s, dkv_s,
):
    tile = pl.program_id(0)
    rows = q_ref.shape[1]
    place = place_at + tile
    lane = lanes((rows, 128))

    @pl.when(tile == 0)
    def _():
        dkv_s[...] = jnp.zeros(dkv_s.shape, F32)

    for pair in range(QH // 2):
        cols = slice(pair * 128, (pair + 1) * 128)
        both = q_ref[0, :, cols].astype(F32)
        q_s[2 * pair] = jnp.where(lane < 64, both, 0.0).astype(BF16)
        q_s[2 * pair + 1] = jnp.where(lane < 64, pltpu.roll(both, 64, 1), 0.0).astype(BF16)
        grad = gatt_ref[0, :, cols].astype(F32)
        g_s[2 * pair] = jnp.where(lane >= 64, pltpu.roll(grad, 64, 1), 0.0).astype(BF16)
        g_s[2 * pair + 1] = jnp.where(lane >= 64, grad, 0.0).astype(BF16)
        product = (grad * att_ref[0, :, cols].astype(F32)).T
        delta_s[2 * pair : 2 * pair + 1, :] = jnp.sum(product[:64], axis=0, keepdims=True)
        delta_s[2 * pair + 1 : 2 * pair + 2, :] = jnp.sum(product[64:], axis=0, keepdims=True)
    key_rows = min(KEY_TILE, kv_ref.shape[2])
    tiles_each = kv_ref.shape[2] // key_rows
    dq_s[...] = jnp.zeros(dq_s.shape, F32)
    query_row = base_ref[0] + tile * rows + lanes((1, rows))
    segq = segq_ref[0]
    qk_scale = HD ** (-0.5)
    factor = qk_scale * LOG2E

    def step(key_tile, carry):
        at = pl.multiple_of(key_tile * key_rows, key_rows)
        source = key_tile // tiles_each
        offset = pl.multiple_of((key_tile % tiles_each) * key_rows, key_rows)
        bias = visible(segk_ref, segq, query_row, at, key_rows)
        for group in range(KVH):
            kv = kv_ref[source, 0, pl.ds(offset, key_rows), group * 128 : (group + 1) * 128]
            kv_t = kv.astype(F32).T.astype(BF16)
            total = jnp.zeros((key_rows, 128), F32)
            for member in range(QH // KVH):
                head = group * (QH // KVH) + member
                q, g = q_s[head], g_s[head]
                scores = contract(kv, q, 1, 1) * factor + bias
                probs = jnp.exp2(scores - lse_ref[0, head : head + 1, :])
                d_probs = contract(kv, g, 1, 1)
                d_scores = (probs * (d_probs - delta_s[head : head + 1, :]) * qk_scale).astype(BF16)
                total = total + contract(d_scores, q, 1, 0) + contract(probs.astype(BF16), g, 1, 0)
                dq_s[head] += contract(kv_t, d_scores, 1, 0)
            cols = slice(group * 128, (group + 1) * 128)
            dkv_s[source, 0, pl.ds(offset, key_rows), cols] += total
        return carry

    lax.fori_loop(low_ref[place], high_ref[place], step, 0)
    cosine, sine = cos_ref[0], sin_ref[0]
    for pair in range(QH // 2):
        even, odd = dq_s[2 * pair].T, dq_s[2 * pair + 1].T
        even = even * cosine + swap_halves(even * sine)
        odd = odd * cosine + swap_halves(odd * sine)
        dq_ref[0, :, pair * 128 : (pair + 1) * 128] = jnp.where(
            lane < 64, even, pltpu.roll(odd, 64, 1)
        ).astype(BF16)

    @pl.when(tile == pl.num_programs(0) - 1)
    def _():
        dkv_ref[...] = dkv_s[...].astype(BF16)


def attention_specs(seq, length, rows):
    tile = lambda cols, at=seq: pl.BlockSpec((1, rows, cols), lambda t, *_: (at, t, 0))
    whole = lambda cols, at=seq: pl.BlockSpec((1, length, cols), lambda t, *_: (at, 0, 0))
    keys = lambda array, at=seq: pl.BlockSpec(
        (array.shape[0], 1) + array.shape[2:], lambda t, *_: (0, at, 0, 0)
    )
    row = lambda n, at=seq: pl.BlockSpec((1, n, rows), lambda t, *_: (at, 0, t))
    return tile, whole, keys, row


def attend(seq, bounds, q, kv_all, segk, segq):
    _, span, q_width = q.shape
    rows = min(256, span)
    tile, whole, keys, row = attention_specs(seq, segk.shape[1], rows)
    own_keys = kv_all.shape[:1] + (1,) + kv_all.shape[2:]
    return pl.pallas_call(
        functools.partial(attend_kernel, seq * (span // rows)),
        grid_spec=pltpu.PrefetchScalarGridSpec(
            num_scalar_prefetch=3,
            grid=(span // rows,),
            in_specs=[tile(q_width), keys(kv_all), whole(1), row(1)],
            out_specs=[tile(q_width, 0), row(QH, 0)],
            scratch_shapes=[
                pltpu.VMEM((QH, rows, 128), BF16),
                pltpu.VMEM((QH, rows), F32),
                pltpu.VMEM((QH, rows), F32),
                pltpu.VMEM((QH, 128, rows), F32),
            ],
        ),
        out_shape=[
            jax.ShapeDtypeStruct((1, span, q_width), BF16),
            jax.ShapeDtypeStruct((1, QH, span), F32),
        ],
        compiler_params=pltpu.CompilerParams(vmem_limit_bytes=VMEM_BYTES),
        name="attend",
    )(*bounds, q, kv_all, segk, segq)


def attend_back(seq, bounds, q, kv_all, segk, segq, att, grad_att, lse, cosine, sine):
    _, span, q_width = q.shape
    rows = min(256, span)
    tile, whole, keys, row = attention_specs(seq, segk.shape[1], rows)
    own_keys = kv_all.shape[:1] + (1,) + kv_all.shape[2:]
    return pl.pallas_call(
        functools.partial(attend_back_kernel, seq * (span // rows)),
        grid_spec=pltpu.PrefetchScalarGridSpec(
            num_scalar_prefetch=3,
            grid=(span // rows,),
            in_specs=[
                tile(q_width), keys(kv_all), whole(1), row(1), tile(q_width, 0), tile(q_width),
                row(QH, 0), tile(128), tile(128),
            ],
            out_specs=[tile(q_width, 0), keys(kv_all, 0)],
            scratch_shapes=[
                pltpu.VMEM((QH, rows, 128), BF16),
                pltpu.VMEM((QH, rows, 128), BF16),
                pltpu.VMEM((QH, rows), F32),
                pltpu.VMEM((QH, 128, rows), F32),
                pltpu.VMEM(own_keys, F32),
            ],
        ),
        out_shape=[
            jax.ShapeDtypeStruct((1, span, q_width), BF16),
            jax.ShapeDtypeStruct(own_keys, BF16),
        ],
        compiler_params=pltpu.CompilerParams(vmem_limit_bytes=VMEM_BYTES),
        name="attend_back",
    )(*bounds, q, kv_all, segk, segq, att, grad_att, lse, cosine, sine)


def rope_tables(positions):
    half = HD // 2
    frequency = ROPE_BASE ** (-jnp.arange(half, dtype=F32) / half)
    angles = positions.astype(F32)[..., None] * frequency
    cosine, sine = jnp.cos(angles), jnp.sin(angles)
    one, zero = jnp.ones(cosine.shape[:-1] + (HD,), F32), jnp.zeros(cosine.shape[:-1] + (HD,), F32)
    return (
        jnp.concatenate([cosine, cosine, one], axis=-1),
        jnp.concatenate([-sine, sine, zero], axis=-1),
    )


def attention_bounds(segments, seg_own, span_start):
    seqs, span = seg_own.shape
    rows, key_rows = min(256, span), min(KEY_TILE, span)
    first = seg_own[:, ::rows]
    begin = jnp.sum((segments[:, None, :] < first[:, :, None]).astype(jnp.int32), axis=2)
    tiles = jnp.arange(span // rows, dtype=jnp.int32)
    high = (span_start + (tiles + 1) * rows + key_rows - 1) // key_rows
    high = jnp.broadcast_to(high[None], first.shape)
    return (
        (begin // key_rows).reshape(-1),
        high.reshape(-1).astype(jnp.int32),
        jnp.full((1,), span_start, jnp.int32),
    )


CHUNK = 128
DI = MH * MP
CC = DI + 2 * NS
TAP_LANES, PREV_LANE, LAST_LANE, SEG_LANE = 0, 4, 5, 6


def split_three(values):
    high = values.astype(BF16)
    rest = values - high.astype(F32)
    middle = rest.astype(BF16)
    return high, middle, (rest - middle.astype(F32)).astype(BF16)


def product_exact(matrix, values):
    return sum(contract(matrix, part, 1, 0) for part in split_three(values))


def widen(values, spread):
    kept = jnp.where(lanes(values.shape) < 32, values, 0.0)
    high, middle, rest = (part.astype(F32) for part in split_three(kept))
    packed = high + pltpu.roll(middle, 32, 1) + pltpu.roll(rest, 64, 1)
    return contract(packed.astype(BF16), spread, 1, 0)


def gather_heads(values, spread_first):
    high = values.astype(BF16)
    rest = (values - high.astype(F32)).astype(BF16)
    return contract(high, spread_first, 1, 1) + contract(rest, spread_first, 1, 1)


def spread_matrix():
    row = lax.broadcasted_iota(jnp.int32, (128, DI), 0)
    col = lax.broadcasted_iota(jnp.int32, (128, DI), 1)
    return ((row % 32 == col // MP) & (row < 96)).astype(BF16)


def spread_first_matrix():
    row = lax.broadcasted_iota(jnp.int32, (32, DI), 0)
    col = lax.broadcasted_iota(jnp.int32, (32, DI), 1)
    return (row == col // MP).astype(BF16)


def lower_mask():
    row = lax.broadcasted_iota(jnp.int32, (CHUNK, CHUNK), 0)
    return row >= lanes((CHUNK, CHUNK))


def saved_terms(terms_ref):
    return [terms_ref[0, :, at * 128 : (at + 1) * 128] for at in range(6)]


def token_rows(token_ref):
    return jnp.concatenate([token_ref[0]] * 16, axis=0).T


def decay_rows(rate, head_ref, token):
    raw = rate.astype(F32) + head_ref[1:2, :]
    step = jnp.maximum(raw, 0.0) + jnp.log1p(jnp.exp(-jnp.abs(raw)))
    log_decay = -step * jnp.exp(head_ref[0:1, :])
    running = product_exact(lower_mask().astype(BF16), log_decay)
    last = running[CHUNK - 1 :, :]
    weight_end = jnp.exp(last - running) * step * token[:, LAST_LANE : LAST_LANE + 1]
    entry = jnp.exp(running) * token[:, PREV_LANE : PREV_LANE + 1]
    gain = jnp.exp(last) * token[CHUNK - 1 :, PREV_LANE : PREV_LANE + 1]
    return raw, step, log_decay, running, weight_end, entry, gain


def conv_total(ext_s, token, taps_ref, shift_ref):
    total = shift_ref[...] + ext_s[8 : 8 + CHUNK, :] * taps_ref[KC - 1 : KC, :]
    for tap in range(KC - 1):
        total = total + ext_s[5 + tap : 5 + tap + CHUNK, :] * (
            taps_ref[tap : tap + 1, :] * token[:, TAP_LANES + tap : TAP_LANES + tap + 1]
        )
    return total


def mixer_scan_kernel(
    cr_ref, rim_ref, token_ref, head_ref, taps_ref, shift_ref, spread_ref,
    act_ref, states_ref, gains_ref, final_ref, final_gain_ref, terms_ref,
    ext_s, state_s, gain_s,
):
    chunk = pl.program_id(0)

    @pl.when(chunk == 0)
    def _():
        ext_s[0:8, :] = rim_ref[0].astype(F32)
        state_s[...] = jnp.zeros(state_s.shape, F32)
        gain_s[...] = jnp.ones(gain_s.shape, F32)

    @pl.when(chunk > 0)
    def _():
        ext_s[0:8, :] = ext_s[CHUNK : CHUNK + 8, :]

    token = token_rows(token_ref)
    ext_s[8 : 8 + CHUNK, :] = cr_ref[0, :, :CC].astype(F32)
    total = conv_total(ext_s, token, taps_ref, shift_ref)
    act = (total * jax.nn.sigmoid(total)).astype(BF16)
    act_ref[0] = act
    raw, step, log_decay, running, weight_end, entry, gain = decay_rows(
        cr_ref[0, :, CC:], head_ref, token
    )
    for at, term in enumerate((raw, step, log_decay, running, weight_end, entry)):
        terms_ref[0, :, at * 128 : (at + 1) * 128] = term
    states_ref[0, 0] = state_s[...].astype(BF16)
    before = gain_s[...]
    row = lax.broadcasted_iota(jnp.int32, before.shape, 0)
    gains_ref[0, 0] = jnp.where(row == 1, jnp.broadcast_to(gain, before.shape), before)
    spread = spread_ref[...]
    scaled = (act[:, :DI].astype(F32) * widen(weight_end, spread)).astype(BF16)
    gain_rows = jnp.broadcast_to(gain, (8, 128))
    state = state_s[...] * widen(gain_rows, spread)[0:1, :] + contract(
        act[:, DI : DI + NS], scaled, 0, 0
    )
    state_s[...] = state
    gain_s[...] = before * gain_rows

    @pl.when(chunk == pl.num_programs(0) - 1)
    def _():
        final_ref[0] = state.astype(BF16)
        final_gain_ref[0] = widen(before * gain_rows, spread)


def entering_state(local_ref, gains_ref, state_ref, spread):
    factor = widen(gains_ref[0, 0], spread)[0:1, :]
    return (local_ref[0, 0].astype(F32) + factor * state_ref[0].astype(F32)).astype(BF16)


def pair_decay(running, rest_t, bias, head):
    parts = []
    for at in (head, head + 1):
        column = jnp.broadcast_to(running[:, at : at + 1], (CHUNK, CHUNK))
        parts.append(jnp.exp2(column + (rest_t[at : at + 1, :] + bias)))
    return parts


def stack_pair(values):
    lane = lanes(values.shape)
    wide = values.astype(F32)
    return jnp.concatenate(
        [jnp.where(lane < 64, wide, 0.0), jnp.where(lane >= 64, wide, 0.0)], axis=0
    ).astype(BF16)


def inside_terms(running, step, token):
    seg = jnp.broadcast_to(token[:, SEG_LANE : SEG_LANE + 1], (CHUNK, CHUNK))
    bias = jnp.where((seg == seg.T) & lower_mask(), 0.0, MASKED)
    running_two = running * LOG2E
    rest_t = (jnp.log2(step) - running_two).T
    return running_two, rest_t, bias


def mixer_out_kernel(
    gate_ref, terms_ref, act_ref, token_ref, states_ref, gains_ref, state_ref, skip_ref, gain_ref,
    spread_ref, y_ref, out_ref,
):
    token, spread = token_rows(token_ref), spread_ref[...]
    _, step, _, running, _, entry = saved_terms(terms_ref)
    b_rows, c_rows = act_ref[0, :, DI : DI + NS], act_ref[0, :, DI + NS :]
    state = entering_state(states_ref, gains_ref, state_ref, spread)
    carried = contract(c_rows, state, 1, 0) * widen(entry, spread)
    cross = contract(c_rows, b_rows, 1, 1)
    running_two, rest_t, bias = inside_terms(running, step, token)
    square = jnp.zeros((CHUNK, 128), F32)
    for pair in range(MH // 2):
        cols = slice(pair * 128, (pair + 1) * 128)
        xs = act_ref[0, :, cols]
        mix = jnp.concatenate(
            [
                (cross * part).astype(BF16)
                for part in pair_decay(running_two, rest_t, bias, 2 * pair)
            ],
            axis=1,
        )
        y = (
            contract(mix, stack_pair(xs), 1, 0)
            + carried[:, cols]
            + skip_ref[:, cols] * xs.astype(F32)
        )
        y_ref[0, :, cols] = y
        gate = gate_ref[0, :, cols].astype(F32)
        gated = y * (gate * jax.nn.sigmoid(gate))
        square = square + gated * gated
    scale = lax.rsqrt(jnp.sum(square, axis=1, keepdims=True) * (1.0 / DI) + EPSILON)
    for pair in range(MH // 2):
        cols = slice(pair * 128, (pair + 1) * 128)
        gate = gate_ref[0, :, cols].astype(F32)
        gated = y_ref[0, :, cols] * (gate * jax.nn.sigmoid(gate))
        out_ref[0, :, cols] = (gated * scale * gain_ref[:, cols]).astype(BF16)


def mixer_gate_back_kernel(
    gmix_ref, y_ref, gate_ref, terms_ref, act_ref, fgains_ref, gain_ref, spread_ref,
    gy_ref, dgate_ref, gstates_ref, gains_ref, final_ref, dgain_ref, dskip_ref,
    state_s, gain_s, dgain_s, dskip_s,
):
    chunk = pl.program_id(0)

    @pl.when(chunk == 0)
    def _():
        dgain_s[...] = jnp.zeros(dgain_s.shape, F32)
        dskip_s[...] = jnp.zeros(dskip_s.shape, F32)

    @pl.when(chunk == 0)
    def _():
        state_s[...] = jnp.zeros(state_s.shape, F32)
        gain_s[...] = jnp.ones(gain_s.shape, F32)

    spread = spread_ref[...]
    entry, gain = saved_terms(terms_ref)[-1], fgains_ref[0, 0, 1:2, :]
    y = y_ref[0]
    gate = gate_ref[0].astype(F32)
    sig = jax.nn.sigmoid(gate)
    swish = gate * sig
    gated = y * swish
    scale = lax.rsqrt(jnp.mean(gated * gated, axis=1, keepdims=True) + EPSILON)
    grad = gmix_ref[0].astype(F32)
    scaled = grad * gain_ref[...]
    shrink = jnp.mean(scaled * gated, axis=1, keepdims=True) * (scale * scale * scale)
    d_gated = scaled * scale - gated * shrink
    gy = (d_gated * swish).astype(BF16)
    gy_ref[0] = gy
    dgate_ref[0] = (d_gated * y * (sig * (1.0 + gate * (1.0 - sig)))).astype(BF16)
    dgain_s[0:1, :] += jnp.sum(grad * gated * scale, axis=0, keepdims=True)
    gy_float = gy.astype(F32)
    dskip_s[0:1, :] += jnp.sum(gy_float * act_ref[0, :, :DI].astype(F32), axis=0, keepdims=True)
    gstates_ref[0, 0] = state_s[...].astype(BF16)
    after = gain_s[...]
    gains_ref[0, 0] = after
    gain_rows = jnp.broadcast_to(gain, (8, 128))
    carried = (gy_float * widen(entry, spread)).astype(BF16)
    state = state_s[...] * widen(gain_rows, spread)[0:1, :] + contract(
        act_ref[0, :, DI + NS :], carried, 0, 0
    )
    state_s[...] = state
    gain_s[...] = after * gain_rows

    @pl.when(chunk == pl.num_programs(0) - 1)
    def _():
        final_ref[0] = state.astype(BF16)

    dgain_ref[...] = dgain_s[...]
    dskip_ref[...] = dskip_s[...]


def mixer_back_kernel(
    gy_ref, y_ref, terms_ref, cr_ref, halo_ref, rim_ref, act_ref, token_ref,
    states_ref, gains_ref, state_ref, gstates_ref, ggains_ref, gstate_ref,
    head_ref, skip_ref, taps_ref, shift_ref, spread_ref, spread_first_ref,
    dcr_ref, drim_ref, dconv_ref, dhead_ref,
    ext_s, grad_s, carry_s, dconv_s, dhead_s,
):
    step_index = pl.program_id(0)
    last_step = pl.num_programs(0) - 1

    @pl.when(step_index == 0)
    def _():
        dconv_s[...] = jnp.zeros(dconv_s.shape, F32)
        dhead_s[...] = jnp.zeros(dhead_s.shape, F32)

    @pl.when(step_index == 0)
    def _():
        carry_s[...] = jnp.zeros(carry_s.shape, F32)

    @pl.when(step_index == last_step)
    def _():
        ext_s[0:8, :] = rim_ref[0].astype(F32)

    @pl.when(step_index < last_step)
    def _():
        ext_s[0:8, :] = halo_ref[0, :, :CC].astype(F32)[8:16]

    ext_s[8 : 8 + CHUNK, :] = cr_ref[0, :, :CC].astype(F32)
    token, spread, spread_first = token_rows(token_ref), spread_ref[...], spread_first_ref[...]
    raw, step, log_decay, running, weight_end, entry = saved_terms(terms_ref)
    gain = gains_ref[0, 0, 1:2, :]
    b_rows, c_rows = act_ref[0, :, DI : DI + NS], act_ref[0, :, DI + NS :]
    state = entering_state(states_ref, gains_ref, state_ref, spread)
    gstate = entering_state(gstates_ref, ggains_ref, gstate_ref, spread)
    wide_end = widen(weight_end, spread)
    gy = gy_ref[0]
    gy_float = gy.astype(F32)
    gcarried = (gy_float * widen(entry, spread)).astype(BF16)
    xs_float = act_ref[0, :, :DI].astype(F32)
    grad_c = contract(gcarried, state, 1, 1)
    grad_b = contract((xs_float * wide_end).astype(BF16), gstate, 1, 1)
    from_end = contract(b_rows, gstate, 1, 0) * wide_end
    dgain_row = jnp.sum(gstate.astype(F32) * state.astype(F32), axis=0, keepdims=True)
    cross = contract(c_rows, b_rows, 1, 1)
    running_two, rest_t, bias = inside_terms(running, step, token)
    grad_cross = jnp.zeros((CHUNK, CHUNK), F32)
    lane = lanes((CHUNK, 128))
    for pair in range(MH // 2):
        cols = slice(pair * 128, (pair + 1) * 128)
        stacked = stack_pair(act_ref[0, :, cols])
        gy_pair = gy_ref[0, :, cols]
        first, second = pair_decay(running_two, rest_t, bias, 2 * pair)
        mix = jnp.concatenate([(cross * first).astype(BF16), (cross * second).astype(BF16)], axis=1)
        grad_mix = contract(gy_pair, stacked, 1, 1)
        grad_cross = grad_cross + grad_mix[:, :CHUNK] * first + grad_mix[:, CHUNK:] * second
        both = contract(mix, gy_pair, 0, 0)
        grad_s[8 : 8 + CHUNK, cols] = jnp.where(lane < 64, both[:CHUNK], both[CHUNK:])
    inner = grad_s[8 : 8 + CHUNK, :DI]
    skip = skip_ref[...]
    cross_low = grad_cross.astype(BF16)
    grad_c = grad_c + contract(cross_low, b_rows, 1, 0)
    grad_b = grad_b + contract(cross_low, c_rows, 0, 0)
    narrow = lambda values: jnp.concatenate(
        [gather_heads(values, spread_first), jnp.zeros((values.shape[0], 96), F32)], axis=1
    )
    query_part = narrow(gy_float * (y_ref[0] - skip * xs_float))
    key_inner = narrow(xs_float * inner)
    key_end = narrow(xs_float * from_end)
    extra = jnp.sum(key_end, axis=0, keepdims=True) + gain * narrow(
        jnp.broadcast_to(dgain_row, (8, DI))
    )[0:1, :]
    upper = (~lower_mask() | (lax.broadcasted_iota(jnp.int32, (CHUNK, CHUNK), 0) == lanes((CHUNK, CHUNK))))
    grad_log = product_exact(upper.astype(BF16), query_part - key_inner - key_end) + extra
    sig = jax.nn.sigmoid(raw)
    ratio = jnp.where(raw < -15.0, 1.0, sig / jnp.maximum(step, 1e-30))
    grad_rate = (key_inner + key_end) * ratio - grad_log * jnp.exp(head_ref[0:1, :]) * sig
    dhead_s[0:1, :] += jnp.sum(grad_log * log_decay, axis=0, keepdims=True)
    dhead_s[1:2, :] += jnp.sum(grad_rate, axis=0, keepdims=True)
    total = conv_total(ext_s, token, taps_ref, shift_ref)
    grad_act = jnp.concatenate([inner + from_end + skip * gy_float, grad_b, grad_c], axis=1)
    csig = jax.nn.sigmoid(total)
    grad_total = grad_act * (csig * (1.0 + total * (1.0 - csig)))
    dconv_s[KC : KC + 1, :] += jnp.sum(grad_total, axis=0, keepdims=True)
    grad_s[0:8, :] = jnp.zeros((8, CC), F32)
    grad_s[8 : 8 + CHUNK, :] = grad_total * taps_ref[KC - 1 : KC, :]
    dconv_s[KC - 1 : KC, :] += jnp.sum(grad_total * ext_s[8 : 8 + CHUNK, :], axis=0, keepdims=True)
    for tap in range(KC - 1):
        part = grad_total * token[:, TAP_LANES + tap : TAP_LANES + tap + 1]
        dconv_s[tap : tap + 1, :] += jnp.sum(
            part * ext_s[5 + tap : 5 + tap + CHUNK, :], axis=0, keepdims=True
        )
        grad_s[5 + tap : 5 + tap + CHUNK, :] += part * taps_ref[tap : tap + 1, :]
    grad_s[CHUNK : CHUNK + 8, :] += carry_s[...]
    carry_s[...] = grad_s[0:8, :]
    dcr_ref[0, :, :CC] = grad_s[8 : 8 + CHUNK, :].astype(BF16)
    dcr_ref[0, :, CC:] = grad_rate.astype(BF16)

    @pl.when(step_index == last_step)
    def _():
        drim_ref[0] = carry_s[...]

    dconv_ref[...] = dconv_s[...]
    dhead_ref[...] = dhead_s[...]


def mixer_call(kernel, name, seq, chunks, reverse, inputs, outputs, scratch, earlier):
    place = (lambda c: chunks - 1 - c) if reverse else (lambda c: c)
    kinds = {
        "block": lambda array, at: pl.BlockSpec(
            (1, CHUNK, array.shape[2]), lambda c: (at, place(c), 0)
        ),
        "chunk": lambda array, at: pl.BlockSpec(
            (1, 1) + array.shape[2:], lambda c: (at, place(c), 0, 0)
        ),
        "token": lambda array, at: pl.BlockSpec((1, 8, CHUNK), lambda c: (at, 0, place(c))),
        "seq": lambda array, at: pl.BlockSpec((1,) + array.shape[1:], lambda c: (at, 0, 0)),
        "own": lambda array, at: pl.BlockSpec((1,) + array.shape[1:], lambda c: (0, 0, 0)),
        "fixed": lambda array, at: pl.BlockSpec(array.shape, lambda c: (0, 0)),
        "halo": lambda array, at: pl.BlockSpec(
            (1, 16, array.shape[2]),
            lambda c: (at, jnp.maximum(place(c) * (CHUNK // 16) - 1, 0), 0),
        ),
    }
    arrays = [array for _, array in inputs]
    in_specs = [kinds[kind](array, seq) for kind, array in inputs]
    out_specs = [kinds[kind](shape, seq) for kind, shape in outputs]
    count = len(inputs)
    aliases, kept = {}, 0
    if earlier is not None:
        shared = [i for i, (kind, _) in enumerate(outputs) if kind in ("block", "chunk")]
        aliases = {count + i: out for i, out in enumerate(shared)}
        arrays += [earlier[out] for out in shared]
        in_specs += [pl.BlockSpec(memory_space=pl.ANY)] * len(shared)
        kept = len(shared)

    def run(*refs):
        kernel(*refs[:count], *refs[count + kept :])

    return pl.pallas_call(
        run,
        grid=(chunks,),
        in_specs=in_specs,
        out_specs=out_specs,
        out_shape=[shape for _, shape in outputs],
        scratch_shapes=[pltpu.VMEM(shape, F32) for shape in scratch],
        input_output_aliases=aliases,
        compiler_params=pltpu.CompilerParams(vmem_limit_bytes=VMEM_BYTES),
        name=name,
    )(*arrays)


def mixer_scan(seq, earlier, cr, rim, token, heads, taps, shift, spread):
    seqs, span, _ = cr.shape
    chunks = span // CHUNK
    return mixer_call(
        mixer_scan_kernel, "mixer_scan", seq, chunks, False,
        [
            ("block", cr), ("seq", rim), ("token", token), ("fixed", heads), ("fixed", taps),
            ("fixed", shift), ("fixed", spread),
        ],
        [
            ("block", jax.ShapeDtypeStruct((seqs, span, CC), BF16)),
            ("chunk", jax.ShapeDtypeStruct((seqs, chunks, NS, DI), BF16)),
            ("chunk", jax.ShapeDtypeStruct((seqs, chunks, 8, 128), F32)),
            ("own", jax.ShapeDtypeStruct((1, NS, DI), BF16)),
            ("own", jax.ShapeDtypeStruct((1, 8, DI), F32)),
            ("block", jax.ShapeDtypeStruct((seqs, span, 6 * 128), F32)),
        ],
        [(CHUNK + 8, CC), (NS, DI), (8, 128)],
        earlier,
    )


def mixer_out(seq, earlier, gate, terms, act, token, states, gains, state, skip, gain, spread):
    seqs, span, _ = gate.shape
    return mixer_call(
        mixer_out_kernel, "mixer_out", seq, span // CHUNK, False,
        [
            ("block", gate), ("block", terms), ("block", act), ("token", token), ("chunk", states),
            ("chunk", gains), ("own", state), ("fixed", skip),
            ("fixed", gain), ("fixed", spread),
        ],
        [
            ("block", jax.ShapeDtypeStruct((seqs, span, DI), F32)),
            ("block", jax.ShapeDtypeStruct((seqs, span, DI), BF16)),
        ],
        [],
        earlier,
    )


def mixer_gate_back(
    seq, earlier, gmix, y, gate, terms, act, gains, gain, spread
):
    seqs, span, _ = gate.shape
    chunks = span // CHUNK
    return mixer_call(
        mixer_gate_back_kernel, "mixer_gate_back", seq, chunks, True,
        [
            ("block", gmix), ("block", y), ("block", gate), ("block", terms), ("block", act), ("chunk", gains),
            ("fixed", gain), ("fixed", spread),
        ],
        [
            ("block", jax.ShapeDtypeStruct((seqs, span, DI), BF16)),
            ("block", jax.ShapeDtypeStruct((seqs, span, DI), BF16)),
            ("chunk", jax.ShapeDtypeStruct((seqs, chunks, NS, DI), BF16)),
            ("chunk", jax.ShapeDtypeStruct((seqs, chunks, 8, 128), F32)),
            ("own", jax.ShapeDtypeStruct((1, NS, DI), BF16)),
            ("fixed", jax.ShapeDtypeStruct((8, DI), F32)),
            ("fixed", jax.ShapeDtypeStruct((8, DI), F32)),
        ],
        [(NS, DI), (8, 128), (8, DI), (8, DI)],
        earlier,
    )


def mixer_back(
    seq, earlier, gy, y, terms, cr, rim, act, token, states, gains, state, gstates, ggains,
    gstate, heads, skip, taps, shift, spread, spread_first,
):
    seqs, span, width = cr.shape
    return mixer_call(
        mixer_back_kernel, "mixer_back", seq, span // CHUNK, True,
        [
            ("block", gy), ("block", y), ("block", terms), ("block", cr), ("halo", cr),
            ("seq", rim), ("block", act), ("token", token), ("chunk", states), ("chunk", gains),
            ("own", state), ("chunk", gstates), ("chunk", ggains), ("own", gstate),
            ("fixed", heads), ("fixed", skip), ("fixed", taps), ("fixed", shift),
            ("fixed", spread), ("fixed", spread_first),
        ],
        [
            ("block", jax.ShapeDtypeStruct((seqs, span, width), BF16)),
            ("own", jax.ShapeDtypeStruct((1, 8, CC), F32)),
            ("fixed", jax.ShapeDtypeStruct((8, CC), F32)),
            ("fixed", jax.ShapeDtypeStruct((8, 128), F32)),
        ],
        [(CHUNK + 8, CC), (CHUNK + 8, CC), (8, CC), (8, CC), (8, 128)],
        earlier,
    )


def token_table(seg_own, seg_rim):
    seqs, span = seg_own.shape
    extended = jnp.concatenate([seg_rim, seg_own], axis=1)
    matches = [extended[:, tap : tap + span] == seg_own for tap in range(KC - 1)]
    by_chunk = seg_own.reshape(seqs, -1, CHUNK)
    last = by_chunk[:, :, -1:]
    before = jnp.concatenate([seg_rim[:, None, -1:], last[:, :-1]], axis=1)
    spare = jnp.zeros((seqs, span), F32)
    rows = [match.astype(F32) for match in matches] + [
        spare,
        (by_chunk == before).reshape(seqs, span).astype(F32),
        (by_chunk == last).reshape(seqs, span).astype(F32),
        seg_own.astype(F32),
        spare,
    ]
    return jnp.stack(rows, axis=1)


def from_behind(block, axis, distance):
    devices = range(lax.axis_size(axis))
    route = [(i - distance, i) for i in devices if i - distance in devices]
    return lax.ppermute(block, axis, route)


def after(value, *earlier):
    return lax.optimization_barrier((value, earlier))[0]


class Chain:
    def __init__(self, local, gain, reverse):
        self.local, self.gain, self.reverse = local, gain, reverse
        self.state, self.hop, self.flying = jnp.zeros(local.shape, BF16), 0, None
        self.count, self.place = lax.axis_size("ctx"), lax.axis_index("ctx")

    def send(self, *earlier):
        if self.hop == self.count - 1:
            return
        source = self.count - 1 - self.hop if self.reverse else self.hop
        target = source - 1 if self.reverse else source + 1
        sent = self.local
        if self.hop:
            sent = (self.gain * self.state.astype(F32) + sent.astype(F32)).astype(BF16)
        if earlier:
            sent = after(sent, *earlier)
        self.flying = (lax.ppermute(sent, "ctx", [(source, target)]), target)
        self.hop += 1

    def take(self):
        if self.flying is None:
            return
        received, target = self.flying
        self.state, self.flying = jnp.where(self.place == target, received, self.state), None

    def finish(self):
        self.take()
        while self.hop < self.count - 1:
            self.send()
            self.take()
        return self.state


def sum_everywhere(values, axes):
    for axis in axes:
        count = lax.axis_size(axis)
        copies = jnp.broadcast_to(values[None], (count,) + values.shape)
        values = jnp.sum(lax.all_to_all(copies, axis, 0, 0, tiled=True), axis=0)
    return values


def scatter_all(grad, *late):
    count, place = lax.axis_size("ctx"), lax.axis_index("ctx")
    devices, me = lax.axis_size("dp"), lax.axis_index("dp")
    bits = devices.bit_length() - 1
    part = grad.reshape((2,) * bits + (count, -1, grad.shape[1]))
    for bit in [0] + list(range(bits - 1, 0, -1)):
        at = 0 if bit else bits - 1
        first, second = (lax.index_in_dim(part, side, at, False) for side in range(2))
        low = ((me >> bit) & 1) == 0
        sent = jnp.where(low, second, first).astype(BF16)
        received = lax.ppermute(sent, "dp", [(i, i ^ (1 << bit)) for i in range(devices)])
        part = jnp.where(low, first, second).astype(F32) + received.astype(F32)
    relative = lax.dynamic_slice_in_dim(jnp.concatenate([part, part]), place, count, 0)
    total, rounded = relative[0], after(relative.astype(BF16), *late)
    for d in range(1, count):
        route = [(i, (i + d) % count) for i in range(count)]
        total = total + lax.ppermute(rounded[d], "ctx", route).astype(F32)
    return total


def rms_scale(values, gain_vec):
    return (
        values * lax.rsqrt(jnp.mean(values * values, axis=-1, keepdims=True) + EPSILON) * gain_vec
    )


def silu_product(gate_lin, up_lin):
    return jax.nn.silu(gate_lin) * up_lin


def body(
    layer_input, segments, positions, gain_one, w_in, conv_w, conv_b, head_params, gain_m, w_out,
    w_q, w_k, w_v, w_o, gain_two, w_gate, w_up, w_down, cotangent,
):
    seqs, span, width = layer_input.shape
    rows = seqs * span
    axes = ("dp", "ctx")
    own_rows = w_q.shape[0]
    q_width, kv_width = QH * HD, 2 * KVH * HD
    low_dot = lambda a, b: jnp.dot(a, b, preferred_element_type=F32)

    small_parts = [gain_one, gain_two, gain_m, conv_b, conv_w.reshape(-1)]
    small_sizes = [part.shape[0] for part in small_parts]
    slots = own_rows * 128
    small_block = jnp.concatenate(small_parts, axis=0)
    small_block = jnp.pad(small_block, (0, slots - sum(small_sizes))).reshape(own_rows, 128)
    w_kv = jnp.stack(
        [w_k.reshape(own_rows, KVH, HD), w_v.reshape(own_rows, KVH, HD)], axis=2
    ).reshape(own_rows, kv_width)
    count = lax.axis_size("ctx")
    exchange = lambda blocks: lax.all_to_all(blocks, "ctx", 0, 0, tiled=True)
    copies = lambda block: jnp.broadcast_to(block[None], (count,) + block.shape)
    gather = lambda part: lax.all_gather(part, "dp", axis=0, tiled=True)
    w_cr = jnp.pad(w_in[:, DI:], ((0, 0), (0, CR - (w_in.shape[1] - DI))))
    first = jnp.concatenate([w_cr, w_q, w_kv, small_block, w_in[:, :DI]], axis=1)
    first_part = lax.all_gather(first, "ctx", axis=0, tiled=True)
    turned_o = w_o.T
    half_rows, ff = own_rows // 2, w_gate.shape[1]

    def fold(block, cut):
        return jnp.concatenate([block[..., :half_rows, cut:], block[..., half_rows:, cut:]], axis=-1)

    def unfold(block):
        half = block.shape[-1] // 2
        return jnp.concatenate([block[..., :half], block[..., half:]], axis=-2)

    rest = [w_down, w_out, fold(turned_o, 0)]
    for matrix in (w_gate, w_up):
        rest += [matrix[:, at : at + width] for at in range(0, ff, width)]
    rest_sizes = [part.shape[0] for part in rest]
    place = lax.axis_index("ctx")
    span_start = place * span
    seg_own = lax.dynamic_slice_in_dim(segments, span_start, span, 1)
    seg_rim = jnp.where(
        place > 0,
        lax.dynamic_slice_in_dim(segments, jnp.maximum(span_start - (KC - 1), 0), KC - 1, 1),
        -1,
    )
    token = token_table(seg_own, seg_rim)
    bounds = attention_bounds(segments, seg_own, span_start)
    segk, segq = segments[:, :, None], seg_own[:, None, :]
    cosine, sine = rope_tables(positions)
    heads = jnp.pad(head_params, ((0, 5), (0, 128 - MH)))
    skip = jnp.repeat(head_params[2], MP)[None]
    spread, spread_first = spread_matrix(), spread_first_matrix()

    tokens = layer_input.reshape(rows, width)
    small = (token, bounds, segk, segq, cosine, sine, heads, skip, spread, spread_first)
    rest_copies = copies(jnp.concatenate(rest, axis=0))
    first_all = gather(after(first_part, small, rest_copies))
    cosine, sine = cosine.reshape(rows, 128), sine.reshape(rows, 128)
    rest_part = exchange(after(rest_copies, first_part))
    rest_all = gather(rest_part.reshape(-1, width)).reshape(-1, sum(rest_sizes), width)
    cuts, at = [], 0
    for size in rest_sizes:
        cuts.append(rest_all[:, at : at + size])
        at += size
    w_down_all, w_out_all = cuts[0].reshape(-1, width), cuts[1].reshape(-1, width)
    w_o_all = unfold(cuts[2]).reshape(width, q_width)
    w_gates = first_all[:, FIRST:]
    w_gu_all = jnp.concatenate([cut.reshape(width, width) for cut in cuts[3:]], axis=1)
    small_all = first_all[:, FIRST - 128 : FIRST].reshape(-1, slots).astype(F32)
    parts, at = [], 0
    for size in small_sizes:
        parts.append(small_all[:, at : at + size])
        at += size
    gain1_all, gain2_all, gain_m_all, shift_all = [part.reshape(1, -1) for part in parts[:4]]
    taps_all = jnp.swapaxes(parts[4].reshape(-1, KC, small_sizes[3]), 0, 1).reshape(KC, CC)
    taps_all = jnp.pad(taps_all, ((0, 8 - KC), (0, 0)))


    hidden, cr, q, kv = project(tokens, gain1_all, first_all, cosine, sine, count)
    q = q.reshape(seqs, span, q_width)
    kv = kv.reshape(count, seqs, span, kv_width)
    cr = cr.reshape(seqs, span, CR)
    rim = from_behind(cr[:, span - (KC - 1) :, :CC], "ctx", 1)
    kv_all = exchange(after(kv, rim))
    rim = jnp.pad(rim, ((0, 0), (8 - (KC - 1), 0), (0, 0)))
    scanned, chains, wide_gains = None, [], []
    for seq in range(seqs):
        scanned = mixer_scan(
            seq, scanned, cr, rim, token, heads, taps_all,
            shift_all, spread,
        )
        wide_gains.append(scanned[4][:, :1])
        chains.append(Chain(scanned[3], wide_gains[seq], False))
        chains[seq].send()
    act, states, gains, terms = scanned[0], scanned[1], scanned[2], scanned[5]
    for chain in chains:
        chain.take()
        chain.send()
    atts, lses, mixed = [], [], None
    mark = (act, w_down_all, w_out_all, w_o_all, w_gu_all)
    for seq in range(seqs):
        att, lse = attend(seq, bounds, after(q, mark), kv_all, segk, segq)
        atts.append(att)
        lses.append(lse)
        chains[seq].take()
        chains[seq].send(lse)
        mark = lse
    gate = low_dot(hidden, w_gates).astype(BF16).reshape(seqs, span, DI)
    states_in = []
    for seq in range(seqs):
        states_in.append(chains[seq].finish())
        mixed = mixer_out(
            seq, mixed, gate, terms, act, token, states, gains, states_in[seq], skip, gain_m_all,
            spread,
        )
    mixer_y, mixer_in = mixed
    mixer_in = mixer_in.reshape(rows, DI)
    att_rows = jnp.concatenate(atts, axis=0).reshape(rows, q_width)
    middle = (
        tokens.astype(F32)
        + low_dot(mixer_in, w_out_all)
        + jnp.einsum("ra,da->rd", att_rows, w_o_all, preferred_element_type=F32)
    )
    normed_mid, norm2_pull = jax.vjp(rms_scale, middle, gain2_all)
    normed_two = normed_mid.astype(BF16)
    gate_up = low_dot(normed_two, w_gu_all).astype(BF16)
    act_float, act_pull = jax.vjp(
        silu_product, gate_up[:, :ff].astype(F32), gate_up[:, ff:].astype(F32)
    )
    act_rows = act_float.astype(BF16)
    def scatter(grad):
        return lax.psum_scatter(grad, "dp", scatter_dimension=0, tiled=True)

    def weight_grad(left, right):
        return jnp.einsum("ri,ro->io", left, right, preferred_element_type=F32).astype(BF16)

    def back_dot(grad, weight):
        return jnp.einsum("ro,io->ri", grad, weight, preferred_element_type=F32)

    cot_rows = cotangent.reshape(rows, width)
    grad_down = weight_grad(act_rows, cot_rows)
    grad_gate_up = jnp.concatenate(act_pull(back_dot(cot_rows, w_down_all)), axis=1).astype(BF16)
    grad_wgu = weight_grad(normed_two, grad_gate_up)
    grad_normed = back_dot(grad_gate_up, w_gu_all)
    grad_normed, grad_down, grad_wgu = lax.optimization_barrier((grad_normed, grad_down, grad_wgu))
    part_gu = scatter(grad_wgu)
    grad_mid_norm, grad_gain_second = norm2_pull(grad_normed)
    grad_middle = cot_rows.astype(F32) + grad_mid_norm
    grad_mid_low = grad_middle.astype(BF16)
    grad_wout = weight_grad(mixer_in, grad_mid_low)
    grad_wo = weight_grad(grad_mid_low, att_rows)
    grad_mixer_in = back_dot(grad_mid_low, w_out_all).astype(BF16).reshape(seqs, span, DI)
    grad_att = low_dot(grad_mid_low, w_o_all).astype(BF16).reshape(seqs, span, q_width)
    grad_mixer_in, grad_att, grad_wout, grad_wo = lax.optimization_barrier(
        (grad_mixer_in, grad_att, grad_wout, grad_wo)
    )
    grad_wo = grad_wo.reshape(-1, own_rows, q_width)
    gated, chains, grad_gain_mix, grad_skip = None, [], 0.0, 0.0
    for seq in range(seqs):
        gated = mixer_gate_back(
            seq, gated, grad_mixer_in, mixer_y, gate, terms, act, gains, gain_m_all, spread
        )
        grad_gain_mix, grad_skip = grad_gain_mix + gated[5], grad_skip + gated[6]
        chains.append(Chain(gated[4], wide_gains[seq], True))
        chains[seq].send()
    grad_y, grad_gate, gstates, ggains = gated[:4]
    chains[0].take()
    chains[1 % seqs].take()
    grad_wgates = weight_grad(after(hidden, chains[0].state), grad_gate.reshape(rows, DI)).reshape(-1, own_rows, DI)
    blocks = grad_wo.shape[0]
    grad_rest = jnp.concatenate(
        [
            after(grad_down, chains[0].state, chains[1 % seqs].state).reshape(blocks, -1, width), grad_wout.reshape(blocks, -1, width),
            fold(grad_wo, 0), grad_wgates[..., :width], fold(grad_wgates, width),
        ],
        axis=1,
    )
    part_rest = scatter(grad_rest.reshape(-1, width))
    cos3, sin3 = cosine.reshape(seqs, span, 128), sine.reshape(seqs, span, 128)
    dqs, dkvs = [], []
    for seq in range(seqs):
        if seq < 2:
            for chain in chains:
                chain.take()
                chain.send(*dqs[-1:])
        mark = dqs[-1:] + [chain.state for chain in chains] + ([part_gu] if seq == seqs - 1 else [] if seq else [grad_rest])
        dq, dkv = attend_back(
            seq, bounds, after(q, grad_y, *mark), kv_all, segk,
            segq, atts[seq], grad_att, lses[seq], cos3, sin3,
        )
        dqs.append(dq)
        dkvs.append(dkv)
    dq = jnp.concatenate(dqs, axis=0)
    last, rims, grad_conv, grad_heads = None, [], 0.0, 0.0
    waits = [(grad_rest, part_gu)] + [()] * (seqs - 1)
    finals = [chain.finish() for chain in chains]
    dkv_all = exchange(after(jnp.concatenate(dkvs, axis=1), *finals))
    waits[1 % seqs] += tuple(finals)
    for seq in range(seqs):
        gstate = finals[seq]
        if seq == 0:
            gu_blocks = part_gu.reshape(count, own_rows, 2 * ff)
            parts = [after(part_rest, *rims).reshape(count, -1, width)]
            parts += [gu_blocks[..., at : at + width] for at in range(0, 2 * ff, width)]
            rest_low = jnp.concatenate(parts, axis=1).reshape(-1, width)
            waits[seq] += (rest_low,)
        last = mixer_back(
            seq, last, after(grad_y, dqs[-1], *waits[seq]), mixer_y, terms, cr, rim, act, token, states,
            gains, states_in[seq], gstates, ggains, gstate, heads, skip, taps_all, shift_all,
            spread, spread_first,
        )
        rims.append(last[1])
        grad_conv, grad_heads = grad_conv + last[2], grad_heads + last[3]
    grad_cr, grad_rim = last[0], jnp.concatenate(rims, axis=0)
    back_rim = from_behind(grad_rim[:, 8 - (KC - 1) :].astype(BF16), "ctx", -1)
    edge = grad_cr[:, span - (KC - 1) :, :CC].astype(F32) + back_rim.astype(F32)
    grad_cr = lax.dynamic_update_slice(
        grad_cr, after(edge.astype(BF16), dkv_all), (0, span - (KC - 1), 0)
    ).reshape(rows, CR)
    rest_out = lax.psum_scatter(rest_low, "ctx", scatter_dimension=0, tiled=True).astype(F32)
    grad_wcr = weight_grad(hidden, grad_cr)
    grad_wq = weight_grad(hidden, dq.reshape(rows, q_width))
    part_cr = scatter(jnp.concatenate([grad_wcr, grad_wq], axis=1))
    layer_result = (middle + low_dot(after(act_rows, part_cr), w_down_all)).astype(BF16)
    out_cr = lax.psum_scatter(part_cr, "ctx", scatter_dimension=0, tiled=True).astype(F32)
    grad_tokens, grad_kv, grad_gain_first = finish(
        tokens, gain1_all, grad_gate.reshape(rows, DI), after(grad_cr, grad_wcr, rest_out),
        dq.reshape(rows, q_width), dkv_all, cosine, sine, grad_middle, first_all,
    )
    grad_wfirst = weight_grad(hidden, grad_kv)
    grad_gain_first = grad_gain_first[0]

    devices = first_all.shape[0] // own_rows
    small_grads = jnp.concatenate(
        [
            grad_gain_first.reshape(devices, -1),
            grad_gain_second.reshape(devices, -1),
            grad_gain_mix[0].reshape(devices, -1),
            grad_conv[KC].reshape(devices, -1),
            jnp.swapaxes(grad_conv[:KC].reshape(KC, devices, -1), 0, 1).reshape(devices, -1),
        ],
        axis=1,
    )
    small_grads = jnp.pad(small_grads, ((0, 0), (0, slots - small_grads.shape[1])))
    out_first = scatter_all(
        jnp.concatenate([grad_wfirst, small_grads.reshape(-1, 128).astype(BF16)], axis=1), part_cr
    )
    rest_sizes = rest_sizes[:3] + [own_rows, half_rows] + rest_sizes[3:]
    outs, at = [], 0
    for size in rest_sizes:
        outs.append(rest_out[at : at + size])
        at += size
    out_down, out_wout = outs[0], outs[1]
    out_wo = unfold(outs[2])
    out_win = jnp.concatenate(
        [outs[3], unfold(outs[4]), out_cr[:, : w_in.shape[1] - DI]], axis=1
    )
    halves = ff // width
    out_gate = jnp.concatenate(outs[5 : 5 + halves], axis=1)
    out_up = jnp.concatenate(outs[5 + halves :], axis=1)
    out_small = out_first[:, kv_width:].reshape(-1)
    pieces, at = [], 0
    for size in small_sizes:
        pieces.append(out_small[at : at + size])
        at += size
    out_kv = out_first[:, :kv_width].reshape(own_rows, KVH, 2, HD)
    head_grad = sum_everywhere(
        jnp.concatenate(
            [
                after(grad_heads, grad_kv)[:2, :MH],
                grad_skip[0].reshape(MH, MP).sum(axis=1)[None],
            ],
            axis=0,
        ),
        axes,
    )
    return (
        layer_result.reshape(layer_input.shape),
        grad_tokens.reshape(layer_input.shape),
        pieces[0],
        out_win,
        pieces[4].reshape(KC, -1),
        pieces[3],
        head_grad,
        pieces[2],
        out_wout,
        out_cr[:, CR:],
        out_kv[:, :, 0].reshape(own_rows, -1),
        out_kv[:, :, 1].reshape(own_rows, -1),
        out_wo.T,
        pieces[1],
        out_gate,
        out_up,
        out_down,
    )


def solution(mesh):
    in_specs = (
        P("dp", "ctx", None),
        P("dp", None),
        P("dp", "ctx"),
        P(("dp", "ctx")),
        P(("dp", "ctx"), None),
        P(None, ("dp", "ctx")),
        P(("dp", "ctx")),
        P(),
        P(("dp", "ctx")),
        P(("dp", "ctx"), None),
        P(("dp", "ctx"), None),
        P(("dp", "ctx"), None),
        P(("dp", "ctx"), None),
        P(None, ("dp", "ctx")),
        P(("dp", "ctx")),
        P(("dp", "ctx"), None),
        P(("dp", "ctx"), None),
        P(("dp", "ctx"), None),
        P("dp", "ctx", None),
    )
    out_specs = (
        P("dp", "ctx", None),
        P("dp", "ctx", None),
        P(("dp", "ctx")),
        P(("dp", "ctx"), None),
        P(None, ("dp", "ctx")),
        P(("dp", "ctx")),
        P(),
        P(("dp", "ctx")),
        P(("dp", "ctx"), None),
        P(("dp", "ctx"), None),
        P(("dp", "ctx"), None),
        P(("dp", "ctx"), None),
        P(None, ("dp", "ctx")),
        P(("dp", "ctx")),
        P(("dp", "ctx"), None),
        P(("dp", "ctx"), None),
        P(("dp", "ctx"), None),
    )
    return jax.shard_map(body, mesh=mesh, in_specs=in_specs, out_specs=out_specs, check_vma=False)
```
